32 devices in a mesh: wide: 8 (over z, y), narrow: 4 (over x, core).
Axes of the slice: x: 2, y: 2, z: 4, core: 2. Of those that a mesh axis runs over, the one named last changes fastest.
Arguments:
- clips: bfloat16 [128, 16, 64, 768], P(('wide', 'narrow')), may hold values from -6 to 6
- t_emb: bfloat16 [128, 2, 768], P(('wide', 'narrow')), may hold values from -6 to 6
- lengths: int32 [128], P('wide'), may hold values from 1 to 16, as said below
- task: int32 [128, 16], P('wide'), may hold values 0 or 1
- w_mod: bfloat16 [768, 6912], P(('wide', 'narrow')), may hold values from -0.21875 to 0.21875
- b_mod: bfloat16 [6912], P(('wide', 'narrow')), may hold values from -3 to 3
- w_qkv_s: bfloat16 [768, 2304], P(('wide', 'narrow')), may hold values from -0.21875 to 0.21875
- w_o_s: bfloat16 [768, 768], P(('wide', 'narrow')), may hold values from -0.625 to 0.625
- b_o_s: bfloat16 [768], P(('wide', 'narrow')), may hold values from -3 to 3
- w_qkv_t: bfloat16 [768, 2304], P(('wide', 'narrow')), may hold values from -0.21875 to 0.21875
- w_o_t: bfloat16 [768, 768], P(('wide', 'narrow')), may hold values from -0.375 to 0.375
- b_o_t: bfloat16 [768], P(('wide', 'narrow')), may hold values from -3 to 3
- w_in: bfloat16 [768, 3072], P(('wide', 'narrow')), may hold values from -0.21875 to 0.21875
- b_in: bfloat16 [3072], P(('wide', 'narrow')), may hold values from -3 to 3
- w_out: bfloat16 [3072, 768], P(('wide', 'narrow')), may hold values from -0.109375 to 0.109375
- b_out: bfloat16 [768], P(('wide', 'narrow')), may hold values from -3 to 3
- cotangent: bfloat16 [128, 16, 64, 768], P(('wide', 'narrow')), may hold values from -6 to 6
Outputs:
- layer_out: bfloat16 [128, 16, 64, 768], P(('wide', 'narrow'))
- grad_clips: bfloat16 [128, 16, 64, 768], P(('wide', 'narrow'))
- grad_t_emb: bfloat16 [128, 2, 768], P(('wide', 'narrow'))
- grad_w_mod: float32 [768, 6912], P(('wide', 'narrow'))
- grad_b_mod: float32 [6912], P(('wide', 'narrow'))
- grad_w_qkv_s: float32 [768, 2304], P(('wide', 'narrow'))
- grad_w_o_s: float32 [768, 768], P(('wide', 'narrow'))
- grad_b_o_s: float32 [768], P(('wide', 'narrow'))
- grad_w_qkv_t: float32 [768, 2304], P(('wide', 'narrow'))
- grad_w_o_t: float32 [768, 768], P(('wide', 'narrow'))
- grad_b_o_t: float32 [768], P(('wide', 'narrow'))
- grad_w_in: float32 [768, 3072], P(('wide', 'narrow'))
- grad_b_in: float32 [3072], P(('wide', 'narrow'))
- grad_w_out: float32 [3072, 768], P(('wide', 'narrow'))
- grad_b_out: float32 [768], P(('wide', 'narrow'))
The draws below stay inside these ranges and needn't reach their ends.
Inputs may be any that keep to these rules, and one draw needn't show every extreme that they name: `lengths`: write clip i as g * 4 * 4 + s * 4 + c with s, c below 4. For every g and every k, the clips with (s + c) % 4 == k hold exactly 32 live frames together.
All inputs are finite; a program needn't handle non-finite values. No bound on the sum of `task` on one device may be relied on, other than what follows from the above.
Results may differ from the reference program's by a relative error of at most 0.025.
The reference program's roundings to bfloat16 on the way count: a program that leaves them out, or rounds other values in their place, can miss the bound.
Values may be sent and summed in bfloat16 or wider, within the bound.
A program may use at most 384 MiB of HBM per device.

```python
from functools import partial
import jax
import jax.numpy as jnp
from jax import lax

D = 768
HEADS = 12
HEAD = 64
FF = 3072
FR = 16
PATCHES = 64
CLIPS_DEV = 4
CLIPS = 128


def draw_lengths(key, part):
    width = CLIPS_DEV
    groups = CLIPS // (width * width)
    key_heavy, key_parts = jax.random.split(key)
    heavy = jax.random.randint(key_heavy, (groups, 1, 1), 0, width)
    weights = jax.random.randint(key_parts, (groups, width, width), 1, 5)
    source = jnp.arange(width)[None, None, :]
    is_heavy = source == heavy
    light = jnp.where(is_heavy, 0, weights)
    total = jnp.sum(light, axis=2, keepdims=True)
    share = 1 + light * (FR - (width - 1)) // total
    rest = FR - jnp.sum(jnp.where(is_heavy, 0, share), axis=2, keepdims=True)
    first_light = jnp.where(heavy == 0, 1, 0)
    share = jnp.where(is_heavy, FR, share + jnp.where(source == first_light, rest, 0))
    diagonal = (jnp.arange(width)[:, None] + jnp.arange(width)[None, :]) % width
    by_clip = share[:, diagonal, jnp.arange(width)[:, None]]
    return by_clip.reshape(groups * width * width).astype(jnp.int32)


def with_ends(values, own_key, smallest, top_value):
    index_at = [jax.random.randint(jax.random.fold_in(own_key, axis), (), 0, length) for axis, length in enumerate(values.shape)]
    widest = values.shape.index(max(values.shape))
    beside = index_at[:widest] + [(index_at[widest] + 1) % values.shape[widest]] + index_at[widest + 1:]
    return values.at[tuple(index_at)].set(smallest).at[tuple(beside)].set(top_value)


def block_scale(own_key, dims, cuts, least, high):
    def one(dim, shards_of):
        steps = jax.random.uniform(jax.random.fold_in(jax.random.fold_in(own_key, 6), dim), (shards_of,), jnp.float32, least / len(cuts), high / len(cuts))
        return jnp.repeat(jnp.exp(steps), dims[dim] // shards_of).reshape((-1,) + (1,) * (len(dims) - dim - 1))

    factor_of = one(*cuts[0])
    for cut in cuts[1:]:
        factor_of = factor_of * one(*cut)
    return factor_of


def bell_draw(stream_key, extent, deviation, limit, cuts=(), held_as=jnp.bfloat16):
    values = deviation * jax.random.normal(stream_key, extent, jnp.float32)
    if cuts:
        values = values * block_scale(stream_key, extent, cuts, -0.22, 0.18)
    return jnp.clip(values, -limit, limit).astype(held_as)


def setup_inputs(seed: int = 0) -> dict:
    key_list = jax.random.split(jax.random.key(seed), 18)
    return {
        "clips": bell_draw(key_list[0], (CLIPS, FR, PATCHES, D), 1.0, 6.0, ((0, 32),)),
        "t_emb": bell_draw(key_list[1], (CLIPS, 2, D), 1.0, 6.0, ((0, 32),)),
        "lengths": draw_lengths(jax.random.fold_in(key_list[17], 71), 0),
        "task": with_ends((jax.random.randint(key_list[3], (CLIPS, FR), 0, 2) < 1).astype(jnp.int32), jax.random.fold_in(key_list[3], 1), 0, 1),
        "w_mod": bell_draw(key_list[4], (D, 9 * D), D ** -0.5, 0.21875, ((0, 32),)),
        "b_mod": bell_draw(key_list[5], (9 * D,), 0.5, 3.0, ((0, 32),)),
        "w_qkv_s": bell_draw(key_list[6], (D, 3 * D), D ** -0.5, 0.21875, ((0, 32),)),
        "w_o_s": bell_draw(key_list[7], (D, D), (D // 8) ** -0.5, 0.625, ((0, 32),)),
        "b_o_s": bell_draw(key_list[8], (D,), 0.5, 3.0, ((0, 32),)),
        "w_qkv_t": bell_draw(key_list[9], (D, 3 * D), D ** -0.5, 0.21875, ((0, 32),)),
        "w_o_t": bell_draw(key_list[10], (D, D), (D // 3) ** -0.5, 0.375, ((0, 32),)),
        "b_o_t": bell_draw(key_list[11], (D,), 0.5, 3.0, ((0, 32),)),
        "w_in": bell_draw(key_list[12], (D, FF), D ** -0.5, 0.21875, ((0, 32),)),
        "b_in": bell_draw(key_list[13], (FF,), 0.5, 3.0, ((0, 32),)),
        "w_out": bell_draw(key_list[14], (FF, D), FF ** -0.5, 0.109375, ((0, 32),)),
        "b_out": bell_draw(key_list[15], (D,), 0.5, 3.0, ((0, 32),)),
        "cotangent": bell_draw(key_list[16], (CLIPS, FR, PATCHES, D), 1.0, 6.0, ((0, 32),)),
    }


@jax.custom_vjp
def low(v):
    return lax.optimization_barrier(v.astype(jnp.bfloat16)).astype(jnp.float32)

@jax.custom_vjp
def low_back(v):
    return v

def low_keep(v):
    return (low(v), None)

def low_pass(kept, grad):
    return (grad,)

def back_keep(v):
    return (v, None)

def back_low(kept, grad):
    return (low(grad),)
low.defvjp(low_keep, low_pass)
low_back.defvjp(back_keep, back_low)
norm_eps = 1e-06
precise = lax.Precision.HIGHEST

def layer_norm(values):
    mean_value = lax.optimization_barrier(jnp.mean(values, axis=-1, keepdims=True))
    centred = values - mean_value
    variance = lax.optimization_barrier(jnp.mean(centred * centred, axis=-1, keepdims=True))
    return centred * lax.rsqrt(variance + norm_eps)

def softmax_rows(scores):
    row_top = lax.optimization_barrier(jnp.max(scores, axis=-1, keepdims=True))
    exp_terms = jnp.exp(scores - row_top)
    return exp_terms / lax.optimization_barrier(jnp.sum(exp_terms, axis=-1, keepdims=True))

def silu_fn(values):
    return values * jax.nn.sigmoid(values)

def gelu_fn(values):
    return jax.nn.gelu(values, approximate=True)

def project(h_in, weight):
    return jnp.einsum('bfpd,de->bfpe', h_in, weight, precision=precise)

def split_heads(h_in, w_qkv):
    batch_size = h_in.shape[0]
    qkv_rows = low(low_back(project(h_in, w_qkv)))
    qkv_rows = qkv_rows.reshape(batch_size, FR, PATCHES, 3, HEADS, HEAD)
    return (qkv_rows[:, :, :, 0], qkv_rows[:, :, :, 1], qkv_rows[:, :, :, 2])

def attend_frames(h_in, w_qkv, w_proj, b_proj):
    batch_size = h_in.shape[0]
    queries, key_part, value_part = split_heads(h_in, w_qkv)
    scores = low_back(jnp.einsum('bfphc,bfqhc->bfhpq', queries, key_part, precision=precise) * HEAD ** (-0.5))
    probabilities = low(softmax_rows(scores))
    mixture = jnp.einsum('bfhpq,bfqhc->bfphc', probabilities, value_part, precision=precise)
    mixture = low(low_back(mixture)).reshape(batch_size, FR, PATCHES, D)
    return low_back(project(mixture, w_proj) + b_proj)

def attend_times(h_in, live_mask, w_qkv, w_proj, b_proj):
    batch_size = h_in.shape[0]
    queries, key_part, value_part = split_heads(h_in, w_qkv)
    scores = low_back(jnp.einsum('bfphc,bgphc->bphfg', queries, key_part, precision=precise) * HEAD ** (-0.5))
    scores = jnp.where(live_mask[:, None, None, None, :], scores, -1e+30)
    probabilities = low(softmax_rows(scores))
    mixture = jnp.einsum('bphfg,bgphc->bfphc', probabilities, value_part, precision=precise)
    mixture = low(low_back(mixture)).reshape(batch_size, FR, PATCHES, D)
    return low_back(project(mixture, w_proj) + b_proj)

def block_layer(weights, block):
    x_in, mod_frames, live_mask = block
    w_qkv_s, w_o_s, b_o_s, w_qkv_t, w_o_t, b_o_t, w_in, b_in, w_out, b_out = weights
    pieces = [mod_frames[:, :, None, i * D:(i + 1) * D] for i in range(9)]
    h_one = low(layer_norm(x_in) * (1.0 + pieces[1]) + pieces[0])
    x_one = x_in + pieces[2] * attend_frames(h_one, w_qkv_s, w_o_s, b_o_s)
    h_two = low(layer_norm(x_one) * (1.0 + pieces[4]) + pieces[3])
    x_two = x_one + pieces[5] * attend_times(h_two, live_mask, w_qkv_t, w_o_t, b_o_t)
    h_three = low(layer_norm(x_two) * (1.0 + pieces[7]) + pieces[6])
    hidden = low_back(project(h_three, w_in) + b_in)
    active = low(gelu_fn(hidden))
    branch = low_back(jnp.einsum('bfpe,ed->bfpd', active, w_out, precision=precise) + b_out)
    result = x_two + pieces[8] * branch
    return jnp.where(live_mask[:, :, None, None], result, 0.0)

def reference(clips, t_emb, lengths, task, w_mod, b_mod, w_qkv_s, w_o_s, b_o_s, w_qkv_t, w_o_t, b_o_t, w_in, b_in, w_out, b_out, cotangent):
    live_mask = jnp.arange(FR, dtype=jnp.int32)[None, :] < lengths[:, None]
    chosen = task[:, :, None] == 1
    batch_clips = 4

    def forward(x_all, t_all, w_mod_f, b_mod_f, *rest):
        mod_rows = low_back(jnp.einsum('cjd,de->cje', low(silu_fn(t_all)), w_mod_f, precision=precise) + b_mod_f)
        mod_frames = jnp.where(chosen, mod_rows[:, 1:2, :], mod_rows[:, 0:1, :])
        stacked = (x_all.reshape(CLIPS // batch_clips, batch_clips, FR, PATCHES, D), mod_frames.reshape(CLIPS // batch_clips, batch_clips, FR, 9 * D), live_mask.reshape(CLIPS // batch_clips, batch_clips, FR))
        step_fn = jax.checkpoint(partial(block_layer, tuple(rest)))
        outputs = lax.map(step_fn, stacked)
        return outputs.reshape(CLIPS, FR, PATCHES, D)
    floats = tuple((a.astype(jnp.float32) for a in (clips, t_emb, w_mod, b_mod, w_qkv_s, w_o_s, b_o_s, w_qkv_t, w_o_t, b_o_t, w_in, b_in, w_out, b_out)))
    result, pullback = jax.vjp(forward, *floats)
    gradients = pullback(cotangent.astype(jnp.float32))
    return (result.astype(jnp.bfloat16), gradients[0].astype(jnp.bfloat16), gradients[1].astype(jnp.bfloat16), gradients[2], gradients[3], gradients[4], gradients[5], gradients[6], gradients[7], gradients[8], gradients[9], gradients[10], gradients[11], gradients[12], gradients[13])
```

```python
import functools

import jax
import jax.numpy as jnp
from jax import lax
from jax.experimental import pallas as pl
from jax.experimental.pallas import tpu as pltpu
from jax.sharding import PartitionSpec as P

D = 768
HEADS = 12
HEAD = 64
FF = 3072
FR = 16
PATCHES = 64
LIVE = 2 * FR
EPS = 1e-06
BF = jnp.bfloat16
F32 = jnp.float32
ALL = ("wide", "narrow")
PAIRS = HEADS // 2
LANES = 2 * HEAD
TILE = 512
FT = TILE // PATCHES
PT = TILE // LIVE
GRID = LIVE * PATCHES // TILE
GROUPS = TILE // 64
GELU_C = 0.7978845608028654
GELU_A = 0.044715
VMEM_LIMIT = 66 * 1000 * 1000


def dot(a, b):
    return lax.dot_general(a, b, (((1,), (0,)), ((), ())), preferred_element_type=F32)


def dot_nt(a, b):
    return lax.dot_general(a, b, (((1,), (1,)), ((), ())), preferred_element_type=F32)


def dot_tn(a, b):
    return lax.dot_general(a, b, (((0,), (0,)), ((), ())), preferred_element_type=F32)


def normalise(x):
    mean = jnp.mean(x, axis=-1, keepdims=True)
    centred = x - mean
    var = jnp.mean(centred * centred, axis=-1, keepdims=True)
    rstd = lax.rsqrt(var + EPS)
    return centred * rstd, rstd


def norm_back(dn, xhat, rstd):
    m1 = jnp.mean(dn, axis=-1, keepdims=True)
    m2 = jnp.mean(dn * xhat, axis=-1, keepdims=True)
    return rstd * (dn - m1 - xhat * m2)


def lane_masks():
    lane = lax.broadcasted_iota(jnp.int32, (64, LANES), 1)
    low_lanes = lane < HEAD
    low = jnp.where(low_lanes, 1.0, 0.0).astype(BF)
    high = jnp.where(low_lanes, 0.0, 1.0).astype(BF)
    return low_lanes, low, high


def softmax_keys(k, qb, mask):
    s = dot_nt(k, qb) * HEAD ** (-0.5)
    if mask is not None:
        s = jnp.where(mask, s, -1e30)
    top = jnp.max(s, axis=0, keepdims=True)
    e = jnp.exp(s - top)
    return e / jnp.sum(e, axis=0, keepdims=True)


def attend(qkv_ref, o_ref, mask):
    low_lanes, low, high = lane_masks()

    def body(g, carry):
        rows = pl.ds(pl.multiple_of(g * 64, 64), 64)
        for hp in range(PAIRS):
            cols = slice(hp * LANES, (hp + 1) * LANES)
            q = qkv_ref[rows, hp * LANES : (hp + 1) * LANES]
            k = qkv_ref[rows, D + hp * LANES : D + (hp + 1) * LANES]
            v = qkv_ref[rows, 2 * D + hp * LANES : 2 * D + (hp + 1) * LANES]
            qb = jnp.concatenate([q * low, q * high], axis=0)
            p = softmax_keys(k, qb, mask).astype(BF)
            r = dot_tn(p, v)
            o_ref[rows, cols] = jnp.where(low_lanes, r[:64], r[64:]).astype(BF)
        return carry

    lax.fori_loop(0, GROUPS, body, 0)


def attend_back(qkv_ref, do_ref, dqkv_ref, mask):
    low_lanes, low, high = lane_masks()

    def body(g, carry):
        rows = pl.ds(pl.multiple_of(g * 64, 64), 64)
        for hp in range(PAIRS):
            qc = slice(hp * LANES, (hp + 1) * LANES)
            kc = slice(D + hp * LANES, D + (hp + 1) * LANES)
            vc = slice(2 * D + hp * LANES, 2 * D + (hp + 1) * LANES)
            q = qkv_ref[rows, qc]
            k = qkv_ref[rows, kc]
            v = qkv_ref[rows, vc]
            do = do_ref[rows, qc]
            qb = jnp.concatenate([q * low, q * high], axis=0)
            dob = jnp.concatenate([do * low, do * high], axis=0)
            p = softmax_keys(k, qb, mask)
            dp = dot_nt(v, dob)
            delta = jnp.sum(p * dp, axis=0, keepdims=True)
            ds = (p * (dp - delta)).astype(BF)
            r = dot_tn(ds, k)
            dq = jnp.where(low_lanes, r[:64], r[64:]) * HEAD ** (-0.5)
            dqkv_ref[rows, qc] = dq.astype(BF)
            dqkv_ref[rows, kc] = (dot(ds, qb) * HEAD ** (-0.5)).astype(BF)
            dqkv_ref[rows, vc] = dot(p.astype(BF), dob).astype(BF)
        return carry

    lax.fori_loop(0, GROUPS, body, 0)


def swap_major(value, scratch, out_ref, first, second):
    for b in range(D // 128):
        cols = slice(b * 128, (b + 1) * 128)
        for i in range(first):
            scratch[b, pl.ds(i, second, stride=first), :] = value[i * second : (i + 1) * second, cols]
        out_ref[:, :, cols] = scratch[b].reshape(second, first, 128).astype(out_ref.dtype)


def frames_of(refs):
    return jnp.concatenate([r[0] for r in refs], axis=0).astype(F32)


def per_frame(piece):
    return jnp.broadcast_to(piece[:, None, :], (FT, PATCHES, D)).reshape(TILE, D)


def per_patch(piece):
    return jnp.broadcast_to(piece[None], (PT, LIVE, D)).reshape(TILE, D)


def sum_patches(value):
    return jnp.sum(value.reshape(FT, PATCHES, D), axis=1)


def sum_groups(value):
    return jnp.sum(value.reshape(PT, LIVE, D), axis=0)


def attn_mask(seg_ref):
    return seg_ref[...] > 0.0


def frame_forward(rows_ref, *refs):
    x_refs, (mod, wqkv, wo, bo, x1t, qkv, o, a1, scratch) = refs[:FT], refs[FT:]
    x = frames_of(x_refs)
    xhat, _ = normalise(x)
    h = (xhat * (1.0 + per_frame(mod[1])) + per_frame(mod[0])).astype(BF)
    qkv[...] = dot(h, wqkv[...]).astype(BF)
    attend(qkv, o, None)
    branch = dot(o[...], wo[...]) + bo[...]
    a1[...] = branch
    x1 = x + per_frame(mod[2]) * branch
    swap_major(x1, scratch, x1t, FT, PATCHES)


def turn_frames(rows_ref, *refs):
    x_refs, (out, scratch) = refs[:FT], refs[FT:]
    swap_major(frames_of(x_refs), scratch, out, FT, PATCHES)


def time_forward(x1, mod, seg, wqkv, wo, bo, x2, qkv, o, a2):
    x = x1[...].reshape(TILE, D)
    xhat, _ = normalise(x)
    h = (xhat * (1.0 + per_patch(mod[1])) + per_patch(mod[0])).astype(BF)
    qkv[...] = dot(h, wqkv[...]).astype(BF)
    attend(qkv, o, attn_mask(seg))
    branch = dot(o[...], wo[...]) + bo[...]
    a2[...] = branch
    x2[...] = (x + per_patch(mod[2]) * branch).reshape(PT, LIVE, D)


def mlp_both(x2, dy, mod, win, bin_, wout, bout, out, dx2, gwin, gwout, gbin, gbout, dmod, scratch):
    first = pl.program_id(0) == 0

    @pl.when(first)
    def _():
        gwin[...] = jnp.zeros_like(gwin)
        gwout[...] = jnp.zeros_like(gwout)
        gbin[...] = jnp.zeros_like(gbin)
        gbout[...] = jnp.zeros_like(gbout)
        dmod[...] = jnp.zeros_like(dmod)

    x = x2[...].reshape(TILE, D)
    xhat, rstd = normalise(x)
    h = (xhat * (1.0 + per_patch(mod[1])) + per_patch(mod[0])).astype(BF)
    gate = per_patch(mod[2])
    grad = dy[...].reshape(TILE, D)
    da = (grad * gate).astype(BF)
    gbout[...] += jnp.sum(da.astype(F32), axis=0, keepdims=True)
    branch = jnp.zeros((TILE, D), F32) + bout[...]
    dh = jnp.zeros((TILE, D), F32)
    for j in range(FF // D):
        cols = slice(j * D, (j + 1) * D)
        u = dot(h, win[:, cols]) + bin_[:, cols]
        u2 = u * u
        t = jnp.tanh(GELU_C * u * (1.0 + GELU_A * u2))
        half = 0.5 * (1.0 + t)
        g = (u * half).astype(BF)
        slope = half + (0.5 * GELU_C) * u * (1.0 - t * t) * (1.0 + 3.0 * GELU_A * u2)
        branch = branch + dot(g, wout[cols, :])
        du = (dot_nt(da, wout[cols, :]) * slope).astype(BF)
        gwout[cols, :] += dot_tn(g, da)
        gbin[:, cols] += jnp.sum(du.astype(F32), axis=0, keepdims=True)
        gwin[:, cols] += dot_tn(h, du)
        dh = dh + dot_nt(du, win[:, cols])
    swap_major(x + gate * branch, scratch, out, PT, LIVE)
    dmod[2] += sum_groups(grad * branch)
    dmod[0] += sum_groups(dh)
    dmod[1] += sum_groups(dh * xhat)
    back = norm_back(dh * (1.0 + per_patch(mod[1])), xhat, rstd)
    dx2[...] = (grad + back).reshape(PT, LIVE, D)


def attn_back_tile(x, grad, shift, scale, gate, branch, qkv, o, wqkv, wo, gwqkv, gwo, gbo, do, dqkv, mask):
    first = pl.program_id(0) == 0

    @pl.when(first)
    def _():
        gwqkv[...] = jnp.zeros_like(gwqkv)
        gwo[...] = jnp.zeros_like(gwo)
        gbo[...] = jnp.zeros_like(gbo)

    da = (grad * gate).astype(BF)
    do[...] = dot_nt(da, wo[...]).astype(BF)
    gwo[...] += dot_tn(o[...], da)
    gbo[...] += jnp.sum(da.astype(F32), axis=0, keepdims=True)
    attend_back(qkv, do, dqkv, mask)
    xhat, rstd = normalise(x)
    h = (xhat * (1.0 + scale) + shift).astype(BF)
    dh = jnp.zeros((TILE, D), F32)
    for j in range(3):
        cols = slice(j * D, (j + 1) * D)
        part = dqkv[:, cols]
        gwqkv[:, cols] += dot_tn(h, part)
        dh = dh + dot_nt(part, wqkv[:, cols])
    dx = grad + norm_back(dh * (1.0 + scale), xhat, rstd)
    return dx, dh, dh * xhat, grad * branch


def time_back(x1, dx2, mod, seg, qkv, o, a2, wqkv, wo, dx1, gwqkv, gwo, gbo, dmod, do, dqkv, scratch):
    @pl.when(pl.program_id(0) == 0)
    def _():
        dmod[...] = jnp.zeros_like(dmod)

    dx, d_shift, d_scale, d_gate = attn_back_tile(
        x1[...].reshape(TILE, D), dx2[...].reshape(TILE, D), per_patch(mod[0]), per_patch(mod[1]),
        per_patch(mod[2]), a2[...], qkv, o, wqkv, wo, gwqkv, gwo, gbo, do, dqkv, attn_mask(seg))
    dmod[0] += sum_groups(d_shift)
    dmod[1] += sum_groups(d_scale)
    dmod[2] += sum_groups(d_gate)
    swap_major(dx, scratch, dx1, PT, LIVE)


def frame_back(rows_ref, *refs):
    x_refs, (dx1, mod, qkv, o, a1, wqkv, wo, dx0, gwqkv, gwo, gbo, dmod, do, dqkv) = refs[:FT], refs[FT:]
    dx, d_shift, d_scale, d_gate = attn_back_tile(
        frames_of(x_refs), dx1[...].reshape(TILE, D), per_frame(mod[0]), per_frame(mod[1]),
        per_frame(mod[2]), a1[...], qkv, o, wqkv, wo, gwqkv, gwo, gbo, do, dqkv, None)
    dmod[0] = sum_patches(d_shift)
    dmod[1] = sum_patches(d_scale)
    dmod[2] = sum_patches(d_gate)
    dx0[...] = dx.reshape(FT, PATCHES, D).astype(BF)


def frame_specs():
    return [
        pl.BlockSpec((1, PATCHES, D), functools.partial(lambda j, i, rows: (rows[FT * i + j], 0, 0), j))
        for j in range(FT)
    ]


def whole(shape):
    return pl.BlockSpec(shape, lambda i, *_: (0,) * len(shape), pipeline_mode=pl.Buffered(1))


def tiles(shape, dim):
    return pl.BlockSpec(shape, lambda i, *_: tuple(i if a == dim else 0 for a in range(len(shape))))


def piece_spec(number, frames, by_tile):
    return pl.BlockSpec((3, frames, D), lambda i, *_: (number, i if by_tile else 0, 0))


ROWS = tiles((TILE, D), 0)
ROWS3 = tiles((TILE, 3 * D), 0)
TURNED = tiles((PT, LIVE, D), 0)


TURN = pltpu.VMEM((D // 128, TILE, 128), F32)


def shape_of(shape, dtype):
    return jax.ShapeDtypeStruct(shape, dtype)


def call(kernel, name, ins, in_specs, outs, out_specs, scratch, flops, prefetch=None):
    moved = sum(a.size * a.dtype.itemsize for a in tuple(ins) + tuple(outs))
    grid_spec = pltpu.PrefetchScalarGridSpec(
        num_scalar_prefetch=0 if prefetch is None else 1,
        grid=(GRID,),
        in_specs=in_specs,
        out_specs=out_specs,
        scratch_shapes=scratch,
    )
    fn = pl.pallas_call(
        kernel,
        grid_spec=grid_spec,
        out_shape=outs,
        name=name,
        cost_estimate=pl.CostEstimate(flops=flops, bytes_accessed=moved, transcendentals=0),
        compiler_params=pltpu.CompilerParams(
            dimension_semantics=("arbitrary",), vmem_limit_bytes=VMEM_LIMIT
        ),
    )
    return fn(*ins) if prefetch is None else fn(prefetch, *ins)


TOKENS = LIVE * PATCHES


def run_frame_forward(frames, rows, mod, wqkv, wo, bo):
    return call(
        frame_forward, "frame_forward",
        [frames] * FT + [mod, wqkv, wo, bo],
        frame_specs() + [piece_spec(0, FT, True), whole((D, 3 * D)), whole((D, D)), whole((1, D))],
        [shape_of((PATCHES, LIVE, D), F32), shape_of((TOKENS, 3 * D), BF), shape_of((TOKENS, D), BF),
         shape_of((TOKENS, D), F32)],
        [tiles((PATCHES, FT, D), 1), ROWS3, ROWS, ROWS],
        [TURN],
        2 * TOKENS * D * 4 * D, rows)


def run_turn_frames(frames, rows):
    return call(
        turn_frames, "turn_frames", [frames] * FT, frame_specs(),
        [shape_of((PATCHES, LIVE, D), F32)], [tiles((PATCHES, FT, D), 1)],
        [TURN], 1000, rows)[0]


def run_time_forward(x1, mod, seg, wqkv, wo, bo):
    return call(
        time_forward, "time_forward",
        [x1, mod, seg, wqkv, wo, bo],
        [TURNED, piece_spec(1, LIVE, False), whole((64, LANES)), whole((D, 3 * D)), whole((D, D)),
         whole((1, D))],
        [shape_of((PATCHES, LIVE, D), F32), shape_of((TOKENS, 3 * D), BF), shape_of((TOKENS, D), BF),
         shape_of((TOKENS, D), F32)],
        [TURNED, ROWS3, ROWS, ROWS],
        [], 2 * TOKENS * D * 4 * D)


def run_mlp(x2, dy, mod, win, bin_, wout, bout):
    return call(
        mlp_both, "mlp_both",
        [x2, dy, mod, win, bin_, wout, bout],
        [TURNED, TURNED, piece_spec(2, LIVE, False), whole((D, FF)), whole((1, FF)), whole((FF, D)),
         whole((1, D))],
        [shape_of((LIVE, PATCHES, D), BF), shape_of((PATCHES, LIVE, D), F32), shape_of((D, FF), F32),
         shape_of((FF, D), F32), shape_of((1, FF), F32), shape_of((1, D), F32), shape_of((3, LIVE, D), F32)],
        [tiles((LIVE, PT, D), 1), TURNED, whole((D, FF)), whole((FF, D)), whole((1, FF)), whole((1, D)),
         whole((3, LIVE, D))],
        [TURN],
        6 * 2 * TOKENS * D * FF)


def run_time_back(x1, dx2, mod, seg, qkv, o, a2, wqkv, wo):
    return call(
        time_back, "time_back",
        [x1, dx2, mod, seg, qkv, o, a2, wqkv, wo],
        [TURNED, TURNED, piece_spec(1, LIVE, False), whole((64, LANES)), ROWS3, ROWS, ROWS,
         whole((D, 3 * D)), whole((D, D))],
        [shape_of((LIVE, PATCHES, D), F32), shape_of((D, 3 * D), F32), shape_of((D, D), F32),
         shape_of((1, D), F32), shape_of((3, LIVE, D), F32)],
        [tiles((LIVE, PT, D), 1), whole((D, 3 * D)), whole((D, D)), whole((1, D)), whole((3, LIVE, D))],
        [pltpu.VMEM((TILE, D), BF), pltpu.VMEM((TILE, 3 * D), BF), TURN],
        2 * 2 * TOKENS * D * 4 * D)


def run_frame_back(frames, rows, dx1, mod, qkv, o, a1, wqkv, wo):
    return call(
        frame_back, "frame_back",
        [frames] * FT + [dx1, mod, qkv, o, a1, wqkv, wo],
        frame_specs() + [tiles((FT, PATCHES, D), 0), piece_spec(0, FT, True), ROWS3, ROWS, ROWS,
                         whole((D, 3 * D)), whole((D, D))],
        [shape_of((LIVE, PATCHES, D), BF), shape_of((D, 3 * D), F32), shape_of((D, D), F32),
         shape_of((1, D), F32), shape_of((3, LIVE, D), F32)],
        [tiles((FT, PATCHES, D), 0), whole((D, 3 * D)), whole((D, D)), whole((1, D)),
         piece_spec(0, FT, True)],
        [pltpu.VMEM((TILE, D), BF), pltpu.VMEM((TILE, 3 * D), BF)],
        2 * 2 * TOKENS * D * 4 * D, rows)


def exchange(x):
    return lax.all_to_all(x, ALL, split_axis=0, concat_axis=0, tiled=True)


def shift_clips(clips, back):
    n = lax.axis_size("narrow")
    parts = [clips[0]]
    for j in range(1, n):
        step = -j if back else j
        parts.append(lax.ppermute(clips[j], "narrow", [(s, (s + step) % n) for s in range(n)]))
    return jnp.stack(parts)


def local(clips, t_emb, lengths, task, w_mod, b_mod, w_qkv_s, w_o_s, b_o_s, w_qkv_t, w_o_t, b_o_t,
          w_in, b_in, w_out, b_out, cotangent):
    n = lax.axis_size("narrow")
    wide = lax.axis_size("wide")
    devices = n * wide
    part = w_mod.shape[0]
    mod_cols = w_mod.shape[1] // devices
    rank = lax.axis_index("narrow")
    slots = jnp.arange(n, dtype=jnp.int32)
    from_clip = (rank - slots) % n
    recv_len = lengths.reshape(n, n)[from_clip, slots]
    recv_task = task.reshape(n, n, FR)[from_clip, slots]
    ends = jnp.cumsum(recv_len)
    starts = ends - recv_len
    ids = jnp.arange(LIVE, dtype=jnp.int32)
    source = jnp.sum((ends[None, :] <= ids[:, None]).astype(jnp.int32), axis=1)
    within = ids - starts[source]
    pack_rows = source * FR + within
    row_choice = source * 2 + recv_task[source, within]
    frame_ids = jnp.arange(FR, dtype=jnp.int32)
    live_back = frame_ids[None, :] < recv_len[:, None]
    unpack_rows = jnp.where(live_back, starts[:, None] + frame_ids[None, :], 0).reshape(-1)
    row_id = jnp.arange(64, dtype=jnp.int32)
    col_id = jnp.arange(LANES, dtype=jnp.int32) % 64
    seg = (
        (row_id[:, None] // LIVE == col_id[None, :] // LIVE)
        & (source[row_id % LIVE][:, None] == source[col_id % LIVE][None, :])
    ).astype(F32)

    def gather(w):
        return lax.all_gather(w, ALL, axis=0, tiled=True)

    frames = shift_clips(clips, False).reshape(n * FR, PATCHES, D)

    wm = jnp.swapaxes(w_mod.reshape(part, devices, mod_cols), 0, 1).reshape(devices, -1)
    emb = jnp.broadcast_to(t_emb.reshape(1, -1), (devices, t_emb.size))
    small = jnp.concatenate([b_o_s, b_o_t, b_in, b_out])
    small_all = jnp.broadcast_to(small[None], (devices, small.size))
    got = exchange(jnp.concatenate([wm, emb, small_all], axis=1))
    wm_cols = got[:, : part * mod_cols].reshape(D, mod_cols)
    emb_all = got[:, part * mod_cols : part * mod_cols + t_emb.size].reshape(-1, D)
    small_got = got[:, part * mod_cols + t_emb.size :]
    b1 = b_o_s.size
    bias_s = small_got[:, :b1].reshape(1, -1).astype(F32)
    bias_t = small_got[:, b1 : 2 * b1].reshape(1, -1).astype(F32)
    bias_in = small_got[:, 2 * b1 : 2 * b1 + b_in.size].reshape(1, -1).astype(F32)
    bias_out = small_got[:, 2 * b1 + b_in.size :].reshape(1, -1).astype(F32)
    emb_f = emb_all.astype(F32)
    silu_low = (emb_f * jax.nn.sigmoid(emb_f)).astype(BF)
    mod_part = dot(silu_low, wm_cols) + b_mod.astype(F32)[None]
    mod_part = mod_part.reshape(wide, n, n, 2, mod_cols)
    mod_part = jnp.stack([jnp.roll(mod_part[:, :, c], c, axis=1) for c in range(n)], axis=2)
    mod_rows = exchange(mod_part.reshape(devices, -1)).reshape(devices, 2 * n, mod_cols)
    mod_rows = jnp.swapaxes(mod_rows, 0, 1).reshape(2 * n, 9, D)
    mod = jnp.swapaxes(mod_rows[row_choice], 0, 1)

    wqkv_s, wo_s = gather(w_qkv_s), gather(w_o_s)
    wqkv_t, wo_t = gather(w_qkv_t), gather(w_o_t)
    win, wout = gather(w_in), gather(w_out)

    x1, qkv1, o1, a1 = run_frame_forward(frames, pack_rows, mod, wqkv_s, wo_s, bias_s)
    x2, qkv2, o2, a2 = run_time_forward(x1, mod, seg, wqkv_t, wo_t, bias_t)
    cots = shift_clips(cotangent, False).reshape(n * FR, PATCHES, D)
    dy = run_turn_frames(cots, pack_rows)
    out, dx2, g_in, g_out, gb_in, gb_out, dmod3 = run_mlp(x2, dy, mod, win, bias_in, wout, bias_out)

    def unpack(packed):
        spread = jnp.take(packed, unpack_rows, axis=0).reshape(n, FR, PATCHES, D)
        spread = jnp.where(live_back[:, :, None, None], spread, jnp.zeros((), packed.dtype))
        return shift_clips(spread, True)

    def scatter(g):
        return lax.psum_scatter(g.astype(BF), ALL, scatter_dimension=0, tiled=True).astype(F32)

    layer_out = unpack(out)
    s_in, s_out = scatter(g_in), scatter(g_out)
    dx1, g_qkv_t, g_o_t, gb_t, dmod2 = run_time_back(x1, dx2, mod, seg, qkv2, o2, a2, wqkv_t, wo_t)
    s_qkv_t, s_o_t = scatter(g_qkv_t), scatter(g_o_t)
    dx0, g_qkv_s, g_o_s, gb_s, dmod1 = run_frame_back(
        frames, pack_rows, dx1, mod, qkv1, o1, a1, wqkv_s, wo_s)
    grad_clips = unpack(dx0)
    s_qkv_s, s_o_s = scatter(g_qkv_s), scatter(g_o_s)

    grad_frames = jnp.swapaxes(jnp.concatenate([dmod1, dmod2, dmod3], axis=0), 0, 1).reshape(LIVE, 9 * D)
    chooser = (row_choice[:, None] == jnp.arange(2 * n, dtype=jnp.int32)[None, :]).astype(F32)
    grad_rows = lax.dot_general(
        chooser, grad_frames, (((0,), (0,)), ((), ())), precision=lax.Precision.HIGHEST
    ).astype(BF)
    d_cols = exchange(jnp.swapaxes(grad_rows.reshape(2 * n, devices, mod_cols), 0, 1).reshape(devices, -1))
    d_cols = d_cols.reshape(wide, n, n, 2, mod_cols)
    d_cols = jnp.stack([jnp.roll(d_cols[:, :, c], -c, axis=1) for c in range(n)], axis=2)
    d_cols = d_cols.reshape(devices * 2 * n, mod_cols)
    grad_b_mod = jnp.sum(d_cols.astype(F32), axis=0)
    gwm_cols = dot_tn(silu_low, d_cols)
    g_emb = dot_nt(d_cols, wm_cols)
    gb_all = jnp.concatenate(
        [gb_s.reshape(devices, -1), gb_t.reshape(devices, -1), gb_in.reshape(devices, -1),
         gb_out.reshape(devices, -1)], axis=1)
    final = exchange(jnp.concatenate(
        [gwm_cols.reshape(devices, -1), g_emb.reshape(devices, -1), gb_all], axis=1))
    cut1 = part * mod_cols
    cut2 = cut1 + t_emb.size
    grad_w_mod = jnp.swapaxes(final[:, :cut1].reshape(devices, part, mod_cols), 0, 1).reshape(part, -1)
    emb_own = t_emb.astype(F32)
    sig = jax.nn.sigmoid(emb_own)
    grad_emb = jnp.sum(final[:, cut1:cut2], axis=0).reshape(t_emb.shape)
    grad_t_emb = (grad_emb * (sig * (1.0 + emb_own * (1.0 - sig)))).astype(BF)
    gb = jnp.sum(final[:, cut2:], axis=0)
    return (
        layer_out,
        grad_clips,
        grad_t_emb,
        grad_w_mod,
        grad_b_mod,
        s_qkv_s,
        s_o_s,
        gb[:b1],
        s_qkv_t,
        s_o_t,
        gb[b1 : 2 * b1],
        s_in,
        gb[2 * b1 : 2 * b1 + b_in.size],
        s_out,
        gb[2 * b1 + b_in.size :],
    )


def solution(mesh):
    full = P(ALL)
    placed = (full, full, P("wide"), P("wide")) + (full,) * 13
    return jax.shard_map(local, mesh=mesh, in_specs=placed, out_specs=(full,) * 15, check_vma=False)
```

```python
import functools

import jax
import jax.numpy as jnp
from jax import lax
from jax.experimental import pallas as pl
from jax.experimental.pallas import tpu as pltpu
from jax.sharding import PartitionSpec as P

D = 768
HEADS = 12
HEAD = 64
FF = 3072
FR = 16
PATCHES = 64
LIVE = 2 * FR
EPS = 1e-06
BF = jnp.bfloat16
F32 = jnp.float32
ALL = ("wide", "narrow")
PAIRS = HEADS // 2
LANES = 2 * HEAD
TILE = 512
FT = TILE // PATCHES
PT = TILE // LIVE
GRID = LIVE * PATCHES // TILE
GROUPS = TILE // 64
GELU_C = 0.7978845608028654
GELU_A = 0.044715
VMEM_LIMIT = 66 * 1000 * 1000


def dot(a, b):
    return lax.dot_general(a, b, (((1,), (0,)), ((), ())), preferred_element_type=F32)


def dot_nt(a, b):
    return lax.dot_general(a, b, (((1,), (1,)), ((), ())), preferred_element_type=F32)


def dot_tn(a, b):
    return lax.dot_general(a, b, (((0,), (0,)), ((), ())), preferred_element_type=F32)


def normalise(x):
    mean = jnp.mean(x, axis=-1, keepdims=True)
    centred = x - mean
    var = jnp.mean(centred * centred, axis=-1, keepdims=True)
    rstd = lax.rsqrt(var + EPS)
    return centred * rstd, rstd


def norm_back(dn, xhat, rstd):
    m1 = jnp.mean(dn, axis=-1, keepdims=True)
    m2 = jnp.mean(dn * xhat, axis=-1, keepdims=True)
    return rstd * (dn - m1 - xhat * m2)


def lane_masks():
    lane = lax.broadcasted_iota(jnp.int32, (64, LANES), 1)
    low_lanes = lane < HEAD
    low = jnp.where(low_lanes, 1.0, 0.0).astype(BF)
    high = jnp.where(low_lanes, 0.0, 1.0).astype(BF)
    return low_lanes, low, high


def softmax_keys(k, qb, mask):
    s = dot_nt(k, qb) * HEAD ** (-0.5)
    if mask is not None:
        s = jnp.where(mask, s, -1e30)
    top = jnp.max(s, axis=0, keepdims=True)
    e = jnp.exp(s - top)
    return e / jnp.sum(e, axis=0, keepdims=True)


def attend(qkv_ref, o_ref, mask):
    low_lanes, low, high = lane_masks()

    def body(g, carry):
        rows = pl.ds(pl.multiple_of(g * 64, 64), 64)
        for hp in range(PAIRS):
            cols = slice(hp * LANES, (hp + 1) * LANES)
            q = qkv_ref[rows, hp * LANES : (hp + 1) * LANES]
            k = qkv_ref[rows, D + hp * LANES : D + (hp + 1) * LANES]
            v = qkv_ref[rows, 2 * D + hp * LANES : 2 * D + (hp + 1) * LANES]
            qb = jnp.concatenate([q * low, q * high], axis=0)
            p = softmax_keys(k, qb, mask).astype(BF)
            r = dot_tn(p, v)
            o_ref[rows, cols] = jnp.where(low_lanes, r[:64], r[64:]).astype(BF)
        return carry

    lax.fori_loop(0, GROUPS, body, 0)


def attend_back(qkv_ref, do_ref, dqkv_ref, mask):
    low_lanes, low, high = lane_masks()

    def body(g, carry):
        rows = pl.ds(pl.multiple_of(g * 64, 64), 64)
        for hp in range(PAIRS):
            qc = slice(hp * LANES, (hp + 1) * LANES)
            kc = slice(D + hp * LANES, D + (hp + 1) * LANES)
            vc = slice(2 * D + hp * LANES, 2 * D + (hp + 1) * LANES)
            q = qkv_ref[rows, qc]
            k = qkv_ref[rows, kc]
            v = qkv_ref[rows, vc]
            do = do_ref[rows, qc]
            qb = jnp.concatenate([q * low, q * high], axis=0)
            dob = jnp.concatenate([do * low, do * high], axis=0)
            p = softmax_keys(k, qb, mask)
            dp = dot_nt(v, dob)
            delta = jnp.sum(p * dp, axis=0, keepdims=True)
            ds = (p * (dp - delta)).astype(BF)
            r = dot_tn(ds, k)
            dq = jnp.where(low_lanes, r[:64], r[64:]) * HEAD ** (-0.5)
            dqkv_ref[rows, qc] = dq.astype(BF)
            dqkv_ref[rows, kc] = (dot(ds, qb) * HEAD ** (-0.5)).astype(BF)
            dqkv_ref[rows, vc] = dot(p.astype(BF), dob).astype(BF)
        return carry

    lax.fori_loop(0, GROUPS, body, 0)


def swap_major(value, scratch, out_ref, first, second):
    for b in range(D // 128):
        cols = slice(b * 128, (b + 1) * 128)
        for i in range(first):
            scratch[b, pl.ds(i, second, stride=first), :] = value[i * second : (i + 1) * second, cols]
        out_ref[:, :, cols] = scratch[b].reshape(second, first, 128).astype(out_ref.dtype)


def frames_of(refs):
    return jnp.concatenate([r[0] for r in refs], axis=0).astype(F32)


def per_frame(piece):
    return jnp.broadcast_to(piece[:, None, :], (FT, PATCHES, D)).reshape(TILE, D)


def per_patch(piece):
    return jnp.broadcast_to(piece[None], (PT, LIVE, D)).reshape(TILE, D)


def sum_patches(value):
    return jnp.sum(value.reshape(FT, PATCHES, D), axis=1)


def sum_groups(value):
    return jnp.sum(value.reshape(PT, LIVE, D), axis=0)


def attn_mask(seg_ref):
    return seg_ref[...] > 0.0


def frame_forward(rows_ref, *refs):
    x_refs, (mod, wqkv, wo, bo, x1t, qkv, o, a1, scratch) = refs[:FT], refs[FT:]
    x = frames_of(x_refs)
    xhat, _ = normalise(x)
    h = (xhat * (1.0 + per_frame(mod[1])) + per_frame(mod[0])).astype(BF)
    qkv[...] = dot(h, wqkv[...]).astype(BF)
    attend(qkv, o, None)
    branch = dot(o[...], wo[...]) + bo[...]
    a1[...] = branch
    x1 = x + per_frame(mod[2]) * branch
    swap_major(x1, scratch, x1t, FT, PATCHES)


def turn_frames(rows_ref, *refs):
    x_refs, (out, scratch) = refs[:FT], refs[FT:]
    swap_major(frames_of(x_refs), scratch, out, FT, PATCHES)


def time_forward(x1, mod, seg, wqkv, wo, bo, x2, qkv, o, a2):
    x = x1[...].reshape(TILE, D)
    xhat, _ = normalise(x)
    h = (xhat * (1.0 + per_patch(mod[1])) + per_patch(mod[0])).astype(BF)
    qkv[...] = dot(h, wqkv[...]).astype(BF)
    attend(qkv, o, attn_mask(seg))
    branch = dot(o[...], wo[...]) + bo[...]
    a2[...] = branch
    x2[...] = (x + per_patch(mod[2]) * branch).reshape(PT, LIVE, D)


def mlp_both(x2, dy, mod, win, bin_, wout, bout, out, dx2, gwin, gwout, gbin, gbout, dmod, scratch):
    first = pl.program_id(0) == 0

    @pl.when(first)
    def _():
        gwin[...] = jnp.zeros_like(gwin)
        gwout[...] = jnp.zeros_like(gwout)
        gbin[...] = jnp.zeros_like(gbin)
        gbout[...] = jnp.zeros_like(gbout)
        dmod[...] = jnp.zeros_like(dmod)

    x = x2[...].reshape(TILE, D)
    xhat, rstd = normalise(x)
    h = (xhat * (1.0 + per_patch(mod[1])) + per_patch(mod[0])).astype(BF)
    gate = per_patch(mod[2])
    grad = dy[...].reshape(TILE, D)
    da = (grad * gate).astype(BF)
    gbout[...] += jnp.sum(da.astype(F32), axis=0, keepdims=True)
    branch = jnp.zeros((TILE, D), F32) + bout[...]
    dh = jnp.zeros((TILE, D), F32)
    for j in range(FF // D):
        cols = slice(j * D, (j + 1) * D)
        u = dot(h, win[:, cols]) + bin_[:, cols]
        u2 = u * u
        t = jnp.tanh(GELU_C * u * (1.0 + GELU_A * u2))
        half = 0.5 * (1.0 + t)
        g = (u * half).astype(BF)
        slope = half + (0.5 * GELU_C) * u * (1.0 - t * t) * (1.0 + 3.0 * GELU_A * u2)
        branch = branch + dot(g, wout[cols, :])
        du = (dot_nt(da, wout[cols, :]) * slope).astype(BF)
        gwout[cols, :] += dot_tn(g, da)
        gbin[:, cols] += jnp.sum(du.astype(F32), axis=0, keepdims=True)
        gwin[:, cols] += dot_tn(h, du)
        dh = dh + dot_nt(du, win[:, cols])
    swap_major(x + gate * branch, scratch, out, PT, LIVE)
    dmod[2] += sum_groups(grad * branch)
    dmod[0] += sum_groups(dh)
    dmod[1] += sum_groups(dh * xhat)
    back = norm_back(dh * (1.0 + per_patch(mod[1])), xhat, rstd)
    dx2[...] = (grad + back).reshape(PT, LIVE, D)


def attn_back_tile(x, grad, shift, scale, gate, branch, qkv, o, wqkv, wo, gw, gbo, do, dqkv, mask):
    first = pl.program_id(0) == 0

    @pl.when(first)
    def _():
        gw[...] = jnp.zeros_like(gw)
        gbo[...] = jnp.zeros_like(gbo)

    da = (grad * gate).astype(BF)
    do[...] = dot_nt(da, wo[...]).astype(BF)
    gw[:, 3 * D :] += dot_tn(o[...], da)
    gbo[...] += jnp.sum(da.astype(F32), axis=0, keepdims=True)
    attend_back(qkv, do, dqkv, mask)
    xhat, rstd = normalise(x)
    h = (xhat * (1.0 + scale) + shift).astype(BF)
    dh = jnp.zeros((TILE, D), F32)
    for j in range(3):
        cols = slice(j * D, (j + 1) * D)
        part = dqkv[:, cols]
        gw[:, cols] += dot_tn(h, part)
        dh = dh + dot_nt(part, wqkv[:, cols])
    dx = grad + norm_back(dh * (1.0 + scale), xhat, rstd)
    return dx, dh, dh * xhat, grad * branch


def time_back(x1, dx2, mod, seg, qkv, o, a2, wqkv, wo, dx1, gw, gbo, dmod, do, dqkv, scratch):
    @pl.when(pl.program_id(0) == 0)
    def _():
        dmod[...] = jnp.zeros_like(dmod)

    dx, d_shift, d_scale, d_gate = attn_back_tile(
        x1[...].reshape(TILE, D), dx2[...].reshape(TILE, D), per_patch(mod[0]), per_patch(mod[1]),
        per_patch(mod[2]), a2[...], qkv, o, wqkv, wo, gw, gbo, do, dqkv, attn_mask(seg))
    dmod[0] += sum_groups(d_shift)
    dmod[1] += sum_groups(d_scale)
    dmod[2] += sum_groups(d_gate)
    swap_major(dx, scratch, dx1, PT, LIVE)


def frame_back(rows_ref, *refs):
    x_refs, (dx1, mod, qkv, o, a1, wqkv, wo, dx0, gw, gbo, dmod, do, dqkv) = refs[:FT], refs[FT:]
    dx, d_shift, d_scale, d_gate = attn_back_tile(
        frames_of(x_refs), dx1[...].reshape(TILE, D), per_frame(mod[0]), per_frame(mod[1]),
        per_frame(mod[2]), a1[...], qkv, o, wqkv, wo, gw, gbo, do, dqkv, None)
    dmod[0] = sum_patches(d_shift)
    dmod[1] = sum_patches(d_scale)
    dmod[2] = sum_patches(d_gate)
    dx0[...] = dx.reshape(FT, PATCHES, D).astype(BF)


def frame_specs():
    return [
        pl.BlockSpec((1, PATCHES, D), functools.partial(lambda j, i, rows: (rows[FT * i + j], 0, 0), j))
        for j in range(FT)
    ]


def whole(shape):
    return pl.BlockSpec(shape, lambda i, *_: (0,) * len(shape), pipeline_mode=pl.Buffered(1))


def tiles(shape, dim):
    return pl.BlockSpec(shape, lambda i, *_: tuple(i if a == dim else 0 for a in range(len(shape))))


def piece_spec(number, frames, by_tile):
    return pl.BlockSpec((3, frames, D), lambda i, *_: (number, i if by_tile else 0, 0))


ROWS = tiles((TILE, D), 0)
ROWS3 = tiles((TILE, 3 * D), 0)
TURNED = tiles((PT, LIVE, D), 0)


TURN = pltpu.VMEM((D // 128, TILE, 128), F32)


def shape_of(shape, dtype):
    return jax.ShapeDtypeStruct(shape, dtype)


def call(kernel, name, ins, in_specs, outs, out_specs, scratch, flops, prefetch=None):
    moved = sum(a.size * a.dtype.itemsize for a in tuple(ins) + tuple(outs))
    grid_spec = pltpu.PrefetchScalarGridSpec(
        num_scalar_prefetch=0 if prefetch is None else 1,
        grid=(GRID,),
        in_specs=in_specs,
        out_specs=out_specs,
        scratch_shapes=scratch,
    )
    fn = pl.pallas_call(
        kernel,
        grid_spec=grid_spec,
        out_shape=outs,
        name=name,
        cost_estimate=pl.CostEstimate(flops=flops, bytes_accessed=moved, transcendentals=0),
        compiler_params=pltpu.CompilerParams(
            dimension_semantics=("arbitrary",), vmem_limit_bytes=VMEM_LIMIT
        ),
    )
    return fn(*ins) if prefetch is None else fn(prefetch, *ins)


TOKENS = LIVE * PATCHES


def run_frame_forward(frames, rows, mod, wqkv, wo, bo):
    return call(
        frame_forward, "frame_forward",
        [frames] * FT + [mod, wqkv, wo, bo],
        frame_specs() + [piece_spec(0, FT, True), whole((D, 3 * D)), whole((D, D)), whole((1, D))],
        [shape_of((PATCHES, LIVE, D), F32), shape_of((TOKENS, 3 * D), BF), shape_of((TOKENS, D), BF),
         shape_of((TOKENS, D), F32)],
        [tiles((PATCHES, FT, D), 1), ROWS3, ROWS, ROWS],
        [TURN],
        2 * TOKENS * D * 4 * D, rows)


def run_turn_frames(frames, rows):
    return call(
        turn_frames, "turn_frames", [frames] * FT, frame_specs(),
        [shape_of((PATCHES, LIVE, D), F32)], [tiles((PATCHES, FT, D), 1)],
        [TURN], 1000, rows)[0]


def run_time_forward(x1, mod, seg, wqkv, wo, bo):
    return call(
        time_forward, "time_forward",
        [x1, mod, seg, wqkv, wo, bo],
        [TURNED, piece_spec(1, LIVE, False), whole((64, LANES)), whole((D, 3 * D)), whole((D, D)),
         whole((1, D))],
        [shape_of((PATCHES, LIVE, D), F32), shape_of((TOKENS, 3 * D), BF), shape_of((TOKENS, D), BF),
         shape_of((TOKENS, D), F32)],
        [TURNED, ROWS3, ROWS, ROWS],
        [], 2 * TOKENS * D * 4 * D)


def run_mlp(x2, dy, mod, win, bin_, wout, bout):
    return call(
        mlp_both, "mlp_both",
        [x2, dy, mod, win, bin_, wout, bout],
        [TURNED, TURNED, piece_spec(2, LIVE, False), whole((D, FF)), whole((1, FF)), whole((FF, D)),
         whole((1, D))],
        [shape_of((LIVE, PATCHES, D), BF), shape_of((PATCHES, LIVE, D), F32), shape_of((D, FF), F32),
         shape_of((FF, D), F32), shape_of((1, FF), F32), shape_of((1, D), F32), shape_of((3, LIVE, D), F32)],
        [tiles((LIVE, PT, D), 1), TURNED, whole((D, FF)), whole((FF, D)), whole((1, FF)), whole((1, D)),
         whole((3, LIVE, D))],
        [TURN],
        6 * 2 * TOKENS * D * FF)


def run_time_back(x1, dx2, mod, seg, qkv, o, a2, wqkv, wo):
    return call(
        time_back, "time_back",
        [x1, dx2, mod, seg, qkv, o, a2, wqkv, wo],
        [TURNED, TURNED, piece_spec(1, LIVE, False), whole((64, LANES)), ROWS3, ROWS, ROWS,
         whole((D, 3 * D)), whole((D, D))],
        [shape_of((LIVE, PATCHES, D), F32), shape_of((D, 4 * D), F32), shape_of((1, D), F32), shape_of((3, LIVE, D), F32)],
        [tiles((LIVE, PT, D), 1), whole((D, 4 * D)), whole((1, D)), whole((3, LIVE, D))],
        [pltpu.VMEM((TILE, D), BF), pltpu.VMEM((TILE, 3 * D), BF), TURN],
        2 * 2 * TOKENS * D * 4 * D)


def run_frame_back(frames, rows, dx1, mod, qkv, o, a1, wqkv, wo):
    return call(
        frame_back, "frame_back",
        [frames] * FT + [dx1, mod, qkv, o, a1, wqkv, wo],
        frame_specs() + [tiles((FT, PATCHES, D), 0), piece_spec(0, FT, True), ROWS3, ROWS, ROWS,
                         whole((D, 3 * D)), whole((D, D))],
        [shape_of((LIVE, PATCHES, D), BF), shape_of((D, 4 * D), F32), shape_of((1, D), F32), shape_of((3, LIVE, D), F32)],
        [tiles((FT, PATCHES, D), 0), whole((D, 4 * D)), whole((1, D)), piece_spec(0, FT, True)],
        [pltpu.VMEM((TILE, D), BF), pltpu.VMEM((TILE, 3 * D), BF)],
        2 * 2 * TOKENS * D * 4 * D, rows)


MESH = pl.DeviceIdType.MESH
ANY = pl.BlockSpec(memory_space=pl.ANY)


def place_of(wide):
    ring = wide
    turn = ring // 2
    w = lax.axis_index("wide")
    k = lax.axis_index("narrow")
    z, y = w // 2, w % 2
    r = z + y * (ring - 1 - 2 * z)

    def wide_at(position):
        side = position // turn
        return 2 * ((1 - side) * position + side * (ring - 1 - position)) + side

    return w, k, r, k // 2, k % 2, wide_at


def greet(peers):
    barrier = pltpu.get_barrier_semaphore()
    for peer in peers:
        pl.semaphore_signal(barrier, inc=1, device_id=peer, device_id_type=MESH)
    pl.semaphore_wait(barrier, len(peers))


def send(src, dst, send_sem, recv_sem, peer):
    return pltpu.make_async_remote_copy(
        src_ref=src, dst_ref=dst, send_sem=send_sem, recv_sem=recv_sem, device_id=peer, device_id_type=MESH
    )


def gather_kernel(ring, n, heights, ways, *refs):
    count = len(heights)
    clips, shards = refs[0], refs[1 : 1 + count]
    frames, full = refs[1 + count], refs[2 + count : 2 + 2 * count]
    clip_buf, bufs = refs[2 + 2 * count], refs[3 + 2 * count : 3 + 3 * count]
    ring_s, ring_r, core_s, core_r, x_s, x_r, clip_s, clip_r, load_sem, keep_sem = refs[3 + 3 * count :]
    w, k, r, x, c, wide_at = place_of(ring)
    other_x = (w, 2 * (1 - x) + c)
    other_c = (w, 2 * x + 1 - c)
    steps = ((wide_at((r + 1) % ring), k), (wide_at((r + ring - 1) % ring), k))
    greet(steps + tuple((w, (k + j) % n) for j in range(1, n)))

    def rows(t, position, column):
        block = 4 * wide_at(position) + 2 * column + c
        return pl.ds(pl.multiple_of(block * heights[t], 8), heights[t])

    def ring_copy(t, b, s, src=None):
        place = (r + ring - s) % ring if ways[t] == 0 else (r + s) % ring
        dst = full[t].at[rows(t, place, x if b == 0 else 1 - x)]
        return send(dst if src is None else src, dst, ring_s.at[t, b, s], ring_r.at[t, b, s], steps[ways[t]])

    def core_copy(t, b, s, src=None):
        place = (r + ring - s) % ring if ways[t] == 0 else (r + s) % ring
        dst = full[t].at[rows(t, place, x if b == 0 else 1 - x)]
        return send(dst if src is None else src, dst, core_s.at[t, b, s], core_r.at[t, b, s], other_c)

    def x_copy(t):
        dst = full[t].at[rows(t, r, x)]
        return send(shards[t], dst, x_s.at[t], x_r.at[t], other_x)

    def clip_copy(j):
        return send(clips.at[j], frames.at[j], clip_s.at[j], clip_r.at[j], (w, (k + j) % n))

    for t in range(count):
        x_copy(t).start()
        ring_copy(t, 0, 0, shards[t]).start()
    for j in range(1, n):
        clip_copy(j).start()
    for t in range(count):
        core_copy(t, 0, 0, shards[t]).start()
    loads = [pltpu.make_async_copy(clips.at[0], clip_buf, load_sem.at[count])]
    loads += [pltpu.make_async_copy(shards[t], bufs[t], load_sem.at[t]) for t in range(count)]
    keeps = [pltpu.make_async_copy(clip_buf, frames.at[0], keep_sem.at[count])]
    keeps += [pltpu.make_async_copy(bufs[t], full[t].at[rows(t, r, x)], keep_sem.at[t]) for t in range(count)]
    for copy in loads:
        copy.start()
    for copy, keep in zip(loads, keeps):
        copy.wait()
        keep.start()
    for t in range(count):
        x_copy(t).wait_recv()
        ring_copy(t, 1, 0).start()
        core_copy(t, 1, 0).start()
    for s in range(1, ring):
        for b in range(2):
            for t in range(count):
                ring_copy(t, b, s - 1).wait_recv()
                if s < ring - 1:
                    ring_copy(t, b, s).start()
                core_copy(t, b, s).start()
    for copy in keeps:
        copy.wait()
    for t in range(count):
        x_copy(t).wait_send()
        for b in range(2):
            for s in range(ring):
                if s < ring - 1:
                    ring_copy(t, b, s).wait_send()
                core_copy(t, b, s).wait()
    for j in range(1, n):
        clip_copy(j).wait()


def gather_all(clips, shards, ways, ring, n):
    count = len(shards)
    devices = ring * n
    heights = tuple(a.shape[0] for a in shards)
    sems = pltpu.SemaphoreType.DMA
    got = pl.pallas_call(
        functools.partial(gather_kernel, ring, n, heights, ways),
        name="gather_all",
        out_shape=[shape_of(clips.shape, clips.dtype)]
        + [shape_of((a.shape[0] * devices, a.shape[1]), a.dtype) for a in shards],
        in_specs=[ANY] * (1 + count),
        out_specs=[ANY] * (1 + count),
        scratch_shapes=[pltpu.VMEM(clips.shape[1:], clips.dtype)]
        + [pltpu.VMEM(a.shape, a.dtype) for a in shards]
        + [sems((count, 2, ring))] * 4
        + [sems((count,))] * 2
        + [sems((n,))] * 2
        + [sems((count + 1,))] * 2,
        compiler_params=pltpu.CompilerParams(collective_id=0, has_side_effects=True),
    )(clips, *shards)
    return got[0], got[1:]


def scatter_kernel(ring, heights, ways, *refs):
    count = len(heights)
    grads, outs, stages = refs[:count], refs[count : 2 * count], refs[2 * count : 3 * count]
    local, part, came, went, last, fin_s, fin_r = (
        refs[(3 + i) * count : (4 + i) * count] for i in range(7)
    )
    ring_s, ring_r, core_s, core_r, x_s, x_r, load_sem, part_sem = refs[10 * count :]
    w, k, r, x, c, wide_at = place_of(ring)
    other_x = (w, 2 * (1 - x) + c)
    other_c = (w, 2 * x + 1 - c)
    steps = ((wide_at((r + 1) % ring), k), (wide_at((r + ring - 1) % ring), k))
    greet(steps + (other_x, other_c))
    final = ring - 1

    def place(t, s):
        return (r + 2 * ring - 1 - s) % ring if ways[t] == 0 else (r + 1 + s) % ring

    def rows(t, s, column, core):
        block = 4 * wide_at(place(t, s)) + 2 * column + core
        return pl.ds(pl.multiple_of(block * heights[t], 8), heights[t])

    def half(t, column):
        return pl.ds(column * heights[t], heights[t])

    def core_copy(t, s, column):
        return send(grads[t].at[rows(t, s, column, 1 - c)], stages[t].at[s, half(t, column)],
                    core_s.at[t, s, column], core_r.at[t, s, column], other_c)

    def local_load(t, s, slot, column):
        return pltpu.make_async_copy(grads[t].at[rows(t, s, column, c)], local[t].at[slot, half(t, column)],
                                     load_sem.at[t, slot, column])

    def part_load(t, s, slot):
        return pltpu.make_async_copy(stages[t].at[s], part[t].at[slot], part_sem.at[t, slot])

    def ring_copy(t, s):
        return send(went[t].at[s], came[t].at[s], ring_s.at[t, s], ring_r.at[t, s], steps[ways[t]])

    def x_copy(t):
        return send(fin_s[t], fin_r[t], x_s.at[t], x_r.at[t], other_x)

    order = (0, 2, 1, 3)

    def fetch(t, s, slot):
        for column in range(2):
            core_copy(t, s, column).wait_recv()
        part_load(t, s, slot).start()
        for column in range(2):
            local_load(t, s, slot, column).start()

    def total(t, s, slot):
        for column in range(2):
            local_load(t, s, slot, column).wait()
        part_load(t, s, slot).wait()
        return local[t][slot] + part[t][slot]

    for t in order:
        for column in range(2):
            core_copy(t, 0, column).start()
    for s in range(1, ring):
        for t in order:
            for column in range(2):
                core_copy(t, s, column).start()
    for t in order:
        fetch(t, 0, 0)
    for t in order:
        fetch(t, 1, 1)
        went[t][0] = total(t, 0, 0).astype(BF)
        ring_copy(t, 0).start()

    def body(s, carry):
        slot = s % 2
        for t in order:
            fetch(t, s + 1, 1 - slot)
            value = total(t, s, slot)
            ring_copy(t, s - 1).wait_recv()
            went[t][s] = (value + came[t][s - 1].astype(F32)).astype(BF)
            ring_copy(t, s).start()
        return carry

    lax.fori_loop(1, final, body, 0)
    for t in order:
        value = total(t, final, final % 2)
        ring_copy(t, final - 1).wait_recv()
        value = value + came[t][final - 1].astype(F32)
        last[t][0] = value[: heights[t]]
        last[t][1] = value[heights[t] :]
        fin_s[t][...] = last[t][1 - x].astype(BF)
        x_copy(t).start()
    for t in order:
        x_copy(t).wait_recv()
        outs[t][...] = last[t][x] + fin_r[t][...].astype(F32)
    for t in order:
        x_copy(t).wait_send()
        for s in range(final):
            ring_copy(t, s).wait_send()
        for s in range(ring):
            for column in range(2):
                core_copy(t, s, column).wait_send()


def scatter_all(grads, ways, ring, n):
    count = len(grads)
    devices = ring * n
    heights = tuple(g.shape[0] // devices for g in grads)
    widths = tuple(g.shape[1] for g in grads)
    each = tuple(zip(heights, widths))
    sems = pltpu.SemaphoreType.DMA
    vmem = pltpu.VMEM
    got = pl.pallas_call(
        functools.partial(scatter_kernel, ring, heights, ways),
        name="scatter_all",
        out_shape=[shape_of(hw, F32) for hw in each]
        + [shape_of((ring, 2 * h, wd), F32) for h, wd in each],
        in_specs=[ANY] * count,
        out_specs=[pl.BlockSpec(memory_space=pltpu.VMEM)] * count + [ANY] * count,
        scratch_shapes=[vmem((2, 2 * h, wd), F32) for h, wd in each]
        + [vmem((2, 2 * h, wd), F32) for h, wd in each]
        + [vmem((ring - 1, 2 * h, wd), BF) for h, wd in each]
        + [vmem((ring - 1, 2 * h, wd), BF) for h, wd in each]
        + [vmem((2, h, wd), F32) for h, wd in each]
        + [vmem((h, wd), BF) for h, wd in each]
        + [vmem((h, wd), BF) for h, wd in each]
        + [sems((count, ring))] * 2
        + [sems((count, ring, 2))] * 2
        + [sems((count,))] * 2
        + [sems((count, 2, 2)), sems((count, 2))],
        compiler_params=pltpu.CompilerParams(
            collective_id=1, has_side_effects=True, vmem_limit_bytes=VMEM_LIMIT
        ),
    )(*grads)
    return got[:count]


def tuned(mesh):
    wide, n = mesh.shape["wide"], mesh.shape["narrow"]
    if n != 4 or wide < 4 or wide % 2 or D % (8 * wide * n):
        return False
    for w in range(wide):
        for k in range(n):
            device = mesh.devices[w, k]
            here = (getattr(device, "coords", None), getattr(device, "core_on_chip", None))
            if here[0] is None or tuple(here[0]) != (k // 2, w % 2, w // 2) or here[1] != k % 2:
                return False
    return True


def exchange(x):
    return lax.all_to_all(x, ALL, split_axis=0, concat_axis=0, tiled=True)


def shift_clips(clips, back):
    n = lax.axis_size("narrow")
    parts = [clips[0]]
    for j in range(1, n):
        step = -j if back else j
        parts.append(lax.ppermute(clips[j], "narrow", [(s, (s + step) % n) for s in range(n)]))
    return jnp.stack(parts)


def local(fast, clips, t_emb, lengths, task, w_mod, b_mod, w_qkv_s, w_o_s, b_o_s, w_qkv_t, w_o_t, b_o_t,
          w_in, b_in, w_out, b_out, cotangent):
    n = lax.axis_size("narrow")
    wide = lax.axis_size("wide")
    devices = n * wide
    part = w_mod.shape[0]
    mod_cols = w_mod.shape[1] // devices
    rank = lax.axis_index("narrow")
    slots = jnp.arange(n, dtype=jnp.int32)
    from_clip = (rank - slots) % n
    recv_len = lengths.reshape(n, n)[from_clip, slots]
    recv_task = task.reshape(n, n, FR)[from_clip, slots]
    ends = jnp.cumsum(recv_len)
    starts = ends - recv_len
    ids = jnp.arange(LIVE, dtype=jnp.int32)
    source = jnp.sum((ends[None, :] <= ids[:, None]).astype(jnp.int32), axis=1)
    within = ids - starts[source]
    pack_rows = source * FR + within
    row_choice = source * 2 + recv_task[source, within]
    frame_ids = jnp.arange(FR, dtype=jnp.int32)
    live_back = frame_ids[None, :] < recv_len[:, None]
    unpack_rows = jnp.where(live_back, starts[:, None] + frame_ids[None, :], 0).reshape(-1)
    row_id = jnp.arange(64, dtype=jnp.int32)
    col_id = jnp.arange(LANES, dtype=jnp.int32) % 64
    seg = (
        (row_id[:, None] // LIVE == col_id[None, :] // LIVE)
        & (source[row_id % LIVE][:, None] == source[col_id % LIVE][None, :])
    ).astype(F32)

    def gather(w):
        return lax.all_gather(w, ALL, axis=0, tiled=True)

    weights = (w_in, w_out, w_qkv_t, w_o_t, w_qkv_s, w_o_s)
    if fast:
        frames, weights = gather_all(clips, weights, (0, 0, 1, 1, 1, 1), wide, n)
    else:
        frames = shift_clips(clips, False)
        weights = [gather(w) for w in weights]
    win, wout, wqkv_t, wo_t, wqkv_s, wo_s = weights
    frames = frames.reshape(n * FR, PATCHES, D)

    wm = jnp.swapaxes(w_mod.reshape(part, devices, mod_cols), 0, 1).reshape(devices, -1)
    emb = jnp.broadcast_to(t_emb.reshape(1, -1), (devices, t_emb.size))
    small = jnp.concatenate([b_o_s, b_o_t, b_in, b_out])
    small_all = jnp.broadcast_to(small[None], (devices, small.size))
    got = exchange(jnp.concatenate([wm, emb, small_all], axis=1))
    wm_cols = got[:, : part * mod_cols].reshape(D, mod_cols)
    emb_all = got[:, part * mod_cols : part * mod_cols + t_emb.size].reshape(-1, D)
    small_got = got[:, part * mod_cols + t_emb.size :]
    b1 = b_o_s.size
    bias_s = small_got[:, :b1].reshape(1, -1).astype(F32)
    bias_t = small_got[:, b1 : 2 * b1].reshape(1, -1).astype(F32)
    bias_in = small_got[:, 2 * b1 : 2 * b1 + b_in.size].reshape(1, -1).astype(F32)
    bias_out = small_got[:, 2 * b1 + b_in.size :].reshape(1, -1).astype(F32)
    emb_f = emb_all.astype(F32)
    silu_low = (emb_f * jax.nn.sigmoid(emb_f)).astype(BF)
    mod_part = dot(silu_low, wm_cols) + b_mod.astype(F32)[None]
    mod_part = mod_part.reshape(wide, n, n, 2, mod_cols)
    mod_part = jnp.stack([jnp.roll(mod_part[:, :, c], c, axis=1) for c in range(n)], axis=2)
    mod_rows = exchange(mod_part.reshape(devices, -1)).reshape(devices, 2 * n, mod_cols)
    mod_rows = jnp.swapaxes(mod_rows, 0, 1).reshape(2 * n, 9, D)
    mod = jnp.swapaxes(mod_rows[row_choice], 0, 1)

    x1, qkv1, o1, a1 = run_frame_forward(frames, pack_rows, mod, wqkv_s, wo_s, bias_s)
    x2, qkv2, o2, a2 = run_time_forward(x1, mod, seg, wqkv_t, wo_t, bias_t)
    cots = shift_clips(cotangent, False).reshape(n * FR, PATCHES, D)
    dy = run_turn_frames(cots, pack_rows)
    out, dx2, g_in, g_out, gb_in, gb_out, dmod3 = run_mlp(x2, dy, mod, win, bias_in, wout, bias_out)

    def unpack(packed):
        spread = jnp.take(packed, unpack_rows, axis=0).reshape(n, FR, PATCHES, D)
        spread = jnp.where(live_back[:, :, None, None], spread, jnp.zeros((), packed.dtype))
        return shift_clips(spread, True)

    def scatter(g):
        return lax.psum_scatter(g.astype(BF), ALL, scatter_dimension=0, tiled=True).astype(F32)

    layer_out = unpack(out)
    dx1, g_t, gb_t, dmod2 = run_time_back(x1, dx2, mod, seg, qkv2, o2, a2, wqkv_t, wo_t)
    dx0, g_s, gb_s, dmod1 = run_frame_back(
        frames, pack_rows, dx1, mod, qkv1, o1, a1, wqkv_s, wo_s)
    grad_clips = unpack(dx0)
    grads = (g_in, g_out, g_t, g_s)
    if fast:
        s_in, s_out, s_t, s_s = scatter_all(grads, (0, 0, 1, 1), wide, n)
    else:
        s_in, s_out, s_t, s_s = [scatter(g) for g in grads]

    grad_frames = jnp.swapaxes(jnp.concatenate([dmod1, dmod2, dmod3], axis=0), 0, 1).reshape(LIVE, 9 * D)
    chooser = (row_choice[:, None] == jnp.arange(2 * n, dtype=jnp.int32)[None, :]).astype(F32)
    grad_rows = lax.dot_general(
        chooser, grad_frames, (((0,), (0,)), ((), ())), precision=lax.Precision.HIGHEST
    ).astype(BF)
    d_cols = exchange(jnp.swapaxes(grad_rows.reshape(2 * n, devices, mod_cols), 0, 1).reshape(devices, -1))
    d_cols = d_cols.reshape(wide, n, n, 2, mod_cols)
    d_cols = jnp.stack([jnp.roll(d_cols[:, :, c], -c, axis=1) for c in range(n)], axis=2)
    d_cols = d_cols.reshape(devices * 2 * n, mod_cols)
    grad_b_mod = jnp.sum(d_cols.astype(F32), axis=0)
    gwm_cols = dot_tn(silu_low, d_cols)
    g_emb = dot_nt(d_cols, wm_cols)
    gb_all = jnp.concatenate(
        [gb_s.reshape(devices, -1), gb_t.reshape(devices, -1), gb_in.reshape(devices, -1),
         gb_out.reshape(devices, -1)], axis=1)
    final = exchange(jnp.concatenate(
        [gwm_cols.reshape(devices, -1), g_emb.reshape(devices, -1), gb_all], axis=1))
    cut1 = part * mod_cols
    cut2 = cut1 + t_emb.size
    grad_w_mod = jnp.swapaxes(final[:, :cut1].reshape(devices, part, mod_cols), 0, 1).reshape(part, -1)
    emb_own = t_emb.astype(F32)
    sig = jax.nn.sigmoid(emb_own)
    grad_emb = jnp.sum(final[:, cut1:cut2], axis=0).reshape(t_emb.shape)
    grad_t_emb = (grad_emb * (sig * (1.0 + emb_own * (1.0 - sig)))).astype(BF)
    gb = jnp.sum(final[:, cut2:], axis=0)
    return (
        layer_out,
        grad_clips,
        grad_t_emb,
        grad_w_mod,
        grad_b_mod,
        s_s[:, : 3 * D],
        s_s[:, 3 * D :],
        gb[:b1],
        s_t[:, : 3 * D],
        s_t[:, 3 * D :],
        gb[b1 : 2 * b1],
        s_in,
        gb[2 * b1 : 2 * b1 + b_in.size],
        s_out,
        gb[2 * b1 + b_in.size :],
    )


def solution(mesh):
    full = P(ALL)
    placed = (full, full, P("wide"), P("wide")) + (full,) * 13
    return jax.shard_map(functools.partial(local, tuned(mesh)), mesh=mesh, in_specs=placed, out_specs=(full,) * 15, check_vma=False)
```

```python
import functools

import jax
import jax.numpy as jnp
from jax import lax
from jax.experimental import pallas as pl
from jax.experimental.pallas import tpu as pltpu
from jax.sharding import PartitionSpec as P

D = 768
HEADS = 12
HEAD = 64
FF = 3072
FR = 16
PATCHES = 64
LIVE = 2 * FR
EPS = 1e-06
BF = jnp.bfloat16
F32 = jnp.float32
ALL = ("wide", "narrow")
PAIRS = HEADS // 2
LANES = 2 * HEAD
BACK_PAIRS = 6
TILE = 512
FT = TILE // PATCHES
PT = TILE // LIVE
GRID = LIVE * PATCHES // TILE
GROUPS = TILE // 64
GELU_C = 0.7978845608028654
GELU_A = 0.044715
VMEM_LIMIT = 66 * 1000 * 1000
MESH = pl.DeviceIdType.MESH
ANY = pl.BlockSpec(memory_space=pl.ANY)


def dot(a, b):
    return lax.dot_general(a, b, (((1,), (0,)), ((), ())), preferred_element_type=F32)


def dot_nt(a, b):
    return lax.dot_general(a, b, (((1,), (1,)), ((), ())), preferred_element_type=F32)


def dot_tn(a, b):
    return lax.dot_general(a, b, (((0,), (0,)), ((), ())), preferred_element_type=F32)


def normalise(x):
    mean = jnp.mean(x, axis=-1, keepdims=True)
    centred = x - mean
    var = jnp.mean(centred * centred, axis=-1, keepdims=True)
    rstd = lax.rsqrt(var + EPS)
    return centred * rstd, rstd


def norm_back(dn, xhat, rstd):
    m1 = jnp.mean(dn, axis=-1, keepdims=True)
    m2 = jnp.mean(dn * xhat, axis=-1, keepdims=True)
    return rstd * (dn - m1 - xhat * m2)


def lane_masks():
    lane = lax.broadcasted_iota(jnp.int32, (64, LANES), 1)
    low_lanes = lane < HEAD
    low = jnp.where(low_lanes, 1.0, 0.0).astype(BF)
    high = jnp.where(low_lanes, 0.0, 1.0).astype(BF)
    return low_lanes, low, high


def split_heads(x, low, high):
    return jnp.concatenate([x * low, x * high], axis=0)


def softmax_keys(s, mask):
    if mask is not None:
        s = jnp.where(mask, s, -1e30)
    top = jnp.max(s, axis=0, keepdims=True)
    e = jnp.exp(s - top)
    return e * (1.0 / jnp.sum(e, axis=0, keepdims=True))


def pair_cols(part, hp):
    return slice(part * D + hp * LANES, part * D + (hp + 1) * LANES)


def attend(qkv_ref, o_ref, mask):
    low_lanes, low, high = lane_masks()
    scale = HEAD ** (-0.5)

    def body(g, carry):
        rows = pl.ds(pl.multiple_of(g * 64, 64), 64)
        pairs = range(PAIRS)
        s = [dot_nt(qkv_ref[rows, pair_cols(1, hp)], split_heads(qkv_ref[rows, pair_cols(0, hp)], low * scale, high * scale))
             for hp in pairs]
        p = [softmax_keys(t, mask).astype(BF) for t in s]
        r = [dot_tn(p[hp], qkv_ref[rows, pair_cols(2, hp)]) for hp in pairs]
        for hp in pairs:
            o_ref[rows, pair_cols(0, hp)] = jnp.where(low_lanes, r[hp][:64], r[hp][64:]).astype(BF)
        return carry

    lax.fori_loop(0, GROUPS, body, 0)


def attend_back(qkv_ref, do_ref, dqkv_ref, mask):
    low_lanes, low, high = lane_masks()
    scale = HEAD ** (-0.5)

    def body(g, carry):
        rows = pl.ds(pl.multiple_of(g * 64, 64), 64)
        for first in range(0, PAIRS, BACK_PAIRS):
            pairs = range(first, first + BACK_PAIRS)
            qb = [split_heads(qkv_ref[rows, pair_cols(0, hp)], low * scale, high * scale) for hp in pairs]
            dob = [split_heads(do_ref[rows, pair_cols(0, hp)], low, high) for hp in pairs]
            s = [dot_nt(qkv_ref[rows, pair_cols(1, hp)], q) for hp, q in zip(pairs, qb)]
            dp = [dot_nt(qkv_ref[rows, pair_cols(2, hp)], d) for hp, d in zip(pairs, dob)]
            p = [softmax_keys(t, mask) for t in s]
            delta = [jnp.sum(a * b, axis=0, keepdims=True) for a, b in zip(p, dp)]
            ds = [(a * (b - c)).astype(BF) for a, b, c in zip(p, dp, delta)]
            dv = [dot(a.astype(BF), d) for a, d in zip(p, dob)]
            dk = [dot(a, q) for a, q in zip(ds, qb)]
            r = [dot_tn(a, qkv_ref[rows, pair_cols(1, hp)]) for hp, a in zip(pairs, ds)]
            for i, hp in enumerate(pairs):
                dqkv_ref[rows, pair_cols(2, hp)] = dv[i].astype(BF)
                dqkv_ref[rows, pair_cols(1, hp)] = dk[i].astype(BF)
                dq = jnp.where(low_lanes, r[i][:64], r[i][64:]) * scale
                dqkv_ref[rows, pair_cols(0, hp)] = dq.astype(BF)
        return carry

    lax.fori_loop(0, GROUPS, body, 0)


def swap_major(value, scratch, out_ref, first, second):
    for b in range(D // 128):
        cols = slice(b * 128, (b + 1) * 128)
        for i in range(first):
            scratch[b, pl.ds(i, second, stride=first), :] = value[i * second : (i + 1) * second, cols]
        out_ref[:, :, cols] = scratch[b].reshape(second, first, 128).astype(out_ref.dtype)


def frames_of(refs):
    return jnp.concatenate([r[0] for r in refs], axis=0).astype(F32)


def per_frame(piece):
    return jnp.broadcast_to(piece[:, None, :], (FT, PATCHES, D)).reshape(TILE, D)


def per_patch(piece):
    return jnp.broadcast_to(piece[None], (PT, LIVE, D)).reshape(TILE, D)


def sum_patches(value):
    return jnp.sum(value.reshape(FT, PATCHES, D), axis=1)


def sum_groups(value):
    return jnp.sum(value.reshape(PT, LIVE, D), axis=0)


def attn_mask(seg_ref):
    return seg_ref[...] > 0.0


def frame_forward(frames, mod, wqkv, wo, bo, x1t, qkv, o, a1, scratch):
    x = frames[...].reshape(TILE, D).astype(F32)
    xhat, _ = normalise(x)
    h = (xhat * (1.0 + per_frame(mod[1])) + per_frame(mod[0])).astype(BF)
    qkv[...] = dot(h, wqkv[...]).astype(BF)
    attend(qkv, o, None)
    branch = dot(o[...], wo[...]) + bo[...]
    a1[...] = branch
    x1 = x + per_frame(mod[2]) * branch
    swap_major(x1, scratch, x1t, FT, PATCHES)


def turn_frames(rows_ref, *refs):
    x_refs, (out, scratch) = refs[:FT], refs[FT:]
    swap_major(frames_of(x_refs), scratch, out, FT, PATCHES)


def time_forward(x1, mod, seg, wqkv, wo, bo, x2, qkv, o, a2):
    x = x1[...].reshape(TILE, D)
    xhat, _ = normalise(x)
    h = (xhat * (1.0 + per_patch(mod[1])) + per_patch(mod[0])).astype(BF)
    qkv[...] = dot(h, wqkv[...]).astype(BF)
    attend(qkv, o, attn_mask(seg))
    branch = dot(o[...], wo[...]) + bo[...]
    a2[...] = branch
    x2[...] = (x + per_patch(mod[2]) * branch).reshape(PT, LIVE, D)


def mlp_both(x2, dy, mod, win, bin_, wout, bout, out, dx2, gwin, gwout, gbin, gbout, dmod, scratch):
    first = pl.program_id(0) == 0

    @pl.when(first)
    def _():
        gwin[...] = jnp.zeros_like(gwin)
        gwout[...] = jnp.zeros_like(gwout)
        gbin[...] = jnp.zeros_like(gbin)
        gbout[...] = jnp.zeros_like(gbout)
        dmod[...] = jnp.zeros_like(dmod)

    x = x2[...].reshape(TILE, D)
    xhat, rstd = normalise(x)
    h = (xhat * (1.0 + per_patch(mod[1])) + per_patch(mod[0])).astype(BF)
    gate = per_patch(mod[2])
    grad = dy[...].reshape(TILE, D)
    da = (grad * gate).astype(BF)
    gbout[...] += jnp.sum(da.astype(F32), axis=0, keepdims=True)
    branch = jnp.zeros((TILE, D), F32) + bout[...]
    dh = jnp.zeros((TILE, D), F32)
    for j in range(FF // D):
        cols = slice(j * D, (j + 1) * D)
        u = dot(h, win[:, cols]) + bin_[:, cols]
        u2 = u * u
        t = jnp.tanh(GELU_C * u * (1.0 + GELU_A * u2))
        half = 0.5 * (1.0 + t)
        g = (u * half).astype(BF)
        slope = half + (0.5 * GELU_C) * u * (1.0 - t * t) * (1.0 + 3.0 * GELU_A * u2)
        branch = branch + dot(g, wout[cols, :])
        du = (dot_nt(da, wout[cols, :]) * slope).astype(BF)
        gwout[cols, :] += dot_tn(g, da)
        gbin[:, cols] += jnp.sum(du.astype(F32), axis=0, keepdims=True)
        gwin[:, cols] += dot_tn(h, du)
        dh = dh + dot_nt(du, win[:, cols])
    swap_major(x + gate * branch, scratch, out, PT, LIVE)
    dmod[2] += sum_groups(grad * branch)
    dmod[0] += sum_groups(dh)
    dmod[1] += sum_groups(dh * xhat)
    back = norm_back(dh * (1.0 + per_patch(mod[1])), xhat, rstd)
    dx2[...] = (grad + back).reshape(PT, LIVE, D)


def attn_back_tile(x, grad, shift, scale, gate, branch, qkv, o, wqkv, wo, gw, gbo, do, dqkv, mask):
    first = pl.program_id(0) == 0

    @pl.when(first)
    def _():
        gw[...] = jnp.zeros_like(gw)
        gbo[...] = jnp.zeros_like(gbo)

    da = (grad * gate).astype(BF)
    do[...] = dot_nt(da, wo[...]).astype(BF)
    gw[:, 3 * D :] += dot_tn(o[...], da)
    gbo[...] += jnp.sum(da.astype(F32), axis=0, keepdims=True)
    attend_back(qkv, do, dqkv, mask)
    xhat, rstd = normalise(x)
    h = (xhat * (1.0 + scale) + shift).astype(BF)
    dh = jnp.zeros((TILE, D), F32)
    for j in range(3):
        cols = slice(j * D, (j + 1) * D)
        part = dqkv[:, cols]
        gw[:, cols] += dot_tn(h, part)
        dh = dh + dot_nt(part, wqkv[:, cols])
    dx = grad + norm_back(dh * (1.0 + scale), xhat, rstd)
    return dx, dh, dh * xhat, grad * branch


def time_back(x1, dx2, mod, seg, qkv, o, a2, wqkv, wo, dx1, gw, gbo, dmod, do, dqkv, scratch):
    @pl.when(pl.program_id(0) == 0)
    def _():
        dmod[...] = jnp.zeros_like(dmod)

    dx, d_shift, d_scale, d_gate = attn_back_tile(
        x1[...].reshape(TILE, D), dx2[...].reshape(TILE, D), per_patch(mod[0]), per_patch(mod[1]),
        per_patch(mod[2]), a2[...], qkv, o, wqkv, wo, gw, gbo, do, dqkv, attn_mask(seg))
    dmod[0] += sum_groups(d_shift)
    dmod[1] += sum_groups(d_scale)
    dmod[2] += sum_groups(d_gate)
    swap_major(dx, scratch, dx1, PT, LIVE)


def frame_back(frames, dx1, mod, qkv, o, a1, wqkv, wo, dx0, gw, gbo, dmod, do, dqkv):
    dx, d_shift, d_scale, d_gate = attn_back_tile(
        frames[...].reshape(TILE, D).astype(F32), dx1[...].reshape(TILE, D), per_frame(mod[0]), per_frame(mod[1]),
        per_frame(mod[2]), a1[...], qkv, o, wqkv, wo, gw, gbo, do, dqkv, None)
    dmod[0] = sum_patches(d_shift)
    dmod[1] = sum_patches(d_scale)
    dmod[2] = sum_patches(d_gate)
    dx0[...] = dx.reshape(FT, PATCHES, D).astype(BF)


def frame_specs():
    return [
        pl.BlockSpec((1, PATCHES, D), functools.partial(lambda j, i, rows: (rows[FT * i + j], 0, 0), j))
        for j in range(FT)
    ]


def whole(shape):
    return pl.BlockSpec(shape, lambda i, *_: (0,) * len(shape), pipeline_mode=pl.Buffered(1))


def tiles(shape, dim):
    return pl.BlockSpec(shape, lambda i, *_: tuple(i if a == dim else 0 for a in range(len(shape))))


def piece_spec(number, frames, by_tile):
    return pl.BlockSpec((3, frames, D), lambda i, *_: (number, i if by_tile else 0, 0))


ROWS = tiles((TILE, D), 0)
ROWS3 = tiles((TILE, 3 * D), 0)
TURNED = tiles((PT, LIVE, D), 0)


TURN = pltpu.VMEM((D // 128, TILE, 128), F32)


def shape_of(shape, dtype):
    return jax.ShapeDtypeStruct(shape, dtype)


def clip_copies(n, js, back, src, dst, send_sem, recv_sem):
    w, k = lax.axis_index("wide"), lax.axis_index("narrow")
    return [
        send(src.at[j], dst.at[i], send_sem.at[i], recv_sem.at[i], (w, (k + (n - j if back else j)) % n))
        for i, j in enumerate(js)
    ]


def carrying(kernel, count, n, js, back, *refs):
    src, ins, dst, rest = refs[0], refs[1 : 1 + count], refs[1 + count], refs[2 + count : -2]
    copies = clip_copies(n, js, back, src, dst, *refs[-2:])

    @pl.when(pl.program_id(0) == 0)
    def _():
        w, k = lax.axis_index("wide"), lax.axis_index("narrow")
        greet([(w, (k + j) % n) for j in js])
        for copy in copies:
            copy.start()

    kernel(*ins, *rest)

    @pl.when(pl.program_id(0) == GRID - 1)
    def _():
        for copy in copies:
            copy.wait()


def call(kernel, name, ins, in_specs, outs, out_specs, scratch, flops, prefetch=None, carry=None):
    moved = sum(a.size * a.dtype.itemsize for a in tuple(ins) + tuple(outs))
    params = {}
    if carry is not None:
        src, n, js, back, number = carry
        kernel = functools.partial(carrying, kernel, len(ins), n, js, back)
        ins, in_specs = [src] + ins, [ANY] + in_specs
        outs, out_specs = [shape_of((len(js),) + src.shape[1:], src.dtype)] + outs, [ANY] + out_specs
        scratch = scratch + [pltpu.SemaphoreType.DMA((len(js),))] * 2
        params = dict(collective_id=number, has_side_effects=True)
    grid_spec = pltpu.PrefetchScalarGridSpec(
        num_scalar_prefetch=0 if prefetch is None else 1,
        grid=(GRID,),
        in_specs=in_specs,
        out_specs=out_specs,
        scratch_shapes=scratch,
    )
    fn = pl.pallas_call(
        kernel,
        grid_spec=grid_spec,
        out_shape=outs,
        name=name,
        cost_estimate=pl.CostEstimate(flops=flops, bytes_accessed=moved, transcendentals=0),
        compiler_params=pltpu.CompilerParams(
            dimension_semantics=("arbitrary",), vmem_limit_bytes=VMEM_LIMIT, **params
        ),
    )
    return fn(*ins) if prefetch is None else fn(prefetch, *ins)


TOKENS = LIVE * PATCHES


def run_frame_forward(frames, mod, wqkv, wo, bo, carry=None):
    return call(
        frame_forward, "frame_forward",
        [frames, mod, wqkv, wo, bo],
        [tiles((FT, PATCHES, D), 0), piece_spec(0, FT, True), whole((D, 3 * D)), whole((D, D)), whole((1, D))],
        [shape_of((PATCHES, LIVE, D), F32), shape_of((TOKENS, 3 * D), BF), shape_of((TOKENS, D), BF),
         shape_of((TOKENS, D), F32)],
        [tiles((PATCHES, FT, D), 1), ROWS3, ROWS, ROWS],
        [TURN],
        2 * TOKENS * D * 4 * D, carry=carry)


def run_turn_frames(frames, rows):
    return call(
        turn_frames, "turn_frames", [frames] * FT, frame_specs(),
        [shape_of((PATCHES, LIVE, D), F32)], [tiles((PATCHES, FT, D), 1)],
        [TURN], 1000, rows)[0]


def run_time_forward(x1, mod, seg, wqkv, wo, bo, carry=None):
    return call(
        time_forward, "time_forward",
        [x1, mod, seg, wqkv, wo, bo],
        [TURNED, piece_spec(1, LIVE, False), whole((64, LANES)), whole((D, 3 * D)), whole((D, D)),
         whole((1, D))],
        [shape_of((PATCHES, LIVE, D), F32), shape_of((TOKENS, 3 * D), BF), shape_of((TOKENS, D), BF),
         shape_of((TOKENS, D), F32)],
        [TURNED, ROWS3, ROWS, ROWS],
        [], 2 * TOKENS * D * 4 * D, carry=carry)


def run_mlp(x2, dy, mod, win, bin_, wout, bout):
    return call(
        mlp_both, "mlp_both",
        [x2, dy, mod, win, bin_, wout, bout],
        [TURNED, TURNED, piece_spec(2, LIVE, False), whole((D, FF)), whole((1, FF)), whole((FF, D)),
         whole((1, D))],
        [shape_of((LIVE, PATCHES, D), BF), shape_of((PATCHES, LIVE, D), F32), shape_of((D, FF), F32),
         shape_of((FF, D), F32), shape_of((1, FF), F32), shape_of((1, D), F32), shape_of((3, LIVE, D), F32)],
        [tiles((LIVE, PT, D), 1), TURNED, whole((D, FF)), whole((FF, D)), whole((1, FF)), whole((1, D)),
         whole((3, LIVE, D))],
        [TURN],
        6 * 2 * TOKENS * D * FF)


def run_time_back(x1, dx2, mod, seg, qkv, o, a2, wqkv, wo, carry=None):
    return call(
        time_back, "time_back",
        [x1, dx2, mod, seg, qkv, o, a2, wqkv, wo],
        [TURNED, TURNED, piece_spec(1, LIVE, False), whole((64, LANES)), ROWS3, ROWS, ROWS,
         whole((D, 3 * D)), whole((D, D))],
        [shape_of((LIVE, PATCHES, D), F32), shape_of((D, 4 * D), F32), shape_of((1, D), F32), shape_of((3, LIVE, D), F32)],
        [tiles((LIVE, PT, D), 1), whole((D, 4 * D)), whole((1, D)), whole((3, LIVE, D))],
        [pltpu.VMEM((TILE, D), BF), pltpu.VMEM((TILE, 3 * D), BF), TURN],
        2 * 2 * TOKENS * D * 4 * D, carry=carry)


def run_frame_back(frames, dx1, mod, qkv, o, a1, wqkv, wo, carry=None):
    return call(
        frame_back, "frame_back",
        [frames, dx1, mod, qkv, o, a1, wqkv, wo],
        [tiles((FT, PATCHES, D), 0), tiles((FT, PATCHES, D), 0), piece_spec(0, FT, True), ROWS3, ROWS, ROWS,
                         whole((D, 3 * D)), whole((D, D))],
        [shape_of((LIVE, PATCHES, D), BF), shape_of((D, 4 * D), F32), shape_of((1, D), F32), shape_of((3, LIVE, D), F32)],
        [tiles((FT, PATCHES, D), 0), whole((D, 4 * D)), whole((1, D)), piece_spec(0, FT, True)],
        [pltpu.VMEM((TILE, D), BF), pltpu.VMEM((TILE, 3 * D), BF)],
        2 * 2 * TOKENS * D * 4 * D, carry=carry)


def place_of(wide):
    ring = wide
    turn = ring // 2
    w = lax.axis_index("wide")
    k = lax.axis_index("narrow")
    z, y = w // 2, w % 2
    r = z + y * (ring - 1 - 2 * z)

    def wide_at(position):
        side = position // turn
        return 2 * ((1 - side) * position + side * (ring - 1 - position)) + side

    return w, k, r, k // 2, k % 2, wide_at


def greet(peers):
    barrier = pltpu.get_barrier_semaphore()
    for peer in peers:
        pl.semaphore_signal(barrier, inc=1, device_id=peer, device_id_type=MESH)
    pl.semaphore_wait(barrier, len(peers))


def send(src, dst, send_sem, recv_sem, peer):
    return pltpu.make_async_remote_copy(
        src_ref=src, dst_ref=dst, send_sem=send_sem, recv_sem=recv_sem, device_id=peer, device_id_type=MESH
    )


def gather_kernel(ring, n, heights, ways, *refs):
    count = len(heights)
    clips, shards = refs[0], refs[1 : 1 + count]
    frames, full = refs[1 + count], refs[2 + count : 2 + 2 * count]
    clip_buf, bufs = refs[2 + 2 * count], refs[3 + 2 * count : 3 + 3 * count]
    ring_s, ring_r, core_s, core_r, x_s, x_r, clip_s, clip_r, load_sem, keep_sem = refs[3 + 3 * count :]
    w, k, r, x, c, wide_at = place_of(ring)
    other_x = (w, 2 * (1 - x) + c)
    other_c = (w, 2 * x + 1 - c)
    steps = ((wide_at((r + 1) % ring), k), (wide_at((r + ring - 1) % ring), k))
    greet(steps + tuple((w, (k + j) % n) for j in range(1, n)))

    def rows(t, position, column):
        block = 4 * wide_at(position) + 2 * column + c
        return pl.ds(pl.multiple_of(block * heights[t], 8), heights[t])

    def ring_copy(t, b, s, src=None):
        place = (r + ring - s) % ring if ways[t] == 0 else (r + s) % ring
        dst = full[t].at[rows(t, place, x if b == 0 else 1 - x)]
        return send(dst if src is None else src, dst, ring_s.at[t, b, s], ring_r.at[t, b, s], steps[ways[t]])

    def core_copy(t, b, s, src=None):
        place = (r + ring - s) % ring if ways[t] == 0 else (r + s) % ring
        dst = full[t].at[rows(t, place, x if b == 0 else 1 - x)]
        return send(dst if src is None else src, dst, core_s.at[t, b, s], core_r.at[t, b, s], other_c)

    def x_copy(t):
        dst = full[t].at[rows(t, r, x)]
        return send(shards[t], dst, x_s.at[t], x_r.at[t], other_x)

    def clip_copy(j):
        return send(clips.at[j], frames.at[j], clip_s.at[j], clip_r.at[j], (w, (k + j) % n))

    for t in range(count):
        x_copy(t).start()
        ring_copy(t, 0, 0, shards[t]).start()
    for j in range(1, n):
        clip_copy(j).start()
    for t in range(count):
        core_copy(t, 0, 0, shards[t]).start()
    loads = [pltpu.make_async_copy(clips.at[0], clip_buf, load_sem.at[count])]
    loads += [pltpu.make_async_copy(shards[t], bufs[t], load_sem.at[t]) for t in range(count)]
    keeps = [pltpu.make_async_copy(clip_buf, frames.at[0], keep_sem.at[count])]
    keeps += [pltpu.make_async_copy(bufs[t], full[t].at[rows(t, r, x)], keep_sem.at[t]) for t in range(count)]
    for copy in loads:
        copy.start()
    for copy, keep in zip(loads, keeps):
        copy.wait()
        keep.start()
    for t in range(count):
        x_copy(t).wait_recv()
        ring_copy(t, 1, 0).start()
        core_copy(t, 1, 0).start()
    for s in range(1, ring):
        for b in range(2):
            for t in range(count):
                ring_copy(t, b, s - 1).wait_recv()
                if s < ring - 1:
                    ring_copy(t, b, s).start()
                core_copy(t, b, s).start()
    for copy in keeps:
        copy.wait()
    for t in range(count):
        x_copy(t).wait_send()
        for b in range(2):
            for s in range(ring):
                if s < ring - 1:
                    ring_copy(t, b, s).wait_send()
                core_copy(t, b, s).wait()
    for j in range(1, n):
        clip_copy(j).wait()


def gather_all(clips, shards, ways, ring, n):
    count = len(shards)
    devices = ring * n
    heights = tuple(a.shape[0] for a in shards)
    sems = pltpu.SemaphoreType.DMA
    got = pl.pallas_call(
        functools.partial(gather_kernel, ring, n, heights, ways),
        name="gather_all",
        out_shape=[shape_of(clips.shape, clips.dtype)]
        + [shape_of((a.shape[0] * devices, a.shape[1]), a.dtype) for a in shards],
        in_specs=[ANY] * (1 + count),
        out_specs=[ANY] * (1 + count),
        scratch_shapes=[pltpu.VMEM(clips.shape[1:], clips.dtype)]
        + [pltpu.VMEM(a.shape, a.dtype) for a in shards]
        + [sems((count, 2, ring))] * 4
        + [sems((count,))] * 2
        + [sems((n,))] * 2
        + [sems((count + 1,))] * 2,
        compiler_params=pltpu.CompilerParams(collective_id=0, has_side_effects=True),
    )(clips, *shards)
    return got[0], got[1:]


def scatter_kernel(ring, heights, ways, *refs):
    count = len(heights)
    grads, outs, stages = refs[:count], refs[count : 2 * count], refs[2 * count : 3 * count]
    local, part, came, went, last, fin_s, fin_r = (
        refs[(3 + i) * count : (4 + i) * count] for i in range(7)
    )
    ring_s, ring_r, core_s, core_r, x_s, x_r, load_sem, part_sem = refs[10 * count :]
    w, k, r, x, c, wide_at = place_of(ring)
    other_x = (w, 2 * (1 - x) + c)
    other_c = (w, 2 * x + 1 - c)
    steps = ((wide_at((r + 1) % ring), k), (wide_at((r + ring - 1) % ring), k))
    greet(steps + (other_x, other_c))
    final = ring - 1

    def place(t, s):
        return (r + 2 * ring - 1 - s) % ring if ways[t] == 0 else (r + 1 + s) % ring

    def rows(t, s, column, core):
        block = 4 * wide_at(place(t, s)) + 2 * column + core
        return pl.ds(pl.multiple_of(block * heights[t], 8), heights[t])

    def half(t, column):
        return pl.ds(column * heights[t], heights[t])

    def core_copy(t, s, column):
        return send(grads[t].at[rows(t, s, column, 1 - c)], stages[t].at[s, half(t, column)],
                    core_s.at[t, s, column], core_r.at[t, s, column], other_c)

    def local_load(t, s, slot, column):
        return pltpu.make_async_copy(grads[t].at[rows(t, s, column, c)], local[t].at[slot, half(t, column)],
                                     load_sem.at[t, slot, column])

    def part_load(t, s, slot):
        return pltpu.make_async_copy(stages[t].at[s], part[t].at[slot], part_sem.at[t, slot])

    def ring_copy(t, s):
        return send(went[t].at[s], came[t].at[s], ring_s.at[t, s], ring_r.at[t, s], steps[ways[t]])

    def x_copy(t):
        return send(fin_s[t], fin_r[t], x_s.at[t], x_r.at[t], other_x)

    order = (0, 2, 1, 3)

    def fetch(t, s, slot):
        for column in range(2):
            core_copy(t, s, column).wait_recv()
        part_load(t, s, slot).start()
        for column in range(2):
            local_load(t, s, slot, column).start()

    def total(t, s, slot):
        for column in range(2):
            local_load(t, s, slot, column).wait()
        part_load(t, s, slot).wait()
        return local[t][slot] + part[t][slot]

    for t in order:
        for column in range(2):
            core_copy(t, 0, column).start()
    for s in range(1, ring):
        for t in order:
            for column in range(2):
                core_copy(t, s, column).start()
    for t in order:
        fetch(t, 0, 0)
    for t in order:
        fetch(t, 1, 1)
        went[t][0] = total(t, 0, 0).astype(BF)
        ring_copy(t, 0).start()

    def body(s, carry):
        slot = s % 2
        for t in order:
            fetch(t, s + 1, 1 - slot)
            value = total(t, s, slot)
            ring_copy(t, s - 1).wait_recv()
            went[t][s] = (value + came[t][s - 1].astype(F32)).astype(BF)
            ring_copy(t, s).start()
        return carry

    lax.fori_loop(1, final, body, 0)
    for t in order:
        value = total(t, final, final % 2)
        ring_copy(t, final - 1).wait_recv()
        value = value + came[t][final - 1].astype(F32)
        last[t][0] = value[: heights[t]]
        last[t][1] = value[heights[t] :]
        fin_s[t][...] = last[t][1 - x].astype(BF)
        x_copy(t).start()
    for t in order:
        x_copy(t).wait_recv()
        outs[t][...] = last[t][x] + fin_r[t][...].astype(F32)
    for t in order:
        x_copy(t).wait_send()
        for s in range(final):
            ring_copy(t, s).wait_send()
        for s in range(ring):
            for column in range(2):
                core_copy(t, s, column).wait_send()


def scatter_all(grads, ways, ring, n):
    count = len(grads)
    devices = ring * n
    heights = tuple(g.shape[0] // devices for g in grads)
    widths = tuple(g.shape[1] for g in grads)
    each = tuple(zip(heights, widths))
    sems = pltpu.SemaphoreType.DMA
    vmem = pltpu.VMEM
    got = pl.pallas_call(
        functools.partial(scatter_kernel, ring, heights, ways),
        name="scatter_all",
        out_shape=[shape_of(hw, F32) for hw in each]
        + [shape_of((ring, 2 * h, wd), F32) for h, wd in each],
        in_specs=[ANY] * count,
        out_specs=[pl.BlockSpec(memory_space=pltpu.VMEM)] * count + [ANY] * count,
        scratch_shapes=[vmem((2, 2 * h, wd), F32) for h, wd in each]
        + [vmem((2, 2 * h, wd), F32) for h, wd in each]
        + [vmem((ring - 1, 2 * h, wd), BF) for h, wd in each]
        + [vmem((ring - 1, 2 * h, wd), BF) for h, wd in each]
        + [vmem((2, h, wd), F32) for h, wd in each]
        + [vmem((h, wd), BF) for h, wd in each]
        + [vmem((h, wd), BF) for h, wd in each]
        + [sems((count, ring))] * 2
        + [sems((count, ring, 2))] * 2
        + [sems((count,))] * 2
        + [sems((count, 2, 2)), sems((count, 2))],
        compiler_params=pltpu.CompilerParams(
            collective_id=1, has_side_effects=True, vmem_limit_bytes=VMEM_LIMIT
        ),
    )(*grads)
    return got[:count]


def tuned(mesh):
    wide, n = mesh.shape["wide"], mesh.shape["narrow"]
    if n != 4 or wide < 4 or wide % 2 or D % (8 * wide * n):
        return False
    for w in range(wide):
        for k in range(n):
            device = mesh.devices[w, k]
            here = (getattr(device, "coords", None), getattr(device, "core_on_chip", None))
            if here[0] is None or tuple(here[0]) != (k // 2, w % 2, w // 2) or here[1] != k % 2:
                return False
    return True


def exchange(x):
    return lax.all_to_all(x, ALL, split_axis=0, concat_axis=0, tiled=True)


def shift_clips(clips, back):
    n = lax.axis_size("narrow")
    parts = [clips[0]]
    for j in range(1, n):
        step = -j if back else j
        parts.append(lax.ppermute(clips[j], "narrow", [(s, (s + step) % n) for s in range(n)]))
    return jnp.stack(parts)


def local(fast, clips, t_emb, lengths, task, w_mod, b_mod, w_qkv_s, w_o_s, b_o_s, w_qkv_t, w_o_t, b_o_t,
          w_in, b_in, w_out, b_out, cotangent):
    n = lax.axis_size("narrow")
    wide = lax.axis_size("wide")
    devices = n * wide
    part = w_mod.shape[0]
    mod_cols = w_mod.shape[1] // devices
    rank = lax.axis_index("narrow")
    slots = jnp.arange(n, dtype=jnp.int32)
    from_clip = (rank - slots) % n
    recv_len = lengths.reshape(n, n)[from_clip, slots]
    recv_task = task.reshape(n, n, FR)[from_clip, slots]
    ends = jnp.cumsum(recv_len)
    starts = ends - recv_len
    ids = jnp.arange(LIVE, dtype=jnp.int32)
    source = jnp.sum((ends[None, :] <= ids[:, None]).astype(jnp.int32), axis=1)
    within = ids - starts[source]
    pack_rows = source * FR + within
    row_choice = source * 2 + recv_task[source, within]
    frame_ids = jnp.arange(FR, dtype=jnp.int32)
    live_back = frame_ids[None, :] < recv_len[:, None]
    unpack_rows = jnp.where(live_back, starts[:, None] + frame_ids[None, :], 0).reshape(-1)
    row_id = jnp.arange(64, dtype=jnp.int32)
    col_id = jnp.arange(LANES, dtype=jnp.int32) % 64
    seg = (
        (row_id[:, None] // LIVE == col_id[None, :] // LIVE)
        & (source[row_id % LIVE][:, None] == source[col_id % LIVE][None, :])
    ).astype(F32)

    def gather(w):
        return lax.all_gather(w, ALL, axis=0, tiled=True)

    weights = (w_in, w_out, w_qkv_t, w_o_t, w_qkv_s, w_o_s)
    if fast:
        frames, weights = gather_all(clips, weights, (0, 0, 1, 1, 1, 1), wide, n)
    else:
        frames = shift_clips(clips, False)
        weights = [gather(w) for w in weights]
    win, wout, wqkv_t, wo_t, wqkv_s, wo_s = weights
    frames = jnp.take(frames.reshape(n * FR, PATCHES, D), pack_rows, axis=0, mode="clip")

    wm = jnp.swapaxes(w_mod.reshape(part, devices, mod_cols), 0, 1).reshape(devices, -1)
    emb = jnp.broadcast_to(t_emb.reshape(1, -1), (devices, t_emb.size))
    small = jnp.concatenate([b_o_s, b_o_t, b_in, b_out])
    small_all = jnp.broadcast_to(small[None], (devices, small.size))
    got = exchange(jnp.concatenate([wm, emb, small_all], axis=1))
    wm_cols = got[:, : part * mod_cols].reshape(D, mod_cols)
    emb_all = got[:, part * mod_cols : part * mod_cols + t_emb.size].reshape(-1, D)
    small_got = got[:, part * mod_cols + t_emb.size :]
    b1 = b_o_s.size
    bias_s = small_got[:, :b1].reshape(1, -1).astype(F32)
    bias_t = small_got[:, b1 : 2 * b1].reshape(1, -1).astype(F32)
    bias_in = small_got[:, 2 * b1 : 2 * b1 + b_in.size].reshape(1, -1).astype(F32)
    bias_out = small_got[:, 2 * b1 + b_in.size :].reshape(1, -1).astype(F32)
    emb_f = emb_all.astype(F32)
    silu_low = (emb_f * jax.nn.sigmoid(emb_f)).astype(BF)
    mod_part = dot(silu_low, wm_cols) + b_mod.astype(F32)[None]
    mod_part = mod_part.reshape(wide, n, n, 2, mod_cols)
    mod_part = jnp.stack([jnp.roll(mod_part[:, :, c], c, axis=1) for c in range(n)], axis=2)
    mod_rows = exchange(mod_part.reshape(devices, -1)).reshape(devices, 2 * n, mod_cols)
    mod_rows = jnp.swapaxes(mod_rows, 0, 1).reshape(2 * n, 9, D)
    mod = jnp.swapaxes(mod_rows[row_choice], 0, 1)

    def carry(clips, js, back, number):
        return (clips, n, js, back, number) if fast else None

    def regroup(clips, back, half, odd):
        if fast:
            return jnp.stack([clips[0], odd[0], half[0], odd[1]])
        return shift_clips(clips, back)

    *half, x1, qkv1, o1, a1 = run_frame_forward(
        frames, mod, wqkv_s, wo_s, bias_s, carry(cotangent, (2,), False, 2))
    *odd, x2, qkv2, o2, a2 = run_time_forward(
        x1, mod, seg, wqkv_t, wo_t, bias_t, carry(cotangent, (1, 3), False, 3))
    cots = regroup(cotangent, False, *(half or [None]), *(odd or [None]))
    dy = run_turn_frames(cots.reshape(n * FR, PATCHES, D), pack_rows)
    out, dx2, g_in, g_out, gb_in, gb_out, dmod3 = run_mlp(x2, dy, mod, win, bias_in, wout, bias_out)

    own_live = frame_ids[None, :] < lengths.reshape(n, n)[rank][:, None]

    def spread(packed):
        return jnp.take(packed, unpack_rows, axis=0, mode="clip").reshape(n, FR, PATCHES, D)

    def only_live(parts):
        return jnp.where(own_live[:, :, None, None], parts, jnp.zeros((), parts.dtype))

    def scatter(g):
        return lax.psum_scatter(g.astype(BF), ALL, scatter_dimension=0, tiled=True).astype(F32)

    out = spread(out)
    *half, dx1, g_t, gb_t, dmod2 = run_time_back(
        x1, dx2, mod, seg, qkv2, o2, a2, wqkv_t, wo_t, carry(out, (2,), True, 4))
    *odd, dx0, g_s, gb_s, dmod1 = run_frame_back(
        frames, dx1, mod, qkv1, o1, a1, wqkv_s, wo_s, carry(out, (1, 3), True, 5))
    layer_out = only_live(regroup(out, True, *(half or [None]), *(odd or [None])))
    grad_clips = only_live(shift_clips(spread(dx0), True))
    grads = (g_in, g_out, g_t, g_s)
    if fast:
        s_in, s_out, s_t, s_s = scatter_all(grads, (0, 0, 1, 1), wide, n)
    else:
        s_in, s_out, s_t, s_s = [scatter(g) for g in grads]

    grad_frames = jnp.swapaxes(jnp.concatenate([dmod1, dmod2, dmod3], axis=0), 0, 1).reshape(LIVE, 9 * D)
    chooser = (row_choice[:, None] == jnp.arange(2 * n, dtype=jnp.int32)[None, :]).astype(F32)
    grad_rows = lax.dot_general(
        chooser, grad_frames, (((0,), (0,)), ((), ())), precision=lax.Precision.HIGHEST
    ).astype(BF)
    d_cols = exchange(jnp.swapaxes(grad_rows.reshape(2 * n, devices, mod_cols), 0, 1).reshape(devices, -1))
    d_cols = d_cols.reshape(wide, n, n, 2, mod_cols)
    d_cols = jnp.stack([jnp.roll(d_cols[:, :, c], -c, axis=1) for c in range(n)], axis=2)
    d_cols = d_cols.reshape(devices * 2 * n, mod_cols)
    grad_b_mod = jnp.sum(d_cols.astype(F32), axis=0)
    gwm_cols = dot_tn(silu_low, d_cols)
    g_emb = dot_nt(d_cols, wm_cols)
    gb_all = jnp.concatenate(
        [gb_s.reshape(devices, -1), gb_t.reshape(devices, -1), gb_in.reshape(devices, -1),
         gb_out.reshape(devices, -1)], axis=1)
    final = exchange(jnp.concatenate(
        [gwm_cols.reshape(devices, -1), g_emb.reshape(devices, -1), gb_all], axis=1))
    cut1 = part * mod_cols
    cut2 = cut1 + t_emb.size
    grad_w_mod = jnp.swapaxes(final[:, :cut1].reshape(devices, part, mod_cols), 0, 1).reshape(part, -1)
    emb_own = t_emb.astype(F32)
    sig = jax.nn.sigmoid(emb_own)
    grad_emb = jnp.sum(final[:, cut1:cut2], axis=0).reshape(t_emb.shape)
    grad_t_emb = (grad_emb * (sig * (1.0 + emb_own * (1.0 - sig)))).astype(BF)
    gb = jnp.sum(final[:, cut2:], axis=0)
    return (
        layer_out,
        grad_clips,
        grad_t_emb,
        grad_w_mod,
        grad_b_mod,
        s_s[:, : 3 * D],
        s_s[:, 3 * D :],
        gb[:b1],
        s_t[:, : 3 * D],
        s_t[:, 3 * D :],
        gb[b1 : 2 * b1],
        s_in,
        gb[2 * b1 : 2 * b1 + b_in.size],
        s_out,
        gb[2 * b1 + b_in.size :],
    )


def solution(mesh):
    full = P(ALL)
    placed = (full, full, P("wide"), P("wide")) + (full,) * 13
    return jax.shard_map(functools.partial(local, tuned(mesh)), mesh=mesh, in_specs=placed, out_specs=(full,) * 15, check_vma=False)
```

```python
import functools

import jax
import jax.numpy as jnp
from jax import lax
from jax.experimental import pallas as pl
from jax.experimental.pallas import tpu as pltpu
from jax.sharding import PartitionSpec as P

D = 768
HEADS = 12
HEAD = 64
FF = 3072
FR = 16
PATCHES = 64
LIVE = 2 * FR
EPS = 1e-06
BF = jnp.bfloat16
F32 = jnp.float32
ALL = ("wide", "narrow")
PAIRS = HEADS // 2
LANES = 2 * HEAD
BACK_PAIRS = 6
TILE = 512
FT = TILE // PATCHES
PT = TILE // LIVE
GRID = LIVE * PATCHES // TILE
GROUPS = TILE // 64
GELU_C = 0.7978845608028654
GELU_A = 0.044715
VMEM_LIMIT = 66 * 1000 * 1000
MESH = pl.DeviceIdType.MESH
ANY = pl.BlockSpec(memory_space=pl.ANY)


def dot(a, b):
    return lax.dot_general(a, b, (((1,), (0,)), ((), ())), preferred_element_type=F32)


def dot_nt(a, b):
    return lax.dot_general(a, b, (((1,), (1,)), ((), ())), preferred_element_type=F32)


def dot_tn(a, b):
    return lax.dot_general(a, b, (((0,), (0,)), ((), ())), preferred_element_type=F32)


def normalise(x):
    mean = jnp.mean(x, axis=-1, keepdims=True)
    centred = x - mean
    var = jnp.mean(centred * centred, axis=-1, keepdims=True)
    rstd = lax.rsqrt(var + EPS)
    return centred * rstd, rstd


def norm_back(dn, xhat, rstd):
    m1 = jnp.mean(dn, axis=-1, keepdims=True)
    m2 = jnp.mean(dn * xhat, axis=-1, keepdims=True)
    return rstd * (dn - m1 - xhat * m2)


def lane_masks():
    lane = lax.broadcasted_iota(jnp.int32, (64, LANES), 1)
    low_lanes = lane < HEAD
    low = jnp.where(low_lanes, 1.0, 0.0).astype(BF)
    high = jnp.where(low_lanes, 0.0, 1.0).astype(BF)
    return low_lanes, low, high


def split_heads(x, low, high):
    return jnp.concatenate([x * low, x * high], axis=0)


def softmax_keys(s, mask):
    if mask is not None:
        s = jnp.where(mask, s, -1e30)
    top = jnp.max(s, axis=0, keepdims=True)
    e = jnp.exp(s - top)
    return e * (1.0 / jnp.sum(e, axis=0, keepdims=True))


def pair_cols(part, hp):
    return slice(part * D + hp * LANES, part * D + (hp + 1) * LANES)


def attend(qkv_ref, o_ref, mask):
    low_lanes, low, high = lane_masks()
    scale = HEAD ** (-0.5)

    def body(g, carry):
        rows = pl.ds(pl.multiple_of(g * 64, 64), 64)
        pairs = range(PAIRS)
        s = [dot_nt(qkv_ref[rows, pair_cols(1, hp)], split_heads(qkv_ref[rows, pair_cols(0, hp)], low * scale, high * scale))
             for hp in pairs]
        p = [softmax_keys(t, mask).astype(BF) for t in s]
        r = [dot_tn(p[hp], qkv_ref[rows, pair_cols(2, hp)]) for hp in pairs]
        for hp in pairs:
            o_ref[rows, pair_cols(0, hp)] = jnp.where(low_lanes, r[hp][:64], r[hp][64:]).astype(BF)
        return carry

    lax.fori_loop(0, GROUPS, body, 0)


def attend_back(qkv_ref, do_ref, dqkv_ref, mask):
    low_lanes, low, high = lane_masks()
    scale = HEAD ** (-0.5)

    def body(g, carry):
        rows = pl.ds(pl.multiple_of(g * 64, 64), 64)
        for first in range(0, PAIRS, BACK_PAIRS):
            pairs = range(first, first + BACK_PAIRS)
            qb = [split_heads(qkv_ref[rows, pair_cols(0, hp)], low * scale, high * scale) for hp in pairs]
            dob = [split_heads(do_ref[rows, pair_cols(0, hp)], low, high) for hp in pairs]
            s = [dot_nt(qkv_ref[rows, pair_cols(1, hp)], q) for hp, q in zip(pairs, qb)]
            dp = [dot_nt(qkv_ref[rows, pair_cols(2, hp)], d) for hp, d in zip(pairs, dob)]
            p = [softmax_keys(t, mask) for t in s]
            delta = [jnp.sum(a * b, axis=0, keepdims=True) for a, b in zip(p, dp)]
            ds = [(a * (b - c)).astype(BF) for a, b, c in zip(p, dp, delta)]
            dv = [dot(a.astype(BF), d) for a, d in zip(p, dob)]
            dk = [dot(a, q) for a, q in zip(ds, qb)]
            r = [dot_tn(a, qkv_ref[rows, pair_cols(1, hp)]) for hp, a in zip(pairs, ds)]
            for i, hp in enumerate(pairs):
                dqkv_ref[rows, pair_cols(2, hp)] = dv[i].astype(BF)
                dqkv_ref[rows, pair_cols(1, hp)] = dk[i].astype(BF)
                dq = jnp.where(low_lanes, r[i][:64], r[i][64:]) * scale
                dqkv_ref[rows, pair_cols(0, hp)] = dq.astype(BF)
        return carry

    lax.fori_loop(0, GROUPS, body, 0)


def swap_major(value, scratch, out_ref, first, second):
    for b in range(D // 128):
        cols = slice(b * 128, (b + 1) * 128)
        for i in range(first):
            scratch[b, pl.ds(i, second, stride=first), :] = value[i * second : (i + 1) * second, cols]
        out_ref[:, :, cols] = scratch[b].reshape(second, first, 128).astype(out_ref.dtype)


def frames_of(refs):
    return jnp.concatenate([r[0] for r in refs], axis=0).astype(F32)


def per_frame(piece):
    return jnp.broadcast_to(piece[:, None, :], (FT, PATCHES, D)).reshape(TILE, D)


def per_patch(piece):
    return jnp.broadcast_to(piece[None], (PT, LIVE, D)).reshape(TILE, D)


def sum_patches(value):
    return jnp.sum(value.reshape(FT, PATCHES, D), axis=1)


def sum_groups(value):
    return jnp.sum(value.reshape(PT, LIVE, D), axis=0)


def attn_mask(seg_ref):
    return seg_ref[...] > 0.0


def frame_forward(frames, mod, wqkv, wo, bo, x1t, qkv, o, a1, scratch):
    x = frames[...].reshape(TILE, D).astype(F32)
    xhat, _ = normalise(x)
    h = (xhat * (1.0 + per_frame(mod[1])) + per_frame(mod[0])).astype(BF)
    qkv[...] = dot(h, wqkv[...]).astype(BF)
    attend(qkv, o, None)
    branch = dot(o[...], wo[...]) + bo[...]
    a1[...] = branch
    x1 = x + per_frame(mod[2]) * branch
    swap_major(x1, scratch, x1t, FT, PATCHES)


def turn_frames(rows_ref, *refs):
    x_refs, (out, scratch) = refs[:FT], refs[FT:]
    swap_major(frames_of(x_refs), scratch, out, FT, PATCHES)


def time_forward(x1, mod, seg, wqkv, wo, bo, x2, qkv, o, a2):
    x = x1[...].reshape(TILE, D)
    xhat, _ = normalise(x)
    h = (xhat * (1.0 + per_patch(mod[1])) + per_patch(mod[0])).astype(BF)
    qkv[...] = dot(h, wqkv[...]).astype(BF)
    attend(qkv, o, attn_mask(seg))
    branch = dot(o[...], wo[...]) + bo[...]
    a2[...] = branch
    x2[...] = (x + per_patch(mod[2]) * branch).reshape(PT, LIVE, D)


def mlp_both(x2, dy, mod, win, bin_, wout, bout, out, dx2, gwin, gwout, gbin, gbout, dmod, scratch):
    first = pl.program_id(0) == 0

    @pl.when(first)
    def _():
        gwin[...] = jnp.zeros_like(gwin)
        gwout[...] = jnp.zeros_like(gwout)
        gbin[...] = jnp.zeros_like(gbin)
        gbout[...] = jnp.zeros_like(gbout)
        dmod[...] = jnp.zeros_like(dmod)

    x = x2[...].reshape(TILE, D)
    xhat, rstd = normalise(x)
    h = (xhat * (1.0 + per_patch(mod[1])) + per_patch(mod[0])).astype(BF)
    gate = per_patch(mod[2])
    grad = dy[...].reshape(TILE, D)
    da = (grad * gate).astype(BF)
    gbout[...] += jnp.sum(da.astype(F32), axis=0, keepdims=True)
    branch = jnp.zeros((TILE, D), F32) + bout[...]
    dh = jnp.zeros((TILE, D), F32)
    for j in range(FF // D):
        cols = slice(j * D, (j + 1) * D)
        u = dot(h, win[:, cols]) + bin_[:, cols]
        u2 = u * u
        t = jnp.tanh(GELU_C * u * (1.0 + GELU_A * u2))
        half = 0.5 * (1.0 + t)
        g = (u * half).astype(BF)
        slope = half + (0.5 * GELU_C) * u * (1.0 - t * t) * (1.0 + 3.0 * GELU_A * u2)
        branch = branch + dot(g, wout[cols, :])
        du = (dot_nt(da, wout[cols, :]) * slope).astype(BF)
        gwout[cols, :] += dot_tn(g, da)
        gbin[:, cols] += jnp.sum(du.astype(F32), axis=0, keepdims=True)
        gwin[:, cols] += dot_tn(h, du)
        dh = dh + dot_nt(du, win[:, cols])
    swap_major(x + gate * branch, scratch, out, PT, LIVE)
    dmod[2] += sum_groups(grad * branch)
    dmod[0] += sum_groups(dh)
    dmod[1] += sum_groups(dh * xhat)
    back = norm_back(dh * (1.0 + per_patch(mod[1])), xhat, rstd)
    dx2[...] = (grad + back).reshape(PT, LIVE, D)


def attn_back_tile(x, grad, shift, scale, gate, branch, qkv, o, wqkv, wo, gw, gbo, do, dqkv, mask, tick):
    first = pl.program_id(0) == 0

    @pl.when(first)
    def _():
        gw[...] = jnp.zeros_like(gw)
        gbo[...] = jnp.zeros_like(gbo)

    da = (grad * gate).astype(BF)
    do[...] = dot_nt(da, wo[...]).astype(BF)
    gw[:, 3 * D :] += dot_tn(o[...], da)
    gbo[...] += jnp.sum(da.astype(F32), axis=0, keepdims=True)
    tick(0)
    attend_back(qkv, do, dqkv, mask)
    tick(1)
    xhat, rstd = normalise(x)
    h = (xhat * (1.0 + scale) + shift).astype(BF)
    dh = jnp.zeros((TILE, D), F32)
    for j in range(3):
        cols = slice(j * D, (j + 1) * D)
        part = dqkv[:, cols]
        gw[:, cols] += dot_tn(h, part)
        dh = dh + dot_nt(part, wqkv[:, cols])
    dx = grad + norm_back(dh * (1.0 + scale), xhat, rstd)
    return dx, dh, dh * xhat, grad * branch


def no_tick(place):
    pass


def time_back(x1, dx2, mod, seg, qkv, o, a2, wqkv, wo, dx1, gw, gbo, dmod, do, dqkv, scratch, tick=no_tick):
    @pl.when(pl.program_id(0) == 0)
    def _():
        dmod[...] = jnp.zeros_like(dmod)

    dx, d_shift, d_scale, d_gate = attn_back_tile(
        x1[...].reshape(TILE, D), dx2[...].reshape(TILE, D), per_patch(mod[0]), per_patch(mod[1]),
        per_patch(mod[2]), a2[...], qkv, o, wqkv, wo, gw, gbo, do, dqkv, attn_mask(seg), tick)
    dmod[0] += sum_groups(d_shift)
    dmod[1] += sum_groups(d_scale)
    dmod[2] += sum_groups(d_gate)
    swap_major(dx, scratch, dx1, PT, LIVE)


def frame_back(frames, dx1, mod, qkv, o, a1, wqkv, wo, dx0, gw, gbo, dmod, do, dqkv, tick=no_tick):
    dx, d_shift, d_scale, d_gate = attn_back_tile(
        frames[...].reshape(TILE, D).astype(F32), dx1[...].reshape(TILE, D), per_frame(mod[0]), per_frame(mod[1]),
        per_frame(mod[2]), a1[...], qkv, o, wqkv, wo, gw, gbo, do, dqkv, None, tick)
    dmod[0] = sum_patches(d_shift)
    dmod[1] = sum_patches(d_scale)
    dmod[2] = sum_patches(d_gate)
    dx0[...] = dx.reshape(FT, PATCHES, D).astype(BF)


def frame_specs():
    return [
        pl.BlockSpec((1, PATCHES, D), functools.partial(lambda j, i, rows: (rows[FT * i + j], 0, 0), j))
        for j in range(FT)
    ]


def whole(shape):
    return pl.BlockSpec(shape, lambda i, *_: (0,) * len(shape), pipeline_mode=pl.Buffered(1))


def tiles(shape, dim):
    return pl.BlockSpec(shape, lambda i, *_: tuple(i if a == dim else 0 for a in range(len(shape))))


def piece_spec(number, frames, by_tile):
    return pl.BlockSpec((3, frames, D), lambda i, *_: (number, i if by_tile else 0, 0))


ROWS = tiles((TILE, D), 0)
ROWS3 = tiles((TILE, 3 * D), 0)
TURNED = tiles((PT, LIVE, D), 0)


TURN = pltpu.VMEM((D // 128, TILE, 128), F32)


def shape_of(shape, dtype):
    return jax.ShapeDtypeStruct(shape, dtype)


def clip_copies(n, js, back, src, dst, send_sem, recv_sem):
    w, k = lax.axis_index("wide"), lax.axis_index("narrow")
    return [
        send(src.at[j], dst.at[i], send_sem.at[i], recv_sem.at[i], (w, (k + (n - j if back else j)) % n))
        for i, j in enumerate(js)
    ]


def carrying(kernel, count, n, js, back, plan, *refs):
    sent = 0 if plan is None else plan.inputs
    made = 0 if plan is None else plan.outputs
    held = 0 if plan is None else plan.scratches
    src, grads, ins = refs[0], refs[1 : 1 + sent], refs[1 + sent : 1 + sent + count]
    at = 1 + sent + count
    dst, results, rest = refs[at], refs[at + 1 : at + 1 + made], refs[at + 1 + made : len(refs) - 2 - held]
    copies = clip_copies(n, js, back, src, dst, *refs[len(refs) - 2 - held : len(refs) - held])
    step = pl.program_id(0)
    sums = None if plan is None else plan.steps(grads + results + refs[len(refs) - held :])

    @pl.when(step == 0)
    def _():
        w, k = lax.axis_index("wide"), lax.axis_index("narrow")
        peers = [(w, (k + j) % n) for j in js]
        greet(peers if sums is None else peers + list(sums.peers))
        if sums is not None:
            sums.begin()
        for copy in copies:
            copy.start()

    if sums is None:
        kernel(*ins, *rest)
    else:
        @pl.when(step > 0)
        def _():
            sums.hop(2 * step - 1)

        def tick(place):
            @pl.when(step == 0)
            def _():
                if place == 0:
                    sums.load_first()
                else:
                    sums.first_hop()

            if place == 1:
                @pl.when(step > 0)
                def _():
                    sums.hop(2 * step)

        kernel(*ins, *rest, tick=tick)

    @pl.when(step == GRID - 1)
    def _():
        if sums is not None:
            sums.finish()
        for copy in copies:
            copy.wait()


def call(kernel, name, ins, in_specs, outs, out_specs, scratch, flops, prefetch=None, carry=None):
    moved = sum(a.size * a.dtype.itemsize for a in tuple(ins) + tuple(outs))
    params = {}
    if carry is not None:
        src, n, js, back, number, plan, grads = carry
        kernel = functools.partial(carrying, kernel, len(ins), n, js, back, plan)
        ins, in_specs = [src] + grads + ins, [ANY] * (1 + len(grads)) + in_specs
        first = [shape_of((len(js),) + src.shape[1:], src.dtype)]
        first_specs = [ANY]
        scratch = scratch + [pltpu.SemaphoreType.DMA((len(js),))] * 2
        if plan is not None:
            first, first_specs = first + plan.out_shapes, first_specs + plan.out_specs
            scratch = scratch + plan.scratch
        outs, out_specs = first + outs, first_specs + out_specs
        params = dict(collective_id=number, has_side_effects=True)
    grid_spec = pltpu.PrefetchScalarGridSpec(
        num_scalar_prefetch=0 if prefetch is None else 1,
        grid=(GRID,),
        in_specs=in_specs,
        out_specs=out_specs,
        scratch_shapes=scratch,
    )
    fn = pl.pallas_call(
        kernel,
        grid_spec=grid_spec,
        out_shape=outs,
        name=name,
        cost_estimate=pl.CostEstimate(flops=flops, bytes_accessed=moved, transcendentals=0),
        compiler_params=pltpu.CompilerParams(
            dimension_semantics=("arbitrary",), vmem_limit_bytes=VMEM_LIMIT, **params
        ),
    )
    return fn(*ins) if prefetch is None else fn(prefetch, *ins)


TOKENS = LIVE * PATCHES


def run_frame_forward(frames, mod, wqkv, wo, bo, carry=None):
    return call(
        frame_forward, "frame_forward",
        [frames, mod, wqkv, wo, bo],
        [tiles((FT, PATCHES, D), 0), piece_spec(0, FT, True), whole((D, 3 * D)), whole((D, D)), whole((1, D))],
        [shape_of((PATCHES, LIVE, D), F32), shape_of((TOKENS, 3 * D), BF), shape_of((TOKENS, D), BF),
         shape_of((TOKENS, D), F32)],
        [tiles((PATCHES, FT, D), 1), ROWS3, ROWS, ROWS],
        [TURN],
        2 * TOKENS * D * 4 * D, carry=carry)


def run_turn_frames(frames, rows):
    return call(
        turn_frames, "turn_frames", [frames] * FT, frame_specs(),
        [shape_of((PATCHES, LIVE, D), F32)], [tiles((PATCHES, FT, D), 1)],
        [TURN], 1000, rows)[0]


def run_time_forward(x1, mod, seg, wqkv, wo, bo, carry=None):
    return call(
        time_forward, "time_forward",
        [x1, mod, seg, wqkv, wo, bo],
        [TURNED, piece_spec(1, LIVE, False), whole((64, LANES)), whole((D, 3 * D)), whole((D, D)),
         whole((1, D))],
        [shape_of((PATCHES, LIVE, D), F32), shape_of((TOKENS, 3 * D), BF), shape_of((TOKENS, D), BF),
         shape_of((TOKENS, D), F32)],
        [TURNED, ROWS3, ROWS, ROWS],
        [], 2 * TOKENS * D * 4 * D, carry=carry)


def run_mlp(x2, dy, mod, win, bin_, wout, bout):
    return call(
        mlp_both, "mlp_both",
        [x2, dy, mod, win, bin_, wout, bout],
        [TURNED, TURNED, piece_spec(2, LIVE, False), whole((D, FF)), whole((1, FF)), whole((FF, D)),
         whole((1, D))],
        [shape_of((LIVE, PATCHES, D), BF), shape_of((PATCHES, LIVE, D), F32), shape_of((D, FF), F32),
         shape_of((FF, D), F32), shape_of((1, FF), F32), shape_of((1, D), F32), shape_of((3, LIVE, D), F32)],
        [tiles((LIVE, PT, D), 1), TURNED, whole((D, FF)), whole((FF, D)), whole((1, FF)), whole((1, D)),
         whole((3, LIVE, D))],
        [TURN],
        6 * 2 * TOKENS * D * FF)


def run_time_back(x1, dx2, mod, seg, qkv, o, a2, wqkv, wo, carry=None):
    return call(
        time_back, "time_back",
        [x1, dx2, mod, seg, qkv, o, a2, wqkv, wo],
        [TURNED, TURNED, piece_spec(1, LIVE, False), whole((64, LANES)), ROWS3, ROWS, ROWS,
         whole((D, 3 * D)), whole((D, D))],
        [shape_of((LIVE, PATCHES, D), F32), shape_of((D, 4 * D), F32), shape_of((1, D), F32), shape_of((3, LIVE, D), F32)],
        [tiles((LIVE, PT, D), 1), whole((D, 4 * D)), whole((1, D)), whole((3, LIVE, D))],
        [pltpu.VMEM((TILE, D), BF), pltpu.VMEM((TILE, 3 * D), BF), TURN],
        2 * 2 * TOKENS * D * 4 * D, carry=carry)


def run_frame_back(frames, dx1, mod, qkv, o, a1, wqkv, wo, carry=None):
    return call(
        frame_back, "frame_back",
        [frames, dx1, mod, qkv, o, a1, wqkv, wo],
        [tiles((FT, PATCHES, D), 0), tiles((FT, PATCHES, D), 0), piece_spec(0, FT, True), ROWS3, ROWS, ROWS,
                         whole((D, 3 * D)), whole((D, D))],
        [shape_of((LIVE, PATCHES, D), BF), shape_of((D, 4 * D), F32), shape_of((1, D), F32), shape_of((3, LIVE, D), F32)],
        [tiles((FT, PATCHES, D), 0), whole((D, 4 * D)), whole((1, D)), piece_spec(0, FT, True)],
        [pltpu.VMEM((TILE, D), BF), pltpu.VMEM((TILE, 3 * D), BF)],
        2 * 2 * TOKENS * D * 4 * D, carry=carry)


def place_of(wide):
    ring = wide
    turn = ring // 2
    w = lax.axis_index("wide")
    k = lax.axis_index("narrow")
    z, y = w // 2, w % 2
    r = z + y * (ring - 1 - 2 * z)

    def wide_at(position):
        side = position // turn
        return 2 * ((1 - side) * position + side * (ring - 1 - position)) + side

    return w, k, r, k // 2, k % 2, wide_at


def greet(peers):
    barrier = pltpu.get_barrier_semaphore()
    for peer in peers:
        pl.semaphore_signal(barrier, inc=1, device_id=peer, device_id_type=MESH)
    pl.semaphore_wait(barrier, len(peers))


def send(src, dst, send_sem, recv_sem, peer):
    return pltpu.make_async_remote_copy(
        src_ref=src, dst_ref=dst, send_sem=send_sem, recv_sem=recv_sem, device_id=peer, device_id_type=MESH
    )


def gather_kernel(ring, n, heights, ways, *refs):
    count = len(heights)
    clips, shards = refs[0], refs[1 : 1 + count]
    frames, full = refs[1 + count], refs[2 + count : 2 + 2 * count]
    clip_buf, bufs = refs[2 + 2 * count], refs[3 + 2 * count : 3 + 3 * count]
    ring_s, ring_r, core_s, core_r, x_s, x_r, clip_s, clip_r, load_sem, keep_sem = refs[3 + 3 * count :]
    w, k, r, x, c, wide_at = place_of(ring)
    other_x = (w, 2 * (1 - x) + c)
    other_c = (w, 2 * x + 1 - c)
    steps = ((wide_at((r + 1) % ring), k), (wide_at((r + ring - 1) % ring), k))
    greet(steps + tuple((w, (k + j) % n) for j in range(1, n)))

    def rows(t, position, column):
        block = 4 * wide_at(position) + 2 * column + c
        return pl.ds(pl.multiple_of(block * heights[t], 8), heights[t])

    def ring_copy(t, b, s, src=None):
        place = (r + ring - s) % ring if ways[t] == 0 else (r + s) % ring
        dst = full[t].at[rows(t, place, x if b == 0 else 1 - x)]
        return send(dst if src is None else src, dst, ring_s.at[t, b, s], ring_r.at[t, b, s], steps[ways[t]])

    def core_copy(t, b, s, src=None):
        place = (r + ring - s) % ring if ways[t] == 0 else (r + s) % ring
        dst = full[t].at[rows(t, place, x if b == 0 else 1 - x)]
        return send(dst if src is None else src, dst, core_s.at[t, b, s], core_r.at[t, b, s], other_c)

    def x_copy(t):
        dst = full[t].at[rows(t, r, x)]
        return send(shards[t], dst, x_s.at[t], x_r.at[t], other_x)

    def clip_copy(j):
        return send(clips.at[j], frames.at[j], clip_s.at[j], clip_r.at[j], (w, (k + j) % n))

    for t in range(count):
        x_copy(t).start()
        ring_copy(t, 0, 0, shards[t]).start()
    for j in range(1, n):
        clip_copy(j).start()
    for t in range(count):
        core_copy(t, 0, 0, shards[t]).start()
    loads = [pltpu.make_async_copy(clips.at[0], clip_buf, load_sem.at[count])]
    loads += [pltpu.make_async_copy(shards[t], bufs[t], load_sem.at[t]) for t in range(count)]
    keeps = [pltpu.make_async_copy(clip_buf, frames.at[0], keep_sem.at[count])]
    keeps += [pltpu.make_async_copy(bufs[t], full[t].at[rows(t, r, x)], keep_sem.at[t]) for t in range(count)]
    for copy in loads:
        copy.start()
    for copy, keep in zip(loads, keeps):
        copy.wait()
        keep.start()
    for t in range(count):
        x_copy(t).wait_recv()
        ring_copy(t, 1, 0).start()
        core_copy(t, 1, 0).start()
    for s in range(1, ring):
        for b in range(2):
            for t in range(count):
                ring_copy(t, b, s - 1).wait_recv()
                if s < ring - 1:
                    ring_copy(t, b, s).start()
                core_copy(t, b, s).start()
    for copy in keeps:
        copy.wait()
    for t in range(count):
        x_copy(t).wait_send()
        for b in range(2):
            for s in range(ring):
                if s < ring - 1:
                    ring_copy(t, b, s).wait_send()
                core_copy(t, b, s).wait()
    for j in range(1, n):
        clip_copy(j).wait()


def gather_all(clips, shards, ways, ring, n):
    count = len(shards)
    devices = ring * n
    heights = tuple(a.shape[0] for a in shards)
    sems = pltpu.SemaphoreType.DMA
    got = pl.pallas_call(
        functools.partial(gather_kernel, ring, n, heights, ways),
        name="gather_all",
        out_shape=[shape_of(clips.shape, clips.dtype)]
        + [shape_of((a.shape[0] * devices, a.shape[1]), a.dtype) for a in shards],
        in_specs=[ANY] * (1 + count),
        out_specs=[ANY] * (1 + count),
        scratch_shapes=[pltpu.VMEM(clips.shape[1:], clips.dtype)]
        + [pltpu.VMEM(a.shape, a.dtype) for a in shards]
        + [sems((count, 2, ring))] * 4
        + [sems((count,))] * 2
        + [sems((n,))] * 2
        + [sems((count + 1,))] * 2,
        compiler_params=pltpu.CompilerParams(collective_id=0, has_side_effects=True),
    )(clips, *shards)
    return got[0], got[1:]


class Sums:
    def __init__(self, plan, refs):
        self.plan, count = plan, len(plan.pieces)
        self.grads, refs = refs[: plan.inputs], refs[plan.inputs :]
        self.outs, refs = refs[: len(plan.shapes)], refs[len(plan.shapes) :]
        self.stages, refs = refs[:count], refs[count:]
        self.own, self.part, self.came, self.went, self.last, self.fin_s, self.fin_r = (
            refs[i * count : (i + 1) * count] for i in range(7)
        )
        (self.ring_s, self.ring_r, self.core_s, self.core_r, self.x_s, self.x_r, self.load_sem,
         self.part_sem) = refs[7 * count :]
        ring = plan.ring
        self.w, self.k, self.r, self.x, self.c, self.wide_at = place_of(ring)
        self.other_x = (self.w, 2 * (1 - self.x) + self.c)
        self.other_c = (self.w, 2 * self.x + 1 - self.c)
        self.next = ((self.wide_at((self.r + 1) % ring), self.k), (self.wide_at((self.r + ring - 1) % ring), self.k))
        self.peers = self.next + (self.other_x, self.other_c)
        self.final = ring - 1

    def source(self, t, s, column, core):
        ring = self.plan.ring
        g, col, width, height, way = self.plan.pieces[t]
        place = (self.r + 2 * ring - 1 - s) % ring if way == 0 else (self.r + 1 + s) % ring
        block = 4 * self.wide_at(place) + 2 * column + core
        return self.grads[g].at[pl.ds(pl.multiple_of(block * height, 8), height), pl.ds(col, width)]

    def half(self, t, column):
        height = self.plan.pieces[t][3]
        return pl.ds(column * height, height)

    def core_copy(self, t, s, column):
        return send(self.source(t, s, column, 1 - self.c), self.stages[t].at[s, self.half(t, column)],
                    self.core_s.at[t, s, column], self.core_r.at[t, s, column], self.other_c)

    def own_load(self, t, s, slot, column):
        return pltpu.make_async_copy(self.source(t, s, column, self.c), self.own[t].at[slot, self.half(t, column)],
                                     self.load_sem.at[t, slot, column])

    def part_load(self, t, s, slot):
        return pltpu.make_async_copy(self.stages[t].at[s], self.part[t].at[slot], self.part_sem.at[t, slot])

    def ring_copy(self, t, s):
        return send(self.went[t].at[s], self.came[t].at[s], self.ring_s.at[t, s], self.ring_r.at[t, s],
                    self.next[self.plan.pieces[t][4]])

    def x_copy(self, t):
        return send(self.fin_s[t], self.fin_r[t], self.x_s.at[t], self.x_r.at[t], self.other_x)

    def each(self):
        return range(len(self.plan.pieces))

    def fetch(self, t, s, slot):
        for column in range(2):
            self.core_copy(t, s, column).wait_recv()
        self.part_load(t, s, slot).start()
        for column in range(2):
            self.own_load(t, s, slot, column).start()

    def total(self, t, s, slot):
        for column in range(2):
            self.own_load(t, s, slot, column).wait()
        self.part_load(t, s, slot).wait()
        return self.own[t][slot] + self.part[t][slot]

    def begin(self):
        for s in range(self.plan.ring):
            for t in self.each():
                for column in range(2):
                    self.core_copy(t, s, column).start()

    def load_first(self):
        for t in self.each():
            self.fetch(t, 0, 0)

    def first_hop(self):
        for t in self.each():
            self.fetch(t, 1, 1)
            self.went[t][0] = self.total(t, 0, 0).astype(BF)
            self.ring_copy(t, 0).start()

    def hop(self, s):
        slot = s % 2
        for t in self.each():
            self.fetch(t, s + 1, 1 - slot)
            value = self.total(t, s, slot)
            self.ring_copy(t, s - 1).wait_recv()
            self.went[t][s] = (value + self.came[t][s - 1].astype(F32)).astype(BF)
            self.ring_copy(t, s).start()

    def finish(self):
        final = self.final
        for t in self.each():
            height = self.plan.pieces[t][3]
            value = self.total(t, final, final % 2)
            self.ring_copy(t, final - 1).wait_recv()
            value = value + self.came[t][final - 1].astype(F32)
            self.last[t][0] = value[:height]
            self.last[t][1] = value[height:]
            self.fin_s[t][...] = self.last[t][1 - self.x].astype(BF)
            self.x_copy(t).start()
        for t in self.each():
            self.x_copy(t).wait_recv()
            value = self.last[t][self.x] + self.fin_r[t][...].astype(F32)
            for o, out_col, col, width in self.plan.places[t]:
                self.outs[o][:, out_col : out_col + width] = value[:, col : col + width]
        for t in self.each():
            self.x_copy(t).wait_send()
            for s in range(final):
                self.ring_copy(t, s).wait_send()
            for s in range(self.plan.ring):
                for column in range(2):
                    self.core_copy(t, s, column).wait_send()


class Plan:
    def __init__(self, ring, inputs, pieces, shapes, places):
        self.ring, self.inputs, self.pieces, self.shapes, self.places = ring, inputs, pieces, shapes, places
        count = len(pieces)
        sizes = [(height, width) for _, _, width, height, _ in pieces]
        sems, vmem = pltpu.SemaphoreType.DMA, pltpu.VMEM
        self.out_shapes = [shape_of(hw, F32) for hw in shapes]
        self.out_shapes += [shape_of((ring, 2 * h, wd), F32) for h, wd in sizes]
        self.out_specs = [pl.BlockSpec(memory_space=pltpu.VMEM)] * len(shapes) + [ANY] * count
        self.outputs = len(self.out_shapes)
        self.scratch = (
            [vmem((2, 2 * h, wd), F32) for h, wd in sizes]
            + [vmem((2, 2 * h, wd), F32) for h, wd in sizes]
            + [vmem((ring - 1, 2 * h, wd), BF) for h, wd in sizes]
            + [vmem((ring - 1, 2 * h, wd), BF) for h, wd in sizes]
            + [vmem((2, h, wd), F32) for h, wd in sizes]
            + [vmem((h, wd), BF) for h, wd in sizes]
            + [vmem((h, wd), BF) for h, wd in sizes]
            + [sems((count, ring))] * 2
            + [sems((count, ring, 2))] * 2
            + [sems((count,))] * 2
            + [sems((count, 2, 2)), sems((count, 2))]
        )
        self.scratches = len(self.scratch)

    def steps(self, refs):
        return Sums(self, refs)


def mlp_plan(ring, g_in, g_out, devices):
    a, b = g_in.shape[0] // devices, g_out.shape[0] // devices
    wa, wb = g_in.shape[1], g_out.shape[1]
    return Plan(ring, 2, [(0, 0, wa, a, 0), (1, 0, wb, b, 1)], [(a, wa), (b, wb)], [[(0, 0, 0, wa)], [(1, 0, 0, wb)]])


def attn_plan(ring, g, devices):
    h, half, cut = g.shape[0] // devices, 2 * D, 3 * D
    return Plan(ring, 1, [(0, 0, half, h, 0), (0, half, half, h, 1)], [(h, cut), (h, D)],
                [[(0, 0, 0, half)], [(0, half, 0, cut - half), (1, 0, cut - half, D)]])


def scatter_kernel(plan, *refs):
    sums = plan.steps(refs)
    greet(sums.peers)
    sums.begin()
    sums.load_first()
    sums.first_hop()

    def body(s, carry):
        sums.hop(s)
        return carry

    lax.fori_loop(1, sums.final, body, 0)
    sums.finish()


def scatter_last(g, plan):
    got = pl.pallas_call(
        functools.partial(scatter_kernel, plan),
        name="scatter_last",
        out_shape=plan.out_shapes,
        in_specs=[ANY],
        out_specs=plan.out_specs,
        scratch_shapes=plan.scratch,
        compiler_params=pltpu.CompilerParams(
            collective_id=1, has_side_effects=True, vmem_limit_bytes=VMEM_LIMIT
        ),
    )(g)
    return got[:2]


def tuned(mesh):
    wide, n = mesh.shape["wide"], mesh.shape["narrow"]
    if n != 4 or wide != 2 * GRID or D % (8 * wide * n):
        return False
    for w in range(wide):
        for k in range(n):
            device = mesh.devices[w, k]
            here = (getattr(device, "coords", None), getattr(device, "core_on_chip", None))
            if here[0] is None or tuple(here[0]) != (k // 2, w % 2, w // 2) or here[1] != k % 2:
                return False
    return True


def exchange(x):
    return lax.all_to_all(x, ALL, split_axis=0, concat_axis=0, tiled=True)


def shift_clips(clips, back):
    n = lax.axis_size("narrow")
    parts = [clips[0]]
    for j in range(1, n):
        step = -j if back else j
        parts.append(lax.ppermute(clips[j], "narrow", [(s, (s + step) % n) for s in range(n)]))
    return jnp.stack(parts)


def local(fast, clips, t_emb, lengths, task, w_mod, b_mod, w_qkv_s, w_o_s, b_o_s, w_qkv_t, w_o_t, b_o_t,
          w_in, b_in, w_out, b_out, cotangent):
    n = lax.axis_size("narrow")
    wide = lax.axis_size("wide")
    devices = n * wide
    part = w_mod.shape[0]
    mod_cols = w_mod.shape[1] // devices
    rank = lax.axis_index("narrow")
    slots = jnp.arange(n, dtype=jnp.int32)
    from_clip = (rank - slots) % n
    recv_len = lengths.reshape(n, n)[from_clip, slots]
    recv_task = task.reshape(n, n, FR)[from_clip, slots]
    ends = jnp.cumsum(recv_len)
    starts = ends - recv_len
    ids = jnp.arange(LIVE, dtype=jnp.int32)
    source = jnp.sum((ends[None, :] <= ids[:, None]).astype(jnp.int32), axis=1)
    within = ids - starts[source]
    pack_rows = source * FR + within
    row_choice = source * 2 + recv_task[source, within]
    frame_ids = jnp.arange(FR, dtype=jnp.int32)
    live_back = frame_ids[None, :] < recv_len[:, None]
    unpack_rows = jnp.where(live_back, starts[:, None] + frame_ids[None, :], 0).reshape(-1)
    row_id = jnp.arange(64, dtype=jnp.int32)
    col_id = jnp.arange(LANES, dtype=jnp.int32) % 64
    seg = (
        (row_id[:, None] // LIVE == col_id[None, :] // LIVE)
        & (source[row_id % LIVE][:, None] == source[col_id % LIVE][None, :])
    ).astype(F32)

    def gather(w):
        return lax.all_gather(w, ALL, axis=0, tiled=True)

    weights = (w_in, w_out, w_qkv_t, w_o_t, w_qkv_s, w_o_s)
    if fast:
        frames, weights = gather_all(clips, weights, (0, 0, 1, 1, 1, 1), wide, n)
    else:
        frames = shift_clips(clips, False)
        weights = [gather(w) for w in weights]
    win, wout, wqkv_t, wo_t, wqkv_s, wo_s = weights
    frames = jnp.take(frames.reshape(n * FR, PATCHES, D), pack_rows, axis=0, mode="clip")

    wm = jnp.swapaxes(w_mod.reshape(part, devices, mod_cols), 0, 1).reshape(devices, -1)
    emb = jnp.broadcast_to(t_emb.reshape(1, -1), (devices, t_emb.size))
    small = jnp.concatenate([b_o_s, b_o_t, b_in, b_out])
    small_all = jnp.broadcast_to(small[None], (devices, small.size))
    got = exchange(jnp.concatenate([wm, emb, small_all], axis=1))
    wm_cols = got[:, : part * mod_cols].reshape(D, mod_cols)
    emb_all = got[:, part * mod_cols : part * mod_cols + t_emb.size].reshape(-1, D)
    small_got = got[:, part * mod_cols + t_emb.size :]
    b1 = b_o_s.size
    bias_s = small_got[:, :b1].reshape(1, -1).astype(F32)
    bias_t = small_got[:, b1 : 2 * b1].reshape(1, -1).astype(F32)
    bias_in = small_got[:, 2 * b1 : 2 * b1 + b_in.size].reshape(1, -1).astype(F32)
    bias_out = small_got[:, 2 * b1 + b_in.size :].reshape(1, -1).astype(F32)
    emb_f = emb_all.astype(F32)
    silu_low = (emb_f * jax.nn.sigmoid(emb_f)).astype(BF)
    mod_part = dot(silu_low, wm_cols) + b_mod.astype(F32)[None]
    mod_part = mod_part.reshape(wide, n, n, 2, mod_cols)
    mod_part = jnp.stack([jnp.roll(mod_part[:, :, c], c, axis=1) for c in range(n)], axis=2)
    mod_rows = exchange(mod_part.reshape(devices, -1)).reshape(devices, 2 * n, mod_cols)
    mod_rows = jnp.swapaxes(mod_rows, 0, 1).reshape(2 * n, 9, D)
    mod = jnp.swapaxes(mod_rows[row_choice], 0, 1)

    def carry(clips, js, back, number, plan=None, grads=()):
        return (clips, n, js, back, number, plan, list(grads)) if fast else None

    def regroup(clips, back, half, odd):
        if fast:
            return jnp.stack([clips[0], odd[0], half[0], odd[1]])
        return shift_clips(clips, back)

    *half, x1, qkv1, o1, a1 = run_frame_forward(
        frames, mod, wqkv_s, wo_s, bias_s, carry(cotangent, (2,), False, 2))
    *odd, x2, qkv2, o2, a2 = run_time_forward(
        x1, mod, seg, wqkv_t, wo_t, bias_t, carry(cotangent, (1, 3), False, 3))
    cots = regroup(cotangent, False, *(half or [None]), *(odd or [None]))
    dy = run_turn_frames(cots.reshape(n * FR, PATCHES, D), pack_rows)
    out, dx2, g_in, g_out, gb_in, gb_out, dmod3 = run_mlp(x2, dy, mod, win, bias_in, wout, bias_out)

    own_live = frame_ids[None, :] < lengths.reshape(n, n)[rank][:, None]

    def spread(packed):
        return jnp.take(packed, unpack_rows, axis=0, mode="clip").reshape(n, FR, PATCHES, D)

    def only_live(parts):
        return jnp.where(own_live[:, :, None, None], parts, jnp.zeros((), parts.dtype))

    def scatter(g):
        return lax.psum_scatter(g.astype(BF), ALL, scatter_dimension=0, tiled=True).astype(F32)

    out = spread(out)
    if fast:
        half, s_in, s_out, _, _, dx1, g_t, gb_t, dmod2 = run_time_back(
            x1, dx2, mod, seg, qkv2, o2, a2, wqkv_t, wo_t,
            carry(out, (2,), True, 4, mlp_plan(wide, g_in, g_out, devices), (g_in, g_out)))
        odd, s_qkv_t, s_o_t, _, _, dx0, g_s, gb_s, dmod1 = run_frame_back(
            frames, dx1, mod, qkv1, o1, a1, wqkv_s, wo_s,
            carry(out, (1, 3), True, 5, attn_plan(wide, g_t, devices), (g_t,)))
    else:
        half = odd = None
        dx1, g_t, gb_t, dmod2 = run_time_back(x1, dx2, mod, seg, qkv2, o2, a2, wqkv_t, wo_t)
        dx0, g_s, gb_s, dmod1 = run_frame_back(frames, dx1, mod, qkv1, o1, a1, wqkv_s, wo_s)
    layer_out = only_live(regroup(out, True, half, odd))
    grad_clips = only_live(shift_clips(spread(dx0), True))
    if fast:
        s_qkv_s, s_o_s = scatter_last(g_s, attn_plan(wide, g_s, devices))
    else:
        s_in, s_out, s_t, s_s = [scatter(g) for g in (g_in, g_out, g_t, g_s)]
        s_qkv_t, s_o_t, s_qkv_s, s_o_s = s_t[:, : 3 * D], s_t[:, 3 * D :], s_s[:, : 3 * D], s_s[:, 3 * D :]

    grad_frames = jnp.swapaxes(jnp.concatenate([dmod1, dmod2, dmod3], axis=0), 0, 1).reshape(LIVE, 9 * D)
    chooser = (row_choice[:, None] == jnp.arange(2 * n, dtype=jnp.int32)[None, :]).astype(F32)
    grad_rows = lax.dot_general(
        chooser, grad_frames, (((0,), (0,)), ((), ())), precision=lax.Precision.HIGHEST
    ).astype(BF)
    d_cols = exchange(jnp.swapaxes(grad_rows.reshape(2 * n, devices, mod_cols), 0, 1).reshape(devices, -1))
    d_cols = d_cols.reshape(wide, n, n, 2, mod_cols)
    d_cols = jnp.stack([jnp.roll(d_cols[:, :, c], -c, axis=1) for c in range(n)], axis=2)
    d_cols = d_cols.reshape(devices * 2 * n, mod_cols)
    grad_b_mod = jnp.sum(d_cols.astype(F32), axis=0)
    gwm_cols = dot_tn(silu_low, d_cols)
    g_emb = dot_nt(d_cols, wm_cols)
    gb_all = jnp.concatenate(
        [gb_s.reshape(devices, -1), gb_t.reshape(devices, -1), gb_in.reshape(devices, -1),
         gb_out.reshape(devices, -1)], axis=1)
    final = exchange(jnp.concatenate(
        [gwm_cols.reshape(devices, -1), g_emb.reshape(devices, -1), gb_all], axis=1))
    cut1 = part * mod_cols
    cut2 = cut1 + t_emb.size
    grad_w_mod = jnp.swapaxes(final[:, :cut1].reshape(devices, part, mod_cols), 0, 1).reshape(part, -1)
    emb_own = t_emb.astype(F32)
    sig = jax.nn.sigmoid(emb_own)
    grad_emb = jnp.sum(final[:, cut1:cut2], axis=0).reshape(t_emb.shape)
    grad_t_emb = (grad_emb * (sig * (1.0 + emb_own * (1.0 - sig)))).astype(BF)
    gb = jnp.sum(final[:, cut2:], axis=0)
    return (
        layer_out,
        grad_clips,
        grad_t_emb,
        grad_w_mod,
        grad_b_mod,
        s_qkv_s,
        s_o_s,
        gb[:b1],
        s_qkv_t,
        s_o_t,
        gb[b1 : 2 * b1],
        s_in,
        gb[2 * b1 : 2 * b1 + b_in.size],
        s_out,
        gb[2 * b1 + b_in.size :],
    )


def solution(mesh):
    full = P(ALL)
    placed = (full, full, P("wide"), P("wide")) + (full,) * 13
    return jax.shard_map(functools.partial(local, tuned(mesh)), mesh=mesh, in_specs=placed, out_specs=(full,) * 15, check_vma=False)
```

```python
import functools

import jax
import jax.numpy as jnp
from jax import lax
from jax.experimental import pallas as pl
from jax.experimental.pallas import tpu as pltpu
from jax.sharding import PartitionSpec as P

D = 768
HEADS = 12
HEAD = 64
FF = 3072
FR = 16
PATCHES = 64
LIVE = 2 * FR
EPS = 1e-06
BF = jnp.bfloat16
F32 = jnp.float32
ALL = ("wide", "narrow")
PAIRS = HEADS // 2
LANES = 2 * HEAD
BACK_PAIRS = 6
TILE = 512
FT = TILE // PATCHES
PT = TILE // LIVE
GRID = LIVE * PATCHES // TILE
GROUPS = TILE // 64
GELU_C = 0.7978845608028654
GELU_A = 0.044715
VMEM_LIMIT = 66 * 1000 * 1000
MESH = pl.DeviceIdType.MESH
ANY = pl.BlockSpec(memory_space=pl.ANY)


def dot(a, b):
    return lax.dot_general(a, b, (((1,), (0,)), ((), ())), preferred_element_type=F32)


def dot_nt(a, b):
    return lax.dot_general(a, b, (((1,), (1,)), ((), ())), preferred_element_type=F32)


def dot_tn(a, b):
    return lax.dot_general(a, b, (((0,), (0,)), ((), ())), preferred_element_type=F32)


def normalise(x):
    mean = jnp.mean(x, axis=-1, keepdims=True)
    centred = x - mean
    var = jnp.mean(centred * centred, axis=-1, keepdims=True)
    rstd = lax.rsqrt(var + EPS)
    return centred * rstd, rstd


def norm_back(dn, xhat, rstd):
    m1 = jnp.mean(dn, axis=-1, keepdims=True)
    m2 = jnp.mean(dn * xhat, axis=-1, keepdims=True)
    return rstd * (dn - m1 - xhat * m2)


def lane_masks():
    lane = lax.broadcasted_iota(jnp.int32, (64, LANES), 1)
    low_lanes = lane < HEAD
    low = jnp.where(low_lanes, 1.0, 0.0).astype(BF)
    high = jnp.where(low_lanes, 0.0, 1.0).astype(BF)
    return low_lanes, low, high


def split_heads(x, low, high):
    return jnp.concatenate([x * low, x * high], axis=0)


def softmax_keys(s, mask):
    if mask is not None:
        s = jnp.where(mask, s, -1e30)
    top = jnp.max(s, axis=0, keepdims=True)
    e = jnp.exp(s - top)
    return e * (1.0 / jnp.sum(e, axis=0, keepdims=True))


def pair_cols(part, hp):
    return slice(part * D + hp * LANES, part * D + (hp + 1) * LANES)


def attend(qkv_ref, o_ref, mask):
    low_lanes, low, high = lane_masks()
    scale = HEAD ** (-0.5)

    def body(g, carry):
        rows = pl.ds(pl.multiple_of(g * 64, 64), 64)
        pairs = range(PAIRS)
        s = [dot_nt(qkv_ref[rows, pair_cols(1, hp)], split_heads(qkv_ref[rows, pair_cols(0, hp)], low * scale, high * scale))
             for hp in pairs]
        p = [softmax_keys(t, mask).astype(BF) for t in s]
        r = [dot_tn(p[hp], qkv_ref[rows, pair_cols(2, hp)]) for hp in pairs]
        for hp in pairs:
            o_ref[rows, pair_cols(0, hp)] = jnp.where(low_lanes, r[hp][:64], r[hp][64:]).astype(BF)
        return carry

    lax.fori_loop(0, GROUPS, body, 0)


def attend_back(qkv_ref, do_ref, dqkv_ref, mask):
    low_lanes, low, high = lane_masks()
    scale = HEAD ** (-0.5)

    def body(g, carry):
        rows = pl.ds(pl.multiple_of(g * 64, 64), 64)
        for first in range(0, PAIRS, BACK_PAIRS):
            pairs = range(first, first + BACK_PAIRS)
            qb = [split_heads(qkv_ref[rows, pair_cols(0, hp)], low * scale, high * scale) for hp in pairs]
            dob = [split_heads(do_ref[rows, pair_cols(0, hp)], low, high) for hp in pairs]
            s = [dot_nt(qkv_ref[rows, pair_cols(1, hp)], q) for hp, q in zip(pairs, qb)]
            dp = [dot_nt(qkv_ref[rows, pair_cols(2, hp)], d) for hp, d in zip(pairs, dob)]
            p = [softmax_keys(t, mask) for t in s]
            delta = [jnp.sum(a * b, axis=0, keepdims=True) for a, b in zip(p, dp)]
            ds = [(a * (b - c)).astype(BF) for a, b, c in zip(p, dp, delta)]
            dv = [dot(a.astype(BF), d) for a, d in zip(p, dob)]
            dk = [dot(a, q) for a, q in zip(ds, qb)]
            r = [dot_tn(a, qkv_ref[rows, pair_cols(1, hp)]) for hp, a in zip(pairs, ds)]
            for i, hp in enumerate(pairs):
                dqkv_ref[rows, pair_cols(2, hp)] = dv[i].astype(BF)
                dqkv_ref[rows, pair_cols(1, hp)] = dk[i].astype(BF)
                dq = jnp.where(low_lanes, r[i][:64], r[i][64:]) * scale
                dqkv_ref[rows, pair_cols(0, hp)] = dq.astype(BF)
        return carry

    lax.fori_loop(0, GROUPS, body, 0)


def swap_major(value, scratch, out_ref, first, second):
    for b in range(D // 128):
        cols = slice(b * 128, (b + 1) * 128)
        for i in range(first):
            scratch[b, pl.ds(i, second, stride=first), :] = value[i * second : (i + 1) * second, cols]
        out_ref[:, :, cols] = scratch[b].reshape(second, first, 128).astype(out_ref.dtype)


def frames_of(refs):
    return jnp.concatenate([r[0] for r in refs], axis=0).astype(F32)


def per_frame(piece):
    return jnp.broadcast_to(piece[:, None, :], (FT, PATCHES, D)).reshape(TILE, D)


def per_patch(piece):
    return jnp.broadcast_to(piece[None], (PT, LIVE, D)).reshape(TILE, D)


def sum_patches(value):
    return jnp.sum(value.reshape(FT, PATCHES, D), axis=1)


def sum_groups(value):
    return jnp.sum(value.reshape(PT, LIVE, D), axis=0)


def attn_mask(seg_ref):
    return seg_ref[...] > 0.0


def frame_forward(frames, mod, wqkv, wo, bo, x1t, qkv, o, a1, scratch):
    x = frames[...].reshape(TILE, D).astype(F32)
    xhat, _ = normalise(x)
    h = (xhat * (1.0 + per_frame(mod[1])) + per_frame(mod[0])).astype(BF)
    qkv[...] = dot(h, wqkv[...]).astype(BF)
    attend(qkv, o, None)
    branch = dot(o[...], wo[...]) + bo[...]
    a1[...] = branch
    x1 = x + per_frame(mod[2]) * branch
    swap_major(x1, scratch, x1t, FT, PATCHES)


def turn_frames(rows_ref, *refs):
    x_refs, (out, scratch) = refs[:FT], refs[FT:]
    swap_major(frames_of(x_refs), scratch, out, FT, PATCHES)


def time_forward(x1, mod, seg, wqkv, wo, bo, x2, qkv, o, a2):
    x = x1[...].reshape(TILE, D)
    xhat, _ = normalise(x)
    h = (xhat * (1.0 + per_patch(mod[1])) + per_patch(mod[0])).astype(BF)
    qkv[...] = dot(h, wqkv[...]).astype(BF)
    attend(qkv, o, attn_mask(seg))
    branch = dot(o[...], wo[...]) + bo[...]
    a2[...] = branch
    x2[...] = (x + per_patch(mod[2]) * branch).reshape(PT, LIVE, D)


def mlp_both(x2, dy, mod, win, bin_, wout, bout, out, dx2, gwin, gwout, gbin, gbout, dmod, scratch):
    first = pl.program_id(0) == 0

    @pl.when(first)
    def _():
        gwin[...] = jnp.zeros_like(gwin)
        gwout[...] = jnp.zeros_like(gwout)
        gbin[...] = jnp.zeros_like(gbin)
        gbout[...] = jnp.zeros_like(gbout)
        dmod[...] = jnp.zeros_like(dmod)

    x = x2[...].reshape(TILE, D)
    xhat, rstd = normalise(x)
    h = (xhat * (1.0 + per_patch(mod[1])) + per_patch(mod[0])).astype(BF)
    gate = per_patch(mod[2])
    grad = dy[...].reshape(TILE, D)
    da = (grad * gate).astype(BF)
    gbout[...] += jnp.sum(da.astype(F32), axis=0, keepdims=True)
    branch = jnp.zeros((TILE, D), F32) + bout[...]
    dh = jnp.zeros((TILE, D), F32)
    for j in range(FF // D):
        cols = slice(j * D, (j + 1) * D)
        u = dot(h, win[:, cols]) + bin_[:, cols]
        u2 = u * u
        t = jnp.tanh(GELU_C * u * (1.0 + GELU_A * u2))
        half = 0.5 * (1.0 + t)
        g = (u * half).astype(BF)
        slope = half + (0.5 * GELU_C) * u * (1.0 - t * t) * (1.0 + 3.0 * GELU_A * u2)
        branch = branch + dot(g, wout[cols, :])
        du = (dot_nt(da, wout[cols, :]) * slope).astype(BF)
        gwout[cols, :] += dot_tn(g, da)
        gbin[:, cols] += jnp.sum(du.astype(F32), axis=0, keepdims=True)
        gwin[:, cols] += dot_tn(h, du)
        dh = dh + dot_nt(du, win[:, cols])
    swap_major(x + gate * branch, scratch, out, PT, LIVE)
    dmod[2] += sum_groups(grad * branch)
    dmod[0] += sum_groups(dh)
    dmod[1] += sum_groups(dh * xhat)
    back = norm_back(dh * (1.0 + per_patch(mod[1])), xhat, rstd)
    dx2[...] = (grad + back).reshape(PT, LIVE, D)


def attn_back_tile(x, grad, shift, scale, gate, branch, qkv, o, wqkv, wo, gw, gbo, do, dqkv, mask, tick):
    first = pl.program_id(0) == 0

    @pl.when(first)
    def _():
        gw[...] = jnp.zeros_like(gw)
        gbo[...] = jnp.zeros_like(gbo)

    da = (grad * gate).astype(BF)
    do[...] = dot_nt(da, wo[...]).astype(BF)
    gw[:, 3 * D :] += dot_tn(o[...], da)
    gbo[...] += jnp.sum(da.astype(F32), axis=0, keepdims=True)
    tick(0)
    attend_back(qkv, do, dqkv, mask)
    tick(1)
    xhat, rstd = normalise(x)
    h = (xhat * (1.0 + scale) + shift).astype(BF)
    dh = jnp.zeros((TILE, D), F32)
    for j in range(3):
        cols = slice(j * D, (j + 1) * D)
        part = dqkv[:, cols]
        gw[:, cols] += dot_tn(h, part)
        dh = dh + dot_nt(part, wqkv[:, cols])
    dx = grad + norm_back(dh * (1.0 + scale), xhat, rstd)
    return dx, dh, dh * xhat, grad * branch


def no_tick(place):
    pass


def time_back(x1, dx2, mod, seg, qkv, o, a2, wqkv, wo, dx1, gw, gbo, dmod, do, dqkv, scratch, tick=no_tick):
    @pl.when(pl.program_id(0) == 0)
    def _():
        dmod[...] = jnp.zeros_like(dmod)

    dx, d_shift, d_scale, d_gate = attn_back_tile(
        x1[...].reshape(TILE, D), dx2[...].reshape(TILE, D), per_patch(mod[0]), per_patch(mod[1]),
        per_patch(mod[2]), a2[...], qkv, o, wqkv, wo, gw, gbo, do, dqkv, attn_mask(seg), tick)
    dmod[0] += sum_groups(d_shift)
    dmod[1] += sum_groups(d_scale)
    dmod[2] += sum_groups(d_gate)
    swap_major(dx, scratch, dx1, PT, LIVE)


def frame_back(frames, dx1, mod, qkv, o, a1, wqkv, wo, dx0, gw, gbo, dmod, do, dqkv, tick=no_tick):
    dx, d_shift, d_scale, d_gate = attn_back_tile(
        frames[...].reshape(TILE, D).astype(F32), dx1[...].reshape(TILE, D), per_frame(mod[0]), per_frame(mod[1]),
        per_frame(mod[2]), a1[...], qkv, o, wqkv, wo, gw, gbo, do, dqkv, None, tick)
    dmod[0] = sum_patches(d_shift)
    dmod[1] = sum_patches(d_scale)
    dmod[2] = sum_patches(d_gate)
    dx0[...] = dx.reshape(FT, PATCHES, D).astype(BF)


def frame_specs():
    return [
        pl.BlockSpec((1, PATCHES, D), functools.partial(lambda j, i, rows: (rows[FT * i + j], 0, 0), j))
        for j in range(FT)
    ]


def whole(shape):
    return pl.BlockSpec(shape, lambda i, *_: (0,) * len(shape), pipeline_mode=pl.Buffered(1))


def tiles(shape, dim):
    return pl.BlockSpec(shape, lambda i, *_: tuple(i if a == dim else 0 for a in range(len(shape))))


def piece_spec(number, frames, by_tile):
    return pl.BlockSpec((3, frames, D), lambda i, *_: (number, i if by_tile else 0, 0))


ROWS = tiles((TILE, D), 0)
ROWS3 = tiles((TILE, 3 * D), 0)
TURNED = tiles((PT, LIVE, D), 0)


TURN = pltpu.VMEM((D // 128, TILE, 128), F32)


def shape_of(shape, dtype):
    return jax.ShapeDtypeStruct(shape, dtype)


class Carrier:
    def __init__(self, wrap, number, ins, outs, out_specs, scratch, aliases=None):
        self.wrap, self.number, self.ins, self.outs = wrap, number, ins, outs
        self.out_specs, self.scratch, self.aliases = out_specs, scratch, aliases or {}


def call(kernel, name, ins, in_specs, outs, out_specs, scratch, flops, prefetch=None, carrier=None):
    moved = sum(a.size * a.dtype.itemsize for a in tuple(ins) + tuple(outs))
    params, aliases = {}, {}
    if carrier is not None:
        kernel = functools.partial(carrier.wrap, kernel, len(ins), len(outs), len(scratch))
        ins, in_specs = carrier.ins + ins, [ANY] * len(carrier.ins) + in_specs
        outs, out_specs = carrier.outs + outs, carrier.out_specs + out_specs
        scratch = scratch + carrier.scratch
        params, aliases = dict(collective_id=carrier.number, has_side_effects=True), carrier.aliases
    grid_spec = pltpu.PrefetchScalarGridSpec(
        num_scalar_prefetch=0 if prefetch is None else 1,
        grid=(GRID,),
        in_specs=in_specs,
        out_specs=out_specs,
        scratch_shapes=scratch,
    )
    fn = pl.pallas_call(
        kernel,
        grid_spec=grid_spec,
        out_shape=outs,
        name=name,
        input_output_aliases=aliases,
        cost_estimate=pl.CostEstimate(flops=flops, bytes_accessed=moved, transcendentals=0),
        compiler_params=pltpu.CompilerParams(
            dimension_semantics=("arbitrary",), vmem_limit_bytes=VMEM_LIMIT, **params
        ),
    )
    return fn(*ins) if prefetch is None else fn(prefetch, *ins)


def split_refs(refs, *counts):
    parts = []
    for count in counts:
        parts.append(refs[:count])
        refs = refs[count:]
    return parts + [refs]


def clips_carrier(clips, js, n, number):
    def wrap(kernel, n_in, n_out, n_scratch, *refs):
        (src,), ins, (dst,), outs, scratch, (send_sem, recv_sem) = split_refs(refs, 1, n_in, 1, n_out, n_scratch)
        w, k = lax.axis_index("wide"), lax.axis_index("narrow")
        peers = [(w, (k + j) % n) for j in js]
        copies = [send(src.at[j], dst.at[i], send_sem.at[i], recv_sem.at[i], peers[i]) for i, j in enumerate(js)]

        @pl.when(pl.program_id(0) == 0)
        def _():
            greet(peers)
            for copy in copies:
                copy.start()

        kernel(*ins, *outs, *scratch)

        @pl.when(pl.program_id(0) == GRID - 1)
        def _():
            for copy in copies:
                copy.wait()

    sems = pltpu.SemaphoreType.DMA((len(js),))
    return Carrier(wrap, number, [clips], [shape_of((len(js),) + clips.shape[1:], clips.dtype)], [ANY], [sems, sems])


def packed(slot, first=0, count=LIVE):
    return pl.ds(pl.multiple_of(slot * LIVE + first, 8), count)


def slot_for(k):
    return 3 - 2 * (k % 2)


def ticks(sums, step):
    @pl.when(step > 0)
    def _():
        sums.hop(2 * step - 1)

    def tick(place):
        @pl.when(step == 0)
        def _():
            if place == 0:
                sums.load_first()
            else:
                sums.first_hop()

        if place == 1:
            @pl.when(step > 0)
            def _():
                sums.hop(2 * step)

    return tick


def share_carrier(frames, grads, plan, number):
    n_grads = len(grads)

    def wrap(kernel, n_in, n_out, n_scratch, *refs):
        (_,), grad_refs, ins, (dst,), left, outs, scratch, (send_sem, recv_sem), own = split_refs(
            refs, 1, n_grads, n_in, 1, plan.outputs, n_out, n_scratch, 2)
        step = pl.program_id(0)
        sums = plan.steps(grad_refs + left + own)
        targets = ((slot_for(sums.k), sums.other_c), (2, sums.other_x))
        copies = [send(dst.at[packed(0)], dst.at[packed(slot)], send_sem.at[i], recv_sem.at[i], peer)
                  for i, (slot, peer) in enumerate(targets)]

        @pl.when(step == 0)
        def _():
            greet(sums.peers)
            sums.begin()
            for copy in copies:
                copy.start()

        kernel(*ins, *outs, *scratch, tick=ticks(sums, step))

        @pl.when(step == GRID - 1)
        def _():
            sums.leave()
            for copy in copies:
                copy.wait()

    sems = pltpu.SemaphoreType.DMA((2,))
    return Carrier(wrap, number, [frames] + grads, [shape_of(frames.shape, frames.dtype)] + plan.out_shapes,
                   [ANY] + plan.out_specs, [sems, sems] + plan.scratch, {0: 0})


def tile_copies(k, other_c, other_x, src, dst, i, send_sem, recv_sem):
    return [send(src, dst.at[packed(slot, i * FT, FT)], send_sem.at[a, i], recv_sem.at[a, i], peer)
            for a, (slot, peer) in enumerate(((slot_for(k), other_c), (2, other_x)))]


def relay_carrier(frames, grads, plan, number):
    n_grads = len(grads)

    def wrap(kernel, n_in, n_out, n_scratch, *refs):
        (_,), grad_refs, ins, (dst, made), left, outs, scratch, (send_sem, recv_sem, tile_s, tile_r, keep, buf), own = (
            split_refs(refs, 1, n_grads, n_in, 2, plan.outputs, n_out, n_scratch, 6))
        step = pl.program_id(0)
        sums = plan.steps(grad_refs + left + own)
        relay = send(dst.at[packed(2)], dst.at[packed(4 - slot_for(sums.k))],
                     send_sem.at[0], recv_sem.at[0], sums.other_c)

        def tile(i):
            return tile_copies(sums.k, sums.other_c, sums.other_x, buf.at[i], made, i, tile_s, tile_r)

        def store(i):
            return pltpu.make_async_copy(buf.at[i], made.at[packed(0, i * FT, FT)], keep.at[i])

        @pl.when(step == 0)
        def _():
            greet(sums.peers)
            sums.begin()
            relay.start()

        kernel(*ins, buf.at[step], *outs, *scratch, tick=ticks(sums, step))
        store(step).start()

        @pl.when(step < GRID - 1)
        def _():
            for copy in tile(step):
                copy.start()

        @pl.when(step == GRID - 1)
        def _():
            sums.leave()
            relay.wait()
            for i in range(GRID):
                store(i).wait()
            for i in range(GRID - 1):
                for copy in tile(i):
                    copy.wait()

    sems = pltpu.SemaphoreType.DMA
    shape = shape_of(frames.shape, frames.dtype)
    return Carrier(wrap, number, [frames] + grads, [shape, shape] + plan.out_shapes, [ANY, ANY] + plan.out_specs,
                   [sems((1,)), sems((1,)), sems((2, GRID - 1)), sems((2, GRID - 1)), sems((GRID,)),
                    pltpu.VMEM((GRID, FT, PATCHES, D), BF)] + plan.scratch, {0: 0})


TOKENS = LIVE * PATCHES


def run_frame_forward(frames, mod, wqkv, wo, bo, carrier=None):
    return call(
        frame_forward, "frame_forward",
        [frames, mod, wqkv, wo, bo],
        [tiles((FT, PATCHES, D), 0), piece_spec(0, FT, True), whole((D, 3 * D)), whole((D, D)), whole((1, D))],
        [shape_of((PATCHES, LIVE, D), F32), shape_of((TOKENS, 3 * D), BF), shape_of((TOKENS, D), BF),
         shape_of((TOKENS, D), F32)],
        [tiles((PATCHES, FT, D), 1), ROWS3, ROWS, ROWS],
        [TURN],
        2 * TOKENS * D * 4 * D, carrier=carrier)


def run_turn_frames(frames, rows):
    return call(
        turn_frames, "turn_frames", [frames] * FT, frame_specs(),
        [shape_of((PATCHES, LIVE, D), F32)], [tiles((PATCHES, FT, D), 1)],
        [TURN], 1000, rows)[0]


def unpack_frames(rows_ref, *refs):
    x_refs, (out,) = refs[:FT], refs[FT:]
    first = pl.program_id(0) * FT
    for j in range(FT):
        x = x_refs[j][0]
        out[j] = jnp.where(rows_ref[first + j] >= 0, x, jnp.zeros_like(x))


def run_unpack(frames, rows):
    specs = [
        pl.BlockSpec((1, PATCHES, D), functools.partial(lambda j, i, r: (jnp.maximum(r[FT * i + j], 0), 0, 0), j))
        for j in range(FT)
    ]
    return pl.pallas_call(
        unpack_frames,
        grid_spec=pltpu.PrefetchScalarGridSpec(
            num_scalar_prefetch=1, grid=(rows.shape[0] // FT,), in_specs=specs, out_specs=tiles((FT, PATCHES, D), 0)),
        out_shape=shape_of((rows.shape[0], PATCHES, D), frames.dtype),
        name="unpack_frames",
        cost_estimate=pl.CostEstimate(flops=1000, bytes_accessed=4 * rows.shape[0] * PATCHES * D, transcendentals=0),
        compiler_params=pltpu.CompilerParams(dimension_semantics=("arbitrary",)),
    )(rows, *[frames] * FT)


def run_time_forward(x1, mod, seg, wqkv, wo, bo, carrier=None):
    return call(
        time_forward, "time_forward",
        [x1, mod, seg, wqkv, wo, bo],
        [TURNED, piece_spec(1, LIVE, False), whole((64, LANES)), whole((D, 3 * D)), whole((D, D)),
         whole((1, D))],
        [shape_of((PATCHES, LIVE, D), F32), shape_of((TOKENS, 3 * D), BF), shape_of((TOKENS, D), BF),
         shape_of((TOKENS, D), F32)],
        [TURNED, ROWS3, ROWS, ROWS],
        [], 2 * TOKENS * D * 4 * D, carrier=carrier)


def run_mlp(x2, dy, mod, win, bin_, wout, bout, slots=1):
    return call(
        mlp_both, "mlp_both",
        [x2, dy, mod, win, bin_, wout, bout],
        [TURNED, TURNED, piece_spec(2, LIVE, False), whole((D, FF)), whole((1, FF)), whole((FF, D)),
         whole((1, D))],
        [shape_of((slots * LIVE, PATCHES, D), BF), shape_of((PATCHES, LIVE, D), F32), shape_of((D, FF), F32),
         shape_of((FF, D), F32), shape_of((1, FF), F32), shape_of((1, D), F32), shape_of((3, LIVE, D), F32)],
        [tiles((LIVE, PT, D), 1), TURNED, whole((D, FF)), whole((FF, D)), whole((1, FF)), whole((1, D)),
         whole((3, LIVE, D))],
        [TURN],
        6 * 2 * TOKENS * D * FF)


def run_time_back(x1, dx2, mod, seg, qkv, o, a2, wqkv, wo, carrier=None):
    return call(
        time_back, "time_back",
        [x1, dx2, mod, seg, qkv, o, a2, wqkv, wo],
        [TURNED, TURNED, piece_spec(1, LIVE, False), whole((64, LANES)), ROWS3, ROWS, ROWS,
         whole((D, 3 * D)), whole((D, D))],
        [shape_of((LIVE, PATCHES, D), F32), shape_of((D, 4 * D), F32), shape_of((1, D), F32), shape_of((3, LIVE, D), F32)],
        [tiles((LIVE, PT, D), 1), whole((D, 4 * D)), whole((1, D)), whole((3, LIVE, D))],
        [pltpu.VMEM((TILE, D), BF), pltpu.VMEM((TILE, 3 * D), BF), TURN],
        2 * 2 * TOKENS * D * 4 * D, carrier=carrier)


def run_frame_back(frames, dx1, mod, qkv, o, a1, wqkv, wo, carrier=None):
    frames_out = [] if carrier else [shape_of((LIVE, PATCHES, D), BF)]
    frames_spec = [] if carrier else [tiles((FT, PATCHES, D), 0)]
    return call(
        frame_back, "frame_back",
        [frames, dx1, mod, qkv, o, a1, wqkv, wo],
        [tiles((FT, PATCHES, D), 0), tiles((FT, PATCHES, D), 0), piece_spec(0, FT, True), ROWS3, ROWS, ROWS,
                         whole((D, 3 * D)), whole((D, D))],
        frames_out + [shape_of((D, 4 * D), F32), shape_of((1, D), F32), shape_of((3, LIVE, D), F32)],
        frames_spec + [whole((D, 4 * D)), whole((1, D)), piece_spec(0, FT, True)],
        [pltpu.VMEM((TILE, D), BF), pltpu.VMEM((TILE, 3 * D), BF)],
        2 * 2 * TOKENS * D * 4 * D, carrier=carrier)


def place_of(wide):
    ring = wide
    turn = ring // 2
    w = lax.axis_index("wide")
    k = lax.axis_index("narrow")
    z, y = w // 2, w % 2
    r = z + y * (ring - 1 - 2 * z)

    def wide_at(position):
        side = position // turn
        return 2 * ((1 - side) * position + side * (ring - 1 - position)) + side

    return w, k, r, k // 2, k % 2, wide_at


def greet(peers):
    barrier = pltpu.get_barrier_semaphore()
    for peer in peers:
        pl.semaphore_signal(barrier, inc=1, device_id=peer, device_id_type=MESH)
    pl.semaphore_wait(barrier, len(peers))


def send(src, dst, send_sem, recv_sem, peer):
    return pltpu.make_async_remote_copy(
        src_ref=src, dst_ref=dst, send_sem=send_sem, recv_sem=recv_sem, device_id=peer, device_id_type=MESH
    )


def gather_kernel(ring, n, heights, ways, *refs):
    count = len(heights)
    clips, shards = refs[0], refs[1 : 1 + count]
    frames, full = refs[1 + count], refs[2 + count : 2 + 2 * count]
    clip_buf, bufs = refs[2 + 2 * count], refs[3 + 2 * count : 3 + 3 * count]
    ring_s, ring_r, core_s, core_r, x_s, x_r, clip_s, clip_r, load_sem, keep_sem = refs[3 + 3 * count :]
    w, k, r, x, c, wide_at = place_of(ring)
    other_x = (w, 2 * (1 - x) + c)
    other_c = (w, 2 * x + 1 - c)
    steps = ((wide_at((r + 1) % ring), k), (wide_at((r + ring - 1) % ring), k))
    greet(steps + tuple((w, (k + j) % n) for j in range(1, n)))

    def rows(t, position, column):
        block = 4 * wide_at(position) + 2 * column + c
        return pl.ds(pl.multiple_of(block * heights[t], 8), heights[t])

    def ring_copy(t, b, s, src=None):
        place = (r + ring - s) % ring if ways[t] == 0 else (r + s) % ring
        dst = full[t].at[rows(t, place, x if b == 0 else 1 - x)]
        return send(dst if src is None else src, dst, ring_s.at[t, b, s], ring_r.at[t, b, s], steps[ways[t]])

    def core_copy(t, b, s, src=None):
        place = (r + ring - s) % ring if ways[t] == 0 else (r + s) % ring
        dst = full[t].at[rows(t, place, x if b == 0 else 1 - x)]
        return send(dst if src is None else src, dst, core_s.at[t, b, s], core_r.at[t, b, s], other_c)

    def x_copy(t):
        dst = full[t].at[rows(t, r, x)]
        return send(shards[t], dst, x_s.at[t], x_r.at[t], other_x)

    def clip_copy(j):
        return send(clips.at[j], frames.at[j], clip_s.at[j], clip_r.at[j], (w, (k + j) % n))

    for t in range(count):
        x_copy(t).start()
        ring_copy(t, 0, 0, shards[t]).start()
    for j in range(1, n):
        clip_copy(j).start()
    for t in range(count):
        core_copy(t, 0, 0, shards[t]).start()
    loads = [pltpu.make_async_copy(clips.at[0], clip_buf, load_sem.at[count])]
    loads += [pltpu.make_async_copy(shards[t], bufs[t], load_sem.at[t]) for t in range(count)]
    keeps = [pltpu.make_async_copy(clip_buf, frames.at[0], keep_sem.at[count])]
    keeps += [pltpu.make_async_copy(bufs[t], full[t].at[rows(t, r, x)], keep_sem.at[t]) for t in range(count)]
    for copy in loads:
        copy.start()
    for copy, keep in zip(loads, keeps):
        copy.wait()
        keep.start()
    for t in range(count):
        x_copy(t).wait_recv()
        ring_copy(t, 1, 0).start()
        core_copy(t, 1, 0).start()
    for s in range(1, ring):
        for b in range(2):
            for t in range(count):
                ring_copy(t, b, s - 1).wait_recv()
                if s < ring - 1:
                    ring_copy(t, b, s).start()
                core_copy(t, b, s).start()
    for copy in keeps:
        copy.wait()
    for t in range(count):
        x_copy(t).wait_send()
        for b in range(2):
            for s in range(ring):
                if s < ring - 1:
                    ring_copy(t, b, s).wait_send()
                core_copy(t, b, s).wait()
    for j in range(1, n):
        clip_copy(j).wait()


def gather_all(clips, shards, ways, ring, n):
    count = len(shards)
    devices = ring * n
    heights = tuple(a.shape[0] for a in shards)
    sems = pltpu.SemaphoreType.DMA
    got = pl.pallas_call(
        functools.partial(gather_kernel, ring, n, heights, ways),
        name="gather_all",
        out_shape=[shape_of(clips.shape, clips.dtype)]
        + [shape_of((a.shape[0] * devices, a.shape[1]), a.dtype) for a in shards],
        in_specs=[ANY] * (1 + count),
        out_specs=[ANY] * (1 + count),
        scratch_shapes=[pltpu.VMEM(clips.shape[1:], clips.dtype)]
        + [pltpu.VMEM(a.shape, a.dtype) for a in shards]
        + [sems((count, 2, ring))] * 4
        + [sems((count,))] * 2
        + [sems((n,))] * 2
        + [sems((count + 1,))] * 2,
        compiler_params=pltpu.CompilerParams(collective_id=0, has_side_effects=True),
    )(clips, *shards)
    return got[0], got[1:]


def put(outs, places, value):
    for o, out_col, col, width in places:
        outs[o][:, out_col : out_col + width] = value[:, col : col + width]


class Sums:
    def __init__(self, plan, refs):
        self.plan, count = plan, len(plan.pieces)
        self.grads, refs = refs[: plan.inputs], refs[plan.inputs :]
        self.outs, refs = refs[: plan.results], refs[plan.results :]
        self.stages, refs = refs[:count], refs[count:]
        self.own, self.part, self.came, self.went, self.last, self.fin_s, self.fin_r = (
            refs[i * count : (i + 1) * count] for i in range(7)
        )
        (self.ring_s, self.ring_r, self.core_s, self.core_r, self.x_s, self.x_r, self.load_sem,
         self.part_sem) = refs[7 * count :]
        ring = plan.ring
        self.w, self.k, self.r, self.x, self.c, self.wide_at = place_of(ring)
        self.other_x = (self.w, 2 * (1 - self.x) + self.c)
        self.other_c = (self.w, 2 * self.x + 1 - self.c)
        self.next = ((self.wide_at((self.r + 1) % ring), self.k), (self.wide_at((self.r + ring - 1) % ring), self.k))
        self.peers = self.next + (self.other_x, self.other_c)
        self.final = ring - 1

    def source(self, t, s, column, core):
        ring = self.plan.ring
        g, col, width, height, way = self.plan.pieces[t]
        place = (self.r + 2 * ring - 1 - s) % ring if way == 0 else (self.r + 1 + s) % ring
        block = 4 * self.wide_at(place) + 2 * column + core
        return self.grads[g].at[pl.ds(pl.multiple_of(block * height, 8), height), pl.ds(col, width)]

    def half(self, t, column):
        height = self.plan.pieces[t][3]
        return pl.ds(column * height, height)

    def core_copy(self, t, s, column):
        return send(self.source(t, s, column, 1 - self.c), self.stages[t].at[s, self.half(t, column)],
                    self.core_s.at[t, s, column], self.core_r.at[t, s, column], self.other_c)

    def own_load(self, t, s, slot, column):
        return pltpu.make_async_copy(self.source(t, s, column, self.c), self.own[t].at[slot, self.half(t, column)],
                                     self.load_sem.at[t, slot, column])

    def part_load(self, t, s, slot):
        return pltpu.make_async_copy(self.stages[t].at[s], self.part[t].at[slot], self.part_sem.at[t, slot])

    def ring_copy(self, t, s):
        return send(self.went[t].at[s], self.came[t].at[s], self.ring_s.at[t, s], self.ring_r.at[t, s],
                    self.next[self.plan.pieces[t][4]])

    def x_copy(self, t):
        return send(self.fin_s[t], self.fin_r[t], self.x_s.at[t], self.x_r.at[t], self.other_x)

    def each(self):
        return range(len(self.plan.pieces))

    def fetch(self, t, s, slot):
        for column in range(2):
            self.core_copy(t, s, column).wait_recv()
        self.part_load(t, s, slot).start()
        for column in range(2):
            self.own_load(t, s, slot, column).start()

    def total(self, t, s, slot):
        for column in range(2):
            self.own_load(t, s, slot, column).wait()
        self.part_load(t, s, slot).wait()
        return self.own[t][slot] + self.part[t][slot]

    def begin(self):
        for s in range(self.plan.ring):
            for t in self.each():
                for column in range(2):
                    self.core_copy(t, s, column).start()

    def load_first(self):
        for t in self.each():
            self.fetch(t, 0, 0)

    def first_hop(self):
        for t in self.each():
            self.fetch(t, 1, 1)
            self.went[t][0] = self.total(t, 0, 0).astype(BF)
            self.ring_copy(t, 0).start()

    def hop(self, s):
        slot = s % 2
        for t in self.each():
            self.fetch(t, s + 1, 1 - slot)
            value = self.total(t, s, slot)
            self.ring_copy(t, s - 1).wait_recv()
            self.went[t][s] = (value + self.came[t][s - 1].astype(F32)).astype(BF)
            self.ring_copy(t, s).start()

    def end_ring(self, t):
        final, height = self.final, self.plan.pieces[t][3]
        value = self.total(t, final, final % 2)
        self.ring_copy(t, final - 1).wait_recv()
        value = value + self.came[t][final - 1].astype(F32)
        self.last[t][0] = value[:height]
        self.last[t][1] = value[height:]

    def leave(self):
        count = len(self.plan.pieces)
        for t in self.each():
            self.end_ring(t)
            self.outs[t][...] = self.last[t][self.x]
            self.outs[count + t][...] = self.last[t][1 - self.x].astype(BF)
        self.drain()

    def finish(self):
        for t in self.each():
            self.end_ring(t)
            self.fin_s[t][...] = self.last[t][1 - self.x].astype(BF)
            self.x_copy(t).start()
        for t in self.each():
            self.x_copy(t).wait_recv()
            value = self.last[t][self.x] + self.fin_r[t][...].astype(F32)
            put(self.outs, self.plan.places[t], value)
        for t in self.each():
            self.x_copy(t).wait_send()
        self.drain()

    def drain(self):
        for t in self.each():
            for s in range(self.final):
                self.ring_copy(t, s).wait_send()
            for s in range(self.plan.ring):
                for column in range(2):
                    self.core_copy(t, s, column).wait_send()


class Plan:
    def __init__(self, ring, inputs, pieces, shapes, places, leave):
        self.ring, self.inputs, self.pieces, self.shapes, self.places = ring, inputs, pieces, shapes, places
        count = len(pieces)
        sizes = [(height, width) for _, _, width, height, _ in pieces]
        sems, vmem = pltpu.SemaphoreType.DMA, pltpu.VMEM
        self.out_shapes = [shape_of(hw, F32) for hw in shapes]
        if leave:
            self.out_shapes = [shape_of(hw, F32) for hw in sizes] + [shape_of(hw, BF) for hw in sizes]
        self.results = len(self.out_shapes)
        self.out_shapes += [shape_of((ring, 2 * h, wd), F32) for h, wd in sizes]
        self.out_specs = [pl.BlockSpec(memory_space=pltpu.VMEM)] * self.results + [ANY] * count
        self.outputs = len(self.out_shapes)
        self.scratch = (
            [vmem((2, 2 * h, wd), F32) for h, wd in sizes]
            + [vmem((2, 2 * h, wd), F32) for h, wd in sizes]
            + [vmem((ring - 1, 2 * h, wd), BF) for h, wd in sizes]
            + [vmem((ring - 1, 2 * h, wd), BF) for h, wd in sizes]
            + [vmem((2, h, wd), F32) for h, wd in sizes]
            + [vmem((h, wd), BF) for h, wd in sizes]
            + [vmem((h, wd), BF) for h, wd in sizes]
            + [sems((count, ring))] * 2
            + [sems((count, ring, 2))] * 2
            + [sems((count,))] * 2
            + [sems((count, 2, 2)), sems((count, 2))]
        )
        self.scratches = len(self.scratch)

    def steps(self, refs):
        return Sums(self, refs)


def mlp_plan(ring, g_in, g_out, devices):
    a, b = g_in.shape[0] // devices, g_out.shape[0] // devices
    wa, wb = g_in.shape[1], g_out.shape[1]
    return Plan(ring, 2, [(0, 0, wa, a, 0), (1, 0, wb, b, 1)], [(a, wa), (b, wb)], [[(0, 0, 0, wa)], [(1, 0, 0, wb)]], True)


def attn_plan(ring, g, devices, leave):
    h, half, cut = g.shape[0] // devices, 2 * D, 3 * D
    return Plan(ring, 1, [(0, 0, half, h, 0), (0, half, half, h, 1)], [(h, cut), (h, D)],
                [[(0, 0, 0, half)], [(0, half, 0, cut - half), (1, 0, cut - half, D)]], leave)


def last_kernel(plan, left, shapes, *refs):
    places = [part for p in left for part in p.places]
    offsets = [sum(len(p.shapes) for p in left[:i]) for i, p in enumerate(left) for _ in p.pieces]
    count, made = len(places), sum(len(p.shapes) for p in left)
    ((_,), grads, keeps, fins, (frames,), left_outs, own_outs, fins_r,
     (fin_send, fin_recv, tile_s, tile_r, relay_s, relay_r), own) = split_refs(
        refs, 1, plan.inputs, count, count, 1, made, plan.outputs, count, 6)
    sums = plan.steps(grads + own_outs + own)
    final_tile = GRID - 1
    tile = tile_copies(sums.k, sums.other_c, sums.other_x, frames.at[packed(0, final_tile * FT, FT)], frames, final_tile,
                       tile_s, tile_r)

    def fin_copy(t):
        return send(fins[t], fins_r[t], fin_send.at[t], fin_recv.at[t], sums.other_x)

    def relay(i, first, frames_count):
        return send(frames.at[packed(2, first, frames_count)],
                    frames.at[packed(4 - slot_for(sums.k), first, frames_count)],
                    relay_s.at[i], relay_r.at[i], sums.other_c)

    early, late = relay(0, 0, final_tile * FT), relay(1, final_tile * FT, FT)
    greet(sums.peers)
    sums.begin()
    for copy in tile:
        copy.start()
    for t in range(count):
        fin_copy(t).start()
    early.start()
    sums.load_first()
    sums.first_hop()

    def body(s, carry):
        sums.hop(s)
        return carry

    lax.fori_loop(1, sums.final, body, 0)
    sums.finish()
    tile[1].wait_recv()
    late.start()
    for t in range(count):
        fin_copy(t).wait_recv()
        value = keeps[t][...] + fins_r[t][...].astype(F32)
        put(left_outs[offsets[t] :], places[t], value)
    for t in range(count):
        fin_copy(t).wait_send()
    tile[0].wait()
    tile[1].wait_send()
    early.wait()
    late.wait()


def scatter_last(frames, g, keeps, fins, plan, left):
    shapes = [shape for p in left for shape in p.shapes]
    sems = pltpu.SemaphoreType.DMA
    vmem = pl.BlockSpec(memory_space=pltpu.VMEM)
    return pl.pallas_call(
        functools.partial(last_kernel, plan, left, shapes),
        name="scatter_last",
        out_shape=[shape_of(frames.shape, frames.dtype)] + [shape_of(hw, F32) for hw in shapes] + plan.out_shapes,
        in_specs=[ANY] * 2 + [vmem] * len(keeps) + [ANY] * len(fins),
        out_specs=[ANY] + [vmem] * len(shapes) + plan.out_specs,
        scratch_shapes=[pltpu.VMEM(f.shape, f.dtype) for f in fins]
        + [sems((len(fins),))] * 2 + [sems((2, GRID))] * 2 + [sems((2,))] * 2 + plan.scratch,
        input_output_aliases={0: 0},
        compiler_params=pltpu.CompilerParams(
            collective_id=1, has_side_effects=True, vmem_limit_bytes=VMEM_LIMIT
        ),
    )(frames, g, *keeps, *fins)


def tuned(mesh):
    wide, n = mesh.shape["wide"], mesh.shape["narrow"]
    if n != 4 or wide != 2 * GRID or D % (8 * wide * n):
        return False
    for w in range(wide):
        for k in range(n):
            device = mesh.devices[w, k]
            here = (getattr(device, "coords", None), getattr(device, "core_on_chip", None))
            if here[0] is None or tuple(here[0]) != (k // 2, w % 2, w // 2) or here[1] != k % 2:
                return False
    return True


def exchange(x):
    return lax.all_to_all(x, ALL, split_axis=0, concat_axis=0, tiled=True)


def shift_clips(clips, back):
    n = lax.axis_size("narrow")
    parts = [clips[0]]
    for j in range(1, n):
        step = -j if back else j
        parts.append(lax.ppermute(clips[j], "narrow", [(s, (s + step) % n) for s in range(n)]))
    return jnp.stack(parts)


def local(fast, clips, t_emb, lengths, task, w_mod, b_mod, w_qkv_s, w_o_s, b_o_s, w_qkv_t, w_o_t, b_o_t,
          w_in, b_in, w_out, b_out, cotangent):
    n = lax.axis_size("narrow")
    wide = lax.axis_size("wide")
    devices = n * wide
    part = w_mod.shape[0]
    mod_cols = w_mod.shape[1] // devices
    rank = lax.axis_index("narrow")
    slots = jnp.arange(n, dtype=jnp.int32)
    from_clip = (rank - slots) % n
    recv_len = lengths.reshape(n, n)[from_clip, slots]
    recv_task = task.reshape(n, n, FR)[from_clip, slots]
    ends = jnp.cumsum(recv_len)
    starts = ends - recv_len
    ids = jnp.arange(LIVE, dtype=jnp.int32)
    source = jnp.sum((ends[None, :] <= ids[:, None]).astype(jnp.int32), axis=1)
    within = ids - starts[source]
    pack_rows = source * FR + within
    row_choice = source * 2 + recv_task[source, within]
    frame_ids = jnp.arange(FR, dtype=jnp.int32)
    live_back = frame_ids[None, :] < recv_len[:, None]
    unpack_rows = jnp.where(live_back, starts[:, None] + frame_ids[None, :], 0).reshape(-1)
    row_id = jnp.arange(64, dtype=jnp.int32)
    col_id = jnp.arange(LANES, dtype=jnp.int32) % 64
    seg = (
        (row_id[:, None] // LIVE == col_id[None, :] // LIVE)
        & (source[row_id % LIVE][:, None] == source[col_id % LIVE][None, :])
    ).astype(F32)

    def gather(w):
        return lax.all_gather(w, ALL, axis=0, tiled=True)

    weights = (w_in, w_out, w_qkv_t, w_o_t, w_qkv_s, w_o_s)
    if fast:
        frames, weights = gather_all(clips, weights, (0, 0, 1, 1, 1, 1), wide, n)
    else:
        frames = shift_clips(clips, False)
        weights = [gather(w) for w in weights]
    win, wout, wqkv_t, wo_t, wqkv_s, wo_s = weights
    frames = jnp.take(frames.reshape(n * FR, PATCHES, D), pack_rows, axis=0, mode="clip")

    wm = jnp.swapaxes(w_mod.reshape(part, devices, mod_cols), 0, 1).reshape(devices, -1)
    emb = jnp.broadcast_to(t_emb.reshape(1, -1), (devices, t_emb.size))
    small = jnp.concatenate([b_o_s, b_o_t, b_in, b_out])
    small_all = jnp.broadcast_to(small[None], (devices, small.size))
    got = exchange(jnp.concatenate([wm, emb, small_all], axis=1))
    wm_cols = got[:, : part * mod_cols].reshape(D, mod_cols)
    emb_all = got[:, part * mod_cols : part * mod_cols + t_emb.size].reshape(-1, D)
    small_got = got[:, part * mod_cols + t_emb.size :]
    b1 = b_o_s.size
    bias_s = small_got[:, :b1].reshape(1, -1).astype(F32)
    bias_t = small_got[:, b1 : 2 * b1].reshape(1, -1).astype(F32)
    bias_in = small_got[:, 2 * b1 : 2 * b1 + b_in.size].reshape(1, -1).astype(F32)
    bias_out = small_got[:, 2 * b1 + b_in.size :].reshape(1, -1).astype(F32)
    emb_f = emb_all.astype(F32)
    silu_low = (emb_f * jax.nn.sigmoid(emb_f)).astype(BF)
    mod_part = dot(silu_low, wm_cols) + b_mod.astype(F32)[None]
    mod_part = mod_part.reshape(wide, n, n, 2, mod_cols)
    mod_part = jnp.stack([jnp.roll(mod_part[:, :, c], c, axis=1) for c in range(n)], axis=2)
    mod_rows = exchange(mod_part.reshape(devices, -1)).reshape(devices, 2 * n, mod_cols)
    mod_rows = jnp.swapaxes(mod_rows, 0, 1).reshape(2 * n, 9, D)
    mod = jnp.swapaxes(mod_rows[row_choice], 0, 1)

    def carry(js, number):
        return clips_carrier(cotangent, js, n, number) if fast else None

    *half, x1, qkv1, o1, a1 = run_frame_forward(
        frames, mod, wqkv_s, wo_s, bias_s, carry((2,), 2))
    *odd, x2, qkv2, o2, a2 = run_time_forward(
        x1, mod, seg, wqkv_t, wo_t, bias_t, carry((1, 3), 3))
    if fast:
        cots = jnp.stack([cotangent[0], odd[0][0], half[0][0], odd[0][1]])
    else:
        cots = shift_clips(cotangent, False)
    dy = run_turn_frames(cots.reshape(n * FR, PATCHES, D), pack_rows)
    out, dx2, g_in, g_out, gb_in, gb_out, dmod3 = run_mlp(x2, dy, mod, win, bias_in, wout, bias_out, n if fast else 1)

    own_len = lengths.reshape(n, n)[rank]
    own_live = frame_ids[None, :] < own_len[:, None]

    def spread(frames):
        return jnp.take(frames, unpack_rows, axis=0, mode="clip").reshape(n, FR, PATCHES, D)

    def only_live(parts):
        return jnp.where(own_live[:, :, None, None], parts, jnp.zeros((), parts.dtype))

    def scatter(g):
        return lax.psum_scatter(g.astype(BF), ALL, scatter_dimension=0, tiled=True).astype(F32)

    if fast:
        ahead = lengths.reshape(n, n)[(rank + slots[:, None] - slots[None, :]) % n, slots[None, :]]
        own_start = jnp.sum(jnp.where(slots[None, :] < slots[:, None], ahead, 0), axis=1)
        own_rows = slots[:, None] * LIVE + own_start[:, None] + frame_ids[None, :]
        own_rows = jnp.where(own_live, own_rows, -1).reshape(-1)
        plan_mlp = mlp_plan(wide, g_in, g_out, devices)
        out, *got, dx1, g_t, gb_t, dmod2 = run_time_back(
            x1, dx2, mod, seg, qkv2, o2, a2, wqkv_t, wo_t, share_carrier(out, [g_in, g_out], plan_mlp, 4))
        keeps, fins = got[:2], got[2:4]
        plan_t = attn_plan(wide, g_t, devices, True)
        out, dx0, *got, g_s, gb_s, dmod1 = run_frame_back(
            frames, dx1, mod, qkv1, o1, a1, wqkv_s, wo_s, relay_carrier(out, [g_t], plan_t, 5))
        keeps, fins = keeps + got[:2], fins + got[2:4]
        dx0, s_in, s_out, s_qkv_t, s_o_t, s_qkv_s, s_o_s, _, _ = scatter_last(
            dx0, g_s, keeps, fins, attn_plan(wide, g_s, devices, False), (plan_mlp, plan_t))
        layer_out = run_unpack(out, own_rows).reshape(n, FR, PATCHES, D)
        grad_clips = run_unpack(dx0, own_rows).reshape(n, FR, PATCHES, D)
    else:
        dx1, g_t, gb_t, dmod2 = run_time_back(x1, dx2, mod, seg, qkv2, o2, a2, wqkv_t, wo_t)
        dx0, g_s, gb_s, dmod1 = run_frame_back(frames, dx1, mod, qkv1, o1, a1, wqkv_s, wo_s)
        layer_out = only_live(shift_clips(spread(out), True))
        grad_clips = only_live(shift_clips(spread(dx0), True))
        s_in, s_out, s_t, s_s = [scatter(g) for g in (g_in, g_out, g_t, g_s)]
        s_qkv_t, s_o_t, s_qkv_s, s_o_s = s_t[:, : 3 * D], s_t[:, 3 * D :], s_s[:, : 3 * D], s_s[:, 3 * D :]

    grad_frames = jnp.swapaxes(jnp.concatenate([dmod1, dmod2, dmod3], axis=0), 0, 1).reshape(LIVE, 9 * D)
    chooser = (row_choice[:, None] == jnp.arange(2 * n, dtype=jnp.int32)[None, :]).astype(F32)
    grad_rows = lax.dot_general(
        chooser, grad_frames, (((0,), (0,)), ((), ())), precision=lax.Precision.HIGHEST
    ).astype(BF)
    d_cols = exchange(jnp.swapaxes(grad_rows.reshape(2 * n, devices, mod_cols), 0, 1).reshape(devices, -1))
    d_cols = d_cols.reshape(wide, n, n, 2, mod_cols)
    d_cols = jnp.stack([jnp.roll(d_cols[:, :, c], -c, axis=1) for c in range(n)], axis=2)
    d_cols = d_cols.reshape(devices * 2 * n, mod_cols)
    grad_b_mod = jnp.sum(d_cols.astype(F32), axis=0)
    gwm_cols = dot_tn(silu_low, d_cols)
    g_emb = dot_nt(d_cols, wm_cols)
    gb_all = jnp.concatenate(
        [gb_s.reshape(devices, -1), gb_t.reshape(devices, -1), gb_in.reshape(devices, -1),
         gb_out.reshape(devices, -1)], axis=1)
    final = exchange(jnp.concatenate(
        [gwm_cols.reshape(devices, -1), g_emb.reshape(devices, -1), gb_all], axis=1))
    cut1 = part * mod_cols
    cut2 = cut1 + t_emb.size
    grad_w_mod = jnp.swapaxes(final[:, :cut1].reshape(devices, part, mod_cols), 0, 1).reshape(part, -1)
    emb_own = t_emb.astype(F32)
    sig = jax.nn.sigmoid(emb_own)
    grad_emb = jnp.sum(final[:, cut1:cut2], axis=0).reshape(t_emb.shape)
    grad_t_emb = (grad_emb * (sig * (1.0 + emb_own * (1.0 - sig)))).astype(BF)
    gb = jnp.sum(final[:, cut2:], axis=0)
    return (
        layer_out,
        grad_clips,
        grad_t_emb,
        grad_w_mod,
        grad_b_mod,
        s_qkv_s,
        s_o_s,
        gb[:b1],
        s_qkv_t,
        s_o_t,
        gb[b1 : 2 * b1],
        s_in,
        gb[2 * b1 : 2 * b1 + b_in.size],
        s_out,
        gb[2 * b1 + b_in.size :],
    )


def solution(mesh):
    full = P(ALL)
    placed = (full, full, P("wide"), P("wide")) + (full,) * 13
    return jax.shard_map(functools.partial(local, tuned(mesh)), mesh=mesh, in_specs=placed, out_specs=(full,) * 15, check_vma=False)
```

```python
import functools

import jax
import jax.numpy as jnp
from jax import lax
from jax.experimental import pallas as pl
from jax.experimental.pallas import tpu as pltpu
from jax.sharding import PartitionSpec as P

D = 768
HEADS = 12
HEAD = 64
FF = 3072
FR = 16
PATCHES = 64
LIVE = 2 * FR
EPS = 1e-06
BF = jnp.bfloat16
F32 = jnp.float32
ALL = ("wide", "narrow")
PAIRS = HEADS // 2
LANES = 2 * HEAD
BACK_PAIRS = 6
TILE = 512
FT = TILE // PATCHES
PT = TILE // LIVE
GRID = LIVE * PATCHES // TILE
GROUPS = TILE // 64
EARLY_TILES = GRID // 2
GELU_C = 0.7978845608028654
GELU_A = 0.044715
VMEM_LIMIT = 66 * 1000 * 1000
MESH = pl.DeviceIdType.MESH
ANY = pl.BlockSpec(memory_space=pl.ANY)


def dot(a, b):
    return lax.dot_general(a, b, (((1,), (0,)), ((), ())), preferred_element_type=F32)


def dot_nt(a, b):
    return lax.dot_general(a, b, (((1,), (1,)), ((), ())), preferred_element_type=F32)


def dot_tn(a, b):
    return lax.dot_general(a, b, (((0,), (0,)), ((), ())), preferred_element_type=F32)


def normalise(x):
    mean = jnp.mean(x, axis=-1, keepdims=True)
    centred = x - mean
    var = jnp.mean(centred * centred, axis=-1, keepdims=True)
    rstd = lax.rsqrt(var + EPS)
    return centred * rstd, rstd


def norm_back(dn, xhat, rstd):
    m1 = jnp.mean(dn, axis=-1, keepdims=True)
    m2 = jnp.mean(dn * xhat, axis=-1, keepdims=True)
    return rstd * (dn - m1 - xhat * m2)


def lane_masks():
    lane = lax.broadcasted_iota(jnp.int32, (64, LANES), 1)
    low_lanes = lane < HEAD
    low = jnp.where(low_lanes, 1.0, 0.0).astype(BF)
    high = jnp.where(low_lanes, 0.0, 1.0).astype(BF)
    return low_lanes, low, high


def split_heads(x, low, high):
    return jnp.concatenate([x * low, x * high], axis=0)


def softmax_keys(s, mask):
    if mask is not None:
        s = jnp.where(mask, s, -1e30)
    top = jnp.max(s, axis=0, keepdims=True)
    e = jnp.exp(s - top)
    return e * (1.0 / jnp.sum(e, axis=0, keepdims=True))


def pair_cols(part, hp):
    return slice(part * D + hp * LANES, part * D + (hp + 1) * LANES)


def attend(qkv_ref, o_ref, mask):
    low_lanes, low, high = lane_masks()
    scale = HEAD ** (-0.5)

    def body(g, carry):
        rows = pl.ds(pl.multiple_of(g * 64, 64), 64)
        pairs = range(PAIRS)
        s = [dot_nt(qkv_ref[rows, pair_cols(1, hp)], split_heads(qkv_ref[rows, pair_cols(0, hp)], low * scale, high * scale))
             for hp in pairs]
        p = [softmax_keys(t, mask).astype(BF) for t in s]
        r = [dot_tn(p[hp], qkv_ref[rows, pair_cols(2, hp)]) for hp in pairs]
        for hp in pairs:
            o_ref[rows, pair_cols(0, hp)] = jnp.where(low_lanes, r[hp][:64], r[hp][64:]).astype(BF)
        return carry

    lax.fori_loop(0, GROUPS, body, 0)


def attend_back(qkv_ref, do_ref, dqkv_ref, mask):
    low_lanes, low, high = lane_masks()
    scale = HEAD ** (-0.5)

    def body(g, carry):
        rows = pl.ds(pl.multiple_of(g * 64, 64), 64)
        for first in range(0, PAIRS, BACK_PAIRS):
            pairs = range(first, first + BACK_PAIRS)
            qb = [split_heads(qkv_ref[rows, pair_cols(0, hp)], low * scale, high * scale) for hp in pairs]
            dob = [split_heads(do_ref[rows, pair_cols(0, hp)], low, high) for hp in pairs]
            s = [dot_nt(qkv_ref[rows, pair_cols(1, hp)], q) for hp, q in zip(pairs, qb)]
            dp = [dot_nt(qkv_ref[rows, pair_cols(2, hp)], d) for hp, d in zip(pairs, dob)]
            p = [softmax_keys(t, mask) for t in s]
            delta = [jnp.sum(a * b, axis=0, keepdims=True) for a, b in zip(p, dp)]
            ds = [(a * (b - c)).astype(BF) for a, b, c in zip(p, dp, delta)]
            dv = [dot(a.astype(BF), d) for a, d in zip(p, dob)]
            dk = [dot(a, q) for a, q in zip(ds, qb)]
            r = [dot_tn(a, qkv_ref[rows, pair_cols(1, hp)]) for hp, a in zip(pairs, ds)]
            for i, hp in enumerate(pairs):
                dqkv_ref[rows, pair_cols(2, hp)] = dv[i].astype(BF)
                dqkv_ref[rows, pair_cols(1, hp)] = dk[i].astype(BF)
                dq = jnp.where(low_lanes, r[i][:64], r[i][64:]) * scale
                dqkv_ref[rows, pair_cols(0, hp)] = dq.astype(BF)
        return carry

    lax.fori_loop(0, GROUPS, body, 0)


def swap_major(value, scratch, out_ref, first, second):
    for b in range(D // 128):
        cols = slice(b * 128, (b + 1) * 128)
        for i in range(first):
            scratch[b, pl.ds(i, second, stride=first), :] = value[i * second : (i + 1) * second, cols]
        out_ref[:, :, cols] = scratch[b].reshape(second, first, 128).astype(out_ref.dtype)


def frames_of(refs):
    return jnp.concatenate([r[0] for r in refs], axis=0).astype(F32)


def per_frame(piece):
    return jnp.broadcast_to(piece[:, None, :], (FT, PATCHES, D)).reshape(TILE, D)


def per_patch(piece):
    return jnp.broadcast_to(piece[None], (PT, LIVE, D)).reshape(TILE, D)


def sum_patches(value):
    return jnp.sum(value.reshape(FT, PATCHES, D), axis=1)


def sum_groups(value):
    return jnp.sum(value.reshape(PT, LIVE, D), axis=0)


def attn_mask(seg_ref):
    return seg_ref[...] > 0.0


def no_tick(place):
    pass


def frame_forward(frames, mod, wqkv, wo, bo, x1t, qkv, o, a1, scratch, tick=no_tick):
    x = frames[...].reshape(TILE, D).astype(F32)
    xhat, _ = normalise(x)
    h = (xhat * (1.0 + per_frame(mod[1])) + per_frame(mod[0])).astype(BF)
    qkv[...] = dot(h, wqkv[...]).astype(BF)
    tick(0)
    attend(qkv, o, None)
    tick(1)
    branch = dot(o[...], wo[...]) + bo[...]
    a1[...] = branch
    x1 = x + per_frame(mod[2]) * branch
    swap_major(x1, scratch, x1t, FT, PATCHES)


def turn_frames(rows_ref, *refs):
    x_refs, (out, scratch) = refs[:FT], refs[FT:]
    swap_major(frames_of(x_refs), scratch, out, FT, PATCHES)


def time_forward(x1, mod, seg, wqkv, wo, bo, x2, qkv, o, a2, tick=no_tick):
    x = x1[...].reshape(TILE, D)
    xhat, _ = normalise(x)
    h = (xhat * (1.0 + per_patch(mod[1])) + per_patch(mod[0])).astype(BF)
    qkv[...] = dot(h, wqkv[...]).astype(BF)
    tick(0)
    attend(qkv, o, attn_mask(seg))
    tick(1)
    branch = dot(o[...], wo[...]) + bo[...]
    a2[...] = branch
    x2[...] = (x + per_patch(mod[2]) * branch).reshape(PT, LIVE, D)


def mlp_both(x2, dy, mod, win, bin_, wout, bout, out, dx2, gwin, gwout, gbin, gbout, dmod, scratch):
    first = pl.program_id(0) == 0

    @pl.when(first)
    def _():
        gwin[...] = jnp.zeros_like(gwin)
        gwout[...] = jnp.zeros_like(gwout)
        gbin[...] = jnp.zeros_like(gbin)
        gbout[...] = jnp.zeros_like(gbout)
        dmod[...] = jnp.zeros_like(dmod)

    x = x2[...].reshape(TILE, D)
    xhat, rstd = normalise(x)
    h = (xhat * (1.0 + per_patch(mod[1])) + per_patch(mod[0])).astype(BF)
    gate = per_patch(mod[2])
    grad = dy[...].reshape(TILE, D)
    da = (grad * gate).astype(BF)
    gbout[...] += jnp.sum(da.astype(F32), axis=0, keepdims=True)
    branch = jnp.zeros((TILE, D), F32) + bout[...]
    dh = jnp.zeros((TILE, D), F32)
    for j in range(FF // D):
        cols = slice(j * D, (j + 1) * D)
        u = dot(h, win[:, cols]) + bin_[:, cols]
        u2 = u * u
        t = jnp.tanh(GELU_C * u * (1.0 + GELU_A * u2))
        half = 0.5 * (1.0 + t)
        g = (u * half).astype(BF)
        slope = half + (0.5 * GELU_C) * u * (1.0 - t * t) * (1.0 + 3.0 * GELU_A * u2)
        branch = branch + dot(g, wout[cols, :])
        du = (dot_nt(da, wout[cols, :]) * slope).astype(BF)
        gwout[cols, :] += dot_tn(g, da)
        gbin[:, cols] += jnp.sum(du.astype(F32), axis=0, keepdims=True)
        gwin[:, cols] += dot_tn(h, du)
        dh = dh + dot_nt(du, win[:, cols])
    swap_major(x + gate * branch, scratch, out, PT, LIVE)
    dmod[2] += sum_groups(grad * branch)
    dmod[0] += sum_groups(dh)
    dmod[1] += sum_groups(dh * xhat)
    back = norm_back(dh * (1.0 + per_patch(mod[1])), xhat, rstd)
    dx2[...] = (grad + back).reshape(PT, LIVE, D)


def attn_back_tile(x, grad, shift, scale, gate, branch, qkv, o, wqkv, wo, gw, gbo, do, dqkv, mask, tick):
    first = pl.program_id(0) == 0

    @pl.when(first)
    def _():
        gw[...] = jnp.zeros_like(gw)
        gbo[...] = jnp.zeros_like(gbo)

    da = (grad * gate).astype(BF)
    do[...] = dot_nt(da, wo[...]).astype(BF)
    gw[:, 3 * D :] += dot_tn(o[...], da)
    gbo[...] += jnp.sum(da.astype(F32), axis=0, keepdims=True)
    tick(0)
    attend_back(qkv, do, dqkv, mask)
    tick(1)
    xhat, rstd = normalise(x)
    h = (xhat * (1.0 + scale) + shift).astype(BF)
    dh = jnp.zeros((TILE, D), F32)
    for j in range(3):
        cols = slice(j * D, (j + 1) * D)
        part = dqkv[:, cols]
        gw[:, cols] += dot_tn(h, part)
        dh = dh + dot_nt(part, wqkv[:, cols])
    dx = grad + norm_back(dh * (1.0 + scale), xhat, rstd)
    return dx, dh, dh * xhat, grad * branch


def time_back(x1, dx2, mod, seg, qkv, o, a2, wqkv, wo, dx1, gw, gbo, dmod, do, dqkv, scratch, tick=no_tick):
    @pl.when(pl.program_id(0) == 0)
    def _():
        dmod[...] = jnp.zeros_like(dmod)

    dx, d_shift, d_scale, d_gate = attn_back_tile(
        x1[...].reshape(TILE, D), dx2[...].reshape(TILE, D), per_patch(mod[0]), per_patch(mod[1]),
        per_patch(mod[2]), a2[...], qkv, o, wqkv, wo, gw, gbo, do, dqkv, attn_mask(seg), tick)
    dmod[0] += sum_groups(d_shift)
    dmod[1] += sum_groups(d_scale)
    dmod[2] += sum_groups(d_gate)
    swap_major(dx, scratch, dx1, PT, LIVE)


def frame_back(frames, dx1, mod, qkv, o, a1, wqkv, wo, dx0, gw, gbo, dmod, do, dqkv, tick=no_tick):
    dx, d_shift, d_scale, d_gate = attn_back_tile(
        frames[...].reshape(TILE, D).astype(F32), dx1[...].reshape(TILE, D), per_frame(mod[0]), per_frame(mod[1]),
        per_frame(mod[2]), a1[...], qkv, o, wqkv, wo, gw, gbo, do, dqkv, None, tick)
    dmod[0] = sum_patches(d_shift)
    dmod[1] = sum_patches(d_scale)
    dmod[2] = sum_patches(d_gate)
    dx0[...] = dx.reshape(FT, PATCHES, D).astype(BF)


def frame_specs():
    return [
        pl.BlockSpec((1, PATCHES, D), functools.partial(lambda j, i, rows: (rows[FT * i + j], 0, 0), j))
        for j in range(FT)
    ]


def whole(shape):
    return pl.BlockSpec(shape, lambda i, *_: (0,) * len(shape), pipeline_mode=pl.Buffered(1))


def tiles(shape, dim):
    return pl.BlockSpec(shape, lambda i, *_: tuple(i if a == dim else 0 for a in range(len(shape))))


def piece_spec(number, frames, by_tile):
    return pl.BlockSpec((3, frames, D), lambda i, *_: (number, i if by_tile else 0, 0))


ROWS = tiles((TILE, D), 0)
ROWS3 = tiles((TILE, 3 * D), 0)
TURNED = tiles((PT, LIVE, D), 0)


TURN = pltpu.VMEM((D // 128, TILE, 128), F32)


def shape_of(shape, dtype):
    return jax.ShapeDtypeStruct(shape, dtype)


class Carrier:
    def __init__(self, wrap, number, ins, outs, out_specs, scratch, aliases=None):
        self.wrap, self.number, self.ins, self.outs = wrap, number, ins, outs
        self.out_specs, self.scratch, self.aliases = out_specs, scratch, aliases or {}


def call(kernel, name, ins, in_specs, outs, out_specs, scratch, flops, prefetch=None, carrier=None):
    moved = sum(a.size * a.dtype.itemsize for a in tuple(ins) + tuple(outs))
    params, aliases = {}, {}
    if carrier is not None:
        kernel = functools.partial(carrier.wrap, kernel, len(ins), len(outs), len(scratch))
        ins, in_specs = carrier.ins + ins, [ANY] * len(carrier.ins) + in_specs
        outs, out_specs = carrier.outs + outs, carrier.out_specs + out_specs
        scratch = scratch + carrier.scratch
        params, aliases = dict(collective_id=carrier.number, has_side_effects=True), carrier.aliases
    grid_spec = pltpu.PrefetchScalarGridSpec(
        num_scalar_prefetch=0 if prefetch is None else 1,
        grid=(GRID,),
        in_specs=in_specs,
        out_specs=out_specs,
        scratch_shapes=scratch,
    )
    fn = pl.pallas_call(
        kernel,
        grid_spec=grid_spec,
        out_shape=outs,
        name=name,
        input_output_aliases=aliases,
        cost_estimate=pl.CostEstimate(flops=flops, bytes_accessed=moved, transcendentals=0),
        compiler_params=pltpu.CompilerParams(
            dimension_semantics=("arbitrary",), vmem_limit_bytes=VMEM_LIMIT, **params
        ),
    )
    return fn(*ins) if prefetch is None else fn(prefetch, *ins)


def split_refs(refs, *counts):
    parts = []
    for count in counts:
        parts.append(refs[:count])
        refs = refs[count:]
    return parts + [refs]


def forward_carrier(clips, js, shard, ring, n, number):
    held = Gather.scratch([shard], ring)

    def wrap(kernel, n_in, n_out, n_scratch, *refs):
        (src, part), ins, (dst, full), outs, scratch, (send_sem, recv_sem), own = split_refs(
            refs, 2, n_in, 2, n_out, n_scratch, 2)
        step = pl.program_id(0)
        gather = Gather(ring, (shard.shape[0],), (part, full) + own)
        targets = [(gather.w, (gather.k + j) % n) for j in js]
        copies = [send(src.at[j], dst.at[i], send_sem.at[i], recv_sem.at[i], targets[i]) for i, j in enumerate(js)]

        @pl.when(step == 0)
        def _():
            greet(tuple(targets) + gather.peers)
            gather.begin()
            for copy in copies:
                copy.start()

        def tick(place):
            if place == 0:
                @pl.when(step == 0)
                def _():
                    gather.second()

                @pl.when(step > 0)
                def _():
                    gather.hop(2 * step)
            else:
                gather.hop(2 * step + 1)

        kernel(*ins, *outs, *scratch, tick=tick)

        @pl.when(step == GRID - 1)
        def _():
            gather.finish()
            for copy in copies:
                copy.wait()

    sems = pltpu.SemaphoreType.DMA((len(js),))
    return Carrier(wrap, number, [clips, shard],
                   [shape_of((len(js),) + clips.shape[1:], clips.dtype)] + Gather.shapes([shard], ring * n),
                   [ANY, ANY], [sems, sems] + held)


def packed(slot, first=0, count=LIVE):
    return pl.ds(pl.multiple_of(slot * LIVE + first, 8), count)


def slot_for(k):
    return 3 - 2 * (k % 2)


def ticks(sums, step):
    def tick(place):
        @pl.when(step == 0)
        def _():
            if place == 0:
                sums.load_first()
            else:
                sums.first_hop()

        @pl.when(step > 0)
        def _():
            sums.hop(2 * step - 1 + place)

    return tick


def share_carrier(frames, grads, plan, number):
    n_grads = len(grads)

    def wrap(kernel, n_in, n_out, n_scratch, *refs):
        (_,), grad_refs, ins, (dst,), left, outs, scratch, (send_sem, recv_sem), own = split_refs(
            refs, 1, n_grads, n_in, 1, plan.outputs, n_out, n_scratch, 2)
        step = pl.program_id(0)
        sums = plan.steps(grad_refs + left + own)
        targets = ((slot_for(sums.k), sums.other_c), (2, sums.other_x))
        copies = [send(dst.at[packed(0)], dst.at[packed(slot)], send_sem.at[i], recv_sem.at[i], peer)
                  for i, (slot, peer) in enumerate(targets)]

        @pl.when(step == 0)
        def _():
            greet(sums.peers)
            sums.begin()
            for copy in copies:
                copy.start()

        kernel(*ins, *outs, *scratch, tick=ticks(sums, step))

        @pl.when(step == GRID - 1)
        def _():
            sums.leave()
            for copy in copies:
                copy.wait()

    sems = pltpu.SemaphoreType.DMA((2,))
    return Carrier(wrap, number, [frames] + grads, [shape_of(frames.shape, frames.dtype)] + plan.out_shapes,
                   [ANY] + plan.out_specs, [sems, sems] + plan.scratch, {0: 0})


def tile_copies(k, other_c, other_x, src, dst, i, send_sem, recv_sem):
    return [send(src, dst.at[packed(slot, i * FT, FT)], send_sem.at[a, i], recv_sem.at[a, i], peer)
            for a, (slot, peer) in enumerate(((slot_for(k), other_c), (2, other_x)))]


def relay_carrier(frames, grads, plan, number):
    n_grads = len(grads)

    def wrap(kernel, n_in, n_out, n_scratch, *refs):
        (_,), grad_refs, ins, (dst, made), left, outs, scratch, (send_sem, recv_sem, tile_s, tile_r, keep, buf), own = (
            split_refs(refs, 1, n_grads, n_in, 2, plan.outputs, n_out, n_scratch, 6))
        step = pl.program_id(0)
        sums = plan.steps(grad_refs + left + own)
        relay = send(dst.at[packed(2)], dst.at[packed(4 - slot_for(sums.k))],
                     send_sem.at[0], recv_sem.at[0], sums.other_c)

        def tile(i):
            return tile_copies(sums.k, sums.other_c, sums.other_x, buf.at[i], made, i, tile_s, tile_r)

        def store(i):
            return pltpu.make_async_copy(buf.at[i], made.at[packed(0, i * FT, FT)], keep.at[i])

        @pl.when(step == 0)
        def _():
            greet(sums.peers)
            sums.begin()
            relay.start()

        kernel(*ins, buf.at[step], *outs, *scratch, tick=ticks(sums, step))
        store(step).start()

        @pl.when(step < EARLY_TILES)
        def _():
            for copy in tile(step):
                copy.start()

        @pl.when(step == GRID - 1)
        def _():
            sums.leave()
            relay.wait()
            for i in range(GRID):
                store(i).wait()
            for i in range(EARLY_TILES):
                for copy in tile(i):
                    copy.wait()

    sems = pltpu.SemaphoreType.DMA
    shape = shape_of(frames.shape, frames.dtype)
    return Carrier(wrap, number, [frames] + grads, [shape, shape] + plan.out_shapes, [ANY, ANY] + plan.out_specs,
                   [sems((1,)), sems((1,)), sems((2, EARLY_TILES)), sems((2, EARLY_TILES)), sems((GRID,)),
                    pltpu.VMEM((GRID, FT, PATCHES, D), BF)] + plan.scratch, {0: 0})


TOKENS = LIVE * PATCHES


def run_frame_forward(frames, mod, wqkv, wo, bo, carrier=None):
    return call(
        frame_forward, "frame_forward",
        [frames, mod, wqkv, wo, bo],
        [tiles((FT, PATCHES, D), 0), piece_spec(0, FT, True), whole((D, 3 * D)), whole((D, D)), whole((1, D))],
        [shape_of((PATCHES, LIVE, D), F32), shape_of((TOKENS, 3 * D), BF), shape_of((TOKENS, D), BF),
         shape_of((TOKENS, D), F32)],
        [tiles((PATCHES, FT, D), 1), ROWS3, ROWS, ROWS],
        [TURN],
        2 * TOKENS * D * 4 * D, carrier=carrier)


def run_turn_frames(frames, rows):
    return call(
        turn_frames, "turn_frames", [frames] * FT, frame_specs(),
        [shape_of((PATCHES, LIVE, D), F32)], [tiles((PATCHES, FT, D), 1)],
        [TURN], 1000, rows)[0]


def unpack_frames(rows_ref, *refs):
    x_refs, (out,) = refs[:FT], refs[FT:]
    first = pl.program_id(0) * FT
    for j in range(FT):
        x = x_refs[j][0]
        out[j] = jnp.where(rows_ref[first + j] >= 0, x, jnp.zeros_like(x))


def run_unpack(frames, rows):
    specs = [
        pl.BlockSpec((1, PATCHES, D), functools.partial(lambda j, i, r: (jnp.maximum(r[FT * i + j], 0), 0, 0), j))
        for j in range(FT)
    ]
    return pl.pallas_call(
        unpack_frames,
        grid_spec=pltpu.PrefetchScalarGridSpec(
            num_scalar_prefetch=1, grid=(rows.shape[0] // FT,), in_specs=specs, out_specs=tiles((FT, PATCHES, D), 0)),
        out_shape=shape_of((rows.shape[0], PATCHES, D), frames.dtype),
        name="unpack_frames",
        cost_estimate=pl.CostEstimate(flops=1000, bytes_accessed=4 * rows.shape[0] * PATCHES * D, transcendentals=0),
        compiler_params=pltpu.CompilerParams(dimension_semantics=("arbitrary",)),
    )(rows, *[frames] * FT)


def run_time_forward(x1, mod, seg, wqkv, wo, bo, carrier=None):
    return call(
        time_forward, "time_forward",
        [x1, mod, seg, wqkv, wo, bo],
        [TURNED, piece_spec(1, LIVE, False), whole((64, LANES)), whole((D, 3 * D)), whole((D, D)),
         whole((1, D))],
        [shape_of((PATCHES, LIVE, D), F32), shape_of((TOKENS, 3 * D), BF), shape_of((TOKENS, D), BF),
         shape_of((TOKENS, D), F32)],
        [TURNED, ROWS3, ROWS, ROWS],
        [], 2 * TOKENS * D * 4 * D, carrier=carrier)


def run_mlp(x2, dy, mod, win, bin_, wout, bout, slots=1):
    return call(
        mlp_both, "mlp_both",
        [x2, dy, mod, win, bin_, wout, bout],
        [TURNED, TURNED, piece_spec(2, LIVE, False), whole((D, FF)), whole((1, FF)), whole((FF, D)),
         whole((1, D))],
        [shape_of((slots * LIVE, PATCHES, D), BF), shape_of((PATCHES, LIVE, D), F32), shape_of((D, FF), F32),
         shape_of((FF, D), F32), shape_of((1, FF), F32), shape_of((1, D), F32), shape_of((3, LIVE, D), F32)],
        [tiles((LIVE, PT, D), 1), TURNED, whole((D, FF)), whole((FF, D)), whole((1, FF)), whole((1, D)),
         whole((3, LIVE, D))],
        [TURN],
        6 * 2 * TOKENS * D * FF)


def run_time_back(x1, dx2, mod, seg, qkv, o, a2, wqkv, wo, carrier=None):
    return call(
        time_back, "time_back",
        [x1, dx2, mod, seg, qkv, o, a2, wqkv, wo],
        [TURNED, TURNED, piece_spec(1, LIVE, False), whole((64, LANES)), ROWS3, ROWS, ROWS,
         whole((D, 3 * D)), whole((D, D))],
        [shape_of((LIVE, PATCHES, D), F32), shape_of((D, 4 * D), F32), shape_of((1, D), F32), shape_of((3, LIVE, D), F32)],
        [tiles((LIVE, PT, D), 1), whole((D, 4 * D)), whole((1, D)), whole((3, LIVE, D))],
        [pltpu.VMEM((TILE, D), BF), pltpu.VMEM((TILE, 3 * D), BF), TURN],
        2 * 2 * TOKENS * D * 4 * D, carrier=carrier)


def run_frame_back(frames, dx1, mod, qkv, o, a1, wqkv, wo, carrier=None):
    frames_out = [] if carrier else [shape_of((LIVE, PATCHES, D), BF)]
    frames_spec = [] if carrier else [tiles((FT, PATCHES, D), 0)]
    return call(
        frame_back, "frame_back",
        [frames, dx1, mod, qkv, o, a1, wqkv, wo],
        [tiles((FT, PATCHES, D), 0), tiles((FT, PATCHES, D), 0), piece_spec(0, FT, True), ROWS3, ROWS, ROWS,
                         whole((D, 3 * D)), whole((D, D))],
        frames_out + [shape_of((D, 4 * D), F32), shape_of((1, D), F32), shape_of((3, LIVE, D), F32)],
        frames_spec + [whole((D, 4 * D)), whole((1, D)), piece_spec(0, FT, True)],
        [pltpu.VMEM((TILE, D), BF), pltpu.VMEM((TILE, 3 * D), BF)],
        2 * 2 * TOKENS * D * 4 * D, carrier=carrier)


def place_of(wide):
    ring = wide
    turn = ring // 2
    w = lax.axis_index("wide")
    k = lax.axis_index("narrow")
    z, y = w // 2, w % 2
    r = z + y * (ring - 1 - 2 * z)

    def wide_at(position):
        side = position // turn
        return 2 * ((1 - side) * position + side * (ring - 1 - position)) + side

    return w, k, r, k // 2, k % 2, wide_at


def greet(peers):
    barrier = pltpu.get_barrier_semaphore()
    for peer in peers:
        pl.semaphore_signal(barrier, inc=1, device_id=peer, device_id_type=MESH)
    pl.semaphore_wait(barrier, len(peers))


def send(src, dst, send_sem, recv_sem, peer):
    return pltpu.make_async_remote_copy(
        src_ref=src, dst_ref=dst, send_sem=send_sem, recv_sem=recv_sem, device_id=peer, device_id_type=MESH
    )


class Gather:
    def __init__(self, ring, heights, refs):
        count = len(heights)
        self.ring, self.heights, self.count = ring, heights, count
        self.shards, self.full, self.bufs, sems = split_refs(refs, count, count, count)
        (self.ring_s, self.ring_r, self.core_s, self.core_r, self.x_s, self.x_r, self.load_sem, self.keep_sem) = sems
        self.w, self.k, self.r, self.x, self.c, self.wide_at = place_of(ring)
        self.other_x = (self.w, 2 * (1 - self.x) + self.c)
        self.other_c = (self.w, 2 * self.x + 1 - self.c)
        self.next = ((self.wide_at((self.r + 1) % ring), self.k), (self.wide_at((self.r + ring - 1) % ring), self.k))
        self.peers = self.next + (self.other_x, self.other_c)

    @staticmethod
    def scratch(shards, ring):
        count, sems = len(shards), pltpu.SemaphoreType.DMA
        return ([pltpu.VMEM(a.shape, a.dtype) for a in shards] + [sems((count, 2, ring))] * 4 + [sems((count,))] * 4)

    @staticmethod
    def shapes(shards, devices):
        return [shape_of((a.shape[0] * devices, a.shape[1]), a.dtype) for a in shards]

    def way(self, t, b):
        return (t + b) % 2

    def block(self, t, b, s):
        r, ring = self.r, self.ring
        place = (r + ring - s) % ring if self.way(t, b) == 0 else (r + s) % ring
        column = self.x if b == 0 else 1 - self.x
        block = 4 * self.wide_at(place) + 2 * column + self.c
        return self.full[t].at[pl.ds(pl.multiple_of(block * self.heights[t], 8), self.heights[t])]

    def ring_copy(self, t, b, s, src=None):
        dst = self.block(t, b, s)
        return send(dst if src is None else src, dst, self.ring_s.at[t, b, s], self.ring_r.at[t, b, s],
                    self.next[self.way(t, b)])

    def core_copy(self, t, b, s, src=None):
        dst = self.block(t, b, s)
        return send(dst if src is None else src, dst, self.core_s.at[t, b, s], self.core_r.at[t, b, s], self.other_c)

    def x_copy(self, t):
        return send(self.shards[t], self.block(t, 0, 0), self.x_s.at[t], self.x_r.at[t], self.other_x)

    def load(self, t):
        return pltpu.make_async_copy(self.shards[t], self.bufs[t], self.load_sem.at[t])

    def keep(self, t):
        return pltpu.make_async_copy(self.bufs[t], self.block(t, 0, 0), self.keep_sem.at[t])

    def begin(self):
        for t in range(self.count):
            self.x_copy(t).start()
            self.ring_copy(t, 0, 0, self.shards[t]).start()
        for t in range(self.count):
            self.core_copy(t, 0, 0, self.shards[t]).start()
            self.load(t).start()

    def second(self):
        for t in range(self.count):
            self.load(t).wait()
            self.keep(t).start()
        for t in range(self.count):
            self.x_copy(t).wait_recv()
            self.ring_copy(t, 1, 0).start()
            self.core_copy(t, 1, 0).start()

    def hop(self, s):
        for b in range(2):
            for t in range(self.count):
                self.ring_copy(t, b, s - 1).wait_recv()

                @pl.when(s < self.ring - 1)
                def _():
                    self.ring_copy(t, b, s).start()

                self.core_copy(t, b, s).start()

    def finish(self):
        for t in range(self.count):
            self.keep(t).wait()
            self.x_copy(t).wait_send()
            for b in range(2):
                for s in range(self.ring):
                    if s < self.ring - 1:
                        self.ring_copy(t, b, s).wait_send()
                    self.core_copy(t, b, s).wait()


def gather_kernel(ring, heights, *refs):
    gather = Gather(ring, heights, refs)
    greet(gather.peers)
    gather.begin()
    gather.second()

    def body(s, carry):
        gather.hop(s)
        return carry

    lax.fori_loop(1, ring, body, 0)
    gather.finish()


def gather_first(shards, ring, n):
    heights = tuple(a.shape[0] for a in shards)
    return pl.pallas_call(
        functools.partial(gather_kernel, ring, heights),
        name="gather_first",
        out_shape=Gather.shapes(shards, ring * n),
        in_specs=[ANY] * len(shards),
        out_specs=[ANY] * len(shards),
        scratch_shapes=Gather.scratch(shards, ring),
        compiler_params=pltpu.CompilerParams(collective_id=0, has_side_effects=True),
    )(*shards)


def put(outs, places, value):
    for o, out_col, col, width in places:
        outs[o][:, out_col : out_col + width] = value[:, col : col + width]


class Sums:
    def __init__(self, plan, refs):
        self.plan, count = plan, len(plan.pieces)
        self.grads, refs = refs[: plan.inputs], refs[plan.inputs :]
        self.outs, refs = refs[: plan.results], refs[plan.results :]
        self.stages, refs = refs[:count], refs[count:]
        self.own, self.part, self.came, self.went, self.last, self.fin_s, self.fin_r = (
            refs[i * count : (i + 1) * count] for i in range(7)
        )
        (self.ring_s, self.ring_r, self.core_s, self.core_r, self.x_s, self.x_r, self.load_sem,
         self.part_sem) = refs[7 * count :]
        ring = plan.ring
        self.w, self.k, self.r, self.x, self.c, self.wide_at = place_of(ring)
        self.other_x = (self.w, 2 * (1 - self.x) + self.c)
        self.other_c = (self.w, 2 * self.x + 1 - self.c)
        self.next = ((self.wide_at((self.r + 1) % ring), self.k), (self.wide_at((self.r + ring - 1) % ring), self.k))
        self.peers = self.next + (self.other_x, self.other_c)
        self.final = ring - 1

    def source(self, t, s, column, core):
        ring = self.plan.ring
        g, col, width, height, way = self.plan.pieces[t]
        place = (self.r + 2 * ring - 1 - s) % ring if way == 0 else (self.r + 1 + s) % ring
        block = 4 * self.wide_at(place) + 2 * column + core
        return self.grads[g].at[pl.ds(pl.multiple_of(block * height, 8), height), pl.ds(col, width)]

    def half(self, t, column):
        height = self.plan.pieces[t][3]
        return pl.ds(column * height, height)

    def core_copy(self, t, s, column):
        return send(self.source(t, s, column, 1 - self.c), self.stages[t].at[s, self.half(t, column)],
                    self.core_s.at[t, s, column], self.core_r.at[t, s, column], self.other_c)

    def own_load(self, t, s, slot, column):
        return pltpu.make_async_copy(self.source(t, s, column, self.c), self.own[t].at[slot, self.half(t, column)],
                                     self.load_sem.at[t, slot, column])

    def part_load(self, t, s, slot):
        return pltpu.make_async_copy(self.stages[t].at[s], self.part[t].at[slot], self.part_sem.at[t, slot])

    def ring_copy(self, t, s):
        return send(self.went[t].at[s], self.came[t].at[s], self.ring_s.at[t, s], self.ring_r.at[t, s],
                    self.next[self.plan.pieces[t][4]])

    def x_copy(self, t):
        return send(self.fin_s[t], self.fin_r[t], self.x_s.at[t], self.x_r.at[t], self.other_x)

    def each(self):
        return range(len(self.plan.pieces))

    def fetch(self, t, s, slot):
        for column in range(2):
            self.core_copy(t, s, column).wait_recv()
        self.part_load(t, s, slot).start()
        for column in range(2):
            self.own_load(t, s, slot, column).start()

    def total(self, t, s, slot):
        for column in range(2):
            self.own_load(t, s, slot, column).wait()
        self.part_load(t, s, slot).wait()
        return self.own[t][slot] + self.part[t][slot]

    def begin(self):
        for s in range(self.plan.ring):
            for t in self.each():
                for column in range(2):
                    self.core_copy(t, s, column).start()

    def load_first(self):
        for t in self.each():
            self.fetch(t, 0, 0)

    def first_hop(self):
        for t in self.each():
            self.fetch(t, 1, 1)
            self.went[t][0] = self.total(t, 0, 0).astype(BF)
            self.ring_copy(t, 0).start()

    def hop(self, s):
        slot = s % 2
        for t in self.each():
            self.fetch(t, s + 1, 1 - slot)
            value = self.total(t, s, slot)
            self.ring_copy(t, s - 1).wait_recv()
            self.went[t][s] = (value + self.came[t][s - 1].astype(F32)).astype(BF)
            self.ring_copy(t, s).start()

    def end_ring(self, t):
        final, height = self.final, self.plan.pieces[t][3]
        value = self.total(t, final, final % 2)
        self.ring_copy(t, final - 1).wait_recv()
        value = value + self.came[t][final - 1].astype(F32)
        self.last[t][0] = value[:height]
        self.last[t][1] = value[height:]

    def leave(self):
        count = len(self.plan.pieces)
        for t in self.each():
            self.end_ring(t)
            self.outs[t][...] = self.last[t][self.x]
            self.outs[count + t][...] = self.last[t][1 - self.x].astype(BF)
        self.drain()

    def finish(self):
        for t in self.each():
            self.end_ring(t)
            self.fin_s[t][...] = self.last[t][1 - self.x].astype(BF)
            self.x_copy(t).start()
        for t in self.each():
            self.x_copy(t).wait_recv()
            value = self.last[t][self.x] + self.fin_r[t][...].astype(F32)
            put(self.outs, self.plan.places[t], value)
        for t in self.each():
            self.x_copy(t).wait_send()
        self.drain()

    def drain(self):
        for t in self.each():
            for s in range(self.final):
                self.ring_copy(t, s).wait_send()
            for s in range(self.plan.ring):
                for column in range(2):
                    self.core_copy(t, s, column).wait_send()


class Plan:
    def __init__(self, ring, inputs, pieces, shapes, places, leave):
        self.ring, self.inputs, self.pieces, self.shapes, self.places = ring, inputs, pieces, shapes, places
        count = len(pieces)
        sizes = [(height, width) for _, _, width, height, _ in pieces]
        sems, vmem = pltpu.SemaphoreType.DMA, pltpu.VMEM
        self.out_shapes = [shape_of(hw, F32) for hw in shapes]
        if leave:
            self.out_shapes = [shape_of(hw, F32) for hw in sizes] + [shape_of(hw, BF) for hw in sizes]
        self.results = len(self.out_shapes)
        self.out_shapes += [shape_of((ring, 2 * h, wd), F32) for h, wd in sizes]
        self.out_specs = [pl.BlockSpec(memory_space=pltpu.VMEM)] * self.results + [ANY] * count
        self.outputs = len(self.out_shapes)
        self.scratch = (
            [vmem((2, 2 * h, wd), F32) for h, wd in sizes]
            + [vmem((2, 2 * h, wd), F32) for h, wd in sizes]
            + [vmem((ring - 1, 2 * h, wd), BF) for h, wd in sizes]
            + [vmem((ring - 1, 2 * h, wd), BF) for h, wd in sizes]
            + [vmem((2, h, wd), F32) for h, wd in sizes]
            + [vmem((h, wd), BF) for h, wd in sizes]
            + [vmem((h, wd), BF) for h, wd in sizes]
            + [sems((count, ring))] * 2
            + [sems((count, ring, 2))] * 2
            + [sems((count,))] * 2
            + [sems((count, 2, 2)), sems((count, 2))]
        )
        self.scratches = len(self.scratch)

    def left(self, results):
        count = len(self.pieces)
        return results[:count], results[count : 2 * count]

    def steps(self, refs):
        return Sums(self, refs)


def mlp_plan(ring, g_in, g_out, devices):
    a, b = g_in.shape[0] // devices, g_out.shape[0] // devices
    wa, wb = g_in.shape[1] // 2, g_out.shape[1] // 2
    return Plan(ring, 2, [(0, 0, wa, a, 0), (1, 0, wb, b, 1), (0, wa, wa, a, 0), (1, wb, wb, b, 1)],
                [(a, 2 * wa), (b, 2 * wb)], [[(0, 0, 0, wa)], [(1, 0, 0, wb)], [(0, wa, 0, wa)], [(1, wb, 0, wb)]], True)


def attn_plan(ring, g, devices, leave):
    h = g.shape[0] // devices
    return Plan(ring, 1, [(0, i * D, D, h, i % 2) for i in range(4)], [(h, 3 * D), (h, D)],
                [[(0, i * D, 0, D)] for i in range(3)] + [[(1, 0, 0, D)]], leave)


def last_kernel(plan, left, shapes, *refs):
    places = [part for p in left for part in p.places]
    offsets = [sum(len(p.shapes) for p in left[:i]) for i, p in enumerate(left) for _ in p.pieces]
    count, made = len(places), sum(len(p.shapes) for p in left)
    ((_,), grads, keeps, fins, (frames,), left_outs, own_outs, fins_r,
     (fin_send, fin_recv, tile_s, tile_r, relay_s, relay_r), own) = split_refs(
        refs, 1, plan.inputs, count, count, 1, made, plan.outputs, count, 6)
    sums = plan.steps(grads + own_outs + own)
    late_tiles = range(EARLY_TILES, GRID)
    tile = {i: tile_copies(sums.k, sums.other_c, sums.other_x, frames.at[packed(0, i * FT, FT)], frames, i, tile_s, tile_r)
            for i in late_tiles}

    def fin_copy(t):
        return send(fins[t], fins_r[t], fin_send.at[t], fin_recv.at[t], sums.other_x)

    def relay(i, first, frames_count):
        return send(frames.at[packed(2, first, frames_count)],
                    frames.at[packed(4 - slot_for(sums.k), first, frames_count)],
                    relay_s.at[i], relay_r.at[i], sums.other_c)

    early = relay(0, 0, EARLY_TILES * FT)
    late = {i: relay(i, i * FT, FT) for i in late_tiles}
    greet(sums.peers)
    sums.begin()
    for i in late_tiles:
        for copy in tile[i]:
            copy.start()
    for t in range(count):
        fin_copy(t).start()
    early.start()
    sums.load_first()
    sums.first_hop()

    def body(s, carry):
        sums.hop(s)
        return carry

    lax.fori_loop(1, sums.final, body, 0)
    sums.finish()
    for i in late_tiles:
        tile[i][1].wait_recv()
        late[i].start()
    for t in range(count):
        fin_copy(t).wait_recv()
        value = keeps[t][...] + fins_r[t][...].astype(F32)
        put(left_outs[offsets[t] :], places[t], value)
    for t in range(count):
        fin_copy(t).wait_send()
    early.wait()
    for i in late_tiles:
        tile[i][0].wait()
        tile[i][1].wait_send()
        late[i].wait()


def scatter_last(frames, g, keeps, fins, plan, left):
    shapes = [shape for p in left for shape in p.shapes]
    sems = pltpu.SemaphoreType.DMA
    vmem = pl.BlockSpec(memory_space=pltpu.VMEM)
    return pl.pallas_call(
        functools.partial(last_kernel, plan, left, shapes),
        name="scatter_last",
        out_shape=[shape_of(frames.shape, frames.dtype)] + [shape_of(hw, F32) for hw in shapes] + plan.out_shapes,
        in_specs=[ANY] * 2 + [vmem] * len(keeps) + [ANY] * len(fins),
        out_specs=[ANY] + [vmem] * len(shapes) + plan.out_specs,
        scratch_shapes=[pltpu.VMEM(f.shape, f.dtype) for f in fins]
        + [sems((len(fins),))] * 2 + [sems((2, GRID))] * 2 + [sems((GRID,))] * 2 + plan.scratch,
        input_output_aliases={0: 0},
        compiler_params=pltpu.CompilerParams(
            collective_id=1, has_side_effects=True, vmem_limit_bytes=VMEM_LIMIT
        ),
    )(frames, g, *keeps, *fins)


def tuned(mesh):
    wide, n = mesh.shape["wide"], mesh.shape["narrow"]
    if n != 4 or wide != 2 * GRID or D % (8 * wide * n):
        return False
    for w in range(wide):
        for k in range(n):
            device = mesh.devices[w, k]
            here = (getattr(device, "coords", None), getattr(device, "core_on_chip", None))
            if here[0] is None or tuple(here[0]) != (k // 2, w % 2, w // 2) or here[1] != k % 2:
                return False
    return True


def exchange(x):
    return lax.all_to_all(x, ALL, split_axis=0, concat_axis=0, tiled=True)


def shift_clips(clips, back):
    n = lax.axis_size("narrow")
    parts = [clips[0]]
    for j in range(1, n):
        step = -j if back else j
        parts.append(lax.ppermute(clips[j], "narrow", [(s, (s + step) % n) for s in range(n)]))
    return jnp.stack(parts)


def local(fast, clips, t_emb, lengths, task, w_mod, b_mod, w_qkv_s, w_o_s, b_o_s, w_qkv_t, w_o_t, b_o_t,
          w_in, b_in, w_out, b_out, cotangent):
    n = lax.axis_size("narrow")
    wide = lax.axis_size("wide")
    devices = n * wide
    part = w_mod.shape[0]
    mod_cols = w_mod.shape[1] // devices
    rank = lax.axis_index("narrow")
    slots = jnp.arange(n, dtype=jnp.int32)
    from_clip = (rank - slots) % n
    recv_len = lengths.reshape(n, n)[from_clip, slots]
    recv_task = task.reshape(n, n, FR)[from_clip, slots]
    ends = jnp.cumsum(recv_len)
    starts = ends - recv_len
    ids = jnp.arange(LIVE, dtype=jnp.int32)
    source = jnp.sum((ends[None, :] <= ids[:, None]).astype(jnp.int32), axis=1)
    within = ids - starts[source]
    pack_rows = source * FR + within
    row_choice = source * 2 + recv_task[source, within]
    frame_ids = jnp.arange(FR, dtype=jnp.int32)
    live_back = frame_ids[None, :] < recv_len[:, None]
    unpack_rows = jnp.where(live_back, starts[:, None] + frame_ids[None, :], 0).reshape(-1)
    row_id = jnp.arange(64, dtype=jnp.int32)
    col_id = jnp.arange(LANES, dtype=jnp.int32) % 64
    seg = (
        (row_id[:, None] // LIVE == col_id[None, :] // LIVE)
        & (source[row_id % LIVE][:, None] == source[col_id % LIVE][None, :])
    ).astype(F32)

    def gather(w):
        return lax.all_gather(w, ALL, axis=0, tiled=True)

    frames = shift_clips(clips, False)
    if fast:
        wqkv_s, wo_s, wqkv_t, wo_t = gather_first((w_qkv_s, w_o_s, w_qkv_t, w_o_t), wide, n)
    else:
        win, wout, wqkv_t, wo_t, wqkv_s, wo_s = [gather(w) for w in (w_in, w_out, w_qkv_t, w_o_t, w_qkv_s, w_o_s)]
    frames = jnp.take(frames.reshape(n * FR, PATCHES, D), pack_rows, axis=0, mode="clip")

    wm = jnp.swapaxes(w_mod.reshape(part, devices, mod_cols), 0, 1).reshape(devices, -1)
    emb = jnp.broadcast_to(t_emb.reshape(1, -1), (devices, t_emb.size))
    small = jnp.concatenate([b_o_s, b_o_t, b_in, b_out])
    small_all = jnp.broadcast_to(small[None], (devices, small.size))
    got = exchange(jnp.concatenate([wm, emb, small_all], axis=1))
    wm_cols = got[:, : part * mod_cols].reshape(D, mod_cols)
    emb_all = got[:, part * mod_cols : part * mod_cols + t_emb.size].reshape(-1, D)
    small_got = got[:, part * mod_cols + t_emb.size :]
    b1 = b_o_s.size
    bias_s = small_got[:, :b1].reshape(1, -1).astype(F32)
    bias_t = small_got[:, b1 : 2 * b1].reshape(1, -1).astype(F32)
    bias_in = small_got[:, 2 * b1 : 2 * b1 + b_in.size].reshape(1, -1).astype(F32)
    bias_out = small_got[:, 2 * b1 + b_in.size :].reshape(1, -1).astype(F32)
    emb_f = emb_all.astype(F32)
    silu_low = (emb_f * jax.nn.sigmoid(emb_f)).astype(BF)
    mod_part = dot(silu_low, wm_cols) + b_mod.astype(F32)[None]
    mod_part = mod_part.reshape(wide, n, n, 2, mod_cols)
    mod_part = jnp.stack([jnp.roll(mod_part[:, :, c], c, axis=1) for c in range(n)], axis=2)
    mod_rows = exchange(mod_part.reshape(devices, -1)).reshape(devices, 2 * n, mod_cols)
    mod_rows = jnp.swapaxes(mod_rows, 0, 1).reshape(2 * n, 9, D)
    mod = jnp.swapaxes(mod_rows[row_choice], 0, 1)

    def carry(js, shard, number):
        return forward_carrier(cotangent, js, shard, wide, n, number) if fast else None

    *half, x1, qkv1, o1, a1 = run_frame_forward(
        frames, mod, wqkv_s, wo_s, bias_s, carry((2,), w_in, 2))
    *odd, x2, qkv2, o2, a2 = run_time_forward(
        x1, mod, seg, wqkv_t, wo_t, bias_t, carry((1, 3), w_out, 3))
    if fast:
        (half, win), (odd, wout) = half, odd
        cots = jnp.stack([cotangent[0], odd[0], half[0], odd[1]])
    else:
        cots = shift_clips(cotangent, False)
    dy = run_turn_frames(cots.reshape(n * FR, PATCHES, D), pack_rows)
    out, dx2, g_in, g_out, gb_in, gb_out, dmod3 = run_mlp(x2, dy, mod, win, bias_in, wout, bias_out, n if fast else 1)

    own_len = lengths.reshape(n, n)[rank]
    own_live = frame_ids[None, :] < own_len[:, None]

    def spread(frames):
        return jnp.take(frames, unpack_rows, axis=0, mode="clip").reshape(n, FR, PATCHES, D)

    def only_live(parts):
        return jnp.where(own_live[:, :, None, None], parts, jnp.zeros((), parts.dtype))

    def scatter(g):
        return lax.psum_scatter(g.astype(BF), ALL, scatter_dimension=0, tiled=True).astype(F32)

    if fast:
        ahead = lengths.reshape(n, n)[(rank + slots[:, None] - slots[None, :]) % n, slots[None, :]]
        own_start = jnp.sum(jnp.where(slots[None, :] < slots[:, None], ahead, 0), axis=1)
        own_rows = slots[:, None] * LIVE + own_start[:, None] + frame_ids[None, :]
        own_rows = jnp.where(own_live, own_rows, -1).reshape(-1)
        plan_mlp = mlp_plan(wide, g_in, g_out, devices)
        out, *got, dx1, g_t, gb_t, dmod2 = run_time_back(
            x1, dx2, mod, seg, qkv2, o2, a2, wqkv_t, wo_t, share_carrier(out, [g_in, g_out], plan_mlp, 4))
        keeps, fins = plan_mlp.left(got)
        plan_t = attn_plan(wide, g_t, devices, True)
        out, dx0, *got, g_s, gb_s, dmod1 = run_frame_back(
            frames, dx1, mod, qkv1, o1, a1, wqkv_s, wo_s, relay_carrier(out, [g_t], plan_t, 5))
        more_keeps, more_fins = plan_t.left(got)
        keeps, fins = keeps + more_keeps, fins + more_fins
        dx0, s_in, s_out, s_qkv_t, s_o_t, s_qkv_s, s_o_s = scatter_last(
            dx0, g_s, keeps, fins, attn_plan(wide, g_s, devices, False), (plan_mlp, plan_t))[:7]
        layer_out = run_unpack(out, own_rows).reshape(n, FR, PATCHES, D)
        grad_clips = run_unpack(dx0, own_rows).reshape(n, FR, PATCHES, D)
    else:
        dx1, g_t, gb_t, dmod2 = run_time_back(x1, dx2, mod, seg, qkv2, o2, a2, wqkv_t, wo_t)
        dx0, g_s, gb_s, dmod1 = run_frame_back(frames, dx1, mod, qkv1, o1, a1, wqkv_s, wo_s)
        layer_out = only_live(shift_clips(spread(out), True))
        grad_clips = only_live(shift_clips(spread(dx0), True))
        s_in, s_out, s_t, s_s = [scatter(g) for g in (g_in, g_out, g_t, g_s)]
        s_qkv_t, s_o_t, s_qkv_s, s_o_s = s_t[:, : 3 * D], s_t[:, 3 * D :], s_s[:, : 3 * D], s_s[:, 3 * D :]

    grad_frames = jnp.swapaxes(jnp.concatenate([dmod1, dmod2, dmod3], axis=0), 0, 1).reshape(LIVE, 9 * D)
    chooser = (row_choice[:, None] == jnp.arange(2 * n, dtype=jnp.int32)[None, :]).astype(F32)
    grad_rows = lax.dot_general(
        chooser, grad_frames, (((0,), (0,)), ((), ())), precision=lax.Precision.HIGHEST
    ).astype(BF)
    d_cols = exchange(jnp.swapaxes(grad_rows.reshape(2 * n, devices, mod_cols), 0, 1).reshape(devices, -1))
    d_cols = d_cols.reshape(wide, n, n, 2, mod_cols)
    d_cols = jnp.stack([jnp.roll(d_cols[:, :, c], -c, axis=1) for c in range(n)], axis=2)
    d_cols = d_cols.reshape(devices * 2 * n, mod_cols)
    grad_b_mod = jnp.sum(d_cols.astype(F32), axis=0)
    gwm_cols = dot_tn(silu_low, d_cols)
    g_emb = dot_nt(d_cols, wm_cols)
    gb_all = jnp.concatenate(
        [gb_s.reshape(devices, -1), gb_t.reshape(devices, -1), gb_in.reshape(devices, -1),
         gb_out.reshape(devices, -1)], axis=1)
    final = exchange(jnp.concatenate(
        [gwm_cols.reshape(devices, -1), g_emb.reshape(devices, -1), gb_all], axis=1))
    cut1 = part * mod_cols
    cut2 = cut1 + t_emb.size
    grad_w_mod = jnp.swapaxes(final[:, :cut1].reshape(devices, part, mod_cols), 0, 1).reshape(part, -1)
    emb_own = t_emb.astype(F32)
    sig = jax.nn.sigmoid(emb_own)
    grad_emb = jnp.sum(final[:, cut1:cut2], axis=0).reshape(t_emb.shape)
    grad_t_emb = (grad_emb * (sig * (1.0 + emb_own * (1.0 - sig)))).astype(BF)
    gb = jnp.sum(final[:, cut2:], axis=0)
    return (
        layer_out,
        grad_clips,
        grad_t_emb,
        grad_w_mod,
        grad_b_mod,
        s_qkv_s,
        s_o_s,
        gb[:b1],
        s_qkv_t,
        s_o_t,
        gb[b1 : 2 * b1],
        s_in,
        gb[2 * b1 : 2 * b1 + b_in.size],
        s_out,
        gb[2 * b1 + b_in.size :],
    )


def solution(mesh):
    full = P(ALL)
    placed = (full, full, P("wide"), P("wide")) + (full,) * 13
    return jax.shard_map(functools.partial(local, tuned(mesh)), mesh=mesh, in_specs=placed, out_specs=(full,) * 15, check_vma=False)
```

```python
import functools

import jax
import jax.numpy as jnp
from jax import lax
from jax.experimental import pallas as pl
from jax.experimental.pallas import tpu as pltpu
from jax.sharding import PartitionSpec as P

D = 768
HEADS = 12
HEAD = 64
FF = 3072
FR = 16
PATCHES = 64
LIVE = 2 * FR
EPS = 1e-06
BF = jnp.bfloat16
F32 = jnp.float32
ALL = ("wide", "narrow")
PAIRS = HEADS // 2
LANES = 2 * HEAD
BACK_PAIRS = 6
TILE = 512
FT = TILE // PATCHES
PT = TILE // LIVE
GRID = LIVE * PATCHES // TILE
GROUPS = TILE // 64
EARLY_TILES = GRID - 1
GELU_C = 0.7978845608028654
GELU_A = 0.044715
VMEM_LIMIT = 66 * 1000 * 1000
MESH = pl.DeviceIdType.MESH
ANY = pl.BlockSpec(memory_space=pl.ANY)


def dot(a, b):
    return lax.dot_general(a, b, (((1,), (0,)), ((), ())), preferred_element_type=F32)


def dot_nt(a, b):
    return lax.dot_general(a, b, (((1,), (1,)), ((), ())), preferred_element_type=F32)


def dot_tn(a, b):
    return lax.dot_general(a, b, (((0,), (0,)), ((), ())), preferred_element_type=F32)


def normalise(x):
    mean = jnp.mean(x, axis=-1, keepdims=True)
    centred = x - mean
    var = jnp.mean(centred * centred, axis=-1, keepdims=True)
    rstd = lax.rsqrt(var + EPS)
    return centred * rstd, rstd


def norm_back(dn, xhat, rstd):
    m1 = jnp.mean(dn, axis=-1, keepdims=True)
    m2 = jnp.mean(dn * xhat, axis=-1, keepdims=True)
    return rstd * (dn - m1 - xhat * m2)


def lane_masks():
    lane = lax.broadcasted_iota(jnp.int32, (64, LANES), 1)
    low_lanes = lane < HEAD
    low = jnp.where(low_lanes, 1.0, 0.0).astype(BF)
    high = jnp.where(low_lanes, 0.0, 1.0).astype(BF)
    return low_lanes, low, high


def split_heads(x, low, high):
    return jnp.concatenate([x * low, x * high], axis=0)


def softmax_keys(s, mask):
    if mask is not None:
        s = jnp.where(mask, s, -1e30)
    top = jnp.max(s, axis=0, keepdims=True)
    e = jnp.exp(s - top)
    return e * (1.0 / jnp.sum(e, axis=0, keepdims=True))


def pair_cols(part, hp):
    return slice(part * D + hp * LANES, part * D + (hp + 1) * LANES)


def attend(qkv_ref, o_ref, mask):
    low_lanes, low, high = lane_masks()
    scale = HEAD ** (-0.5)

    def body(g, carry):
        rows = pl.ds(pl.multiple_of(g * 64, 64), 64)
        pairs = range(PAIRS)
        s = [dot_nt(qkv_ref[rows, pair_cols(1, hp)], split_heads(qkv_ref[rows, pair_cols(0, hp)], low * scale, high * scale))
             for hp in pairs]
        p = [softmax_keys(t, mask).astype(BF) for t in s]
        r = [dot_tn(p[hp], qkv_ref[rows, pair_cols(2, hp)]) for hp in pairs]
        for hp in pairs:
            o_ref[rows, pair_cols(0, hp)] = jnp.where(low_lanes, r[hp][:64], r[hp][64:]).astype(BF)
        return carry

    lax.fori_loop(0, GROUPS, body, 0)


def attend_back(qkv_ref, do_ref, dqkv_ref, mask):
    low_lanes, low, high = lane_masks()
    scale = HEAD ** (-0.5)

    def body(g, carry):
        rows = pl.ds(pl.multiple_of(g * 64, 64), 64)
        for first in range(0, PAIRS, BACK_PAIRS):
            pairs = range(first, first + BACK_PAIRS)
            qb = [split_heads(qkv_ref[rows, pair_cols(0, hp)], low * scale, high * scale) for hp in pairs]
            dob = [split_heads(do_ref[rows, pair_cols(0, hp)], low, high) for hp in pairs]
            s = [dot_nt(qkv_ref[rows, pair_cols(1, hp)], q) for hp, q in zip(pairs, qb)]
            dp = [dot_nt(qkv_ref[rows, pair_cols(2, hp)], d) for hp, d in zip(pairs, dob)]
            p = [softmax_keys(t, mask) for t in s]
            delta = [jnp.sum(a * b, axis=0, keepdims=True) for a, b in zip(p, dp)]
            ds = [(a * (b - c)).astype(BF) for a, b, c in zip(p, dp, delta)]
            dv = [dot(a.astype(BF), d) for a, d in zip(p, dob)]
            dk = [dot(a, q) for a, q in zip(ds, qb)]
            r = [dot_tn(a, qkv_ref[rows, pair_cols(1, hp)]) for hp, a in zip(pairs, ds)]
            for i, hp in enumerate(pairs):
                dqkv_ref[rows, pair_cols(2, hp)] = dv[i].astype(BF)
                dqkv_ref[rows, pair_cols(1, hp)] = dk[i].astype(BF)
                dq = jnp.where(low_lanes, r[i][:64], r[i][64:]) * scale
                dqkv_ref[rows, pair_cols(0, hp)] = dq.astype(BF)
        return carry

    lax.fori_loop(0, GROUPS, body, 0)


def swap_major(value, scratch, out_ref, first, second):
    for b in range(D // 128):
        cols = slice(b * 128, (b + 1) * 128)
        for i in range(first):
            scratch[b, pl.ds(i, second, stride=first), :] = value[i * second : (i + 1) * second, cols]
        out_ref[:, :, cols] = scratch[b].reshape(second, first, 128).astype(out_ref.dtype)


def frames_of(refs):
    return jnp.concatenate([r[0] for r in refs], axis=0).astype(F32)


def per_frame(piece):
    return jnp.broadcast_to(piece[:, None, :], (FT, PATCHES, D)).reshape(TILE, D)


def per_patch(piece):
    return jnp.broadcast_to(piece[None], (PT, LIVE, D)).reshape(TILE, D)


def sum_patches(value):
    return jnp.sum(value.reshape(FT, PATCHES, D), axis=1)


def sum_groups(value):
    return jnp.sum(value.reshape(PT, LIVE, D), axis=0)


def attn_mask(seg_ref):
    return seg_ref[...] > 0.0


def no_tick(place):
    pass


def frame_forward(frames, mod, wqkv, wo, bo, x1t, qkv, o, a1, scratch, tick=no_tick):
    x = frames[...].reshape(TILE, D).astype(F32)
    xhat, _ = normalise(x)
    h = (xhat * (1.0 + per_frame(mod[1])) + per_frame(mod[0])).astype(BF)
    qkv[...] = dot(h, wqkv[...]).astype(BF)
    tick(0)
    attend(qkv, o, None)
    tick(1)
    branch = dot(o[...], wo[...]) + bo[...]
    a1[...] = branch
    x1 = x + per_frame(mod[2]) * branch
    swap_major(x1, scratch, x1t, FT, PATCHES)


def turn_frames(rows_ref, *refs):
    x_refs, (out, scratch) = refs[:FT], refs[FT:]
    swap_major(frames_of(x_refs), scratch, out, FT, PATCHES)


def time_forward(x1, mod, seg, wqkv, wo, bo, x2, qkv, o, a2, tick=no_tick):
    x = x1[...].reshape(TILE, D)
    xhat, _ = normalise(x)
    h = (xhat * (1.0 + per_patch(mod[1])) + per_patch(mod[0])).astype(BF)
    qkv[...] = dot(h, wqkv[...]).astype(BF)
    tick(0)
    attend(qkv, o, attn_mask(seg))
    tick(1)
    branch = dot(o[...], wo[...]) + bo[...]
    a2[...] = branch
    x2[...] = (x + per_patch(mod[2]) * branch).reshape(PT, LIVE, D)


def mlp_both(x2, dy, mod, win, bin_, wout, bout, out, dx2, gwin, gwout, gbin, gbout, dmod, scratch):
    first = pl.program_id(0) == 0

    @pl.when(first)
    def _():
        gwin[...] = jnp.zeros_like(gwin)
        gwout[...] = jnp.zeros_like(gwout)
        gbin[...] = jnp.zeros_like(gbin)
        gbout[...] = jnp.zeros_like(gbout)
        dmod[...] = jnp.zeros_like(dmod)

    x = x2[...].reshape(TILE, D)
    xhat, rstd = normalise(x)
    h = (xhat * (1.0 + per_patch(mod[1])) + per_patch(mod[0])).astype(BF)
    gate = per_patch(mod[2])
    grad = dy[...].reshape(TILE, D)
    da = (grad * gate).astype(BF)
    gbout[...] += jnp.sum(da.astype(F32), axis=0, keepdims=True)
    branch = jnp.zeros((TILE, D), F32) + bout[...]
    dh = jnp.zeros((TILE, D), F32)
    for j in range(FF // D):
        cols = slice(j * D, (j + 1) * D)
        u = dot(h, win[:, cols]) + bin_[:, cols]
        u2 = u * u
        t = jnp.tanh(GELU_C * u * (1.0 + GELU_A * u2))
        half = 0.5 * (1.0 + t)
        g = (u * half).astype(BF)
        slope = half + (0.5 * GELU_C) * u * (1.0 - t * t) * (1.0 + 3.0 * GELU_A * u2)
        branch = branch + dot(g, wout[cols, :])
        du = (dot_nt(da, wout[cols, :]) * slope).astype(BF)
        gwout[cols, :] += dot_tn(g, da)
        gbin[:, cols] += jnp.sum(du.astype(F32), axis=0, keepdims=True)
        gwin[:, cols] += dot_tn(h, du)
        dh = dh + dot_nt(du, win[:, cols])
    swap_major(x + gate * branch, scratch, out, PT, LIVE)
    dmod[2] += sum_groups(grad * branch)
    dmod[0] += sum_groups(dh)
    dmod[1] += sum_groups(dh * xhat)
    back = norm_back(dh * (1.0 + per_patch(mod[1])), xhat, rstd)
    dx2[...] = (grad + back).reshape(PT, LIVE, D)


def attn_back_tile(x, grad, shift, scale, gate, branch, qkv, o, wqkv, wo, gw, gbo, do, dqkv, mask, tick):
    first = pl.program_id(0) == 0

    @pl.when(first)
    def _():
        gw[...] = jnp.zeros_like(gw)
        gbo[...] = jnp.zeros_like(gbo)

    da = (grad * gate).astype(BF)
    do[...] = dot_nt(da, wo[...]).astype(BF)
    gw[:, 3 * D :] += dot_tn(o[...], da)
    gbo[...] += jnp.sum(da.astype(F32), axis=0, keepdims=True)
    tick(0)
    attend_back(qkv, do, dqkv, mask)
    tick(1)
    xhat, rstd = normalise(x)
    h = (xhat * (1.0 + scale) + shift).astype(BF)
    dh = jnp.zeros((TILE, D), F32)
    for j in range(3):
        cols = slice(j * D, (j + 1) * D)
        part = dqkv[:, cols]
        gw[:, cols] += dot_tn(h, part)
        dh = dh + dot_nt(part, wqkv[:, cols])
    dx = grad + norm_back(dh * (1.0 + scale), xhat, rstd)
    return dx, dh, dh * xhat, grad * branch


def time_back(x1, dx2, mod, seg, qkv, o, a2, wqkv, wo, dx1, gw, gbo, dmod, do, dqkv, scratch, tick=no_tick):
    @pl.when(pl.program_id(0) == 0)
    def _():
        dmod[...] = jnp.zeros_like(dmod)

    dx, d_shift, d_scale, d_gate = attn_back_tile(
        x1[...].reshape(TILE, D), dx2[...].reshape(TILE, D), per_patch(mod[0]), per_patch(mod[1]),
        per_patch(mod[2]), a2[...], qkv, o, wqkv, wo, gw, gbo, do, dqkv, attn_mask(seg), tick)
    dmod[0] += sum_groups(d_shift)
    dmod[1] += sum_groups(d_scale)
    dmod[2] += sum_groups(d_gate)
    swap_major(dx, scratch, dx1, PT, LIVE)


def frame_back(frames, dx1, mod, qkv, o, a1, wqkv, wo, dx0, gw, gbo, dmod, do, dqkv, tick=no_tick):
    dx, d_shift, d_scale, d_gate = attn_back_tile(
        frames[...].reshape(TILE, D).astype(F32), dx1[...].reshape(TILE, D), per_frame(mod[0]), per_frame(mod[1]),
        per_frame(mod[2]), a1[...], qkv, o, wqkv, wo, gw, gbo, do, dqkv, None, tick)
    dmod[0] = sum_patches(d_shift)
    dmod[1] = sum_patches(d_scale)
    dmod[2] = sum_patches(d_gate)
    dx0[...] = dx.reshape(FT, PATCHES, D).astype(BF)


def frame_specs():
    return [
        pl.BlockSpec((1, PATCHES, D), functools.partial(lambda j, i, rows: (rows[FT * i + j], 0, 0), j))
        for j in range(FT)
    ]


def whole(shape):
    return pl.BlockSpec(shape, lambda i, *_: (0,) * len(shape), pipeline_mode=pl.Buffered(1))


def tiles(shape, dim):
    return pl.BlockSpec(shape, lambda i, *_: tuple(i if a == dim else 0 for a in range(len(shape))))


def piece_spec(number, frames, by_tile):
    return pl.BlockSpec((3, frames, D), lambda i, *_: (number, i if by_tile else 0, 0))


ROWS = tiles((TILE, D), 0)
ROWS3 = tiles((TILE, 3 * D), 0)
TURNED = tiles((PT, LIVE, D), 0)


TURN = pltpu.VMEM((D // 128, TILE, 128), F32)


def shape_of(shape, dtype):
    return jax.ShapeDtypeStruct(shape, dtype)


class Carrier:
    def __init__(self, wrap, number, ins, outs, out_specs, scratch, aliases=None):
        self.wrap, self.number, self.ins, self.outs = wrap, number, ins, outs
        self.out_specs, self.scratch, self.aliases = out_specs, scratch, aliases or {}


def call(kernel, name, ins, in_specs, outs, out_specs, scratch, flops, prefetch=None, carrier=None):
    moved = sum(a.size * a.dtype.itemsize for a in tuple(ins) + tuple(outs))
    params, aliases = {}, {}
    if carrier is not None:
        kernel = functools.partial(carrier.wrap, kernel, len(ins), len(outs), len(scratch))
        ins, in_specs = carrier.ins + ins, [ANY] * len(carrier.ins) + in_specs
        outs, out_specs = carrier.outs + outs, carrier.out_specs + out_specs
        scratch = scratch + carrier.scratch
        params, aliases = dict(collective_id=carrier.number, has_side_effects=True), carrier.aliases
    grid_spec = pltpu.PrefetchScalarGridSpec(
        num_scalar_prefetch=0 if prefetch is None else 1,
        grid=(GRID,),
        in_specs=in_specs,
        out_specs=out_specs,
        scratch_shapes=scratch,
    )
    fn = pl.pallas_call(
        kernel,
        grid_spec=grid_spec,
        out_shape=outs,
        name=name,
        input_output_aliases=aliases,
        cost_estimate=pl.CostEstimate(flops=flops, bytes_accessed=moved, transcendentals=0),
        compiler_params=pltpu.CompilerParams(
            dimension_semantics=("arbitrary",), vmem_limit_bytes=VMEM_LIMIT, **params
        ),
    )
    return fn(*ins) if prefetch is None else fn(prefetch, *ins)


def split_refs(refs, *counts):
    parts = []
    for count in counts:
        parts.append(refs[:count])
        refs = refs[count:]
    return parts + [refs]


def forward_carrier(clips, js, shard, far, ring, n, number):
    held = Gather.scratch([shard], ring)

    def wrap(kernel, n_in, n_out, n_scratch, *refs):
        (src, part, other), ins, (dst, full), outs, scratch, (send_sem, recv_sem), own = split_refs(
            refs, 3, n_in, 2, n_out, n_scratch, 2)
        step = pl.program_id(0)
        gather = Gather(ring, (shard.shape[0],), (part, other, full) + own)
        targets = [(gather.w, (gather.k + j) % n) for j in js]
        copies = [send(src.at[j], dst.at[i], send_sem.at[i], recv_sem.at[i], targets[i]) for i, j in enumerate(js)]

        @pl.when(step == 0)
        def _():
            greet(tuple(targets) + gather.peers)
            gather.begin()
            for copy in copies:
                copy.start()

        def tick(place):
            if place == 0:
                @pl.when(step == 0)
                def _():
                    gather.second()

                @pl.when(step > 0)
                def _():
                    gather.hop(2 * step)
            else:
                gather.hop(2 * step + 1)

        kernel(*ins, *outs, *scratch, tick=tick)

        @pl.when(step == GRID - 1)
        def _():
            gather.finish()
            for copy in copies:
                copy.wait()

    sems = pltpu.SemaphoreType.DMA((len(js),))
    return Carrier(wrap, number, [clips, shard, far],
                   [shape_of((len(js),) + clips.shape[1:], clips.dtype)] + Gather.shapes([shard], ring * n),
                   [ANY, ANY], [sems, sems] + held)


def packed(slot, first=0, count=LIVE):
    return pl.ds(pl.multiple_of(slot * LIVE + first, 8), count)


def slot_for(k):
    return 3 - 2 * (k % 2)


def ticks(sums, step):
    def tick(place):
        @pl.when(step == 0)
        def _():
            if place == 0:
                sums.load_first()
            else:
                sums.first_hop()

        @pl.when(step > 0)
        def _():
            sums.hop(2 * step - 1 + place)

    return tick


def share_carrier(frames, grads, plan, number):
    n_grads = len(grads)

    def wrap(kernel, n_in, n_out, n_scratch, *refs):
        (_,), grad_refs, ins, (dst,), left, outs, scratch, (send_sem, recv_sem), own = split_refs(
            refs, 1, n_grads, n_in, 1, plan.outputs, n_out, n_scratch, 2)
        step = pl.program_id(0)
        sums = plan.steps(grad_refs + left + own)
        targets = ((slot_for(sums.k), sums.other_c), (2, sums.other_x))
        copies = [send(dst.at[packed(0)], dst.at[packed(slot)], send_sem.at[i], recv_sem.at[i], peer)
                  for i, (slot, peer) in enumerate(targets)]

        @pl.when(step == 0)
        def _():
            greet(sums.peers)
            sums.begin()
            for copy in copies:
                copy.start()

        kernel(*ins, *outs, *scratch, tick=ticks(sums, step))

        @pl.when(step == GRID - 1)
        def _():
            sums.leave()
            for copy in copies:
                copy.wait()

    sems = pltpu.SemaphoreType.DMA((2,))
    return Carrier(wrap, number, [frames] + grads, [shape_of(frames.shape, frames.dtype)] + plan.out_shapes,
                   [ANY] + plan.out_specs, [sems, sems] + plan.scratch, {0: 0})


def tile_copies(k, other_c, other_x, src, dst, i, send_sem, recv_sem):
    return [send(src, dst.at[packed(slot, i * FT, FT)], send_sem.at[a, i], recv_sem.at[a, i], peer)
            for a, (slot, peer) in enumerate(((slot_for(k), other_c), (2, other_x)))]


def relay_carrier(frames, grads, plan, number):
    n_grads = len(grads)

    def wrap(kernel, n_in, n_out, n_scratch, *refs):
        (_,), grad_refs, ins, (dst, made), left, outs, scratch, (send_sem, recv_sem, tile_s, tile_r, keep, buf), own = (
            split_refs(refs, 1, n_grads, n_in, 2, plan.outputs, n_out, n_scratch, 6))
        step = pl.program_id(0)
        sums = plan.steps(grad_refs + left + own)
        relay = send(dst.at[packed(2)], dst.at[packed(4 - slot_for(sums.k))],
                     send_sem.at[0], recv_sem.at[0], sums.other_c)

        def tile(i):
            return tile_copies(sums.k, sums.other_c, sums.other_x, buf.at[i], made, i, tile_s, tile_r)

        def store(i):
            return pltpu.make_async_copy(buf.at[i], made.at[packed(0, i * FT, FT)], keep.at[i])

        @pl.when(step == 0)
        def _():
            greet(sums.peers)
            sums.begin()
            relay.start()

        kernel(*ins, buf.at[step], *outs, *scratch, tick=ticks(sums, step))
        store(step).start()

        @pl.when(step < EARLY_TILES)
        def _():
            for copy in tile(step):
                copy.start()

        @pl.when(step == GRID - 1)
        def _():
            sums.leave()
            relay.wait()
            for i in range(GRID):
                store(i).wait()
            for i in range(EARLY_TILES):
                for copy in tile(i):
                    copy.wait()

    sems = pltpu.SemaphoreType.DMA
    shape = shape_of(frames.shape, frames.dtype)
    return Carrier(wrap, number, [frames] + grads, [shape, shape] + plan.out_shapes, [ANY, ANY] + plan.out_specs,
                   [sems((1,)), sems((1,)), sems((2, EARLY_TILES)), sems((2, EARLY_TILES)), sems((GRID,)),
                    pltpu.VMEM((GRID, FT, PATCHES, D), BF)] + plan.scratch, {0: 0})


TOKENS = LIVE * PATCHES


def run_frame_forward(frames, mod, wqkv, wo, bo, carrier=None):
    return call(
        frame_forward, "frame_forward",
        [frames, mod, wqkv, wo, bo],
        [tiles((FT, PATCHES, D), 0), piece_spec(0, FT, True), whole((D, 3 * D)), whole((D, D)), whole((1, D))],
        [shape_of((PATCHES, LIVE, D), F32), shape_of((TOKENS, 3 * D), BF), shape_of((TOKENS, D), BF),
         shape_of((TOKENS, D), F32)],
        [tiles((PATCHES, FT, D), 1), ROWS3, ROWS, ROWS],
        [TURN],
        2 * TOKENS * D * 4 * D, carrier=carrier)


def run_turn_frames(frames, rows):
    return call(
        turn_frames, "turn_frames", [frames] * FT, frame_specs(),
        [shape_of((PATCHES, LIVE, D), F32)], [tiles((PATCHES, FT, D), 1)],
        [TURN], 1000, rows)[0]


def unpack_frames(rows_ref, *refs):
    x_refs, (out,) = refs[:FT], refs[FT:]
    first = pl.program_id(0) * FT
    for j in range(FT):
        x = x_refs[j][0]
        out[j] = jnp.where(rows_ref[first + j] >= 0, x, jnp.zeros_like(x))


def run_unpack(frames, rows):
    specs = [
        pl.BlockSpec((1, PATCHES, D), functools.partial(lambda j, i, r: (jnp.maximum(r[FT * i + j], 0), 0, 0), j))
        for j in range(FT)
    ]
    return pl.pallas_call(
        unpack_frames,
        grid_spec=pltpu.PrefetchScalarGridSpec(
            num_scalar_prefetch=1, grid=(rows.shape[0] // FT,), in_specs=specs, out_specs=tiles((FT, PATCHES, D), 0)),
        out_shape=shape_of((rows.shape[0], PATCHES, D), frames.dtype),
        name="unpack_frames",
        cost_estimate=pl.CostEstimate(flops=1000, bytes_accessed=4 * rows.shape[0] * PATCHES * D, transcendentals=0),
        compiler_params=pltpu.CompilerParams(dimension_semantics=("arbitrary",)),
    )(rows, *[frames] * FT)


def run_time_forward(x1, mod, seg, wqkv, wo, bo, carrier=None):
    return call(
        time_forward, "time_forward",
        [x1, mod, seg, wqkv, wo, bo],
        [TURNED, piece_spec(1, LIVE, False), whole((64, LANES)), whole((D, 3 * D)), whole((D, D)),
         whole((1, D))],
        [shape_of((PATCHES, LIVE, D), F32), shape_of((TOKENS, 3 * D), BF), shape_of((TOKENS, D), BF),
         shape_of((TOKENS, D), F32)],
        [TURNED, ROWS3, ROWS, ROWS],
        [], 2 * TOKENS * D * 4 * D, carrier=carrier)


def run_mlp(x2, dy, mod, win, bin_, wout, bout, slots=1):
    return call(
        mlp_both, "mlp_both",
        [x2, dy, mod, win, bin_, wout, bout],
        [TURNED, TURNED, piece_spec(2, LIVE, False), whole((D, FF)), whole((1, FF)), whole((FF, D)),
         whole((1, D))],
        [shape_of((slots * LIVE, PATCHES, D), BF), shape_of((PATCHES, LIVE, D), F32), shape_of((D, FF), F32),
         shape_of((FF, D), F32), shape_of((1, FF), F32), shape_of((1, D), F32), shape_of((3, LIVE, D), F32)],
        [tiles((LIVE, PT, D), 1), TURNED, whole((D, FF)), whole((FF, D)), whole((1, FF)), whole((1, D)),
         whole((3, LIVE, D))],
        [TURN],
        6 * 2 * TOKENS * D * FF)


def run_time_back(x1, dx2, mod, seg, qkv, o, a2, wqkv, wo, carrier=None):
    return call(
        time_back, "time_back",
        [x1, dx2, mod, seg, qkv, o, a2, wqkv, wo],
        [TURNED, TURNED, piece_spec(1, LIVE, False), whole((64, LANES)), ROWS3, ROWS, ROWS,
         whole((D, 3 * D)), whole((D, D))],
        [shape_of((LIVE, PATCHES, D), F32), shape_of((D, 4 * D), F32), shape_of((1, D), F32), shape_of((3, LIVE, D), F32)],
        [tiles((LIVE, PT, D), 1), whole((D, 4 * D)), whole((1, D)), whole((3, LIVE, D))],
        [pltpu.VMEM((TILE, D), BF), pltpu.VMEM((TILE, 3 * D), BF), TURN],
        2 * 2 * TOKENS * D * 4 * D, carrier=carrier)


def run_frame_back(frames, dx1, mod, qkv, o, a1, wqkv, wo, carrier=None):
    frames_out = [] if carrier else [shape_of((LIVE, PATCHES, D), BF)]
    frames_spec = [] if carrier else [tiles((FT, PATCHES, D), 0)]
    return call(
        frame_back, "frame_back",
        [frames, dx1, mod, qkv, o, a1, wqkv, wo],
        [tiles((FT, PATCHES, D), 0), tiles((FT, PATCHES, D), 0), piece_spec(0, FT, True), ROWS3, ROWS, ROWS,
                         whole((D, 3 * D)), whole((D, D))],
        frames_out + [shape_of((D, 4 * D), F32), shape_of((1, D), F32), shape_of((3, LIVE, D), F32)],
        frames_spec + [whole((D, 4 * D)), whole((1, D)), piece_spec(0, FT, True)],
        [pltpu.VMEM((TILE, D), BF), pltpu.VMEM((TILE, 3 * D), BF)],
        2 * 2 * TOKENS * D * 4 * D, carrier=carrier)


def place_of(wide):
    ring = wide
    turn = ring // 2
    w = lax.axis_index("wide")
    k = lax.axis_index("narrow")
    z, y = w // 2, w % 2
    r = z + y * (ring - 1 - 2 * z)

    def wide_at(position):
        side = position // turn
        return 2 * ((1 - side) * position + side * (ring - 1 - position)) + side

    return w, k, r, k // 2, k % 2, wide_at


def greet(peers):
    barrier = pltpu.get_barrier_semaphore()
    for peer in peers:
        pl.semaphore_signal(barrier, inc=1, device_id=peer, device_id_type=MESH)
    pl.semaphore_wait(barrier, len(peers))


def send(src, dst, send_sem, recv_sem, peer):
    return pltpu.make_async_remote_copy(
        src_ref=src, dst_ref=dst, send_sem=send_sem, recv_sem=recv_sem, device_id=peer, device_id_type=MESH
    )


class Gather:
    def __init__(self, ring, heights, refs):
        count = len(heights)
        self.ring, self.heights, self.count = ring, heights, count
        near, far, self.full, near_bufs, far_bufs, sems = split_refs(refs, count, count, count, count, count)
        self.shards, self.bufs = (near, far), (near_bufs, far_bufs)
        (self.ring_s, self.ring_r, self.core_s, self.core_r, self.load_sem, self.keep_sem) = sems
        self.w, self.k, self.r, self.x, self.c, self.wide_at = place_of(ring)
        self.other_c = (self.w, 2 * self.x + 1 - self.c)
        self.next = ((self.wide_at((self.r + 1) % ring), self.k), (self.wide_at((self.r + ring - 1) % ring), self.k))
        self.peers = self.next + (self.other_c,)

    @staticmethod
    def scratch(shards, ring):
        count, sems = len(shards), pltpu.SemaphoreType.DMA
        bufs = [pltpu.VMEM(a.shape, a.dtype) for a in shards]
        return bufs + bufs + [sems((count, 2, ring))] * 4 + [sems((count, 2))] * 2

    @staticmethod
    def shapes(shards, devices):
        return [shape_of((a.shape[0] * devices, a.shape[1]), a.dtype) for a in shards]

    def way(self, t, b):
        return (t + b) % 2

    def block(self, t, b, s):
        r, ring = self.r, self.ring
        place = (r + ring - s) % ring if self.way(t, b) == 0 else (r + s) % ring
        column = self.x if b == 0 else 1 - self.x
        block = 4 * self.wide_at(place) + 2 * column + self.c
        return self.full[t].at[pl.ds(pl.multiple_of(block * self.heights[t], 8), self.heights[t])]

    def ring_copy(self, t, b, s, src=None):
        dst = self.block(t, b, s)
        return send(dst if src is None else src, dst, self.ring_s.at[t, b, s], self.ring_r.at[t, b, s],
                    self.next[self.way(t, b)])

    def core_copy(self, t, b, s, src=None):
        dst = self.block(t, b, s)
        return send(dst if src is None else src, dst, self.core_s.at[t, b, s], self.core_r.at[t, b, s], self.other_c)

    def load(self, t, b):
        return pltpu.make_async_copy(self.shards[b][t], self.bufs[b][t], self.load_sem.at[t, b])

    def keep(self, t, b):
        return pltpu.make_async_copy(self.bufs[b][t], self.block(t, b, 0), self.keep_sem.at[t, b])

    def each(self):
        return [(t, b) for b in range(2) for t in range(self.count)]

    def begin(self):
        for t, b in self.each():
            self.ring_copy(t, b, 0, self.shards[b][t]).start()
        for t, b in self.each():
            self.core_copy(t, b, 0, self.shards[b][t]).start()
            self.load(t, b).start()

    def second(self):
        for t, b in self.each():
            self.load(t, b).wait()
            self.keep(t, b).start()

    def hop(self, s):
        for b in range(2):
            for t in range(self.count):
                self.ring_copy(t, b, s - 1).wait_recv()

                @pl.when(s < self.ring - 1)
                def _():
                    self.ring_copy(t, b, s).start()

                self.core_copy(t, b, s).start()

    def finish(self):
        for t, b in self.each():
            self.keep(t, b).wait()
            for s in range(self.ring):
                if s < self.ring - 1:
                    self.ring_copy(t, b, s).wait_send()
                self.core_copy(t, b, s).wait()


def gather_kernel(ring, heights, *refs):
    gather = Gather(ring, heights, refs)
    greet(gather.peers)
    gather.begin()
    gather.second()

    def body(s, carry):
        gather.hop(s)
        return carry

    lax.fori_loop(1, ring, body, 0)
    gather.finish()


def gather_first(shards, far, ring, n):
    heights = tuple(a.shape[0] for a in shards)
    return pl.pallas_call(
        functools.partial(gather_kernel, ring, heights),
        name="gather_first",
        out_shape=Gather.shapes(shards, ring * n),
        in_specs=[ANY] * (2 * len(shards)),
        out_specs=[ANY] * len(shards),
        scratch_shapes=Gather.scratch(shards, ring),
        compiler_params=pltpu.CompilerParams(collective_id=0, has_side_effects=True),
    )(*shards, *far)


def put(outs, places, value):
    for o, out_col, col, width in places:
        outs[o][:, out_col : out_col + width] = value[:, col : col + width]


class Sums:
    def __init__(self, plan, refs):
        self.plan, count = plan, len(plan.pieces)
        self.grads, refs = refs[: plan.inputs], refs[plan.inputs :]
        self.outs, refs = refs[: plan.results], refs[plan.results :]
        self.stages, refs = refs[:count], refs[count:]
        self.own, self.part, self.came, self.went, self.last, self.fin_s, self.fin_r = (
            refs[i * count : (i + 1) * count] for i in range(7)
        )
        (self.ring_s, self.ring_r, self.core_s, self.core_r, self.x_s, self.x_r, self.load_sem,
         self.part_sem) = refs[7 * count :]
        ring = plan.ring
        self.w, self.k, self.r, self.x, self.c, self.wide_at = place_of(ring)
        self.other_x = (self.w, 2 * (1 - self.x) + self.c)
        self.other_c = (self.w, 2 * self.x + 1 - self.c)
        self.next = ((self.wide_at((self.r + 1) % ring), self.k), (self.wide_at((self.r + ring - 1) % ring), self.k))
        self.peers = self.next + (self.other_x, self.other_c)
        self.final = ring - 1

    def source(self, t, s, column, core):
        ring = self.plan.ring
        g, col, width, height, way = self.plan.pieces[t]
        place = (self.r + 2 * ring - 1 - s) % ring if way == 0 else (self.r + 1 + s) % ring
        block = 4 * self.wide_at(place) + 2 * column + core
        return self.grads[g].at[pl.ds(pl.multiple_of(block * height, 8), height), pl.ds(col, width)]

    def half(self, t, column):
        height = self.plan.pieces[t][3]
        return pl.ds(column * height, height)

    def core_copy(self, t, s, column):
        return send(self.source(t, s, column, 1 - self.c), self.stages[t].at[s, self.half(t, column)],
                    self.core_s.at[t, s, column], self.core_r.at[t, s, column], self.other_c)

    def own_load(self, t, s, slot, column):
        return pltpu.make_async_copy(self.source(t, s, column, self.c), self.own[t].at[slot, self.half(t, column)],
                                     self.load_sem.at[t, slot, column])

    def part_load(self, t, s, slot):
        return pltpu.make_async_copy(self.stages[t].at[s], self.part[t].at[slot], self.part_sem.at[t, slot])

    def ring_copy(self, t, s):
        return send(self.went[t].at[s], self.came[t].at[s], self.ring_s.at[t, s], self.ring_r.at[t, s],
                    self.next[self.plan.pieces[t][4]])

    def x_copy(self, t):
        return send(self.fin_s[t], self.fin_r[t], self.x_s.at[t], self.x_r.at[t], self.other_x)

    def each(self):
        return range(len(self.plan.pieces))

    def fetch(self, t, s, slot):
        for column in range(2):
            self.core_copy(t, s, column).wait_recv()
        self.part_load(t, s, slot).start()
        for column in range(2):
            self.own_load(t, s, slot, column).start()

    def total(self, t, s, slot):
        for column in range(2):
            self.own_load(t, s, slot, column).wait()
        self.part_load(t, s, slot).wait()
        return self.own[t][slot] + self.part[t][slot]

    def begin(self):
        for s in range(self.plan.ring):
            for t in self.each():
                for column in range(2):
                    self.core_copy(t, s, column).start()

    def load_first(self):
        for t in self.each():
            self.fetch(t, 0, 0)

    def first_hop(self):
        for t in self.each():
            self.fetch(t, 1, 1)
            self.went[t][0] = self.total(t, 0, 0).astype(BF)
            self.ring_copy(t, 0).start()

    def hop(self, s):
        slot = s % 2
        for t in self.each():
            self.fetch(t, s + 1, 1 - slot)
            value = self.total(t, s, slot)
            self.ring_copy(t, s - 1).wait_recv()
            self.went[t][s] = (value + self.came[t][s - 1].astype(F32)).astype(BF)
            self.ring_copy(t, s).start()

    def end_ring(self, t):
        final, height = self.final, self.plan.pieces[t][3]
        value = self.total(t, final, final % 2)
        self.ring_copy(t, final - 1).wait_recv()
        value = value + self.came[t][final - 1].astype(F32)
        self.last[t][0] = value[:height]
        self.last[t][1] = value[height:]

    def leave(self):
        count = len(self.plan.pieces)
        for t in self.each():
            self.end_ring(t)
            self.outs[t][...] = self.last[t][self.x]
            self.outs[count + t][...] = self.last[t][1 - self.x].astype(BF)
        self.drain()

    def finish(self):
        for t in self.each():
            self.end_ring(t)
            self.fin_s[t][...] = self.last[t][1 - self.x].astype(BF)
            self.x_copy(t).start()
        for t in self.each():
            self.x_copy(t).wait_recv()
            value = self.last[t][self.x] + self.fin_r[t][...].astype(F32)
            put(self.outs, self.plan.places[t], value)
        for t in self.each():
            self.x_copy(t).wait_send()
        self.drain()

    def drain(self):
        for t in self.each():
            for s in range(self.final):
                self.ring_copy(t, s).wait_send()
            for s in range(self.plan.ring):
                for column in range(2):
                    self.core_copy(t, s, column).wait_send()


class Plan:
    def __init__(self, ring, inputs, pieces, places, leave, shapes=()):
        self.ring, self.inputs, self.pieces, self.places = ring, inputs, pieces, places
        count = len(pieces)
        sizes = [(height, width) for _, _, width, height, _ in pieces]
        sems, vmem = pltpu.SemaphoreType.DMA, pltpu.VMEM
        self.out_shapes = [shape_of(hw, F32) for hw in shapes]
        if leave:
            self.out_shapes = [shape_of(hw, F32) for hw in sizes] + [shape_of(hw, BF) for hw in sizes]
        self.results = len(self.out_shapes)
        self.out_shapes += [shape_of((ring, 2 * h, wd), F32) for h, wd in sizes]
        self.out_specs = [pl.BlockSpec(memory_space=pltpu.VMEM)] * self.results + [ANY] * count
        self.outputs = len(self.out_shapes)
        self.scratch = (
            [vmem((2, 2 * h, wd), F32) for h, wd in sizes]
            + [vmem((2, 2 * h, wd), F32) for h, wd in sizes]
            + [vmem((ring - 1, 2 * h, wd), BF) for h, wd in sizes]
            + [vmem((ring - 1, 2 * h, wd), BF) for h, wd in sizes]
            + [vmem((2, h, wd), F32) for h, wd in sizes]
            + [vmem((h, wd), BF) for h, wd in sizes]
            + [vmem((h, wd), BF) for h, wd in sizes]
            + [sems((count, ring))] * 2
            + [sems((count, ring, 2))] * 2
            + [sems((count,))] * 2
            + [sems((count, 2, 2)), sems((count, 2))]
        )
        self.scratches = len(self.scratch)

    def left(self, results):
        count = len(self.pieces)
        return results[:count], results[count : 2 * count]

    def steps(self, refs):
        return Sums(self, refs)


def time_plan(ring, g_in, g_out, devices):
    a, b = g_in.shape[0] // devices, g_out.shape[0] // devices
    wa, wb = g_in.shape[1] // 3, g_out.shape[1] // 3
    return Plan(ring, 2, [(0, 0, wa, a, 0), (1, 0, wb, b, 1), (0, wa, wa, a, 0), (1, wb, wb, b, 1)],
                [[(0, 0, 0, wa)], [(1, 0, 0, wb)], [(0, wa, 0, wa)], [(1, wb, 0, wb)]], True)


def attn_pieces(g, number, devices):
    return [(number, i * D, D, g.shape[0] // devices, i % 2) for i in range(4)]


def attn_places(first):
    return [[(first, i * D, 0, D)] for i in range(3)] + [[(first + 1, 0, 0, D)]]


def frame_plan(ring, g_t, g_in, g_out, devices):
    a, b = g_in.shape[0] // devices, g_out.shape[0] // devices
    wa, wb = g_in.shape[1] // 3, g_out.shape[1] // 3
    return Plan(ring, 3, attn_pieces(g_t, 0, devices) + [(1, 2 * wa, wa, a, 0), (2, 2 * wb, wb, b, 1)],
                attn_places(2) + [[(0, 2 * wa, 0, wa)], [(1, 2 * wb, 0, wb)]], True)


def last_plan(ring, g_s, devices):
    return Plan(ring, 1, attn_pieces(g_s, 0, devices), attn_places(0), False, attn_shapes(g_s, devices))


def attn_shapes(g, devices):
    return [(g.shape[0] // devices, 3 * D), (g.shape[0] // devices, D)]


def last_kernel(plan, left, made, *refs):
    places = [part for p in left for part in p.places]
    count = len(places)
    ((_,), grads, keeps, fins, (frames,), left_outs, own_outs, fins_r,
     (fin_send, fin_recv, send_sem, recv_sem), own) = split_refs(
        refs, 1, plan.inputs, count, count, 1, made, plan.outputs, count, 4)
    sums = plan.steps(grads + own_outs + own)
    early, late = EARLY_TILES * FT, LIVE - EARLY_TILES * FT
    mine, theirs = slot_for(sums.k), 4 - slot_for(sums.k)
    moves = (
        (packed(0, early, late), packed(2, early, late), sums.other_x),
        (packed(0, early, late), packed(mine, early, late), sums.other_c),
        (packed(2, 0, early), packed(theirs, 0, early), sums.other_c),
        (packed(2, early, late), packed(theirs, early, late), sums.other_c),
    )
    copies = [send(frames.at[src], frames.at[dst], send_sem.at[i], recv_sem.at[i], peer)
              for i, (src, dst, peer) in enumerate(moves)]

    def fin_copy(t):
        return send(fins[t], fins_r[t], fin_send.at[t], fin_recv.at[t], sums.other_x)

    greet(sums.peers)
    sums.begin()
    for copy in copies[:3]:
        copy.start()
    for t in range(count):
        fin_copy(t).start()
    sums.load_first()
    sums.first_hop()

    def body(s, carry):
        sums.hop(s)
        return carry

    lax.fori_loop(1, sums.final, body, 0)
    copies[0].wait_recv()
    copies[3].start()
    sums.finish()
    for t in range(count):
        fin_copy(t).wait_recv()
        value = keeps[t][...] + fins_r[t][...].astype(F32)
        put(left_outs, places[t], value)
    for t in range(count):
        fin_copy(t).wait_send()
    copies[0].wait_send()
    for copy in copies[1:]:
        copy.wait()


def scatter_last(frames, g, keeps, fins, plan, left, shapes):
    sems = pltpu.SemaphoreType.DMA
    vmem = pl.BlockSpec(memory_space=pltpu.VMEM)
    return pl.pallas_call(
        functools.partial(last_kernel, plan, left, len(shapes)),
        name="scatter_last",
        out_shape=[shape_of(frames.shape, frames.dtype)] + [shape_of(hw, F32) for hw in shapes] + plan.out_shapes,
        in_specs=[ANY] * 2 + [vmem] * len(keeps) + [ANY] * len(fins),
        out_specs=[ANY] + [vmem] * len(shapes) + plan.out_specs,
        scratch_shapes=[pltpu.VMEM(f.shape, f.dtype) for f in fins]
        + [sems((len(fins),))] * 2 + [sems((4,))] * 2 + plan.scratch,
        input_output_aliases={0: 0},
        compiler_params=pltpu.CompilerParams(
            collective_id=1, has_side_effects=True, vmem_limit_bytes=VMEM_LIMIT
        ),
    )(frames, g, *keeps, *fins)


def tuned(mesh):
    wide, n = mesh.shape["wide"], mesh.shape["narrow"]
    if n != 4 or wide != 2 * GRID or D % (8 * wide * n):
        return False
    for w in range(wide):
        for k in range(n):
            device = mesh.devices[w, k]
            here = (getattr(device, "coords", None), getattr(device, "core_on_chip", None))
            if here[0] is None or tuple(here[0]) != (k // 2, w % 2, w // 2) or here[1] != k % 2:
                return False
    return True


def exchange(x):
    return lax.all_to_all(x, ALL, split_axis=0, concat_axis=0, tiled=True)


def shift_clips(clips, back):
    n = lax.axis_size("narrow")
    parts = [clips[0]]
    for j in range(1, n):
        step = -j if back else j
        parts.append(lax.ppermute(clips[j], "narrow", [(s, (s + step) % n) for s in range(n)]))
    return jnp.stack(parts)


def local(fast, clips, t_emb, lengths, task, w_mod, b_mod, w_qkv_s, w_o_s, b_o_s, w_qkv_t, w_o_t, b_o_t,
          w_in, b_in, w_out, b_out, cotangent):
    n = lax.axis_size("narrow")
    wide = lax.axis_size("wide")
    devices = n * wide
    part = w_mod.shape[0]
    mod_cols = w_mod.shape[1] // devices
    rank = lax.axis_index("narrow")
    slots = jnp.arange(n, dtype=jnp.int32)
    from_clip = (rank - slots) % n
    recv_len = lengths.reshape(n, n)[from_clip, slots]
    recv_task = task.reshape(n, n, FR)[from_clip, slots]
    ends = jnp.cumsum(recv_len)
    starts = ends - recv_len
    ids = jnp.arange(LIVE, dtype=jnp.int32)
    source = jnp.sum((ends[None, :] <= ids[:, None]).astype(jnp.int32), axis=1)
    within = ids - starts[source]
    pack_rows = source * FR + within
    row_choice = source * 2 + recv_task[source, within]
    frame_ids = jnp.arange(FR, dtype=jnp.int32)
    live_back = frame_ids[None, :] < recv_len[:, None]
    unpack_rows = jnp.where(live_back, starts[:, None] + frame_ids[None, :], 0).reshape(-1)
    row_id = jnp.arange(64, dtype=jnp.int32)
    col_id = jnp.arange(LANES, dtype=jnp.int32) % 64
    seg = (
        (row_id[:, None] // LIVE == col_id[None, :] // LIVE)
        & (source[row_id % LIVE][:, None] == source[col_id % LIVE][None, :])
    ).astype(F32)

    def gather(w):
        return lax.all_gather(w, ALL, axis=0, tiled=True)

    def across(value):
        return lax.ppermute(value, "narrow", [(k, (k + n // 2) % n) for k in range(n)])

    if fast:
        flat = (w_qkv_s, w_o_s, w_qkv_t, w_o_t, w_in)
        far, far_out = across(jnp.concatenate(flat, axis=1)), across(w_out)
        clips, far, far_out = lax.optimization_barrier((clips, far, far_out))
        cuts = [sum(a.shape[1] for a in flat[: i + 1]) for i in range(len(flat) - 1)]
        *far_attn, far_in = jnp.split(far, cuts, axis=1)
        frames = shift_clips(clips, False)
        wqkv_s, wo_s, wqkv_t, wo_t = gather_first(flat[:4], far_attn, wide, n)
    else:
        far_in = far_out = None
        frames = shift_clips(clips, False)
        win, wout, wqkv_t, wo_t, wqkv_s, wo_s = [gather(w) for w in (w_in, w_out, w_qkv_t, w_o_t, w_qkv_s, w_o_s)]
    frames = jnp.take(frames.reshape(n * FR, PATCHES, D), pack_rows, axis=0, mode="clip")

    wm = jnp.swapaxes(w_mod.reshape(part, devices, mod_cols), 0, 1).reshape(devices, -1)
    emb = jnp.broadcast_to(t_emb.reshape(1, -1), (devices, t_emb.size))
    small = jnp.concatenate([b_o_s, b_o_t, b_in, b_out])
    small_all = jnp.broadcast_to(small[None], (devices, small.size))
    got = exchange(jnp.concatenate([wm, emb, small_all], axis=1))
    wm_cols = got[:, : part * mod_cols].reshape(D, mod_cols)
    emb_all = got[:, part * mod_cols : part * mod_cols + t_emb.size].reshape(-1, D)
    small_got = got[:, part * mod_cols + t_emb.size :]
    b1 = b_o_s.size
    bias_s = small_got[:, :b1].reshape(1, -1).astype(F32)
    bias_t = small_got[:, b1 : 2 * b1].reshape(1, -1).astype(F32)
    bias_in = small_got[:, 2 * b1 : 2 * b1 + b_in.size].reshape(1, -1).astype(F32)
    bias_out = small_got[:, 2 * b1 + b_in.size :].reshape(1, -1).astype(F32)
    emb_f = emb_all.astype(F32)
    silu_low = (emb_f * jax.nn.sigmoid(emb_f)).astype(BF)
    mod_part = dot(silu_low, wm_cols) + b_mod.astype(F32)[None]
    mod_part = mod_part.reshape(wide, n, n, 2, mod_cols)
    mod_part = jnp.stack([jnp.roll(mod_part[:, :, c], c, axis=1) for c in range(n)], axis=2)
    mod_rows = exchange(mod_part.reshape(devices, -1)).reshape(devices, 2 * n, mod_cols)
    mod_rows = jnp.swapaxes(mod_rows, 0, 1).reshape(2 * n, 9, D)
    mod = jnp.swapaxes(mod_rows[row_choice], 0, 1)

    def carry(js, shard, other, number):
        return forward_carrier(cotangent, js, shard, other, wide, n, number) if fast else None

    *half, x1, qkv1, o1, a1 = run_frame_forward(
        frames, mod, wqkv_s, wo_s, bias_s, carry((2,), w_in, far_in, 2))
    *odd, x2, qkv2, o2, a2 = run_time_forward(
        x1, mod, seg, wqkv_t, wo_t, bias_t, carry((1, 3), w_out, far_out, 3))
    if fast:
        (half, win), (odd, wout) = half, odd
        cots = jnp.stack([cotangent[0], odd[0], half[0], odd[1]])
    else:
        cots = shift_clips(cotangent, False)
    dy = run_turn_frames(cots.reshape(n * FR, PATCHES, D), pack_rows)
    out, dx2, g_in, g_out, gb_in, gb_out, dmod3 = run_mlp(x2, dy, mod, win, bias_in, wout, bias_out, n if fast else 1)

    own_len = lengths.reshape(n, n)[rank]
    own_live = frame_ids[None, :] < own_len[:, None]

    def spread(frames):
        return jnp.take(frames, unpack_rows, axis=0, mode="clip").reshape(n, FR, PATCHES, D)

    def only_live(parts):
        return jnp.where(own_live[:, :, None, None], parts, jnp.zeros((), parts.dtype))

    def scatter(g):
        return lax.psum_scatter(g.astype(BF), ALL, scatter_dimension=0, tiled=True).astype(F32)

    if fast:
        ahead = lengths.reshape(n, n)[(rank + slots[:, None] - slots[None, :]) % n, slots[None, :]]
        own_start = jnp.sum(jnp.where(slots[None, :] < slots[:, None], ahead, 0), axis=1)
        own_rows = slots[:, None] * LIVE + own_start[:, None] + frame_ids[None, :]
        own_rows = jnp.where(own_live, own_rows, -1).reshape(-1)
        plan_a = time_plan(wide, g_in, g_out, devices)
        out, *got, dx1, g_t, gb_t, dmod2 = run_time_back(
            x1, dx2, mod, seg, qkv2, o2, a2, wqkv_t, wo_t, share_carrier(out, [g_in, g_out], plan_a, 4))
        keeps, fins = plan_a.left(got)
        plan_b = frame_plan(wide, g_t, g_in, g_out, devices)
        out, dx0, *got, g_s, gb_s, dmod1 = run_frame_back(
            frames, dx1, mod, qkv1, o1, a1, wqkv_s, wo_s, relay_carrier(out, [g_t, g_in, g_out], plan_b, 5))
        more_keeps, more_fins = plan_b.left(got)
        dx0, s_in, s_out, s_qkv_t, s_o_t, s_qkv_s, s_o_s = scatter_last(
            dx0, g_s, keeps + more_keeps, fins + more_fins, last_plan(wide, g_s, devices), (plan_a, plan_b),
            [w_in.shape, w_out.shape] + attn_shapes(g_t, devices))[:7]
        layer_out = run_unpack(out, own_rows).reshape(n, FR, PATCHES, D)
        grad_clips = run_unpack(dx0, own_rows).reshape(n, FR, PATCHES, D)
    else:
        dx1, g_t, gb_t, dmod2 = run_time_back(x1, dx2, mod, seg, qkv2, o2, a2, wqkv_t, wo_t)
        dx0, g_s, gb_s, dmod1 = run_frame_back(frames, dx1, mod, qkv1, o1, a1, wqkv_s, wo_s)
        layer_out = only_live(shift_clips(spread(out), True))
        grad_clips = only_live(shift_clips(spread(dx0), True))
        s_in, s_out, s_t, s_s = [scatter(g) for g in (g_in, g_out, g_t, g_s)]
        s_qkv_t, s_o_t, s_qkv_s, s_o_s = s_t[:, : 3 * D], s_t[:, 3 * D :], s_s[:, : 3 * D], s_s[:, 3 * D :]

    grad_frames = jnp.swapaxes(jnp.concatenate([dmod1, dmod2, dmod3], axis=0), 0, 1).reshape(LIVE, 9 * D)
    chooser = (row_choice[:, None] == jnp.arange(2 * n, dtype=jnp.int32)[None, :]).astype(F32)
    grad_rows = lax.dot_general(
        chooser, grad_frames, (((0,), (0,)), ((), ())), precision=lax.Precision.HIGHEST
    ).astype(BF)
    d_cols = exchange(jnp.swapaxes(grad_rows.reshape(2 * n, devices, mod_cols), 0, 1).reshape(devices, -1))
    d_cols = d_cols.reshape(wide, n, n, 2, mod_cols)
    d_cols = jnp.stack([jnp.roll(d_cols[:, :, c], -c, axis=1) for c in range(n)], axis=2)
    d_cols = d_cols.reshape(devices * 2 * n, mod_cols)
    grad_b_mod = jnp.sum(d_cols.astype(F32), axis=0)
    gwm_cols = dot_tn(silu_low, d_cols)
    g_emb = dot_nt(d_cols, wm_cols)
    gb_all = jnp.concatenate(
        [gb_s.reshape(devices, -1), gb_t.reshape(devices, -1), gb_in.reshape(devices, -1),
         gb_out.reshape(devices, -1)], axis=1)
    final = exchange(jnp.concatenate(
        [gwm_cols.reshape(devices, -1), g_emb.reshape(devices, -1), gb_all], axis=1))
    cut1 = part * mod_cols
    cut2 = cut1 + t_emb.size
    grad_w_mod = jnp.swapaxes(final[:, :cut1].reshape(devices, part, mod_cols), 0, 1).reshape(part, -1)
    emb_own = t_emb.astype(F32)
    sig = jax.nn.sigmoid(emb_own)
    grad_emb = jnp.sum(final[:, cut1:cut2], axis=0).reshape(t_emb.shape)
    grad_t_emb = (grad_emb * (sig * (1.0 + emb_own * (1.0 - sig)))).astype(BF)
    gb = jnp.sum(final[:, cut2:], axis=0)
    return (
        layer_out,
        grad_clips,
        grad_t_emb,
        grad_w_mod,
        grad_b_mod,
        s_qkv_s,
        s_o_s,
        gb[:b1],
        s_qkv_t,
        s_o_t,
        gb[b1 : 2 * b1],
        s_in,
        gb[2 * b1 : 2 * b1 + b_in.size],
        s_out,
        gb[2 * b1 + b_in.size :],
    )


def solution(mesh):
    full = P(ALL)
    placed = (full, full, P("wide"), P("wide")) + (full,) * 13
    return jax.shard_map(functools.partial(local, tuned(mesh)), mesh=mesh, in_specs=placed, out_specs=(full,) * 15, check_vma=False)
```

```python
import functools

import jax
import jax.numpy as jnp
from jax import lax
from jax.experimental import pallas as pl
from jax.experimental.pallas import tpu as pltpu
from jax.sharding import PartitionSpec as P

D = 768
HEADS = 12
HEAD = 64
FF = 3072
FR = 16
PATCHES = 64
LIVE = 2 * FR
EPS = 1e-06
BF = jnp.bfloat16
F32 = jnp.float32
ALL = ("wide", "narrow")
PAIRS = HEADS // 2
LANES = 2 * HEAD
BACK_PAIRS = 6
TILE = 512
FT = TILE // PATCHES
PT = TILE // LIVE
GRID = LIVE * PATCHES // TILE
GROUPS = TILE // 64
EARLY_TILES = GRID // 2
GELU_C = 0.7978845608028654
GELU_A = 0.044715
VMEM_LIMIT = 66 * 1000 * 1000
MESH = pl.DeviceIdType.MESH
ANY = pl.BlockSpec(memory_space=pl.ANY)


def dot(a, b):
    return lax.dot_general(a, b, (((1,), (0,)), ((), ())), preferred_element_type=F32)


def dot_nt(a, b):
    return lax.dot_general(a, b, (((1,), (1,)), ((), ())), preferred_element_type=F32)


def dot_tn(a, b):
    return lax.dot_general(a, b, (((0,), (0,)), ((), ())), preferred_element_type=F32)


def normalise(x):
    mean = jnp.mean(x, axis=-1, keepdims=True)
    centred = x - mean
    var = jnp.mean(centred * centred, axis=-1, keepdims=True)
    rstd = lax.rsqrt(var + EPS)
    return centred * rstd, rstd


def norm_back(dn, xhat, rstd):
    m1 = jnp.mean(dn, axis=-1, keepdims=True)
    m2 = jnp.mean(dn * xhat, axis=-1, keepdims=True)
    return rstd * (dn - m1 - xhat * m2)


def lane_masks():
    lane = lax.broadcasted_iota(jnp.int32, (64, LANES), 1)
    low_lanes = lane < HEAD
    low = jnp.where(low_lanes, 1.0, 0.0).astype(BF)
    high = jnp.where(low_lanes, 0.0, 1.0).astype(BF)
    return low_lanes, low, high


def split_heads(x, low, high):
    return jnp.concatenate([x * low, x * high], axis=0)


def softmax_keys(s, mask):
    if mask is not None:
        s = jnp.where(mask, s, -1e30)
    top = jnp.max(s, axis=0, keepdims=True)
    e = jnp.exp(s - top)
    return e * (1.0 / jnp.sum(e, axis=0, keepdims=True))


def pair_cols(part, hp):
    return slice(part * D + hp * LANES, part * D + (hp + 1) * LANES)


def attend(qkv_ref, o_ref, mask):
    low_lanes, low, high = lane_masks()
    scale = HEAD ** (-0.5)

    def body(g, carry):
        rows = pl.ds(pl.multiple_of(g * 64, 64), 64)
        pairs = range(PAIRS)
        s = [dot_nt(qkv_ref[rows, pair_cols(1, hp)], split_heads(qkv_ref[rows, pair_cols(0, hp)], low * scale, high * scale))
             for hp in pairs]
        p = [softmax_keys(t, mask).astype(BF) for t in s]
        r = [dot_tn(p[hp], qkv_ref[rows, pair_cols(2, hp)]) for hp in pairs]
        for hp in pairs:
            o_ref[rows, pair_cols(0, hp)] = jnp.where(low_lanes, r[hp][:64], r[hp][64:]).astype(BF)
        return carry

    lax.fori_loop(0, GROUPS, body, 0)


def attend_back(qkv_ref, do_ref, dqkv_ref, mask):
    low_lanes, low, high = lane_masks()
    scale = HEAD ** (-0.5)

    def body(g, carry):
        rows = pl.ds(pl.multiple_of(g * 64, 64), 64)
        for first in range(0, PAIRS, BACK_PAIRS):
            pairs = range(first, first + BACK_PAIRS)
            qb = [split_heads(qkv_ref[rows, pair_cols(0, hp)], low * scale, high * scale) for hp in pairs]
            dob = [split_heads(do_ref[rows, pair_cols(0, hp)], low, high) for hp in pairs]
            s = [dot_nt(qkv_ref[rows, pair_cols(1, hp)], q) for hp, q in zip(pairs, qb)]
            dp = [dot_nt(qkv_ref[rows, pair_cols(2, hp)], d) for hp, d in zip(pairs, dob)]
            p = [softmax_keys(t, mask) for t in s]
            delta = [jnp.sum(a * b, axis=0, keepdims=True) for a, b in zip(p, dp)]
            ds = [(a * (b - c)).astype(BF) for a, b, c in zip(p, dp, delta)]
            dv = [dot(a.astype(BF), d) for a, d in zip(p, dob)]
            dk = [dot(a, q) for a, q in zip(ds, qb)]
            r = [dot_tn(a, qkv_ref[rows, pair_cols(1, hp)]) for hp, a in zip(pairs, ds)]
            for i, hp in enumerate(pairs):
                dqkv_ref[rows, pair_cols(2, hp)] = dv[i].astype(BF)
                dqkv_ref[rows, pair_cols(1, hp)] = dk[i].astype(BF)
                dq = jnp.where(low_lanes, r[i][:64], r[i][64:]) * scale
                dqkv_ref[rows, pair_cols(0, hp)] = dq.astype(BF)
        return carry

    lax.fori_loop(0, GROUPS, body, 0)


def swap_major(value, scratch, out_ref, first, second):
    for b in range(D // 128):
        cols = slice(b * 128, (b + 1) * 128)
        for i in range(first):
            scratch[b, pl.ds(i, second, stride=first), :] = value[i * second : (i + 1) * second, cols]
        out_ref[:, :, cols] = scratch[b].reshape(second, first, 128).astype(out_ref.dtype)


def frames_of(refs):
    return jnp.concatenate([r[0] for r in refs], axis=0).astype(F32)


def per_frame(piece):
    return jnp.broadcast_to(piece[:, None, :], (FT, PATCHES, D)).reshape(TILE, D)


def per_patch(piece):
    return jnp.broadcast_to(piece[None], (PT, LIVE, D)).reshape(TILE, D)


def sum_patches(value):
    return jnp.sum(value.reshape(FT, PATCHES, D), axis=1)


def sum_groups(value):
    return jnp.sum(value.reshape(PT, LIVE, D), axis=0)


def attn_mask(seg_ref):
    return seg_ref[...] > 0.0


def no_tick(place):
    pass


def frame_forward(frames, mod, wqkv, wo, bo, x1t, qkv, o, a1, scratch, tick=no_tick):
    x = frames[...].reshape(TILE, D).astype(F32)
    xhat, _ = normalise(x)
    h = (xhat * (1.0 + per_frame(mod[1])) + per_frame(mod[0])).astype(BF)
    qkv[...] = dot(h, wqkv[...]).astype(BF)
    tick(0)
    attend(qkv, o, None)
    tick(1)
    branch = dot(o[...], wo[...]) + bo[...]
    a1[...] = branch
    x1 = x + per_frame(mod[2]) * branch
    swap_major(x1, scratch, x1t, FT, PATCHES)


def turn_frames(rows_ref, *refs):
    x_refs, (out, scratch) = refs[:FT], refs[FT:]
    swap_major(frames_of(x_refs), scratch, out, FT, PATCHES)


def time_forward(x1, mod, seg, wqkv, wo, bo, x2, qkv, o, a2, tick=no_tick):
    x = x1[...].reshape(TILE, D)
    xhat, _ = normalise(x)
    h = (xhat * (1.0 + per_patch(mod[1])) + per_patch(mod[0])).astype(BF)
    qkv[...] = dot(h, wqkv[...]).astype(BF)
    tick(0)
    attend(qkv, o, attn_mask(seg))
    tick(1)
    branch = dot(o[...], wo[...]) + bo[...]
    a2[...] = branch
    x2[...] = (x + per_patch(mod[2]) * branch).reshape(PT, LIVE, D)


def mlp_both(x2, dy, mod, win, bin_, wout, bout, out, dx2, gwin, gwout, gbin, gbout, dmod, scratch):
    first = pl.program_id(0) == 0

    @pl.when(first)
    def _():
        gwin[...] = jnp.zeros_like(gwin)
        gwout[...] = jnp.zeros_like(gwout)
        gbin[...] = jnp.zeros_like(gbin)
        gbout[...] = jnp.zeros_like(gbout)
        dmod[...] = jnp.zeros_like(dmod)

    x = x2[...].reshape(TILE, D)
    xhat, rstd = normalise(x)
    h = (xhat * (1.0 + per_patch(mod[1])) + per_patch(mod[0])).astype(BF)
    gate = per_patch(mod[2])
    grad = dy[...].reshape(TILE, D)
    da = (grad * gate).astype(BF)
    gbout[...] += jnp.sum(da.astype(F32), axis=0, keepdims=True)
    branch = jnp.zeros((TILE, D), F32) + bout[...]
    dh = jnp.zeros((TILE, D), F32)
    for j in range(FF // D):
        cols = slice(j * D, (j + 1) * D)
        u = dot(h, win[:, cols]) + bin_[:, cols]
        u2 = u * u
        t = jnp.tanh(GELU_C * u * (1.0 + GELU_A * u2))
        half = 0.5 * (1.0 + t)
        g = (u * half).astype(BF)
        slope = half + (0.5 * GELU_C) * u * (1.0 - t * t) * (1.0 + 3.0 * GELU_A * u2)
        branch = branch + dot(g, wout[cols, :])
        du = (dot_nt(da, wout[cols, :]) * slope).astype(BF)
        gwout[cols, :] += dot_tn(g, da)
        gbin[:, cols] += jnp.sum(du.astype(F32), axis=0, keepdims=True)
        gwin[:, cols] += dot_tn(h, du)
        dh = dh + dot_nt(du, win[:, cols])
    swap_major(x + gate * branch, scratch, out, PT, LIVE)
    dmod[2] += sum_groups(grad * branch)
    dmod[0] += sum_groups(dh)
    dmod[1] += sum_groups(dh * xhat)
    back = norm_back(dh * (1.0 + per_patch(mod[1])), xhat, rstd)
    dx2[...] = (grad + back).reshape(PT, LIVE, D)


def attn_back_tile(x, grad, shift, scale, gate, branch, qkv, o, wqkv, wo, gw, gbo, do, dqkv, mask, tick):
    first = pl.program_id(0) == 0

    @pl.when(first)
    def _():
        gw[...] = jnp.zeros_like(gw)
        gbo[...] = jnp.zeros_like(gbo)

    da = (grad * gate).astype(BF)
    do[...] = dot_nt(da, wo[...]).astype(BF)
    gw[:, 3 * D :] += dot_tn(o[...], da)
    gbo[...] += jnp.sum(da.astype(F32), axis=0, keepdims=True)
    tick(0)
    attend_back(qkv, do, dqkv, mask)
    tick(1)
    xhat, rstd = normalise(x)
    h = (xhat * (1.0 + scale) + shift).astype(BF)
    dh = jnp.zeros((TILE, D), F32)
    for j in range(3):
        cols = slice(j * D, (j + 1) * D)
        part = dqkv[:, cols]
        gw[:, cols] += dot_tn(h, part)
        dh = dh + dot_nt(part, wqkv[:, cols])
    dx = grad + norm_back(dh * (1.0 + scale), xhat, rstd)
    return dx, dh, dh * xhat, grad * branch


def time_back(x1, dx2, mod, seg, qkv, o, a2, wqkv, wo, dx1, gw, gbo, dmod, do, dqkv, scratch, tick=no_tick):
    @pl.when(pl.program_id(0) == 0)
    def _():
        dmod[...] = jnp.zeros_like(dmod)

    dx, d_shift, d_scale, d_gate = attn_back_tile(
        x1[...].reshape(TILE, D), dx2[...].reshape(TILE, D), per_patch(mod[0]), per_patch(mod[1]),
        per_patch(mod[2]), a2[...], qkv, o, wqkv, wo, gw, gbo, do, dqkv, attn_mask(seg), tick)
    dmod[0] += sum_groups(d_shift)
    dmod[1] += sum_groups(d_scale)
    dmod[2] += sum_groups(d_gate)
    swap_major(dx, scratch, dx1, PT, LIVE)


def frame_back(frames, dx1, mod, qkv, o, a1, wqkv, wo, dx0, gw, gbo, dmod, do, dqkv, tick=no_tick):
    dx, d_shift, d_scale, d_gate = attn_back_tile(
        frames[...].reshape(TILE, D).astype(F32), dx1[...].reshape(TILE, D), per_frame(mod[0]), per_frame(mod[1]),
        per_frame(mod[2]), a1[...], qkv, o, wqkv, wo, gw, gbo, do, dqkv, None, tick)
    dmod[0] = sum_patches(d_shift)
    dmod[1] = sum_patches(d_scale)
    dmod[2] = sum_patches(d_gate)
    dx0[...] = dx.reshape(FT, PATCHES, D).astype(BF)


def frame_specs():
    return [
        pl.BlockSpec((1, PATCHES, D), functools.partial(lambda j, i, rows: (rows[FT * i + j], 0, 0), j))
        for j in range(FT)
    ]


def whole(shape):
    return pl.BlockSpec(shape, lambda i, *_: (0,) * len(shape), pipeline_mode=pl.Buffered(1))


def tiles(shape, dim):
    return pl.BlockSpec(shape, lambda i, *_: tuple(i if a == dim else 0 for a in range(len(shape))))


def piece_spec(number, frames, by_tile):
    return pl.BlockSpec((3, frames, D), lambda i, *_: (number, i if by_tile else 0, 0))


ROWS = tiles((TILE, D), 0)
ROWS3 = tiles((TILE, 3 * D), 0)
TURNED = tiles((PT, LIVE, D), 0)


TURN = pltpu.VMEM((D // 128, TILE, 128), F32)


def shape_of(shape, dtype):
    return jax.ShapeDtypeStruct(shape, dtype)


class Carrier:
    def __init__(self, wrap, number, ins, outs, out_specs, scratch, aliases=None):
        self.wrap, self.number, self.ins, self.outs = wrap, number, ins, outs
        self.out_specs, self.scratch, self.aliases = out_specs, scratch, aliases or {}


def call(kernel, name, ins, in_specs, outs, out_specs, scratch, flops, prefetch=None, carrier=None):
    moved = sum(a.size * a.dtype.itemsize for a in tuple(ins) + tuple(outs))
    params, aliases = {}, {}
    if carrier is not None:
        kernel = functools.partial(carrier.wrap, kernel, len(ins), len(outs), len(scratch))
        ins, in_specs = carrier.ins + ins, [ANY] * len(carrier.ins) + in_specs
        outs, out_specs = carrier.outs + outs, carrier.out_specs + out_specs
        scratch = scratch + carrier.scratch
        params, aliases = dict(collective_id=carrier.number, has_side_effects=True), carrier.aliases
    grid_spec = pltpu.PrefetchScalarGridSpec(
        num_scalar_prefetch=0 if prefetch is None else 1,
        grid=(GRID,),
        in_specs=in_specs,
        out_specs=out_specs,
        scratch_shapes=scratch,
    )
    fn = pl.pallas_call(
        kernel,
        grid_spec=grid_spec,
        out_shape=outs,
        name=name,
        input_output_aliases=aliases,
        cost_estimate=pl.CostEstimate(flops=flops, bytes_accessed=moved, transcendentals=0),
        compiler_params=pltpu.CompilerParams(
            dimension_semantics=("arbitrary",), vmem_limit_bytes=VMEM_LIMIT, **params
        ),
    )
    return fn(*ins) if prefetch is None else fn(prefetch, *ins)


def split_refs(refs, *counts):
    parts = []
    for count in counts:
        parts.append(refs[:count])
        refs = refs[count:]
    return parts + [refs]


def forward_carrier(clips, js, shard, far, ring, n, number):
    held = Gather.scratch([shard], ring)

    def wrap(kernel, n_in, n_out, n_scratch, *refs):
        (src, part, other), ins, (dst, full), outs, scratch, (send_sem, recv_sem), own = split_refs(
            refs, 3, n_in, 2, n_out, n_scratch, 2)
        step = pl.program_id(0)
        gather = Gather(ring, (shard.shape[0],), (part, other, full) + own)
        targets = [(gather.w, (gather.k + j) % n) for j in js]
        copies = [send(src.at[j], dst.at[i], send_sem.at[i], recv_sem.at[i], targets[i]) for i, j in enumerate(js)]

        @pl.when(step == 0)
        def _():
            greet(tuple(targets) + gather.peers)
            gather.begin()
            for copy in copies:
                copy.start()

        def tick(place):
            if place == 0:
                @pl.when(step == 0)
                def _():
                    gather.second()

                @pl.when(step > 0)
                def _():
                    gather.hop(2 * step)
            else:
                gather.hop(2 * step + 1)

        kernel(*ins, *outs, *scratch, tick=tick)

        @pl.when(step == GRID - 1)
        def _():
            gather.finish()
            for copy in copies:
                copy.wait()

    sems = pltpu.SemaphoreType.DMA((len(js),))
    return Carrier(wrap, number, [clips, shard, far],
                   [shape_of((len(js),) + clips.shape[1:], clips.dtype)] + Gather.shapes([shard], ring * n),
                   [ANY, ANY], [sems, sems] + held)


def packed(slot, first=0, count=LIVE):
    return pl.ds(pl.multiple_of(slot * LIVE + first, 8), count)


def slot_for(k):
    return 3 - 2 * (k % 2)


def ticks(sums, step):
    def tick(place):
        @pl.when(step == 0)
        def _():
            if place == 0:
                sums.load_first()
            else:
                sums.first_hop()

        @pl.when(step > 0)
        def _():
            sums.hop(2 * step - 1 + place)

    return tick


def patches_of(frames, slot, i):
    return frames.at[packed(slot), pl.ds(pl.multiple_of(i * PT, PT), PT)]


def out_carrier(slots, number):
    def wrap(kernel, n_in, n_out, n_scratch, *refs):
        ins, (dst,), outs, scratch, (send_sem, recv_sem, keep, buf) = split_refs(refs, n_in, 1, n_out, n_scratch)
        step = pl.program_id(0)
        w, k = lax.axis_index("wide"), lax.axis_index("narrow")
        other_x, other_c = (w, (k + 2) % 4), (w, k + 1 - 2 * (k % 2))

        def tile(i):
            return [send(buf.at[i], patches_of(dst, slot, i), send_sem.at[a, i], recv_sem.at[a, i], peer)
                    for a, (slot, peer) in enumerate(((slot_for(k), other_c), (2, other_x)))]

        def store(i):
            return pltpu.make_async_copy(buf.at[i], patches_of(dst, 0, i), keep.at[i])

        @pl.when(step == 0)
        def _():
            greet((other_x, other_c))

        kernel(*ins, buf.at[step], *outs, *scratch)
        store(step).start()

        @pl.when(step < GRID - 1)
        def _():
            for copy in tile(step):
                copy.start()

        @pl.when(step == GRID - 1)
        def _():
            for i in range(GRID):
                store(i).wait()
            for i in range(GRID - 1):
                for copy in tile(i):
                    copy.wait()

    sems = pltpu.SemaphoreType.DMA
    return Carrier(wrap, number, [], [shape_of((slots * LIVE, PATCHES, D), BF)], [ANY],
                   [sems((2, GRID - 1)), sems((2, GRID - 1)), sems((GRID,)), pltpu.VMEM((GRID, LIVE, PT, D), BF)])


def share_carrier(frames, grads, plan, number):
    n_grads = len(grads)

    def wrap(kernel, n_in, n_out, n_scratch, *refs):
        (_,), grad_refs, ins, (dst,), left, outs, scratch, (send_sem, recv_sem), own = split_refs(
            refs, 1, n_grads, n_in, 1, plan.outputs, n_out, n_scratch, 2)
        step = pl.program_id(0)
        sums = plan.steps(grad_refs + left + own)
        targets = ((slot_for(sums.k), sums.other_c), (2, sums.other_x))
        final = GRID - 1
        copies = [send(patches_of(dst, 0, final), patches_of(dst, slot, final), send_sem.at[i], recv_sem.at[i], peer)
                  for i, (slot, peer) in enumerate(targets)]

        @pl.when(step == 0)
        def _():
            greet(sums.peers)
            sums.begin()
            for copy in copies:
                copy.start()

        kernel(*ins, *outs, *scratch, tick=ticks(sums, step))

        @pl.when(step == GRID - 1)
        def _():
            sums.leave()
            for copy in copies:
                copy.wait()

    sems = pltpu.SemaphoreType.DMA((2,))
    return Carrier(wrap, number, [frames] + grads, [shape_of(frames.shape, frames.dtype)] + plan.out_shapes,
                   [ANY] + plan.out_specs, [sems, sems] + plan.scratch, {0: 0})


def tile_copies(k, other_c, other_x, src, dst, i, send_sem, recv_sem):
    return [send(src, dst.at[packed(slot, i * FT, FT)], send_sem.at[a, i], recv_sem.at[a, i], peer)
            for a, (slot, peer) in enumerate(((slot_for(k), other_c), (2, other_x)))]


def relay_carrier(frames, grads, plan, number):
    n_grads = len(grads)

    def wrap(kernel, n_in, n_out, n_scratch, *refs):
        (_,), grad_refs, ins, (dst, made), left, outs, scratch, (send_sem, recv_sem, tile_s, tile_r, keep, buf), own = (
            split_refs(refs, 1, n_grads, n_in, 2, plan.outputs, n_out, n_scratch, 6))
        step = pl.program_id(0)
        sums = plan.steps(grad_refs + left + own)
        relay = send(dst.at[packed(2)], dst.at[packed(4 - slot_for(sums.k))],
                     send_sem.at[0], recv_sem.at[0], sums.other_c)

        def tile(i):
            return tile_copies(sums.k, sums.other_c, sums.other_x, buf.at[i], made, i, tile_s, tile_r)

        def store(i):
            return pltpu.make_async_copy(buf.at[i], made.at[packed(0, i * FT, FT)], keep.at[i])

        @pl.when(step == 0)
        def _():
            greet(sums.peers)
            sums.begin()
            relay.start()

        kernel(*ins, buf.at[step], *outs, *scratch, tick=ticks(sums, step))
        store(step).start()

        @pl.when(step < EARLY_TILES)
        def _():
            for copy in tile(step):
                copy.start()

        @pl.when(step == GRID - 1)
        def _():
            sums.leave()
            relay.wait()
            for i in range(GRID):
                store(i).wait()
            for i in range(EARLY_TILES):
                for copy in tile(i):
                    copy.wait()

    sems = pltpu.SemaphoreType.DMA
    shape = shape_of(frames.shape, frames.dtype)
    return Carrier(wrap, number, [frames] + grads, [shape, shape] + plan.out_shapes, [ANY, ANY] + plan.out_specs,
                   [sems((1,)), sems((1,)), sems((2, EARLY_TILES)), sems((2, EARLY_TILES)), sems((GRID,)),
                    pltpu.VMEM((GRID, FT, PATCHES, D), BF)] + plan.scratch, {0: 0})


TOKENS = LIVE * PATCHES


def run_frame_forward(frames, mod, wqkv, wo, bo, carrier=None):
    return call(
        frame_forward, "frame_forward",
        [frames, mod, wqkv, wo, bo],
        [tiles((FT, PATCHES, D), 0), piece_spec(0, FT, True), whole((D, 3 * D)), whole((D, D)), whole((1, D))],
        [shape_of((PATCHES, LIVE, D), F32), shape_of((TOKENS, 3 * D), BF), shape_of((TOKENS, D), BF),
         shape_of((TOKENS, D), F32)],
        [tiles((PATCHES, FT, D), 1), ROWS3, ROWS, ROWS],
        [TURN],
        2 * TOKENS * D * 4 * D, carrier=carrier)


def run_turn_frames(frames, rows):
    return call(
        turn_frames, "turn_frames", [frames] * FT, frame_specs(),
        [shape_of((PATCHES, LIVE, D), F32)], [tiles((PATCHES, FT, D), 1)],
        [TURN], 1000, rows)[0]


def unpack_frames(rows_ref, *refs):
    x_refs, (out,) = refs[:FT], refs[FT:]
    first = pl.program_id(0) * FT
    for j in range(FT):
        x = x_refs[j][0]
        out[j] = jnp.where(rows_ref[first + j] >= 0, x, jnp.zeros_like(x))


def run_unpack(frames, rows):
    specs = [
        pl.BlockSpec((1, PATCHES, D), functools.partial(lambda j, i, r: (jnp.maximum(r[FT * i + j], 0), 0, 0), j))
        for j in range(FT)
    ]
    return pl.pallas_call(
        unpack_frames,
        grid_spec=pltpu.PrefetchScalarGridSpec(
            num_scalar_prefetch=1, grid=(rows.shape[0] // FT,), in_specs=specs, out_specs=tiles((FT, PATCHES, D), 0)),
        out_shape=shape_of((rows.shape[0], PATCHES, D), frames.dtype),
        name="unpack_frames",
        cost_estimate=pl.CostEstimate(flops=1000, bytes_accessed=4 * rows.shape[0] * PATCHES * D, transcendentals=0),
        compiler_params=pltpu.CompilerParams(dimension_semantics=("arbitrary",)),
    )(rows, *[frames] * FT)


def run_time_forward(x1, mod, seg, wqkv, wo, bo, carrier=None):
    return call(
        time_forward, "time_forward",
        [x1, mod, seg, wqkv, wo, bo],
        [TURNED, piece_spec(1, LIVE, False), whole((64, LANES)), whole((D, 3 * D)), whole((D, D)),
         whole((1, D))],
        [shape_of((PATCHES, LIVE, D), F32), shape_of((TOKENS, 3 * D), BF), shape_of((TOKENS, D), BF),
         shape_of((TOKENS, D), F32)],
        [TURNED, ROWS3, ROWS, ROWS],
        [], 2 * TOKENS * D * 4 * D, carrier=carrier)


def run_mlp(x2, dy, mod, win, bin_, wout, bout, carrier=None):
    frames_out = [] if carrier else [shape_of((LIVE, PATCHES, D), BF)]
    frames_spec = [] if carrier else [tiles((LIVE, PT, D), 1)]
    return call(
        mlp_both, "mlp_both",
        [x2, dy, mod, win, bin_, wout, bout],
        [TURNED, TURNED, piece_spec(2, LIVE, False), whole((D, FF)), whole((1, FF)), whole((FF, D)),
         whole((1, D))],
        frames_out + [shape_of((PATCHES, LIVE, D), F32), shape_of((D, FF), F32),
         shape_of((FF, D), F32), shape_of((1, FF), F32), shape_of((1, D), F32), shape_of((3, LIVE, D), F32)],
        frames_spec + [TURNED, whole((D, FF)), whole((FF, D)), whole((1, FF)), whole((1, D)),
         whole((3, LIVE, D))],
        [TURN],
        6 * 2 * TOKENS * D * FF, carrier=carrier)


def run_time_back(x1, dx2, mod, seg, qkv, o, a2, wqkv, wo, carrier=None):
    return call(
        time_back, "time_back",
        [x1, dx2, mod, seg, qkv, o, a2, wqkv, wo],
        [TURNED, TURNED, piece_spec(1, LIVE, False), whole((64, LANES)), ROWS3, ROWS, ROWS,
         whole((D, 3 * D)), whole((D, D))],
        [shape_of((LIVE, PATCHES, D), F32), shape_of((D, 4 * D), F32), shape_of((1, D), F32), shape_of((3, LIVE, D), F32)],
        [tiles((LIVE, PT, D), 1), whole((D, 4 * D)), whole((1, D)), whole((3, LIVE, D))],
        [pltpu.VMEM((TILE, D), BF), pltpu.VMEM((TILE, 3 * D), BF), TURN],
        2 * 2 * TOKENS * D * 4 * D, carrier=carrier)


def run_frame_back(frames, dx1, mod, qkv, o, a1, wqkv, wo, carrier=None):
    frames_out = [] if carrier else [shape_of((LIVE, PATCHES, D), BF)]
    frames_spec = [] if carrier else [tiles((FT, PATCHES, D), 0)]
    return call(
        frame_back, "frame_back",
        [frames, dx1, mod, qkv, o, a1, wqkv, wo],
        [tiles((FT, PATCHES, D), 0), tiles((FT, PATCHES, D), 0), piece_spec(0, FT, True), ROWS3, ROWS, ROWS,
                         whole((D, 3 * D)), whole((D, D))],
        frames_out + [shape_of((D, 4 * D), F32), shape_of((1, D), F32), shape_of((3, LIVE, D), F32)],
        frames_spec + [whole((D, 4 * D)), whole((1, D)), piece_spec(0, FT, True)],
        [pltpu.VMEM((TILE, D), BF), pltpu.VMEM((TILE, 3 * D), BF)],
        2 * 2 * TOKENS * D * 4 * D, carrier=carrier)


def place_of(wide):
    ring = wide
    turn = ring // 2
    w = lax.axis_index("wide")
    k = lax.axis_index("narrow")
    z, y = w // 2, w % 2
    r = z + y * (ring - 1 - 2 * z)

    def wide_at(position):
        side = position // turn
        return 2 * ((1 - side) * position + side * (ring - 1 - position)) + side

    return w, k, r, k // 2, k % 2, wide_at


def greet(peers):
    barrier = pltpu.get_barrier_semaphore()
    for peer in peers:
        pl.semaphore_signal(barrier, inc=1, device_id=peer, device_id_type=MESH)
    pl.semaphore_wait(barrier, len(peers))


def send(src, dst, send_sem, recv_sem, peer):
    return pltpu.make_async_remote_copy(
        src_ref=src, dst_ref=dst, send_sem=send_sem, recv_sem=recv_sem, device_id=peer, device_id_type=MESH
    )


class Gather:
    def __init__(self, ring, heights, refs):
        count = len(heights)
        self.ring, self.heights, self.count = ring, heights, count
        near, far, self.full, near_bufs, far_bufs, sems = split_refs(refs, count, count, count, count, count)
        self.shards, self.bufs = (near, far), (near_bufs, far_bufs)
        (self.ring_s, self.ring_r, self.core_s, self.core_r, self.load_sem, self.keep_sem) = sems
        self.w, self.k, self.r, self.x, self.c, self.wide_at = place_of(ring)
        self.other_c = (self.w, 2 * self.x + 1 - self.c)
        self.next = ((self.wide_at((self.r + 1) % ring), self.k), (self.wide_at((self.r + ring - 1) % ring), self.k))
        self.peers = self.next + (self.other_c,)

    @staticmethod
    def scratch(shards, ring):
        count, sems = len(shards), pltpu.SemaphoreType.DMA
        bufs = [pltpu.VMEM(a.shape, a.dtype) for a in shards]
        return bufs + bufs + [sems((count, 2, ring))] * 4 + [sems((count, 2))] * 2

    @staticmethod
    def shapes(shards, devices):
        return [shape_of((a.shape[0] * devices, a.shape[1]), a.dtype) for a in shards]

    def way(self, t, b):
        return (t + b) % 2

    def block(self, t, b, s):
        r, ring = self.r, self.ring
        place = (r + ring - s) % ring if self.way(t, b) == 0 else (r + s) % ring
        column = self.x if b == 0 else 1 - self.x
        block = 4 * self.wide_at(place) + 2 * column + self.c
        return self.full[t].at[pl.ds(pl.multiple_of(block * self.heights[t], 8), self.heights[t])]

    def ring_copy(self, t, b, s, src=None):
        dst = self.block(t, b, s)
        return send(dst if src is None else src, dst, self.ring_s.at[t, b, s], self.ring_r.at[t, b, s],
                    self.next[self.way(t, b)])

    def core_copy(self, t, b, s, src=None):
        dst = self.block(t, b, s)
        return send(dst if src is None else src, dst, self.core_s.at[t, b, s], self.core_r.at[t, b, s], self.other_c)

    def load(self, t, b):
        return pltpu.make_async_copy(self.shards[b][t], self.bufs[b][t], self.load_sem.at[t, b])

    def keep(self, t, b):
        return pltpu.make_async_copy(self.bufs[b][t], self.block(t, b, 0), self.keep_sem.at[t, b])

    def each(self):
        return [(t, b) for b in range(2) for t in range(self.count)]

    def begin(self):
        for t, b in self.each():
            self.ring_copy(t, b, 0, self.shards[b][t]).start()
        for t, b in self.each():
            self.core_copy(t, b, 0, self.shards[b][t]).start()
            self.load(t, b).start()

    def second(self):
        for t, b in self.each():
            self.load(t, b).wait()
            self.keep(t, b).start()

    def hop(self, s):
        for b in range(2):
            for t in range(self.count):
                self.ring_copy(t, b, s - 1).wait_recv()

                @pl.when(s < self.ring - 1)
                def _():
                    self.ring_copy(t, b, s).start()

                self.core_copy(t, b, s).start()

    def finish(self):
        for t, b in self.each():
            self.keep(t, b).wait()
            for s in range(self.ring):
                if s < self.ring - 1:
                    self.ring_copy(t, b, s).wait_send()
                self.core_copy(t, b, s).wait()


def gather_kernel(ring, heights, *refs):
    gather = Gather(ring, heights, refs)
    greet(gather.peers)
    gather.begin()
    gather.second()

    def body(s, carry):
        gather.hop(s)
        return carry

    lax.fori_loop(1, ring, body, 0)
    gather.finish()


def gather_first(shards, far, ring, n):
    heights = tuple(a.shape[0] for a in shards)
    return pl.pallas_call(
        functools.partial(gather_kernel, ring, heights),
        name="gather_first",
        out_shape=Gather.shapes(shards, ring * n),
        in_specs=[ANY] * (2 * len(shards)),
        out_specs=[ANY] * len(shards),
        scratch_shapes=Gather.scratch(shards, ring),
        compiler_params=pltpu.CompilerParams(collective_id=0, has_side_effects=True),
    )(*shards, *far)


def put(outs, places, value):
    for o, out_col, col, width in places:
        outs[o][:, out_col : out_col + width] = value[:, col : col + width]


class Sums:
    def __init__(self, plan, refs):
        self.plan, count = plan, len(plan.pieces)
        self.grads, refs = refs[: plan.inputs], refs[plan.inputs :]
        self.outs, refs = refs[: plan.results], refs[plan.results :]
        self.stages, refs = refs[:count], refs[count:]
        self.own, self.part, self.came, self.went, self.last, self.fin_s, self.fin_r = (
            refs[i * count : (i + 1) * count] for i in range(7)
        )
        (self.ring_s, self.ring_r, self.core_s, self.core_r, self.x_s, self.x_r, self.load_sem,
         self.part_sem) = refs[7 * count :]
        ring = plan.ring
        self.w, self.k, self.r, self.x, self.c, self.wide_at = place_of(ring)
        self.other_x = (self.w, 2 * (1 - self.x) + self.c)
        self.other_c = (self.w, 2 * self.x + 1 - self.c)
        self.next = ((self.wide_at((self.r + 1) % ring), self.k), (self.wide_at((self.r + ring - 1) % ring), self.k))
        self.peers = self.next + (self.other_x, self.other_c)
        self.final = ring - 1

    def source(self, t, s, column, core):
        ring = self.plan.ring
        g, col, width, height, way = self.plan.pieces[t]
        place = (self.r + 2 * ring - 1 - s) % ring if way == 0 else (self.r + 1 + s) % ring
        block = 4 * self.wide_at(place) + 2 * column + core
        return self.grads[g].at[pl.ds(pl.multiple_of(block * height, 8), height), pl.ds(col, width)]

    def half(self, t, column):
        height = self.plan.pieces[t][3]
        return pl.ds(column * height, height)

    def core_copy(self, t, s, column):
        return send(self.source(t, s, column, 1 - self.c), self.stages[t].at[s, self.half(t, column)],
                    self.core_s.at[t, s, column], self.core_r.at[t, s, column], self.other_c)

    def own_load(self, t, s, slot, column):
        return pltpu.make_async_copy(self.source(t, s, column, self.c), self.own[t].at[slot, self.half(t, column)],
                                     self.load_sem.at[t, slot, column])

    def part_load(self, t, s, slot):
        return pltpu.make_async_copy(self.stages[t].at[s], self.part[t].at[slot], self.part_sem.at[t, slot])

    def ring_copy(self, t, s):
        return send(self.went[t].at[s], self.came[t].at[s], self.ring_s.at[t, s], self.ring_r.at[t, s],
                    self.next[self.plan.pieces[t][4]])

    def x_copy(self, t):
        return send(self.fin_s[t], self.fin_r[t], self.x_s.at[t], self.x_r.at[t], self.other_x)

    def each(self):
        return range(len(self.plan.pieces))

    def fetch(self, t, s, slot):
        for column in range(2):
            self.core_copy(t, s, column).wait_recv()
        self.part_load(t, s, slot).start()
        for column in range(2):
            self.own_load(t, s, slot, column).start()

    def total(self, t, s, slot):
        for column in range(2):
            self.own_load(t, s, slot, column).wait()
        self.part_load(t, s, slot).wait()
        return self.own[t][slot] + self.part[t][slot]

    def begin(self):
        for s in range(self.plan.ring):
            for t in self.each():
                for column in range(2):
                    self.core_copy(t, s, column).start()

    def load_first(self):
        for t in self.each():
            self.fetch(t, 0, 0)

    def first_hop(self):
        for t in self.each():
            self.fetch(t, 1, 1)
            self.went[t][0] = self.total(t, 0, 0).astype(BF)
            self.ring_copy(t, 0).start()

    def hop(self, s):
        slot = s % 2
        for t in self.each():
            self.fetch(t, s + 1, 1 - slot)
            value = self.total(t, s, slot)
            self.ring_copy(t, s - 1).wait_recv()
            self.went[t][s] = (value + self.came[t][s - 1].astype(F32)).astype(BF)
            self.ring_copy(t, s).start()

    def end_ring(self, t):
        final, height = self.final, self.plan.pieces[t][3]
        value = self.total(t, final, final % 2)
        self.ring_copy(t, final - 1).wait_recv()
        value = value + self.came[t][final - 1].astype(F32)
        self.last[t][0] = value[:height]
        self.last[t][1] = value[height:]

    def leave(self):
        count = len(self.plan.pieces)
        for t in self.each():
            self.end_ring(t)
            self.outs[t][...] = self.last[t][self.x]
            self.outs[count + t][...] = self.last[t][1 - self.x].astype(BF)
        self.drain()

    def finish(self):
        for t in self.each():
            self.end_ring(t)
            self.fin_s[t][...] = self.last[t][1 - self.x].astype(BF)
            self.x_copy(t).start()
        for t in self.each():
            self.x_copy(t).wait_recv()
            value = self.last[t][self.x] + self.fin_r[t][...].astype(F32)
            put(self.outs, self.plan.places[t], value)
        for t in self.each():
            self.x_copy(t).wait_send()
        self.drain()

    def drain(self):
        for t in self.each():
            for s in range(self.final):
                self.ring_copy(t, s).wait_send()
            for s in range(self.plan.ring):
                for column in range(2):
                    self.core_copy(t, s, column).wait_send()


class Plan:
    def __init__(self, ring, inputs, pieces, places, leave, shapes=()):
        self.ring, self.inputs, self.pieces, self.places = ring, inputs, pieces, places
        count = len(pieces)
        sizes = [(height, width) for _, _, width, height, _ in pieces]
        sems, vmem = pltpu.SemaphoreType.DMA, pltpu.VMEM
        self.out_shapes = [shape_of(hw, F32) for hw in shapes]
        if leave:
            self.out_shapes = [shape_of(hw, F32) for hw in sizes] + [shape_of(hw, BF) for hw in sizes]
        self.results = len(self.out_shapes)
        self.out_shapes += [shape_of((ring, 2 * h, wd), F32) for h, wd in sizes]
        self.out_specs = [pl.BlockSpec(memory_space=pltpu.VMEM)] * self.results + [ANY] * count
        self.outputs = len(self.out_shapes)
        self.scratch = (
            [vmem((2, 2 * h, wd), F32) for h, wd in sizes]
            + [vmem((2, 2 * h, wd), F32) for h, wd in sizes]
            + [vmem((ring - 1, 2 * h, wd), BF) for h, wd in sizes]
            + [vmem((ring - 1, 2 * h, wd), BF) for h, wd in sizes]
            + [vmem((2, h, wd), F32) for h, wd in sizes]
            + [vmem((h, wd), BF) for h, wd in sizes]
            + [vmem((h, wd), BF) for h, wd in sizes]
            + [sems((count, ring))] * 2
            + [sems((count, ring, 2))] * 2
            + [sems((count,))] * 2
            + [sems((count, 2, 2)), sems((count, 2))]
        )
        self.scratches = len(self.scratch)

    def left(self, results):
        count = len(self.pieces)
        return results[:count], results[count : 2 * count]

    def steps(self, refs):
        return Sums(self, refs)


def mlp_cuts(g):
    lanes = g.shape[1] // LANES
    last = lanes - lanes // 6
    return [0, (last + 1) // 2 * LANES, last * LANES, g.shape[1]]


def mlp_pieces(numbers, grads, parts, devices):
    pieces = []
    for i in parts:
        for way, (number, g) in enumerate(zip(numbers, grads)):
            cuts = mlp_cuts(g)
            pieces.append((number, cuts[i], cuts[i + 1] - cuts[i], g.shape[0] // devices, way))
    return pieces


def mlp_places(pieces):
    return [[(way, col, 0, width)] for _, col, width, _, way in pieces]


def time_plan(ring, g_in, g_out, devices):
    pieces = mlp_pieces((0, 1), (g_in, g_out), (0, 1), devices)
    return Plan(ring, 2, pieces, mlp_places(pieces), True)


def attn_pieces(g, number, devices):
    return [(number, i * D, D, g.shape[0] // devices, i % 2) for i in range(4)]


def attn_places(first):
    return [[(first, i * D, 0, D)] for i in range(3)] + [[(first + 1, 0, 0, D)]]


def frame_plan(ring, g_t, g_in, g_out, devices):
    pieces = mlp_pieces((1, 2), (g_in, g_out), (2,), devices)
    return Plan(ring, 3, attn_pieces(g_t, 0, devices) + pieces, attn_places(2) + mlp_places(pieces), True)


def last_plan(ring, g_s, devices):
    return Plan(ring, 1, attn_pieces(g_s, 0, devices), attn_places(0), False, attn_shapes(g_s, devices))


def attn_shapes(g, devices):
    return [(g.shape[0] // devices, 3 * D), (g.shape[0] // devices, D)]


def last_kernel(plan, left, made, *refs):
    places = [part for p in left for part in p.places]
    count = len(places)
    ((_,), grads, keeps, fins, (frames,), left_outs, own_outs, fins_r,
     (fin_send, fin_recv, send_sem, recv_sem), own) = split_refs(
        refs, 1, plan.inputs, count, count, 1, made, plan.outputs, count, 4)
    sums = plan.steps(grads + own_outs + own)
    early, late = EARLY_TILES * FT, LIVE - EARLY_TILES * FT
    mine, theirs = slot_for(sums.k), 4 - slot_for(sums.k)
    moves = (
        (packed(0, early, late), packed(2, early, late), sums.other_x),
        (packed(0, early, late), packed(mine, early, late), sums.other_c),
        (packed(2, 0, early), packed(theirs, 0, early), sums.other_c),
        (packed(2, early, late), packed(theirs, early, late), sums.other_c),
    )
    copies = [send(frames.at[src], frames.at[dst], send_sem.at[i], recv_sem.at[i], peer)
              for i, (src, dst, peer) in enumerate(moves)]

    def fin_copy(t):
        return send(fins[t], fins_r[t], fin_send.at[t], fin_recv.at[t], sums.other_x)

    greet(sums.peers)
    sums.begin()
    for copy in copies[:3]:
        copy.start()
    for t in range(count):
        fin_copy(t).start()
    sums.load_first()
    sums.first_hop()

    def body(s, carry):
        sums.hop(s)
        return carry

    lax.fori_loop(1, sums.final, body, 0)
    copies[0].wait_recv()
    copies[3].start()
    sums.finish()
    for t in range(count):
        fin_copy(t).wait_recv()
        value = keeps[t][...] + fins_r[t][...].astype(F32)
        put(left_outs, places[t], value)
    for t in range(count):
        fin_copy(t).wait_send()
    copies[0].wait_send()
    for copy in copies[1:]:
        copy.wait()


def scatter_last(frames, g, keeps, fins, plan, left, shapes):
    sems = pltpu.SemaphoreType.DMA
    vmem = pl.BlockSpec(memory_space=pltpu.VMEM)
    return pl.pallas_call(
        functools.partial(last_kernel, plan, left, len(shapes)),
        name="scatter_last",
        out_shape=[shape_of(frames.shape, frames.dtype)] + [shape_of(hw, F32) for hw in shapes] + plan.out_shapes,
        in_specs=[ANY] * 2 + [vmem] * len(keeps) + [ANY] * len(fins),
        out_specs=[ANY] + [vmem] * len(shapes) + plan.out_specs,
        scratch_shapes=[pltpu.VMEM(f.shape, f.dtype) for f in fins]
        + [sems((len(fins),))] * 2 + [sems((4,))] * 2 + plan.scratch,
        input_output_aliases={0: 0},
        compiler_params=pltpu.CompilerParams(
            collective_id=1, has_side_effects=True, vmem_limit_bytes=VMEM_LIMIT
        ),
    )(frames, g, *keeps, *fins)


def tuned(mesh):
    wide, n = mesh.shape["wide"], mesh.shape["narrow"]
    if n != 4 or wide != 2 * GRID or D % (8 * wide * n):
        return False
    for w in range(wide):
        for k in range(n):
            device = mesh.devices[w, k]
            here = (getattr(device, "coords", None), getattr(device, "core_on_chip", None))
            if here[0] is None or tuple(here[0]) != (k // 2, w % 2, w // 2) or here[1] != k % 2:
                return False
    return True


def exchange(x):
    return lax.all_to_all(x, ALL, split_axis=0, concat_axis=0, tiled=True)


def shift_clips(clips, back):
    n = lax.axis_size("narrow")
    parts = [clips[0]]
    for j in range(1, n):
        step = -j if back else j
        parts.append(lax.ppermute(clips[j], "narrow", [(s, (s + step) % n) for s in range(n)]))
    return jnp.stack(parts)


def local(fast, clips, t_emb, lengths, task, w_mod, b_mod, w_qkv_s, w_o_s, b_o_s, w_qkv_t, w_o_t, b_o_t,
          w_in, b_in, w_out, b_out, cotangent):
    n = lax.axis_size("narrow")
    wide = lax.axis_size("wide")
    devices = n * wide
    part = w_mod.shape[0]
    mod_cols = w_mod.shape[1] // devices
    rank = lax.axis_index("narrow")
    slots = jnp.arange(n, dtype=jnp.int32)
    from_clip = (rank - slots) % n
    recv_len = lengths.reshape(n, n)[from_clip, slots]
    recv_task = task.reshape(n, n, FR)[from_clip, slots]
    ends = jnp.cumsum(recv_len)
    starts = ends - recv_len
    ids = jnp.arange(LIVE, dtype=jnp.int32)
    source = jnp.sum((ends[None, :] <= ids[:, None]).astype(jnp.int32), axis=1)
    within = ids - starts[source]
    pack_rows = source * FR + within
    row_choice = source * 2 + recv_task[source, within]
    frame_ids = jnp.arange(FR, dtype=jnp.int32)
    live_back = frame_ids[None, :] < recv_len[:, None]
    unpack_rows = jnp.where(live_back, starts[:, None] + frame_ids[None, :], 0).reshape(-1)
    row_id = jnp.arange(64, dtype=jnp.int32)
    col_id = jnp.arange(LANES, dtype=jnp.int32) % 64
    seg = (
        (row_id[:, None] // LIVE == col_id[None, :] // LIVE)
        & (source[row_id % LIVE][:, None] == source[col_id % LIVE][None, :])
    ).astype(F32)

    def gather(w):
        return lax.all_gather(w, ALL, axis=0, tiled=True)

    def across(value):
        return lax.ppermute(value, "narrow", [(k, (k + n // 2) % n) for k in range(n)])

    if fast:
        flat = (w_qkv_s, w_o_s, w_qkv_t, w_o_t, w_in)
        far, far_out = across(jnp.concatenate(flat, axis=1)), across(w_out)
        clips, far, far_out = lax.optimization_barrier((clips, far, far_out))
        cuts = [sum(a.shape[1] for a in flat[: i + 1]) for i in range(len(flat) - 1)]
        *far_attn, far_in = jnp.split(far, cuts, axis=1)
        frames = shift_clips(clips, False)
        wqkv_s, wo_s, wqkv_t, wo_t = gather_first(flat[:4], far_attn, wide, n)
    else:
        far_in = far_out = None
        frames = shift_clips(clips, False)
        win, wout, wqkv_t, wo_t, wqkv_s, wo_s = [gather(w) for w in (w_in, w_out, w_qkv_t, w_o_t, w_qkv_s, w_o_s)]
    frames = jnp.take(frames.reshape(n * FR, PATCHES, D), pack_rows, axis=0, mode="clip")

    wm = jnp.swapaxes(w_mod.reshape(part, devices, mod_cols), 0, 1).reshape(devices, -1)
    emb = jnp.broadcast_to(t_emb.reshape(1, -1), (devices, t_emb.size))
    small = jnp.concatenate([b_o_s, b_o_t, b_in, b_out])
    small_all = jnp.broadcast_to(small[None], (devices, small.size))
    got = exchange(jnp.concatenate([wm, emb, small_all], axis=1))
    wm_cols = got[:, : part * mod_cols].reshape(D, mod_cols)
    emb_all = got[:, part * mod_cols : part * mod_cols + t_emb.size].reshape(-1, D)
    small_got = got[:, part * mod_cols + t_emb.size :]
    b1 = b_o_s.size
    bias_s = small_got[:, :b1].reshape(1, -1).astype(F32)
    bias_t = small_got[:, b1 : 2 * b1].reshape(1, -1).astype(F32)
    bias_in = small_got[:, 2 * b1 : 2 * b1 + b_in.size].reshape(1, -1).astype(F32)
    bias_out = small_got[:, 2 * b1 + b_in.size :].reshape(1, -1).astype(F32)
    emb_f = emb_all.astype(F32)
    silu_low = (emb_f * jax.nn.sigmoid(emb_f)).astype(BF)
    mod_part = dot(silu_low, wm_cols) + b_mod.astype(F32)[None]
    mod_part = mod_part.reshape(wide, n, n, 2, mod_cols)
    mod_part = jnp.stack([jnp.roll(mod_part[:, :, c], c, axis=1) for c in range(n)], axis=2)
    mod_rows = exchange(mod_part.reshape(devices, -1)).reshape(devices, 2 * n, mod_cols)
    mod_rows = jnp.swapaxes(mod_rows, 0, 1).reshape(2 * n, 9, D)
    mod = jnp.swapaxes(mod_rows[row_choice], 0, 1)

    def carry(js, shard, other, number):
        return forward_carrier(cotangent, js, shard, other, wide, n, number) if fast else None

    *half, x1, qkv1, o1, a1 = run_frame_forward(
        frames, mod, wqkv_s, wo_s, bias_s, carry((2,), w_in, far_in, 2))
    *odd, x2, qkv2, o2, a2 = run_time_forward(
        x1, mod, seg, wqkv_t, wo_t, bias_t, carry((1, 3), w_out, far_out, 3))
    if fast:
        (half, win), (odd, wout) = half, odd
        cots = jnp.stack([cotangent[0], odd[0], half[0], odd[1]])
    else:
        cots = shift_clips(cotangent, False)
    dy = run_turn_frames(cots.reshape(n * FR, PATCHES, D), pack_rows)
    out, dx2, g_in, g_out, gb_in, gb_out, dmod3 = run_mlp(x2, dy, mod, win, bias_in, wout, bias_out, out_carrier(n, 6) if fast else None)

    own_len = lengths.reshape(n, n)[rank]
    own_live = frame_ids[None, :] < own_len[:, None]

    def spread(frames):
        return jnp.take(frames, unpack_rows, axis=0, mode="clip").reshape(n, FR, PATCHES, D)

    def only_live(parts):
        return jnp.where(own_live[:, :, None, None], parts, jnp.zeros((), parts.dtype))

    def scatter(g):
        return lax.psum_scatter(g.astype(BF), ALL, scatter_dimension=0, tiled=True).astype(F32)

    if fast:
        ahead = lengths.reshape(n, n)[(rank + slots[:, None] - slots[None, :]) % n, slots[None, :]]
        own_start = jnp.sum(jnp.where(slots[None, :] < slots[:, None], ahead, 0), axis=1)
        own_rows = slots[:, None] * LIVE + own_start[:, None] + frame_ids[None, :]
        own_rows = jnp.where(own_live, own_rows, -1).reshape(-1)
        plan_a = time_plan(wide, g_in, g_out, devices)
        out, *got, dx1, g_t, gb_t, dmod2 = run_time_back(
            x1, dx2, mod, seg, qkv2, o2, a2, wqkv_t, wo_t, share_carrier(out, [g_in, g_out], plan_a, 4))
        keeps, fins = plan_a.left(got)
        plan_b = frame_plan(wide, g_t, g_in, g_out, devices)
        out, dx0, *got, g_s, gb_s, dmod1 = run_frame_back(
            frames, dx1, mod, qkv1, o1, a1, wqkv_s, wo_s, relay_carrier(out, [g_t, g_in, g_out], plan_b, 5))
        more_keeps, more_fins = plan_b.left(got)
        dx0, s_in, s_out, s_qkv_t, s_o_t, s_qkv_s, s_o_s = scatter_last(
            dx0, g_s, keeps + more_keeps, fins + more_fins, last_plan(wide, g_s, devices), (plan_a, plan_b),
            [w_in.shape, w_out.shape] + attn_shapes(g_t, devices))[:7]
        layer_out = run_unpack(out, own_rows).reshape(n, FR, PATCHES, D)
        grad_clips = run_unpack(dx0, own_rows).reshape(n, FR, PATCHES, D)
    else:
        dx1, g_t, gb_t, dmod2 = run_time_back(x1, dx2, mod, seg, qkv2, o2, a2, wqkv_t, wo_t)
        dx0, g_s, gb_s, dmod1 = run_frame_back(frames, dx1, mod, qkv1, o1, a1, wqkv_s, wo_s)
        layer_out = only_live(shift_clips(spread(out), True))
        grad_clips = only_live(shift_clips(spread(dx0), True))
        s_in, s_out, s_t, s_s = [scatter(g) for g in (g_in, g_out, g_t, g_s)]
        s_qkv_t, s_o_t, s_qkv_s, s_o_s = s_t[:, : 3 * D], s_t[:, 3 * D :], s_s[:, : 3 * D], s_s[:, 3 * D :]

    grad_frames = jnp.swapaxes(jnp.concatenate([dmod1, dmod2, dmod3], axis=0), 0, 1).reshape(LIVE, 9 * D)
    chooser = (row_choice[:, None] == jnp.arange(2 * n, dtype=jnp.int32)[None, :]).astype(F32)
    grad_rows = lax.dot_general(
        chooser, grad_frames, (((0,), (0,)), ((), ())), precision=lax.Precision.HIGHEST
    ).astype(BF)
    d_cols = exchange(jnp.swapaxes(grad_rows.reshape(2 * n, devices, mod_cols), 0, 1).reshape(devices, -1))
    d_cols = d_cols.reshape(wide, n, n, 2, mod_cols)
    d_cols = jnp.stack([jnp.roll(d_cols[:, :, c], -c, axis=1) for c in range(n)], axis=2)
    d_cols = d_cols.reshape(devices * 2 * n, mod_cols)
    grad_b_mod = jnp.sum(d_cols.astype(F32), axis=0)
    gwm_cols = dot_tn(silu_low, d_cols)
    g_emb = dot_nt(d_cols, wm_cols)
    gb_all = jnp.concatenate(
        [gb_s.reshape(devices, -1), gb_t.reshape(devices, -1), gb_in.reshape(devices, -1),
         gb_out.reshape(devices, -1)], axis=1)
    final = exchange(jnp.concatenate(
        [gwm_cols.reshape(devices, -1), g_emb.reshape(devices, -1), gb_all], axis=1))
    cut1 = part * mod_cols
    cut2 = cut1 + t_emb.size
    grad_w_mod = jnp.swapaxes(final[:, :cut1].reshape(devices, part, mod_cols), 0, 1).reshape(part, -1)
    emb_own = t_emb.astype(F32)
    sig = jax.nn.sigmoid(emb_own)
    grad_emb = jnp.sum(final[:, cut1:cut2], axis=0).reshape(t_emb.shape)
    grad_t_emb = (grad_emb * (sig * (1.0 + emb_own * (1.0 - sig)))).astype(BF)
    gb = jnp.sum(final[:, cut2:], axis=0)
    return (
        layer_out,
        grad_clips,
        grad_t_emb,
        grad_w_mod,
        grad_b_mod,
        s_qkv_s,
        s_o_s,
        gb[:b1],
        s_qkv_t,
        s_o_t,
        gb[b1 : 2 * b1],
        s_in,
        gb[2 * b1 : 2 * b1 + b_in.size],
        s_out,
        gb[2 * b1 + b_in.size :],
    )


def solution(mesh):
    full = P(ALL)
    placed = (full, full, P("wide"), P("wide")) + (full,) * 13
    return jax.shard_map(functools.partial(local, tuned(mesh)), mesh=mesh, in_specs=placed, out_specs=(full,) * 15, check_vma=False)
```

```python
import functools

import jax
import jax.numpy as jnp
from jax import lax
from jax.experimental import pallas as pl
from jax.experimental.pallas import tpu as pltpu
from jax.sharding import PartitionSpec as P

D = 768
HEADS = 12
HEAD = 64
FF = 3072
FR = 16
PATCHES = 64
LIVE = 2 * FR
EPS = 1e-06
BF = jnp.bfloat16
F32 = jnp.float32
ALL = ("wide", "narrow")
PAIRS = HEADS // 2
LANES = 2 * HEAD
BACK_PAIRS = 6
TILE = 512
FT = TILE // PATCHES
PT = TILE // LIVE
GRID = LIVE * PATCHES // TILE
GROUPS = TILE // 64
EARLY_TILES = GRID // 2
UNPACK = FR
GELU_C = 0.7978845608028654
GELU_A = 0.044715
VMEM_LIMIT = 66 * 1000 * 1000
MESH = pl.DeviceIdType.MESH
ANY = pl.BlockSpec(memory_space=pl.ANY)


def dot(a, b):
    return lax.dot_general(a, b, (((1,), (0,)), ((), ())), preferred_element_type=F32)


def dot_nt(a, b):
    return lax.dot_general(a, b, (((1,), (1,)), ((), ())), preferred_element_type=F32)


def dot_tn(a, b):
    return lax.dot_general(a, b, (((0,), (0,)), ((), ())), preferred_element_type=F32)


def normalise(x):
    mean = jnp.mean(x, axis=-1, keepdims=True)
    centred = x - mean
    var = jnp.mean(centred * centred, axis=-1, keepdims=True)
    rstd = lax.rsqrt(var + EPS)
    return centred * rstd, rstd


def norm_back(dn, xhat, rstd):
    m1 = jnp.mean(dn, axis=-1, keepdims=True)
    m2 = jnp.mean(dn * xhat, axis=-1, keepdims=True)
    return rstd * (dn - m1 - xhat * m2)


def lane_masks():
    lane = lax.broadcasted_iota(jnp.int32, (64, LANES), 1)
    low_lanes = lane < HEAD
    low = jnp.where(low_lanes, 1.0, 0.0).astype(BF)
    high = jnp.where(low_lanes, 0.0, 1.0).astype(BF)
    return low_lanes, low, high


def split_heads(x, low, high):
    return jnp.concatenate([x * low, x * high], axis=0)


def softmax_keys(s, mask):
    if mask is not None:
        s = jnp.where(mask, s, -1e30)
    top = jnp.max(s, axis=0, keepdims=True)
    e = jnp.exp(s - top)
    return e * (1.0 / jnp.sum(e, axis=0, keepdims=True))


def pair_cols(part, hp):
    return slice(part * D + hp * LANES, part * D + (hp + 1) * LANES)


def attend(qkv_ref, o_ref, mask):
    low_lanes, low, high = lane_masks()
    scale = HEAD ** (-0.5)

    def body(g, carry):
        rows = pl.ds(pl.multiple_of(g * 64, 64), 64)
        pairs = range(PAIRS)
        s = [dot_nt(qkv_ref[rows, pair_cols(1, hp)], split_heads(qkv_ref[rows, pair_cols(0, hp)], low * scale, high * scale))
             for hp in pairs]
        p = [softmax_keys(t, mask).astype(BF) for t in s]
        r = [dot_tn(p[hp], qkv_ref[rows, pair_cols(2, hp)]) for hp in pairs]
        for hp in pairs:
            o_ref[rows, pair_cols(0, hp)] = jnp.where(low_lanes, r[hp][:64], r[hp][64:]).astype(BF)
        return carry

    lax.fori_loop(0, GROUPS, body, 0)


def attend_back(qkv_ref, do_ref, dqkv_ref, mask):
    low_lanes, low, high = lane_masks()
    scale = HEAD ** (-0.5)

    def body(g, carry):
        rows = pl.ds(pl.multiple_of(g * 64, 64), 64)
        for first in range(0, PAIRS, BACK_PAIRS):
            pairs = range(first, first + BACK_PAIRS)
            qb = [split_heads(qkv_ref[rows, pair_cols(0, hp)], low * scale, high * scale) for hp in pairs]
            dob = [split_heads(do_ref[rows, pair_cols(0, hp)], low, high) for hp in pairs]
            s = [dot_nt(qkv_ref[rows, pair_cols(1, hp)], q) for hp, q in zip(pairs, qb)]
            dp = [dot_nt(qkv_ref[rows, pair_cols(2, hp)], d) for hp, d in zip(pairs, dob)]
            p = [softmax_keys(t, mask) for t in s]
            delta = [jnp.sum(a * b, axis=0, keepdims=True) for a, b in zip(p, dp)]
            ds = [(a * (b - c)).astype(BF) for a, b, c in zip(p, dp, delta)]
            dv = [dot(a.astype(BF), d) for a, d in zip(p, dob)]
            dk = [dot(a, q) for a, q in zip(ds, qb)]
            r = [dot_tn(a, qkv_ref[rows, pair_cols(1, hp)]) for hp, a in zip(pairs, ds)]
            for i, hp in enumerate(pairs):
                dqkv_ref[rows, pair_cols(2, hp)] = dv[i].astype(BF)
                dqkv_ref[rows, pair_cols(1, hp)] = dk[i].astype(BF)
                dq = jnp.where(low_lanes, r[i][:64], r[i][64:]) * scale
                dqkv_ref[rows, pair_cols(0, hp)] = dq.astype(BF)
        return carry

    lax.fori_loop(0, GROUPS, body, 0)


def swap_major(value, scratch, out_ref, first, second):
    for b in range(D // 128):
        cols = slice(b * 128, (b + 1) * 128)
        for i in range(first):
            scratch[b, pl.ds(i, second, stride=first), :] = value[i * second : (i + 1) * second, cols]
        out_ref[:, :, cols] = scratch[b].reshape(second, first, 128).astype(out_ref.dtype)


def frames_of(refs):
    return jnp.concatenate([r[0] for r in refs], axis=0).astype(F32)


def per_frame(piece):
    return jnp.broadcast_to(piece[:, None, :], (FT, PATCHES, D)).reshape(TILE, D)


def per_patch(piece):
    return jnp.broadcast_to(piece[None], (PT, LIVE, D)).reshape(TILE, D)


def sum_patches(value):
    return jnp.sum(value.reshape(FT, PATCHES, D), axis=1)


def sum_groups(value):
    return jnp.sum(value.reshape(PT, LIVE, D), axis=0)


def attn_mask(seg_ref):
    return seg_ref[...] > 0.0


def no_tick(place):
    pass


def frame_forward(frames, mod, wqkv, wo, bo, x1t, qkv, o, a1, scratch, tick=no_tick):
    x = frames[...].reshape(TILE, D).astype(F32)
    xhat, _ = normalise(x)
    h = (xhat * (1.0 + per_frame(mod[1])) + per_frame(mod[0])).astype(BF)
    qkv[...] = dot(h, wqkv[...]).astype(BF)
    tick(0)
    attend(qkv, o, None)
    tick(1)
    branch = dot(o[...], wo[...]) + bo[...]
    a1[...] = branch
    x1 = x + per_frame(mod[2]) * branch
    swap_major(x1, scratch, x1t, FT, PATCHES)


def turn_frames(rows_ref, *refs):
    x_refs, (out, scratch) = refs[:FT], refs[FT:]
    swap_major(frames_of(x_refs), scratch, out, FT, PATCHES)


def time_forward(x1, mod, seg, wqkv, wo, bo, x2, qkv, o, a2, tick=no_tick):
    x = x1[...].reshape(TILE, D)
    xhat, _ = normalise(x)
    h = (xhat * (1.0 + per_patch(mod[1])) + per_patch(mod[0])).astype(BF)
    qkv[...] = dot(h, wqkv[...]).astype(BF)
    tick(0)
    attend(qkv, o, attn_mask(seg))
    tick(1)
    branch = dot(o[...], wo[...]) + bo[...]
    a2[...] = branch
    x2[...] = (x + per_patch(mod[2]) * branch).reshape(PT, LIVE, D)


def mlp_both(x2, dy, mod, win, bin_, wout, bout, out, dx2, gwin, gwout, gbin, gbout, dmod, scratch):
    first = pl.program_id(0) == 0

    @pl.when(first)
    def _():
        gwin[...] = jnp.zeros_like(gwin)
        gwout[...] = jnp.zeros_like(gwout)
        gbin[...] = jnp.zeros_like(gbin)
        gbout[...] = jnp.zeros_like(gbout)
        dmod[...] = jnp.zeros_like(dmod)

    x = x2[...].reshape(TILE, D)
    xhat, rstd = normalise(x)
    h = (xhat * (1.0 + per_patch(mod[1])) + per_patch(mod[0])).astype(BF)
    gate = per_patch(mod[2])
    grad = dy[...].reshape(TILE, D)
    da = (grad * gate).astype(BF)
    gbout[...] += jnp.sum(da.astype(F32), axis=0, keepdims=True)
    branch = jnp.zeros((TILE, D), F32) + bout[...]
    dh = jnp.zeros((TILE, D), F32)
    for j in range(FF // D):
        cols = slice(j * D, (j + 1) * D)
        u = dot(h, win[:, cols]) + bin_[:, cols]
        u2 = u * u
        t = jnp.tanh(GELU_C * u * (1.0 + GELU_A * u2))
        half = 0.5 * (1.0 + t)
        g = (u * half).astype(BF)
        slope = half + (0.5 * GELU_C) * u * (1.0 - t * t) * (1.0 + 3.0 * GELU_A * u2)
        branch = branch + dot(g, wout[cols, :])
        du = (dot_nt(da, wout[cols, :]) * slope).astype(BF)
        gwout[cols, :] += dot_tn(g, da)
        gbin[:, cols] += jnp.sum(du.astype(F32), axis=0, keepdims=True)
        gwin[:, cols] += dot_tn(h, du)
        dh = dh + dot_nt(du, win[:, cols])
    swap_major(x + gate * branch, scratch, out, PT, LIVE)
    dmod[2] += sum_groups(grad * branch)
    dmod[0] += sum_groups(dh)
    dmod[1] += sum_groups(dh * xhat)
    back = norm_back(dh * (1.0 + per_patch(mod[1])), xhat, rstd)
    dx2[...] = (grad + back).reshape(PT, LIVE, D)


def attn_back_tile(x, grad, shift, scale, gate, branch, qkv, o, wqkv, wo, gw, gbo, do, dqkv, mask, tick):
    first = pl.program_id(0) == 0

    @pl.when(first)
    def _():
        gw[...] = jnp.zeros_like(gw)
        gbo[...] = jnp.zeros_like(gbo)

    da = (grad * gate).astype(BF)
    do[...] = dot_nt(da, wo[...]).astype(BF)
    gw[:, 3 * D :] += dot_tn(o[...], da)
    gbo[...] += jnp.sum(da.astype(F32), axis=0, keepdims=True)
    tick(0)
    attend_back(qkv, do, dqkv, mask)
    tick(1)
    xhat, rstd = normalise(x)
    h = (xhat * (1.0 + scale) + shift).astype(BF)
    dh = jnp.zeros((TILE, D), F32)
    for j in range(3):
        cols = slice(j * D, (j + 1) * D)
        part = dqkv[:, cols]
        gw[:, cols] += dot_tn(h, part)
        dh = dh + dot_nt(part, wqkv[:, cols])
    dx = grad + norm_back(dh * (1.0 + scale), xhat, rstd)
    return dx, dh, dh * xhat, grad * branch


def time_back(x1, dx2, mod, seg, qkv, o, a2, wqkv, wo, dx1, gw, gbo, dmod, do, dqkv, scratch, tick=no_tick):
    @pl.when(pl.program_id(0) == 0)
    def _():
        dmod[...] = jnp.zeros_like(dmod)

    dx, d_shift, d_scale, d_gate = attn_back_tile(
        x1[...].reshape(TILE, D), dx2[...].reshape(TILE, D), per_patch(mod[0]), per_patch(mod[1]),
        per_patch(mod[2]), a2[...], qkv, o, wqkv, wo, gw, gbo, do, dqkv, attn_mask(seg), tick)
    dmod[0] += sum_groups(d_shift)
    dmod[1] += sum_groups(d_scale)
    dmod[2] += sum_groups(d_gate)
    swap_major(dx, scratch, dx1, PT, LIVE)


def frame_back(frames, dx1, mod, qkv, o, a1, wqkv, wo, dx0, gw, gbo, dmod, do, dqkv, tick=no_tick):
    dx, d_shift, d_scale, d_gate = attn_back_tile(
        frames[...].reshape(TILE, D).astype(F32), dx1[...].reshape(TILE, D), per_frame(mod[0]), per_frame(mod[1]),
        per_frame(mod[2]), a1[...], qkv, o, wqkv, wo, gw, gbo, do, dqkv, None, tick)
    dmod[0] = sum_patches(d_shift)
    dmod[1] = sum_patches(d_scale)
    dmod[2] = sum_patches(d_gate)
    dx0[...] = dx.reshape(FT, PATCHES, D).astype(BF)


def frame_specs():
    return [
        pl.BlockSpec((1, PATCHES, D), functools.partial(lambda j, i, rows: (rows[FT * i + j], 0, 0), j))
        for j in range(FT)
    ]


def whole(shape):
    return pl.BlockSpec(shape, lambda i, *_: (0,) * len(shape), pipeline_mode=pl.Buffered(1))


def tiles(shape, dim):
    return pl.BlockSpec(shape, lambda i, *_: tuple(i if a == dim else 0 for a in range(len(shape))))


def piece_spec(number, frames, by_tile):
    return pl.BlockSpec((3, frames, D), lambda i, *_: (number, i if by_tile else 0, 0))


ROWS = tiles((TILE, D), 0)
ROWS3 = tiles((TILE, 3 * D), 0)
TURNED = tiles((PT, LIVE, D), 0)


TURN = pltpu.VMEM((D // 128, TILE, 128), F32)


def shape_of(shape, dtype):
    return jax.ShapeDtypeStruct(shape, dtype)


class Carrier:
    def __init__(self, wrap, number, ins, outs, out_specs, scratch, aliases=None):
        self.wrap, self.number, self.ins, self.outs = wrap, number, ins, outs
        self.out_specs, self.scratch, self.aliases = out_specs, scratch, aliases or {}


def call(kernel, name, ins, in_specs, outs, out_specs, scratch, flops, prefetch=None, carrier=None):
    moved = sum(a.size * a.dtype.itemsize for a in tuple(ins) + tuple(outs))
    params, aliases = {}, {}
    if carrier is not None:
        kernel = functools.partial(carrier.wrap, kernel, len(ins), len(outs), len(scratch))
        ins, in_specs = carrier.ins + ins, [ANY] * len(carrier.ins) + in_specs
        outs, out_specs = carrier.outs + outs, carrier.out_specs + out_specs
        scratch = scratch + carrier.scratch
        params, aliases = dict(collective_id=carrier.number, has_side_effects=True), carrier.aliases
    grid_spec = pltpu.PrefetchScalarGridSpec(
        num_scalar_prefetch=0 if prefetch is None else 1,
        grid=(GRID,),
        in_specs=in_specs,
        out_specs=out_specs,
        scratch_shapes=scratch,
    )
    fn = pl.pallas_call(
        kernel,
        grid_spec=grid_spec,
        out_shape=outs,
        name=name,
        input_output_aliases=aliases,
        cost_estimate=pl.CostEstimate(flops=flops, bytes_accessed=moved, transcendentals=0),
        compiler_params=pltpu.CompilerParams(
            dimension_semantics=("arbitrary",), vmem_limit_bytes=VMEM_LIMIT, **params
        ),
    )
    return fn(*ins) if prefetch is None else fn(prefetch, *ins)


def split_refs(refs, *counts):
    parts = []
    for count in counts:
        parts.append(refs[:count])
        refs = refs[count:]
    return parts + [refs]


def forward_carrier(clips, js, shard, far, ring, n, number):
    held = Gather.scratch([shard], ring)

    def wrap(kernel, n_in, n_out, n_scratch, *refs):
        (src, part, other), ins, (dst, full), outs, scratch, (send_sem, recv_sem), own = split_refs(
            refs, 3, n_in, 2, n_out, n_scratch, 2)
        step = pl.program_id(0)
        gather = Gather(ring, (shard.shape[0],), (part, other, full) + own)
        targets = [(gather.w, (gather.k + j) % n) for j in js]
        copies = [send(src.at[j], dst.at[i], send_sem.at[i], recv_sem.at[i], targets[i]) for i, j in enumerate(js)]

        @pl.when(step == 0)
        def _():
            greet(tuple(targets) + gather.peers)
            gather.begin()
            for copy in copies:
                copy.start()

        def tick(place):
            if place == 0:
                @pl.when(step == 0)
                def _():
                    gather.second()

                @pl.when(step > 0)
                def _():
                    gather.hop(2 * step)
            else:
                gather.hop(2 * step + 1)

        kernel(*ins, *outs, *scratch, tick=tick)

        @pl.when(step == GRID - 1)
        def _():
            gather.finish()
            for copy in copies:
                copy.wait()

    sems = pltpu.SemaphoreType.DMA((len(js),))
    return Carrier(wrap, number, [clips, shard, far],
                   [shape_of((len(js),) + clips.shape[1:], clips.dtype)] + Gather.shapes([shard], ring * n),
                   [ANY, ANY], [sems, sems] + held)


def packed(slot, first=0, count=LIVE):
    return pl.ds(pl.multiple_of(slot * LIVE + first, 8), count)


def slot_for(k):
    return 3 - 2 * (k % 2)


def ticks(sums, step):
    def tick(place):
        @pl.when(step == 0)
        def _():
            if place == 0:
                sums.load_first()
            else:
                sums.first_hop()

        @pl.when(step > 0)
        def _():
            sums.hop(2 * step - 1 + place)

    return tick


def patches_of(frames, slot, i):
    return frames.at[packed(slot), pl.ds(pl.multiple_of(i * PT, PT), PT)]


def out_carrier(slots, number):
    def wrap(kernel, n_in, n_out, n_scratch, *refs):
        ins, (dst,), outs, scratch, (send_sem, recv_sem, keep, buf) = split_refs(refs, n_in, 1, n_out, n_scratch)
        step = pl.program_id(0)
        w, k = lax.axis_index("wide"), lax.axis_index("narrow")
        other_x, other_c = (w, (k + 2) % 4), (w, k + 1 - 2 * (k % 2))

        def tile(i):
            return [send(buf.at[i], patches_of(dst, slot, i), send_sem.at[a, i], recv_sem.at[a, i], peer)
                    for a, (slot, peer) in enumerate(((slot_for(k), other_c), (2, other_x)))]

        def store(i):
            return pltpu.make_async_copy(buf.at[i], patches_of(dst, 0, i), keep.at[i])

        @pl.when(step == 0)
        def _():
            greet((other_x, other_c))

        kernel(*ins, buf.at[step], *outs, *scratch)
        store(step).start()

        @pl.when(step < GRID - 1)
        def _():
            for copy in tile(step):
                copy.start()

        @pl.when(step == GRID - 1)
        def _():
            for i in range(GRID):
                store(i).wait()
            for i in range(GRID - 1):
                for copy in tile(i):
                    copy.wait()

    sems = pltpu.SemaphoreType.DMA
    return Carrier(wrap, number, [], [shape_of((slots * LIVE, PATCHES, D), BF)], [ANY],
                   [sems((2, GRID - 1)), sems((2, GRID - 1)), sems((GRID,)), pltpu.VMEM((GRID, LIVE, PT, D), BF)])


def share_carrier(frames, grads, plan, number):
    n_grads = len(grads)

    def wrap(kernel, n_in, n_out, n_scratch, *refs):
        (_,), grad_refs, ins, (dst,), left, outs, scratch, (send_sem, recv_sem), own = split_refs(
            refs, 1, n_grads, n_in, 1, plan.outputs, n_out, n_scratch, 2)
        step = pl.program_id(0)
        sums = plan.steps(grad_refs + left + own)
        targets = ((slot_for(sums.k), sums.other_c), (2, sums.other_x))
        final = GRID - 1
        copies = [send(patches_of(dst, 0, final), patches_of(dst, slot, final), send_sem.at[i], recv_sem.at[i], peer)
                  for i, (slot, peer) in enumerate(targets)]

        @pl.when(step == 0)
        def _():
            greet(sums.peers)
            sums.begin()
            for copy in copies:
                copy.start()

        kernel(*ins, *outs, *scratch, tick=ticks(sums, step))

        @pl.when(step == GRID - 1)
        def _():
            sums.leave()
            for copy in copies:
                copy.wait()

    sems = pltpu.SemaphoreType.DMA((2,))
    return Carrier(wrap, number, [frames] + grads, [shape_of(frames.shape, frames.dtype)] + plan.out_shapes,
                   [ANY] + plan.out_specs, [sems, sems] + plan.scratch, {0: 0})


def tile_copies(k, other_c, other_x, src, dst, i, send_sem, recv_sem):
    return [send(src, dst.at[packed(slot, i * FT, FT)], send_sem.at[a, i], recv_sem.at[a, i], peer)
            for a, (slot, peer) in enumerate(((slot_for(k), other_c), (2, other_x)))]


def relay_carrier(frames, grads, plan, number):
    n_grads = len(grads)

    def wrap(kernel, n_in, n_out, n_scratch, *refs):
        (_,), grad_refs, ins, (dst, made), left, outs, scratch, (send_sem, recv_sem, tile_s, tile_r, keep, buf), own = (
            split_refs(refs, 1, n_grads, n_in, 2, plan.outputs, n_out, n_scratch, 6))
        step = pl.program_id(0)
        sums = plan.steps(grad_refs + left + own)
        relay = send(dst.at[packed(2)], dst.at[packed(4 - slot_for(sums.k))],
                     send_sem.at[0], recv_sem.at[0], sums.other_c)

        def tile(i):
            return tile_copies(sums.k, sums.other_c, sums.other_x, buf.at[i], made, i, tile_s, tile_r)

        def store(i):
            return pltpu.make_async_copy(buf.at[i], made.at[packed(0, i * FT, FT)], keep.at[i])

        @pl.when(step == 0)
        def _():
            greet(sums.peers)
            sums.begin()
            relay.start()

        kernel(*ins, buf.at[step], *outs, *scratch, tick=ticks(sums, step))
        store(step).start()

        @pl.when(step < EARLY_TILES)
        def _():
            for copy in tile(step):
                copy.start()

        @pl.when(step == GRID - 1)
        def _():
            sums.leave()
            relay.wait()
            for i in range(GRID):
                store(i).wait()
            for i in range(EARLY_TILES):
                for copy in tile(i):
                    copy.wait()

    sems = pltpu.SemaphoreType.DMA
    shape = shape_of(frames.shape, frames.dtype)
    return Carrier(wrap, number, [frames] + grads, [shape, shape] + plan.out_shapes, [ANY, ANY] + plan.out_specs,
                   [sems((1,)), sems((1,)), sems((2, EARLY_TILES)), sems((2, EARLY_TILES)), sems((GRID,)),
                    pltpu.VMEM((GRID, FT, PATCHES, D), BF)] + plan.scratch, {0: 0})


TOKENS = LIVE * PATCHES


def run_frame_forward(frames, mod, wqkv, wo, bo, carrier=None):
    return call(
        frame_forward, "frame_forward",
        [frames, mod, wqkv, wo, bo],
        [tiles((FT, PATCHES, D), 0), piece_spec(0, FT, True), whole((D, 3 * D)), whole((D, D)), whole((1, D))],
        [shape_of((PATCHES, LIVE, D), F32), shape_of((TOKENS, 3 * D), BF), shape_of((TOKENS, D), BF),
         shape_of((TOKENS, D), F32)],
        [tiles((PATCHES, FT, D), 1), ROWS3, ROWS, ROWS],
        [TURN],
        2 * TOKENS * D * 4 * D, carrier=carrier)


def run_turn_frames(frames, rows):
    return call(
        turn_frames, "turn_frames", [frames] * FT, frame_specs(),
        [shape_of((PATCHES, LIVE, D), F32)], [tiles((PATCHES, FT, D), 1)],
        [TURN], 1000, rows)[0]


def unpack_frames(rows_ref, *refs):
    x_refs, (out,) = refs[:UNPACK], refs[UNPACK:]
    first = pl.program_id(0) * UNPACK
    for j in range(UNPACK):
        x = x_refs[j][0]
        out[j] = jnp.where(rows_ref[first + j] >= 0, x, jnp.zeros_like(x))


def run_unpack(frames, rows):
    specs = [
        pl.BlockSpec((1, PATCHES, D), functools.partial(lambda j, i, r: (jnp.maximum(r[UNPACK * i + j], 0), 0, 0), j))
        for j in range(UNPACK)
    ]
    return pl.pallas_call(
        unpack_frames,
        grid_spec=pltpu.PrefetchScalarGridSpec(
            num_scalar_prefetch=1, grid=(rows.shape[0] // UNPACK,), in_specs=specs, out_specs=tiles((UNPACK, PATCHES, D), 0)),
        out_shape=shape_of((rows.shape[0], PATCHES, D), frames.dtype),
        name="unpack_frames",
        cost_estimate=pl.CostEstimate(flops=1000, bytes_accessed=4 * rows.shape[0] * PATCHES * D, transcendentals=0),
        compiler_params=pltpu.CompilerParams(dimension_semantics=("arbitrary",)),
    )(rows, *[frames] * UNPACK)


def run_time_forward(x1, mod, seg, wqkv, wo, bo, carrier=None):
    return call(
        time_forward, "time_forward",
        [x1, mod, seg, wqkv, wo, bo],
        [TURNED, piece_spec(1, LIVE, False), whole((64, LANES)), whole((D, 3 * D)), whole((D, D)),
         whole((1, D))],
        [shape_of((PATCHES, LIVE, D), F32), shape_of((TOKENS, 3 * D), BF), shape_of((TOKENS, D), BF),
         shape_of((TOKENS, D), F32)],
        [TURNED, ROWS3, ROWS, ROWS],
        [], 2 * TOKENS * D * 4 * D, carrier=carrier)


def run_mlp(x2, dy, mod, win, bin_, wout, bout, carrier=None):
    frames_out = [] if carrier else [shape_of((LIVE, PATCHES, D), BF)]
    frames_spec = [] if carrier else [tiles((LIVE, PT, D), 1)]
    return call(
        mlp_both, "mlp_both",
        [x2, dy, mod, win, bin_, wout, bout],
        [TURNED, TURNED, piece_spec(2, LIVE, False), whole((D, FF)), whole((1, FF)), whole((FF, D)),
         whole((1, D))],
        frames_out + [shape_of((PATCHES, LIVE, D), F32), shape_of((D, FF), F32),
         shape_of((FF, D), F32), shape_of((1, FF), F32), shape_of((1, D), F32), shape_of((3, LIVE, D), F32)],
        frames_spec + [TURNED, whole((D, FF)), whole((FF, D)), whole((1, FF)), whole((1, D)),
         whole((3, LIVE, D))],
        [TURN],
        6 * 2 * TOKENS * D * FF, carrier=carrier)


def run_time_back(x1, dx2, mod, seg, qkv, o, a2, wqkv, wo, carrier=None):
    return call(
        time_back, "time_back",
        [x1, dx2, mod, seg, qkv, o, a2, wqkv, wo],
        [TURNED, TURNED, piece_spec(1, LIVE, False), whole((64, LANES)), ROWS3, ROWS, ROWS,
         whole((D, 3 * D)), whole((D, D))],
        [shape_of((LIVE, PATCHES, D), F32), shape_of((D, 4 * D), F32), shape_of((1, D), F32), shape_of((3, LIVE, D), F32)],
        [tiles((LIVE, PT, D), 1), whole((D, 4 * D)), whole((1, D)), whole((3, LIVE, D))],
        [pltpu.VMEM((TILE, D), BF), pltpu.VMEM((TILE, 3 * D), BF), TURN],
        2 * 2 * TOKENS * D * 4 * D, carrier=carrier)


def run_frame_back(frames, dx1, mod, qkv, o, a1, wqkv, wo, carrier=None):
    frames_out = [] if carrier else [shape_of((LIVE, PATCHES, D), BF)]
    frames_spec = [] if carrier else [tiles((FT, PATCHES, D), 0)]
    return call(
        frame_back, "frame_back",
        [frames, dx1, mod, qkv, o, a1, wqkv, wo],
        [tiles((FT, PATCHES, D), 0), tiles((FT, PATCHES, D), 0), piece_spec(0, FT, True), ROWS3, ROWS, ROWS,
                         whole((D, 3 * D)), whole((D, D))],
        frames_out + [shape_of((D, 4 * D), F32), shape_of((1, D), F32), shape_of((3, LIVE, D), F32)],
        frames_spec + [whole((D, 4 * D)), whole((1, D)), piece_spec(0, FT, True)],
        [pltpu.VMEM((TILE, D), BF), pltpu.VMEM((TILE, 3 * D), BF)],
        2 * 2 * TOKENS * D * 4 * D, carrier=carrier)


def place_of(wide):
    ring = wide
    turn = ring // 2
    w = lax.axis_index("wide")
    k = lax.axis_index("narrow")
    z, y = w // 2, w % 2
    r = z + y * (ring - 1 - 2 * z)

    def wide_at(position):
        side = position // turn
        return 2 * ((1 - side) * position + side * (ring - 1 - position)) + side

    return w, k, r, k // 2, k % 2, wide_at


def greet(peers):
    barrier = pltpu.get_barrier_semaphore()
    for peer in peers:
        pl.semaphore_signal(barrier, inc=1, device_id=peer, device_id_type=MESH)
    pl.semaphore_wait(barrier, len(peers))


def send(src, dst, send_sem, recv_sem, peer):
    return pltpu.make_async_remote_copy(
        src_ref=src, dst_ref=dst, send_sem=send_sem, recv_sem=recv_sem, device_id=peer, device_id_type=MESH
    )


class Gather:
    def __init__(self, ring, heights, refs):
        count = len(heights)
        self.ring, self.heights, self.count = ring, heights, count
        near, far, self.full, near_bufs, far_bufs, sems = split_refs(refs, count, count, count, count, count)
        self.shards, self.bufs = (near, far), (near_bufs, far_bufs)
        (self.ring_s, self.ring_r, self.core_s, self.core_r, self.load_sem, self.keep_sem) = sems
        self.w, self.k, self.r, self.x, self.c, self.wide_at = place_of(ring)
        self.other_c = (self.w, 2 * self.x + 1 - self.c)
        self.next = ((self.wide_at((self.r + 1) % ring), self.k), (self.wide_at((self.r + ring - 1) % ring), self.k))
        self.peers = self.next + (self.other_c,)

    @staticmethod
    def scratch(shards, ring):
        count, sems = len(shards), pltpu.SemaphoreType.DMA
        bufs = [pltpu.VMEM(a.shape, a.dtype) for a in shards]
        return bufs + bufs + [sems((count, 2, ring))] * 4 + [sems((count, 2))] * 2

    @staticmethod
    def shapes(shards, devices):
        return [shape_of((a.shape[0] * devices, a.shape[1]), a.dtype) for a in shards]

    def way(self, t, b):
        return (t + b) % 2

    def block(self, t, b, s):
        r, ring = self.r, self.ring
        place = (r + ring - s) % ring if self.way(t, b) == 0 else (r + s) % ring
        column = self.x if b == 0 else 1 - self.x
        block = 4 * self.wide_at(place) + 2 * column + self.c
        return self.full[t].at[pl.ds(pl.multiple_of(block * self.heights[t], 8), self.heights[t])]

    def ring_copy(self, t, b, s, src=None):
        dst = self.block(t, b, s)
        return send(dst if src is None else src, dst, self.ring_s.at[t, b, s], self.ring_r.at[t, b, s],
                    self.next[self.way(t, b)])

    def core_copy(self, t, b, s, src=None):
        dst = self.block(t, b, s)
        return send(dst if src is None else src, dst, self.core_s.at[t, b, s], self.core_r.at[t, b, s], self.other_c)

    def load(self, t, b):
        return pltpu.make_async_copy(self.shards[b][t], self.bufs[b][t], self.load_sem.at[t, b])

    def keep(self, t, b):
        return pltpu.make_async_copy(self.bufs[b][t], self.block(t, b, 0), self.keep_sem.at[t, b])

    def each(self):
        return [(t, b) for b in range(2) for t in range(self.count)]

    def begin(self):
        for t, b in self.each():
            self.ring_copy(t, b, 0, self.shards[b][t]).start()
        for t, b in self.each():
            self.core_copy(t, b, 0, self.shards[b][t]).start()
            self.load(t, b).start()

    def second(self):
        for t, b in self.each():
            self.load(t, b).wait()
            self.keep(t, b).start()

    def hop(self, s):
        for b in range(2):
            for t in range(self.count):
                self.ring_copy(t, b, s - 1).wait_recv()

                @pl.when(s < self.ring - 1)
                def _():
                    self.ring_copy(t, b, s).start()

                self.core_copy(t, b, s).start()

    def finish(self):
        for t, b in self.each():
            self.keep(t, b).wait()
            for s in range(self.ring):
                if s < self.ring - 1:
                    self.ring_copy(t, b, s).wait_send()
                self.core_copy(t, b, s).wait()


def gather_kernel(ring, heights, *refs):
    gather = Gather(ring, heights, refs)
    greet(gather.peers)
    gather.begin()
    gather.second()

    def body(s, carry):
        gather.hop(s)
        return carry

    lax.fori_loop(1, ring, body, 0)
    gather.finish()


def gather_first(shards, far, ring, n):
    heights = tuple(a.shape[0] for a in shards)
    return pl.pallas_call(
        functools.partial(gather_kernel, ring, heights),
        name="gather_first",
        out_shape=Gather.shapes(shards, ring * n),
        in_specs=[ANY] * (2 * len(shards)),
        out_specs=[ANY] * len(shards),
        scratch_shapes=Gather.scratch(shards, ring),
        compiler_params=pltpu.CompilerParams(collective_id=0, has_side_effects=True),
    )(*shards, *far)


def put(outs, places, value):
    for o, out_col, col, width in places:
        outs[o][:, out_col : out_col + width] = value[:, col : col + width]


class Sums:
    def __init__(self, plan, refs):
        self.plan, count = plan, len(plan.pieces)
        self.grads, refs = refs[: plan.inputs], refs[plan.inputs :]
        self.outs, refs = refs[: plan.results], refs[plan.results :]
        self.stages, refs = refs[:count], refs[count:]
        self.own, self.part, self.came, self.went, self.last, self.fin_s, self.fin_r = (
            refs[i * count : (i + 1) * count] for i in range(7)
        )
        (self.ring_s, self.ring_r, self.core_s, self.core_r, self.x_s, self.x_r, self.load_sem,
         self.part_sem) = refs[7 * count :]
        ring = plan.ring
        self.w, self.k, self.r, self.x, self.c, self.wide_at = place_of(ring)
        self.other_x = (self.w, 2 * (1 - self.x) + self.c)
        self.other_c = (self.w, 2 * self.x + 1 - self.c)
        self.next = ((self.wide_at((self.r + 1) % ring), self.k), (self.wide_at((self.r + ring - 1) % ring), self.k))
        self.peers = self.next + (self.other_x, self.other_c)
        self.final = ring - 1

    def source(self, t, s, column, core):
        ring = self.plan.ring
        g, col, width, height, way = self.plan.pieces[t]
        place = (self.r + 2 * ring - 1 - s) % ring if way == 0 else (self.r + 1 + s) % ring
        block = 4 * self.wide_at(place) + 2 * column + core
        return self.grads[g].at[pl.ds(pl.multiple_of(block * height, 8), height), pl.ds(col, width)]

    def half(self, t, column):
        height = self.plan.pieces[t][3]
        return pl.ds(column * height, height)

    def core_copy(self, t, s, column):
        return send(self.source(t, s, column, 1 - self.c), self.stages[t].at[s, self.half(t, column)],
                    self.core_s.at[t, s, column], self.core_r.at[t, s, column], self.other_c)

    def own_load(self, t, s, slot, column):
        return pltpu.make_async_copy(self.source(t, s, column, self.c), self.own[t].at[slot, self.half(t, column)],
                                     self.load_sem.at[t, slot, column])

    def part_load(self, t, s, slot):
        return pltpu.make_async_copy(self.stages[t].at[s], self.part[t].at[slot], self.part_sem.at[t, slot])

    def ring_copy(self, t, s):
        return send(self.went[t].at[s], self.came[t].at[s], self.ring_s.at[t, s], self.ring_r.at[t, s],
                    self.next[self.plan.pieces[t][4]])

    def x_copy(self, t):
        return send(self.fin_s[t], self.fin_r[t], self.x_s.at[t], self.x_r.at[t], self.other_x)

    def each(self):
        return range(len(self.plan.pieces))

    def fetch(self, t, s, slot):
        for column in range(2):
            self.core_copy(t, s, column).wait_recv()
        self.part_load(t, s, slot).start()
        for column in range(2):
            self.own_load(t, s, slot, column).start()

    def total(self, t, s, slot):
        for column in range(2):
            self.own_load(t, s, slot, column).wait()
        self.part_load(t, s, slot).wait()
        return self.own[t][slot] + self.part[t][slot]

    def begin(self):
        for s in range(self.plan.ring):
            for t in self.each():
                for column in range(2):
                    self.core_copy(t, s, column).start()

    def load_first(self):
        for t in self.each():
            self.fetch(t, 0, 0)

    def first_hop(self):
        for t in self.each():
            self.fetch(t, 1, 1)
            self.went[t][0] = self.total(t, 0, 0).astype(BF)
            self.ring_copy(t, 0).start()

    def hop(self, s):
        slot = s % 2
        for t in self.each():
            self.fetch(t, s + 1, 1 - slot)
            value = self.total(t, s, slot)
            self.ring_copy(t, s - 1).wait_recv()
            self.went[t][s] = (value + self.came[t][s - 1].astype(F32)).astype(BF)
            self.ring_copy(t, s).start()

    def end_ring(self, t):
        final, height = self.final, self.plan.pieces[t][3]
        value = self.total(t, final, final % 2)
        self.ring_copy(t, final - 1).wait_recv()
        value = value + self.came[t][final - 1].astype(F32)
        self.last[t][0] = value[:height]
        self.last[t][1] = value[height:]

    def leave(self):
        count = len(self.plan.pieces)
        for t in self.each():
            self.end_ring(t)
            self.outs[t][...] = self.last[t][self.x]
            self.outs[count + t][...] = self.last[t][1 - self.x].astype(BF)
        self.drain()

    def finish(self):
        for t in self.each():
            self.end_ring(t)
            self.fin_s[t][...] = self.last[t][1 - self.x].astype(BF)
            self.x_copy(t).start()
        for t in self.each():
            self.x_copy(t).wait_recv()
            value = self.last[t][self.x] + self.fin_r[t][...].astype(F32)
            put(self.outs, self.plan.places[t], value)
        for t in self.each():
            self.x_copy(t).wait_send()
        self.drain()

    def drain(self):
        for t in self.each():
            for s in range(self.final):
                self.ring_copy(t, s).wait_send()
            for s in range(self.plan.ring):
                for column in range(2):
                    self.core_copy(t, s, column).wait_send()


class Plan:
    def __init__(self, ring, inputs, pieces, places, leave, shapes=()):
        self.ring, self.inputs, self.pieces, self.places = ring, inputs, pieces, places
        count = len(pieces)
        sizes = [(height, width) for _, _, width, height, _ in pieces]
        sems, vmem = pltpu.SemaphoreType.DMA, pltpu.VMEM
        self.out_shapes = [shape_of(hw, F32) for hw in shapes]
        if leave:
            self.out_shapes = [shape_of(hw, F32) for hw in sizes] + [shape_of(hw, BF) for hw in sizes]
        self.results = len(self.out_shapes)
        self.out_shapes += [shape_of((ring, 2 * h, wd), F32) for h, wd in sizes]
        self.out_specs = [pl.BlockSpec(memory_space=pltpu.VMEM)] * self.results + [ANY] * count
        self.outputs = len(self.out_shapes)
        self.scratch = (
            [vmem((2, 2 * h, wd), F32) for h, wd in sizes]
            + [vmem((2, 2 * h, wd), F32) for h, wd in sizes]
            + [vmem((ring - 1, 2 * h, wd), BF) for h, wd in sizes]
            + [vmem((ring - 1, 2 * h, wd), BF) for h, wd in sizes]
            + [vmem((2, h, wd), F32) for h, wd in sizes]
            + [vmem((h, wd), BF) for h, wd in sizes]
            + [vmem((h, wd), BF) for h, wd in sizes]
            + [sems((count, ring))] * 2
            + [sems((count, ring, 2))] * 2
            + [sems((count,))] * 2
            + [sems((count, 2, 2)), sems((count, 2))]
        )
        self.scratches = len(self.scratch)

    def left(self, results):
        count = len(self.pieces)
        return results[:count], results[count : 2 * count]

    def steps(self, refs):
        return Sums(self, refs)


def mlp_cuts(g):
    lanes = g.shape[1] // LANES
    last = lanes - lanes // 6
    return [0, (last + 1) // 2 * LANES, last * LANES, g.shape[1]]


def mlp_pieces(numbers, grads, parts, devices):
    pieces = []
    for i in parts:
        for way, (number, g) in enumerate(zip(numbers, grads)):
            cuts = mlp_cuts(g)
            pieces.append((number, cuts[i], cuts[i + 1] - cuts[i], g.shape[0] // devices, way))
    return pieces


def mlp_places(pieces):
    return [[(way, col, 0, width)] for _, col, width, _, way in pieces]


def time_plan(ring, g_in, g_out, devices):
    pieces = mlp_pieces((0, 1), (g_in, g_out), (0, 1), devices)
    return Plan(ring, 2, pieces, mlp_places(pieces), True)


def attn_pieces(g, number, devices):
    return [(number, i * D, D, g.shape[0] // devices, i % 2) for i in range(4)]


def attn_places(first):
    return [[(first, i * D, 0, D)] for i in range(3)] + [[(first + 1, 0, 0, D)]]


def frame_plan(ring, g_t, g_in, g_out, devices):
    pieces = mlp_pieces((1, 2), (g_in, g_out), (2,), devices)
    return Plan(ring, 3, attn_pieces(g_t, 0, devices) + pieces, attn_places(2) + mlp_places(pieces), True)


def last_plan(ring, g_s, devices):
    return Plan(ring, 1, attn_pieces(g_s, 0, devices), attn_places(0), False, attn_shapes(g_s, devices))


def attn_shapes(g, devices):
    return [(g.shape[0] // devices, 3 * D), (g.shape[0] // devices, D)]


def last_kernel(plan, left, made, *refs):
    places = [part for p in left for part in p.places]
    count = len(places)
    ((_,), grads, keeps, fins, (frames,), left_outs, own_outs, fins_r,
     (fin_send, fin_recv, send_sem, recv_sem), own) = split_refs(
        refs, 1, plan.inputs, count, count, 1, made, plan.outputs, count, 4)
    sums = plan.steps(grads + own_outs + own)
    early, late = EARLY_TILES * FT, LIVE - EARLY_TILES * FT
    mine, theirs = slot_for(sums.k), 4 - slot_for(sums.k)
    moves = (
        (packed(0, early, late), packed(2, early, late), sums.other_x),
        (packed(0, early, late), packed(mine, early, late), sums.other_c),
        (packed(2, 0, early), packed(theirs, 0, early), sums.other_c),
        (packed(2, early, late), packed(theirs, early, late), sums.other_c),
    )
    copies = [send(frames.at[src], frames.at[dst], send_sem.at[i], recv_sem.at[i], peer)
              for i, (src, dst, peer) in enumerate(moves)]

    def fin_copy(t):
        return send(fins[t], fins_r[t], fin_send.at[t], fin_recv.at[t], sums.other_x)

    greet(sums.peers)
    sums.begin()
    for copy in copies[:3]:
        copy.start()
    for t in range(count):
        fin_copy(t).start()
    sums.load_first()
    sums.first_hop()

    def body(s, carry):
        sums.hop(s)
        return carry

    lax.fori_loop(1, sums.final, body, 0)
    copies[0].wait_recv()
    copies[3].start()
    sums.finish()
    for t in range(count):
        fin_copy(t).wait_recv()
        value = keeps[t][...] + fins_r[t][...].astype(F32)
        put(left_outs, places[t], value)
    for t in range(count):
        fin_copy(t).wait_send()
    copies[0].wait_send()
    for copy in copies[1:]:
        copy.wait()


def scatter_last(frames, g, keeps, fins, plan, left, shapes):
    sems = pltpu.SemaphoreType.DMA
    vmem = pl.BlockSpec(memory_space=pltpu.VMEM)
    return pl.pallas_call(
        functools.partial(last_kernel, plan, left, len(shapes)),
        name="scatter_last",
        out_shape=[shape_of(frames.shape, frames.dtype)] + [shape_of(hw, F32) for hw in shapes] + plan.out_shapes,
        in_specs=[ANY] * 2 + [vmem] * len(keeps) + [ANY] * len(fins),
        out_specs=[ANY] + [vmem] * len(shapes) + plan.out_specs,
        scratch_shapes=[pltpu.VMEM(f.shape, f.dtype) for f in fins]
        + [sems((len(fins),))] * 2 + [sems((4,))] * 2 + plan.scratch,
        input_output_aliases={0: 0},
        compiler_params=pltpu.CompilerParams(
            collective_id=1, has_side_effects=True, vmem_limit_bytes=VMEM_LIMIT
        ),
    )(frames, g, *keeps, *fins)


def tuned(mesh):
    wide, n = mesh.shape["wide"], mesh.shape["narrow"]
    if n != 4 or wide != 2 * GRID or D % (8 * wide * n):
        return False
    for w in range(wide):
        for k in range(n):
            device = mesh.devices[w, k]
            here = (getattr(device, "coords", None), getattr(device, "core_on_chip", None))
            if here[0] is None or tuple(here[0]) != (k // 2, w % 2, w // 2) or here[1] != k % 2:
                return False
    return True


def exchange(x):
    return lax.all_to_all(x, ALL, split_axis=0, concat_axis=0, tiled=True)


def shift_clips(clips, back):
    n = lax.axis_size("narrow")
    parts = [clips[0]]
    for j in range(1, n):
        step = -j if back else j
        parts.append(lax.ppermute(clips[j], "narrow", [(s, (s + step) % n) for s in range(n)]))
    return jnp.stack(parts)


def local(fast, clips, t_emb, lengths, task, w_mod, b_mod, w_qkv_s, w_o_s, b_o_s, w_qkv_t, w_o_t, b_o_t,
          w_in, b_in, w_out, b_out, cotangent):
    n = lax.axis_size("narrow")
    wide = lax.axis_size("wide")
    devices = n * wide
    part = w_mod.shape[0]
    mod_cols = w_mod.shape[1] // devices
    rank = lax.axis_index("narrow")
    slots = jnp.arange(n, dtype=jnp.int32)
    from_clip = (rank - slots) % n
    recv_len = lengths.reshape(n, n)[from_clip, slots]
    recv_task = task.reshape(n, n, FR)[from_clip, slots]
    ends = jnp.cumsum(recv_len)
    starts = ends - recv_len
    ids = jnp.arange(LIVE, dtype=jnp.int32)
    source = jnp.sum((ends[None, :] <= ids[:, None]).astype(jnp.int32), axis=1)
    within = ids - starts[source]
    pack_rows = source * FR + within
    row_choice = source * 2 + recv_task[source, within]
    frame_ids = jnp.arange(FR, dtype=jnp.int32)
    live_back = frame_ids[None, :] < recv_len[:, None]
    unpack_rows = jnp.where(live_back, starts[:, None] + frame_ids[None, :], 0).reshape(-1)
    row_id = jnp.arange(64, dtype=jnp.int32)
    col_id = jnp.arange(LANES, dtype=jnp.int32) % 64
    seg = (
        (row_id[:, None] // LIVE == col_id[None, :] // LIVE)
        & (source[row_id % LIVE][:, None] == source[col_id % LIVE][None, :])
    ).astype(F32)

    def gather(w):
        return lax.all_gather(w, ALL, axis=0, tiled=True)

    def across(value):
        return lax.ppermute(value, "narrow", [(k, (k + n // 2) % n) for k in range(n)])

    if fast:
        flat = (w_qkv_s, w_o_s, w_qkv_t, w_o_t, w_in)
        side, clips = lax.optimization_barrier((jnp.concatenate(flat, axis=1), clips))
        far, far_out = across(side), across(w_out)
        cuts = [sum(a.shape[1] for a in flat[: i + 1]) for i in range(len(flat) - 1)]
        *far_attn, far_in = jnp.split(far, cuts, axis=1)
        frames = shift_clips(clips, False)
        wqkv_s, wo_s, wqkv_t, wo_t = gather_first(flat[:4], far_attn, wide, n)
    else:
        far_in = far_out = None
        frames = shift_clips(clips, False)
        win, wout, wqkv_t, wo_t, wqkv_s, wo_s = [gather(w) for w in (w_in, w_out, w_qkv_t, w_o_t, w_qkv_s, w_o_s)]
    frames = jnp.take(frames.reshape(n * FR, PATCHES, D), pack_rows, axis=0, mode="clip")

    wm = jnp.swapaxes(w_mod.reshape(part, devices, mod_cols), 0, 1).reshape(devices, -1)
    emb = jnp.broadcast_to(t_emb.reshape(1, -1), (devices, t_emb.size))
    small = jnp.concatenate([b_o_s, b_o_t, b_in, b_out])
    small_all = jnp.broadcast_to(small[None], (devices, small.size))
    got = exchange(jnp.concatenate([wm, emb, small_all], axis=1))
    wm_cols = got[:, : part * mod_cols].reshape(D, mod_cols)
    emb_all = got[:, part * mod_cols : part * mod_cols + t_emb.size].reshape(-1, D)
    small_got = got[:, part * mod_cols + t_emb.size :]
    b1 = b_o_s.size
    bias_s = small_got[:, :b1].reshape(1, -1).astype(F32)
    bias_t = small_got[:, b1 : 2 * b1].reshape(1, -1).astype(F32)
    bias_in = small_got[:, 2 * b1 : 2 * b1 + b_in.size].reshape(1, -1).astype(F32)
    bias_out = small_got[:, 2 * b1 + b_in.size :].reshape(1, -1).astype(F32)
    emb_f = emb_all.astype(F32)
    silu_low = (emb_f * jax.nn.sigmoid(emb_f)).astype(BF)
    mod_part = dot(silu_low, wm_cols) + b_mod.astype(F32)[None]
    mod_part = mod_part.reshape(wide, n, n, 2, mod_cols)
    mod_part = jnp.stack([jnp.roll(mod_part[:, :, c], c, axis=1) for c in range(n)], axis=2)
    mod_rows = exchange(mod_part.reshape(devices, -1)).reshape(devices, 2 * n, mod_cols)
    mod_rows = jnp.swapaxes(mod_rows, 0, 1).reshape(2 * n, 9, D)
    mod = jnp.swapaxes(mod_rows[row_choice], 0, 1)

    def carry(js, shard, other, number):
        return forward_carrier(cotangent, js, shard, other, wide, n, number) if fast else None

    *half, x1, qkv1, o1, a1 = run_frame_forward(
        frames, mod, wqkv_s, wo_s, bias_s, carry((2,), w_in, far_in, 2))
    *odd, x2, qkv2, o2, a2 = run_time_forward(
        x1, mod, seg, wqkv_t, wo_t, bias_t, carry((1, 3), w_out, far_out, 3))
    if fast:
        (half, win), (odd, wout) = half, odd
        cots = jnp.stack([cotangent[0], odd[0], half[0], odd[1]])
    else:
        cots = shift_clips(cotangent, False)
    dy = run_turn_frames(cots.reshape(n * FR, PATCHES, D), pack_rows)
    out, dx2, g_in, g_out, gb_in, gb_out, dmod3 = run_mlp(x2, dy, mod, win, bias_in, wout, bias_out, out_carrier(n, 6) if fast else None)

    own_len = lengths.reshape(n, n)[rank]
    own_live = frame_ids[None, :] < own_len[:, None]

    def spread(frames):
        return jnp.take(frames, unpack_rows, axis=0, mode="clip").reshape(n, FR, PATCHES, D)

    def only_live(parts):
        return jnp.where(own_live[:, :, None, None], parts, jnp.zeros((), parts.dtype))

    def scatter(g):
        return lax.psum_scatter(g.astype(BF), ALL, scatter_dimension=0, tiled=True).astype(F32)

    if fast:
        ahead = lengths.reshape(n, n)[(rank + slots[:, None] - slots[None, :]) % n, slots[None, :]]
        own_start = jnp.sum(jnp.where(slots[None, :] < slots[:, None], ahead, 0), axis=1)
        own_rows = slots[:, None] * LIVE + own_start[:, None] + frame_ids[None, :]
        own_rows = jnp.where(own_live, own_rows, -1).reshape(-1)
        plan_a = time_plan(wide, g_in, g_out, devices)
        out, *got, dx1, g_t, gb_t, dmod2 = run_time_back(
            x1, dx2, mod, seg, qkv2, o2, a2, wqkv_t, wo_t, share_carrier(out, [g_in, g_out], plan_a, 4))
        keeps, fins = plan_a.left(got)
        plan_b = frame_plan(wide, g_t, g_in, g_out, devices)
        out, dx0, *got, g_s, gb_s, dmod1 = run_frame_back(
            frames, dx1, mod, qkv1, o1, a1, wqkv_s, wo_s, relay_carrier(out, [g_t, g_in, g_out], plan_b, 5))
        more_keeps, more_fins = plan_b.left(got)
        dx0, s_in, s_out, s_qkv_t, s_o_t, s_qkv_s, s_o_s = scatter_last(
            dx0, g_s, keeps + more_keeps, fins + more_fins, last_plan(wide, g_s, devices), (plan_a, plan_b),
            [w_in.shape, w_out.shape] + attn_shapes(g_t, devices))[:7]
        layer_out = run_unpack(out, own_rows).reshape(n, FR, PATCHES, D)
        grad_clips = run_unpack(dx0, own_rows).reshape(n, FR, PATCHES, D)
    else:
        dx1, g_t, gb_t, dmod2 = run_time_back(x1, dx2, mod, seg, qkv2, o2, a2, wqkv_t, wo_t)
        dx0, g_s, gb_s, dmod1 = run_frame_back(frames, dx1, mod, qkv1, o1, a1, wqkv_s, wo_s)
        layer_out = only_live(shift_clips(spread(out), True))
        grad_clips = only_live(shift_clips(spread(dx0), True))
        s_in, s_out, s_t, s_s = [scatter(g) for g in (g_in, g_out, g_t, g_s)]
        s_qkv_t, s_o_t, s_qkv_s, s_o_s = s_t[:, : 3 * D], s_t[:, 3 * D :], s_s[:, : 3 * D], s_s[:, 3 * D :]

    grad_frames = jnp.swapaxes(jnp.concatenate([dmod1, dmod2, dmod3], axis=0), 0, 1).reshape(LIVE, 9 * D)
    chooser = (row_choice[:, None] == jnp.arange(2 * n, dtype=jnp.int32)[None, :]).astype(F32)
    grad_rows = lax.dot_general(
        chooser, grad_frames, (((0,), (0,)), ((), ())), precision=lax.Precision.HIGHEST
    ).astype(BF)
    d_cols = exchange(jnp.swapaxes(grad_rows.reshape(2 * n, devices, mod_cols), 0, 1).reshape(devices, -1))
    d_cols = d_cols.reshape(wide, n, n, 2, mod_cols)
    d_cols = jnp.stack([jnp.roll(d_cols[:, :, c], -c, axis=1) for c in range(n)], axis=2)
    d_cols = d_cols.reshape(devices * 2 * n, mod_cols)
    grad_b_mod = jnp.sum(d_cols.astype(F32), axis=0)
    gwm_cols = dot_tn(silu_low, d_cols)
    g_emb = dot_nt(d_cols, wm_cols)
    gb_all = jnp.concatenate(
        [gb_s.reshape(devices, -1), gb_t.reshape(devices, -1), gb_in.reshape(devices, -1),
         gb_out.reshape(devices, -1)], axis=1)
    final = exchange(jnp.concatenate(
        [gwm_cols.reshape(devices, -1), g_emb.reshape(devices, -1), gb_all], axis=1))
    cut1 = part * mod_cols
    cut2 = cut1 + t_emb.size
    grad_w_mod = jnp.swapaxes(final[:, :cut1].reshape(devices, part, mod_cols), 0, 1).reshape(part, -1)
    emb_own = t_emb.astype(F32)
    sig = jax.nn.sigmoid(emb_own)
    grad_emb = jnp.sum(final[:, cut1:cut2], axis=0).reshape(t_emb.shape)
    grad_t_emb = (grad_emb * (sig * (1.0 + emb_own * (1.0 - sig)))).astype(BF)
    gb = jnp.sum(final[:, cut2:], axis=0)
    return (
        layer_out,
        grad_clips,
        grad_t_emb,
        grad_w_mod,
        grad_b_mod,
        s_qkv_s,
        s_o_s,
        gb[:b1],
        s_qkv_t,
        s_o_t,
        gb[b1 : 2 * b1],
        s_in,
        gb[2 * b1 : 2 * b1 + b_in.size],
        s_out,
        gb[2 * b1 + b_in.size :],
    )


def solution(mesh):
    full = P(ALL)
    placed = (full, full, P("wide"), P("wide")) + (full,) * 13
    return jax.shard_map(functools.partial(local, tuned(mesh)), mesh=mesh, in_specs=placed, out_specs=(full,) * 15, check_vma=False)
```
